32 devices in a mesh: gx: 4 (over x, core), gy: 8 (over z, y).
Axes of the slice: x: 2, y: 2, z: 4, core: 2. Of those that a mesh axis runs over, the one named last changes fastest.
Arguments:
- target_ids: int32 [2, 4, 512], P(None, 'gx', 'gy'), may hold values from 0 to 16383
- labels: int32 [2, 4, 512], P(None, 'gx', 'gy'), may hold values from 0 to 16383
- lengths: int32 [2, 4], replicated, may hold values from 128 to 512, as said below
- memory: bfloat16 [2, 4, 1024, 512], P(None, 'gx', 'gy'), may hold values from -6 to 6
- embedding: bfloat16 [16384, 512], P(('gx', 'gy')), may hold values from -6 to 6
- head: bfloat16 [16384, 512], P(('gx', 'gy')), may hold values from -0.5 to 0.5
- gain_self: bfloat16 [512], P(('gx', 'gy')), may hold values from 0.5 to 1.5
- w_query: bfloat16 [512, 384], P(('gx', 'gy')), may hold values from -0.0625 to 0.0625
- w_key: bfloat16 [512, 384], P(('gx', 'gy')), may hold values from -0.25 to 0.25
- w_value: bfloat16 [512, 384], P(('gx', 'gy')), may hold values from -0.25 to 0.25
- w_out: bfloat16 [512, 384], P(('gx', 'gy')), may hold values from -1.25 to 1.25
- relative_bias: bfloat16 [6, 32], replicated, may hold values from -4 to 4
- gain_cross: bfloat16 [512], P(('gx', 'gy')), may hold values from 0.5 to 1.5
- c_query: bfloat16 [512, 384], P(('gx', 'gy')), may hold values from -0.0625 to 0.0625
- c_key: bfloat16 [512, 384], P(('gx', 'gy')), may hold values from -0.25 to 0.25
- c_value: bfloat16 [512, 384], P(('gx', 'gy')), may hold values from -0.25 to 0.25
- c_out: bfloat16 [512, 384], P(('gx', 'gy')), may hold values from -1.25 to 1.25
- gain_ff: bfloat16 [512], P(('gx', 'gy')), may hold values from 0.5 to 1.5
- w_gate: bfloat16 [512, 1024], P(('gx', 'gy')), may hold values from -0.25 to 0.25
- w_up: bfloat16 [512, 1024], P(('gx', 'gy')), may hold values from -0.25 to 0.25
- w_down: bfloat16 [512, 1024], P(('gx', 'gy')), may hold values from -0.1875 to 0.1875
- gain_final: bfloat16 [512], P(('gx', 'gy')), may hold values from 0.5 to 1.5
Outputs:
- loss: float32 [], replicated
- memory_grad: float32 [2, 4, 1024, 512], P(None, 'gx', 'gy')
- embedding_grad: float32 [16384, 512], P(('gx', 'gy'))
- head_grad: float32 [16384, 512], P(('gx', 'gy'))
- gain_self_grad: float32 [512], P(('gx', 'gy'))
- w_query_grad: float32 [512, 384], P(('gx', 'gy'))
- w_key_grad: float32 [512, 384], P(('gx', 'gy'))
- w_value_grad: float32 [512, 384], P(('gx', 'gy'))
- w_out_grad: float32 [512, 384], P(('gx', 'gy'))
- rel_bias_grad: float32 [6, 32], replicated
- gain_cross_grad: float32 [512], P(('gx', 'gy'))
- c_query_grad: float32 [512, 384], P(('gx', 'gy'))
- c_key_grad: float32 [512, 384], P(('gx', 'gy'))
- c_value_grad: float32 [512, 384], P(('gx', 'gy'))
- c_out_grad: float32 [512, 384], P(('gx', 'gy'))
- gain_ff_grad: float32 [512], P(('gx', 'gy'))
- w_gate_grad: float32 [512, 1024], P(('gx', 'gy'))
- w_up_grad: float32 [512, 1024], P(('gx', 'gy'))
- w_down_grad: float32 [512, 1024], P(('gx', 'gy'))
- gain_final_grad: float32 [512], P(('gx', 'gy'))
The draws below stay inside these ranges and needn't reach their ends.
Inputs may be any that keep to these rules, and one draw needn't show every extreme that they name: `lengths`: each sequence's count of live target positions; some sequence has all 512, some has a quarter of 512.
All inputs are finite; a program needn't handle non-finite values.
Results may differ from the reference program's by a relative error of at most 0.024.
The reference program's roundings to bfloat16 on the way count: a program that leaves them out, or rounds other values in their place, can miss the bound.
Values may be sent and summed in bfloat16 or wider, within the bound.
A program may use at most 320 MiB of HBM per device.

```python
import math
import jax
import jax.numpy as jnp
import numpy as np
from jax import lax

D = 512
HEADS = 6
HEAD = 64
FF = 1024
BUCKETS = 32
HD = 384
VOCAB = 16384
MEM = 1024
MICRO = 2
SEQ = 512
NSEQ = 4


def draw_lengths(key, part):
    first, second = jax.random.split(key, 2)
    number = MICRO * NSEQ
    values = jax.random.randint(first, (number,), SEQ // 4, SEQ + 1)
    order = jax.random.permutation(second, number)
    values = jnp.where(order == 0, SEQ, values)
    values = jnp.where(order == 1, SEQ // 4, values)
    return values.reshape(MICRO, NSEQ).astype(jnp.int32)


def set_ends(values, own_key, smallest, largest):
    longest = values.shape.index(max(values.shape))
    spots = []
    for shift in (0, 1):
        where = [jax.random.randint(jax.random.fold_in(own_key, axis), (), 0, length) for axis, length in enumerate(values.shape)]
        where[longest] = (where[longest] + shift) % values.shape[longest]
        spots.append(tuple(where))
    return values.at[spots[0]].set(smallest).at[spots[1]].set(largest)


def block_levels(own_key, shape, shards, smallest, top_value):
    level = 1.0
    for position, blocks in shards:
        draws = jax.random.uniform(jax.random.fold_in(jax.random.fold_in(own_key, 6), position), (blocks,), jnp.float32, smallest / len(shards), top_value / len(shards))
        level = level * jnp.repeat(jnp.exp(draws), shape[position] // blocks).reshape((-1,) + (1,) * (len(shape) - 1 - position))
    return level


def rank_bounds(count, slope):
    weights = [(1 << 20) // math.isqrt(grade ** slope) + 1 for grade in range(1, count + 1)]
    deviation = 1 + sum(weights) // (1 << 30)
    return np.cumsum(np.array([max(1, weight // deviation) for weight in weights]))


def ranked_ids(own_key, dims, number_of, skew):
    grid = rank_bounds(number_of, skew)
    ticket = jax.random.randint(jax.random.fold_in(own_key, 1), dims, 0, int(grid[number_of - 1]))
    standing = jnp.searchsorted(jnp.asarray(grid, jnp.int32), ticket, side="right")
    return jax.random.permutation(jax.random.fold_in(own_key, 2), number_of)[standing].astype(jnp.int32)


def centred(key, dims, scale, most, cuts=(), kind=jnp.bfloat16):
    level = block_levels(key, dims, cuts, -0.22, 0.18) if cuts else 1.0
    values = jax.random.normal(key, dims, jnp.float32) * scale * level
    return jnp.minimum(jnp.maximum(values, -most), most).astype(kind)


def setup_inputs(seed: int = 0) -> dict:
    key_list = jax.random.split(jax.random.key(seed), 23)
    target_ids = set_ends(ranked_ids(key_list[0], (MICRO, NSEQ, SEQ), VOCAB, 2), jax.random.fold_in(key_list[0], 3), 0, VOCAB - 1).astype(jnp.int32)
    labels = set_ends(ranked_ids(key_list[1], (MICRO, NSEQ, SEQ), VOCAB, 2), jax.random.fold_in(key_list[1], 3), 0, VOCAB - 1).astype(jnp.int32)
    lengths = draw_lengths(jax.random.fold_in(key_list[22], 71), 0)
    memory = centred(key_list[3], (MICRO, NSEQ, MEM, D), 1.0, 6.0, ((1, 4), (2, 8)))
    embedding = centred(key_list[4], (VOCAB, D), 1.0, 6.0, ((0, 32),))
    head = centred(key_list[5], (VOCAB, D), (D // 4) ** -0.5, 0.5, ((0, 32),))
    gain_self = jnp.clip(1.0 + 0.1 * jax.random.normal(key_list[6], (D,), jnp.float32), 0.5, 1.5).astype(jnp.bfloat16)
    w_query = centred(key_list[7], (D, HD), (16 * D) ** -0.5, 0.0625, ((0, 32),))
    w_key = centred(key_list[8], (D, HD), D ** -0.5, 0.25, ((0, 32),))
    w_value = centred(key_list[9], (D, HD), D ** -0.5, 0.25, ((0, 32),))
    w_out = centred(key_list[10], (D, HD), (HD // 16) ** -0.5, 1.25, ((0, 32),))
    relative_bias = centred(key_list[11], (HEADS, BUCKETS), 1.0, 4.0)
    gain_cross = jnp.clip(1.0 + 0.1 * jax.random.normal(key_list[12], (D,), jnp.float32), 0.5, 1.5).astype(jnp.bfloat16)
    c_query = centred(key_list[13], (D, HD), (16 * D) ** -0.5, 0.0625, ((0, 32),))
    c_key = centred(key_list[14], (D, HD), D ** -0.5, 0.25, ((0, 32),))
    c_value = centred(key_list[15], (D, HD), D ** -0.5, 0.25, ((0, 32),))
    c_out = centred(key_list[16], (D, HD), (HD // 16) ** -0.5, 1.25, ((0, 32),))
    gain_ff = jnp.clip(1.0 + 0.1 * jax.random.normal(key_list[17], (D,), jnp.float32), 0.5, 1.5).astype(jnp.bfloat16)
    w_gate = centred(key_list[18], (D, FF), D ** -0.5, 0.25, ((0, 32),))
    w_up = centred(key_list[19], (D, FF), D ** -0.5, 0.25, ((0, 32),))
    w_down = centred(key_list[20], (D, FF), FF ** -0.5, 0.1875, ((0, 32),))
    gain_final = jnp.clip(1.0 + 0.1 * jax.random.normal(key_list[21], (D,), jnp.float32), 0.5, 1.5).astype(jnp.bfloat16)
    return {"target_ids": target_ids, "labels": labels, "lengths": lengths, "memory": memory, "embedding": embedding, "head": head, "gain_self": gain_self, "w_query": w_query, "w_key": w_key, "w_value": w_value, "w_out": w_out, "relative_bias": relative_bias, "gain_cross": gain_cross, "c_query": c_query, "c_key": c_key, "c_value": c_value, "c_out": c_out, "gain_ff": gain_ff, "w_gate": w_gate, "w_up": w_up, "w_down": w_down, "gain_final": gain_final}


@jax.custom_vjp
def low(v):
    return lax.optimization_barrier(v.astype(jnp.bfloat16)).astype(jnp.float32)

@jax.custom_vjp
def low_back(v):
    return v

def low_keep(v):
    return (low(v), None)

def low_pass(kept, grad):
    return (grad,)

def back_keep(v):
    return (v, None)

def back_low(kept, grad):
    return (low(grad),)
low.defvjp(low_keep, low_pass)
low_back.defvjp(back_keep, back_low)
eps = 1e-06
masked_score = -1000000000.0

def bucket_edges():
    edges = []
    for target in range(1, 32):
        if target < 16:
            edges.append(target)
        else:
            found = 0
            for distance in range(16, 4096):
                value = 16 + int(math.log(distance / 16.0) / math.log(8.0) * 16.0)
                if found == 0 and value >= target:
                    found = distance
            edges.append(found)
    return edges

def bucket_of(distance):
    edges = jnp.array(bucket_edges(), dtype=jnp.int32)
    return lax.optimization_barrier(jnp.sum((distance[..., None] >= edges).astype(jnp.int32), axis=-1)).astype(jnp.int32)

def rms_norm(rows, gain):
    return rows * lax.rsqrt(lax.optimization_barrier(jnp.mean(rows * rows, axis=-1, keepdims=True)) + eps) * gain

def gelu_tanh(value):
    return 0.5 * value * (1.0 + jnp.tanh(0.7978845608028654 * (value + 0.044715 * value * value * value)))

def matmul(left, right):
    return jnp.matmul(left, right, precision=lax.Precision.HIGHEST)

def both(value):
    return low_back(low(value))

def attend(query, keys, values, bias_vector, mask):
    groups, rows, _ = query.shape
    query_heads = query.reshape(groups, rows, HEADS, HEAD)
    key_heads = keys.reshape(groups, keys.shape[1], HEADS, HEAD)
    value_heads = values.reshape(groups, values.shape[1], HEADS, HEAD)
    scores = jnp.einsum('gqhe,gkhe->ghqk', query_heads, key_heads, precision=lax.Precision.HIGHEST)
    if bias_vector is not None:
        scores = scores + bias_vector[None]
    if mask is not None:
        scores = jnp.where(mask[:, None], scores, masked_score)
    scores = low_back(scores)
    highest = lax.optimization_barrier(jnp.max(scores, axis=-1, keepdims=True))
    log_total = highest + jnp.log(lax.optimization_barrier(jnp.sum(jnp.exp(scores - highest), axis=-1, keepdims=True)))
    shares = jnp.exp(scores - log_total)
    output = jnp.einsum('ghqk,gkhe->gqhe', low(shares), value_heads, precision=lax.Precision.HIGHEST)
    return both(output.reshape(groups, rows, HEADS * HEAD))

def group_loss(group_ids, group_labels, group_lengths, group_memory, weights, bucket):
    embedding, head, gain_self, w_query, w_key, w_value, w_out, relative_bias, gain_cross, c_query, c_key, c_value, c_out, gain_ff, w_gate, w_up, w_down, gain_final = weights
    positions = jnp.arange(SEQ, dtype=jnp.int32)
    resid0 = low_back(embedding[group_ids])
    normed = low(rms_norm(resid0, gain_self))
    query = both(matmul(normed, w_query))
    keys = both(matmul(normed, w_key))
    values = both(matmul(normed, w_value))
    bias_vector = relative_bias[:, bucket]
    mask = (positions[None, :] <= positions[:, None])[None] & (positions[None, None, :] < group_lengths[:, None, None])
    attended = attend(query, keys, values, bias_vector, mask)
    resid1 = resid0 + low_back(matmul(attended, w_out.T))
    normed = low(rms_norm(resid1, gain_cross))
    query = both(matmul(normed, c_query))
    keys = both(matmul(group_memory, c_key))
    values = both(matmul(group_memory, c_value))
    attended = attend(query, keys, values, None, None)
    resid2 = resid1 + low_back(matmul(attended, c_out.T))
    normed = low(rms_norm(resid2, gain_ff))
    gate = low_back(matmul(normed, w_gate))
    upper = low_back(matmul(normed, w_up))
    hidden = low(gelu_tanh(gate) * upper)
    resid3 = resid2 + low_back(matmul(hidden, w_down.T))
    final = low(rms_norm(resid3, gain_final))
    total_rows = final.shape[0] * final.shape[1]
    block = math.gcd(total_rows, 512)
    live = (positions[None, :] < group_lengths[:, None]).astype(jnp.float32)

    def block_loss(pieces):
        states, targets, alive = pieces
        logits = low_back(matmul(states, head.T))
        highest = lax.optimization_barrier(jnp.max(logits, axis=-1, keepdims=True))
        log_total = highest[:, 0] + jnp.log(lax.optimization_barrier(jnp.sum(jnp.exp(logits - highest), axis=-1)))
        picked = jnp.take_along_axis(logits, targets[:, None].astype(jnp.int32), axis=1)[:, 0]
        return jnp.sum(alive * (log_total - picked))
    sums = lax.map(jax.checkpoint(block_loss), (final.reshape(total_rows // block, block, D), group_labels.reshape(total_rows // block, block), live.reshape(total_rows // block, block)))
    return jnp.sum(sums)

def reference(target_ids, labels, lengths, memory, embedding, head, gain_self, w_query, w_key, w_value, w_out, relative_bias, gain_cross, c_query, c_key, c_value, c_out, gain_ff, w_gate, w_up, w_down, gain_final):
    seqs = MICRO * NSEQ
    group = math.gcd(seqs, max(1, 4096 // SEQ))
    rounds = seqs // group
    token_rows = target_ids.reshape(rounds, group, SEQ)
    label_rows = labels.reshape(rounds, group, SEQ)
    seq_lengths = lengths.reshape(rounds, group)
    positions = jnp.arange(SEQ, dtype=jnp.int32)
    bucket = bucket_of(jnp.maximum(positions[:, None] - positions[None, :], 0))
    floats = (memory.astype(jnp.float32).reshape(rounds, group, MEM, D), embedding.astype(jnp.float32), head.astype(jnp.float32), gain_self.astype(jnp.float32), w_query.astype(jnp.float32), w_key.astype(jnp.float32), w_value.astype(jnp.float32), w_out.astype(jnp.float32), relative_bias.astype(jnp.float32), gain_cross.astype(jnp.float32), c_query.astype(jnp.float32), c_key.astype(jnp.float32), c_value.astype(jnp.float32), c_out.astype(jnp.float32), gain_ff.astype(jnp.float32), w_gate.astype(jnp.float32), w_up.astype(jnp.float32), w_down.astype(jnp.float32), gain_final.astype(jnp.float32))

    def total_loss(memory_f, *weights):

        def step_fn(carry, pieces):
            return (carry + group_loss(pieces[0], pieces[1], pieces[2], pieces[3], weights, bucket), None)
        total, _ = lax.scan(jax.checkpoint(step_fn), jnp.zeros((), jnp.float32), (token_rows, label_rows, seq_lengths, memory_f))
        return total
    total, pullback = jax.vjp(total_loss, *floats)
    grads = pullback(jnp.ones((), jnp.float32))
    loss = total / jnp.sum(lengths).astype(jnp.float32)
    memory_grad = grads[0].reshape(MICRO, NSEQ, MEM, D)
    return (loss, memory_grad, grads[1], grads[2], grads[3], grads[4], grads[5], grads[6], grads[7], grads[8], grads[9], grads[10], grads[11], grads[12], grads[13], grads[14], grads[15], grads[16], grads[17], grads[18])
```

```python
import functools
import math

import jax
import jax.numpy as jnp
from jax import lax
from jax.experimental import pallas as pl
from jax.experimental.pallas import tpu as pltpu
from jax.sharding import PartitionSpec as P

HEADS = 6
HEAD = 64
HD = HEADS * HEAD
BUCKETS = 32
GAIN_PAD = 128

eps = 1e-06
masked_score = -1000000000.0
bf16 = jnp.bfloat16
f32 = jnp.float32


def bits_of(axis, size):
    weights = []
    weight = size // 2
    while weight >= 1:
        weights.append((axis, weight))
        weight //= 2
    return tuple(weights)


def bit_value(bit):
    return (lax.axis_index(bit[0]) // bit[1]) % 2


def partner_of(bit):
    axis, weight = bit
    index = lax.axis_index(axis)
    return {axis: index + weight - 2 * weight * bit_value(bit)}


class Gather:
    def __init__(self, block, bits, order, halves=False):
        self.value = block
        self.bits = bits
        self.order = order
        self.halves = halves
        shape = block.shape[1:] if halves else block.shape
        self.stages = len(order)
        self.out = jax.ShapeDtypeStruct((2,) * len(bits) + shape, block.dtype)
        self.in_spec = pl.BlockSpec(memory_space=pltpu.VMEM)
        self.out_spec = pl.BlockSpec(memory_space=pl.ANY)
        self.scratch = [
            pltpu.SemaphoreType.DMA((self.stages,)),
            pltpu.SemaphoreType.DMA((self.stages,)),
            pltpu.SemaphoreType.DMA,
        ]

    def prepare(self, refs):
        self.source, self.target, self.send, self.recv, self.local_sem = refs
        self.own = [bit_value(bit) for bit in self.bits]
        self.local = pltpu.make_async_copy(
            self.source.at[self.own[self.order[0]]] if self.halves else self.source,
            self.target.at[tuple(self.own)],
            self.local_sem,
        )
        self.local.start()

    def start(self, stage):
        if stage == 1:
            self.local.wait()
        known = self.order[:stage]
        where = tuple(
            slice(None) if place in known else self.own[place] for place in range(len(self.bits))
        )
        if stage == 0:
            first = self.own[self.order[0]]
            source = self.source.at[1 - first] if self.halves else self.source
        else:
            source = self.target.at[where]
        self.copy = pltpu.make_async_remote_copy(
            src_ref=source,
            dst_ref=self.target.at[where],
            send_sem=self.send.at[stage],
            recv_sem=self.recv.at[stage],
            device_id=partner_of(self.bits[self.order[stage]]),
            device_id_type=pl.DeviceIdType.MESH,
        )
        self.copy.start()

    def finish(self, stage):
        self.copy.wait()
        if stage == self.stages - 1 and self.stages == 1:
            self.local.wait()


class Scatter:
    def __init__(self, value, bits, order, out_dtype=f32, halves=False):
        self.value = value
        self.bits = bits
        self.order = order
        self.halves = halves
        self.stages = len(order)
        count = len(bits)
        block = value.shape[count:]
        self.block = block
        self.out = jax.ShapeDtypeStruct(((2,) if halves else ()) + block, out_dtype)
        self.in_spec = pl.BlockSpec(memory_space=pltpu.VMEM)
        self.out_spec = pl.BlockSpec(memory_space=pltpu.VMEM)
        self.scratch = [
            pltpu.VMEM((2,) * (count - 1 - stage) + block, value.dtype)
            for stage in range(self.stages)
        ] + [
            pltpu.SemaphoreType.DMA((self.stages,)),
            pltpu.SemaphoreType.DMA((self.stages,)),
        ]

    def prepare(self, refs):
        self.source, self.target = refs[0], refs[1]
        self.landing = refs[2 : 2 + self.stages]
        self.send, self.recv = refs[2 + self.stages :]
        self.own = [bit_value(bit) for bit in self.bits]

    def start(self, stage):
        held = self.source if stage == 0 else self.landing[stage - 1]
        left = [place for place in range(len(self.bits)) if place not in self.order[:stage]]
        this = self.order[stage]
        where = tuple(1 - self.own[place] if place == this else slice(None) for place in left)
        self.copy = pltpu.make_async_remote_copy(
            src_ref=held.at[where],
            dst_ref=self.landing[stage],
            send_sem=self.send.at[stage],
            recv_sem=self.recv.at[stage],
            device_id=partner_of(self.bits[this]),
            device_id_type=pl.DeviceIdType.MESH,
        )
        self.copy.start()

    def finish(self, stage):
        held = self.source if stage == 0 else self.landing[stage - 1]
        landed = self.landing[stage]
        left = [place for place in range(len(self.bits)) if place not in self.order[:stage]]
        this = self.order[stage]
        last = stage == self.stages - 1
        self.copy.wait()
        rows, columns = self.block
        step = min(rows, max(16, 32768 // columns // 16 * 16))
        while rows % step:
            step -= 16
        pieces = rows // step
        free = len(left) - 1
        own = self.own[this]

        def piece(number, carry):
            place_rows = pl.ds(pl.multiple_of((number % pieces) * step, step), step)
            which = number // pieces
            inner = []
            for level in reversed(range(free)):
                inner.append((which // (2**level)) % 2)
            inner = tuple(inner)
            spot = left.index(this)
            outer = inner[:spot] + (own,) + inner[spot:]
            mine = held[outer + (place_rows,)]
            theirs = landed[inner + (place_rows,)]
            if not last:
                landed[inner + (place_rows,)] = mine + theirs
            elif self.halves:
                self.target[(own, place_rows)] = mine.astype(self.target.dtype)
                self.target[(1 - own, place_rows)] = theirs.astype(self.target.dtype)
            else:
                self.target[(place_rows,)] = (mine.astype(f32) + theirs.astype(f32)).astype(
                    self.target.dtype
                )
            return carry

        lax.fori_loop(0, pieces * 2**free, piece, 0)


def exchange(name, collective_id, jobs):
    sizes = [len(job.scratch) for job in jobs]
    bits = []
    for job in jobs:
        for bit in job.bits:
            if bit not in bits:
                bits.append(bit)

    def kernel(*refs):
        count = len(jobs)
        scratch = refs[2 * count :]
        offset = 0
        barrier = pltpu.get_barrier_semaphore()
        for bit in bits:
            pl.semaphore_signal(
                barrier, inc=1, device_id=partner_of(bit), device_id_type=pl.DeviceIdType.MESH
            )
        for place, job in enumerate(jobs):
            job.prepare(
                (refs[place], refs[count + place]) + tuple(scratch[offset : offset + sizes[place]])
            )
            offset += sizes[place]
        pl.semaphore_wait(barrier, len(bits))
        for stage in range(max(job.stages for job in jobs)):
            for job in jobs:
                if stage < job.stages:
                    job.start(stage)
            for job in jobs:
                if stage < job.stages:
                    job.finish(stage)

    outs = pl.pallas_call(
        kernel,
        name=name,
        out_shape=tuple(job.out for job in jobs),
        in_specs=[job.in_spec for job in jobs],
        out_specs=tuple(job.out_spec for job in jobs),
        scratch_shapes=[item for job in jobs for item in job.scratch],
        compiler_params=pltpu.CompilerParams(
            collective_id=collective_id, has_side_effects=True, vmem_limit_bytes=60 * 1024 * 1024
        ),
    )(*[job.value for job in jobs])
    return outs


def packed(block):
    rows, columns = block.shape
    if rows % 16 == 0:
        return block
    return block.reshape(16, rows * columns // 16)


def bucket_edges():
    edges = []
    for target in range(1, 32):
        if target < 16:
            edges.append(target)
        else:
            found = 0
            for distance in range(16, 4096):
                value = 16 + int(math.log(distance / 16.0) / math.log(8.0) * 16.0)
                if found == 0 and value >= target:
                    found = distance
            edges.append(found)
    return edges


def bucket_of(distance):
    edges = jnp.array(bucket_edges(), dtype=jnp.int32)
    return jnp.sum((distance[..., None] >= edges).astype(jnp.int32), axis=-1)


def rms_norm(rows, gain):
    return rows * lax.rsqrt(jnp.mean(rows * rows, axis=-1, keepdims=True) + eps) * gain


def gelu_tanh(value):
    return (
        0.5
        * value
        * (1.0 + jnp.tanh(0.7978845608028654 * (value + 0.044715 * value * value * value)))
    )


def norm_back(rows, gain, slope):
    _, pullback = jax.vjp(rms_norm, rows, gain)
    return pullback(slope)


def dot(left, right):
    return jnp.einsum("sd,df->sf", left, right, preferred_element_type=f32)


def dot_t(left, right):
    return jnp.einsum("sf,df->sd", left, right, preferred_element_type=f32)


def t_dot(left, right):
    return jnp.einsum("sd,sf->df", left, right, preferred_element_type=f32)


def heads_of(tensor):
    return tensor.reshape(tensor.shape[0], HEADS, HEAD)


def attend_scores(query, keys, bias, mask):
    scores = jnp.einsum("qhe,khe->hqk", heads_of(query), heads_of(keys), preferred_element_type=f32)
    if bias is not None:
        scores = jnp.where(mask[None], scores + bias, masked_score)
    return scores


def attend(query, keys, values, bias, mask):
    scores = attend_scores(query, keys, bias, mask)
    highest = jnp.max(scores, axis=-1, keepdims=True)
    log_total = highest + jnp.log(jnp.sum(jnp.exp(scores - highest), axis=-1, keepdims=True))
    shares = jnp.exp(scores - log_total).astype(bf16)
    output = jnp.einsum("hqk,khe->qhe", shares, heads_of(values), preferred_element_type=f32)
    return output.reshape(query.shape).astype(bf16), log_total


def attend_back(query, keys, values, bias, mask, log_total, out_slope):
    scores = attend_scores(query, keys, bias, mask)
    shares = jnp.exp(scores - log_total)
    out_heads = heads_of(out_slope)
    share_slope = jnp.einsum("qhe,khe->hqk", out_heads, heads_of(values), preferred_element_type=f32)
    inner = jnp.sum(shares * share_slope, axis=-1, keepdims=True)
    score_slope = (shares * (share_slope - inner)).astype(bf16)
    query_slope = jnp.einsum("hqk,khe->qhe", score_slope, heads_of(keys), preferred_element_type=f32)
    key_slope = jnp.einsum("hqk,qhe->khe", score_slope, heads_of(query), preferred_element_type=f32)
    value_slope = jnp.einsum("hqk,qhe->khe", shares.astype(bf16), out_heads, preferred_element_type=f32)
    return (
        query_slope.reshape(query.shape).astype(bf16),
        jnp.concatenate(
            [key_slope.reshape(keys.shape), value_slope.reshape(values.shape)], axis=1
        ).astype(bf16),
        score_slope,
    )


def per_device(
    target_ids,
    labels,
    lengths,
    memory,
    embedding,
    head,
    gain_self,
    w_query,
    w_key,
    w_value,
    w_out,
    relative_bias,
    gain_cross,
    c_query,
    c_key,
    c_value,
    c_out,
    gain_ff,
    w_gate,
    w_up,
    w_down,
    gain_final,
):
    micro = target_ids.shape[0]
    seq_dev = target_ids.shape[2]
    mem_dev = memory.shape[2]
    voc_dev, width = embedding.shape
    ff = w_gate.shape[1]
    n_gx = lax.axis_size("gx")
    n_gy = lax.axis_size("gy")
    column = lax.axis_index("gy")
    row_group = lax.axis_index("gx")
    seq = seq_dev * n_gy
    rows_total = micro * seq
    tok_dev = rows_total // n_gy
    per_seq = n_gy // micro
    span = n_gx * voc_dev
    own_micro = column // per_seq
    place = column % per_seq

    gx_bits = bits_of("gx", n_gx)
    gy_bits = bits_of("gy", n_gy)
    all_bits = gx_bits + gy_bits
    kx, ky = len(gx_bits), len(gy_bits)
    core = kx - 1
    outer = list(range(kx - 1))
    inner = list(range(kx, kx + ky))
    orders = (
        inner + outer + [core],
        inner[-1:] + outer + inner[:-1] + [core],
        outer + inner + [core],
    )
    gx_order = list(range(kx))
    seq_bits = gy_bits[micro.bit_length() - 1 :]
    ks = len(seq_bits)

    gains = jnp.stack([gain_self, gain_cross, gain_ff, gain_final], axis=1)
    gains = jnp.pad(gains, ((0, 0), (0, GAIN_PAD - 4)))
    shards = (
        jnp.concatenate([w_gate, w_up], axis=1),
        jnp.concatenate([w_down, c_key, c_value, c_out], axis=1),
        jnp.concatenate([w_query, w_key, w_value, w_out, c_query, gains], axis=1),
    )
    own_ids = jnp.stack([target_ids.reshape(-1), labels.reshape(-1)])
    gathered = exchange(
        "gather_weights",
        0,
        [Gather(packed(part), all_bits, order) for part, order in zip(shards, orders)]
        + [
            Gather(embedding, gx_bits, gx_order),
            Gather(head, gx_bits, gx_order),
            Gather(own_ids, gy_bits, list(range(ky))),
        ],
    )
    part_a, part_b, part_c = (
        full.reshape(n_gx * n_gy * part.shape[0], part.shape[1])
        for full, part in zip(gathered[:3], shards)
    )
    embed_rows = gathered[3].reshape(span, width)
    head_rows = gathered[4].reshape(span, width)
    ids = gathered[5].reshape(n_gy, 2, micro, seq_dev).transpose(1, 2, 0, 3).reshape(2, rows_total)

    def local_of(index):
        shard = index // voc_dev
        return jnp.where(shard % n_gy == column, shard // n_gy * voc_dev + index % voc_dev, -1)

    local_ids = local_of(ids[0])
    targets = local_of(ids[1])
    columns = jnp.arange(span, dtype=jnp.int32)
    norm_self, norm_cross, norm_ff, norm_final = (
        part_c[:, 5 * HD + number].astype(f32) for number in range(4)
    )
    qkv_w = part_c[:, : 3 * HD]
    self_query, self_kv = part_c[:, :HD], part_c[:, HD : 3 * HD]
    self_out = part_c[:, 3 * HD : 4 * HD]
    cross_query = part_c[:, 4 * HD : 5 * HD]
    down_full = part_b[:, :ff]
    cross_kv = part_b[:, ff : ff + 2 * HD]
    cross_out = part_b[:, ff + 2 * HD :]

    picked_rows = dot((local_ids[:, None] == columns[None, :]).astype(bf16), embed_rows).astype(bf16)
    memory_own = memory.reshape(micro * mem_dev, width)
    memory_kv = dot(memory_own, cross_kv).astype(bf16).reshape(micro, mem_dev, 2 * HD)
    resid0, mem_kv = exchange(
        "rows_and_memory",
        1,
        [
            Scatter(picked_rows.reshape((2,) * ky + (tok_dev, width)), gy_bits, list(range(ky))[::-1]),
            Gather(memory_kv, gy_bits, list(range(ky)), halves=True),
        ],
    )
    mem_kv = mem_kv.reshape(n_gy * mem_dev, 2 * HD)
    keys_cross, values_cross = mem_kv[:, :HD], mem_kv[:, HD:]

    live_length = lax.dynamic_index_in_dim(
        lax.dynamic_index_in_dim(lengths, own_micro, axis=0, keepdims=False), row_group, keepdims=False
    )
    query_pos = place * tok_dev + jnp.arange(tok_dev, dtype=jnp.int32)
    key_pos = jnp.arange(seq, dtype=jnp.int32)
    bucket = bucket_of(jnp.maximum(query_pos[:, None] - key_pos[None, :], 0))
    indicator = (bucket[None] == jnp.arange(BUCKETS, dtype=jnp.int32)[:, None, None]).astype(bf16)
    bias = jnp.einsum("som,ns->nom", indicator, relative_bias, preferred_element_type=f32)
    mask = (key_pos[None, :] <= query_pos[:, None]) & (key_pos[None, :] < live_length)

    normed_self = rms_norm(resid0, norm_self).astype(bf16)
    qkv = dot(normed_self, qkv_w).astype(bf16)
    query_self = qkv[:, :HD]
    (self_kv_all,) = exchange(
        "self_keys", 2, [Gather(qkv[:, HD:], seq_bits, list(range(ks))[::-1])]
    )
    self_kv_all = self_kv_all.reshape(seq, 2 * HD)
    keys_self, values_self = self_kv_all[:, :HD], self_kv_all[:, HD:]
    attn_self, total_self = attend(query_self, keys_self, values_self, bias, mask)
    resid1 = resid0 + dot_t(attn_self, self_out)
    normed_cross = rms_norm(resid1, norm_cross).astype(bf16)
    query_cross = dot(normed_cross, cross_query).astype(bf16)
    attn_cross, total_cross = attend(query_cross, keys_cross, values_cross, None, None)
    resid2 = resid1 + dot_t(attn_cross, cross_out)
    normed_ff = rms_norm(resid2, norm_ff).astype(bf16)
    gate_up = dot(normed_ff, part_a)
    gate_value, up_value = gate_up[:, :ff], gate_up[:, ff:]
    hidden = (gelu_tanh(gate_value) * up_value).astype(bf16)
    resid3 = resid2 + dot_t(hidden, down_full)
    final_rows = rms_norm(resid3, norm_final).astype(bf16)

    (states,) = exchange("final_rows", 3, [Gather(final_rows, gy_bits, list(range(ky)))])
    states = states.reshape(rows_total, width)
    logits = dot_t(states, head_rows)
    highest = jnp.max(logits, axis=1)
    spread = jnp.sum(jnp.exp(logits - highest[:, None]), axis=1)
    hit = columns[None, :] == targets[:, None]
    picked = jnp.sum(jnp.where(hit, logits, 0.0), axis=1)
    (stats,) = exchange(
        "totals", 4, [Gather(jnp.stack([highest, spread, picked]), gy_bits, list(range(ky)))]
    )
    stats = stats.reshape(n_gy, 3, rows_total)
    top = jnp.max(stats[:, 0], axis=0)
    log_total = top + jnp.log(jnp.sum(stats[:, 1] * jnp.exp(stats[:, 0] - top[None]), axis=0))
    picked = jnp.sum(stats[:, 2], axis=0)
    index = jnp.arange(rows_total, dtype=jnp.int32)
    own_lengths = lax.dynamic_index_in_dim(lengths, row_group, axis=1, keepdims=False)
    alive = (index % seq < jnp.repeat(own_lengths, seq)).astype(f32)
    loss_part = jnp.where(column == 0, jnp.sum(alive * (log_total - picked)), 0.0)
    slope = ((jnp.exp(logits - log_total[:, None]) - hit.astype(f32)) * alive[:, None]).astype(bf16)
    head_part = t_dot(slope, states).astype(bf16)
    final_part = dot(slope, head_rows).astype(bf16)
    final_slope, head_grad = exchange(
        "final_slopes",
        5,
        [
            Scatter(final_part.reshape((2,) * ky + (tok_dev, width)), gy_bits, list(range(ky))[::-1]),
            Scatter(head_part.reshape((2,) * kx + (voc_dev, width)), gx_bits, gx_order[::-1]),
        ],
    )

    grad3, norm_final_grad = norm_back(resid3, norm_final, final_slope)
    down_in = grad3.astype(bf16)
    down_grad = t_dot(down_in, hidden)
    hidden_slope = dot(down_in, down_full)
    activated, gelu_pull = jax.vjp(gelu_tanh, gate_value)
    up_slope = (hidden_slope * activated).astype(bf16)
    gate_slope = gelu_pull(hidden_slope * up_value)[0].astype(bf16)
    gate_up_slope = jnp.concatenate([gate_slope, up_slope], axis=1)
    gate_up_grad = t_dot(normed_ff, gate_up_slope)
    back_part, norm_ff_grad = norm_back(resid2, norm_ff, dot_t(gate_up_slope, part_a))
    grad2 = grad3 + back_part
    cross_in = grad2.astype(bf16)
    cross_out_grad = t_dot(cross_in, attn_cross)
    attn_slope = dot(cross_in, cross_out).astype(bf16)
    cross_query_slope, cross_kv_slope, _ = attend_back(
        query_cross, keys_cross, values_cross, None, None, total_cross, attn_slope
    )
    cross_query_grad = t_dot(normed_cross, cross_query_slope)
    back_part, norm_cross_grad = norm_back(
        resid1, norm_cross, dot_t(cross_query_slope, cross_query)
    )
    grad1 = grad2 + back_part
    self_in = grad1.astype(bf16)
    self_out_grad = t_dot(self_in, attn_self)
    attn_slope = dot(self_in, self_out).astype(bf16)
    query_slope, kv_slope, score_slope = attend_back(
        query_self, keys_self, values_self, bias, mask, total_self, attn_slope
    )
    bias_grad = jnp.einsum("noj,soj->ns", score_slope, indicator, preferred_element_type=f32)
    kv_slope, mem_slope = exchange(
        "key_slopes",
        6,
        [
            Scatter(
                kv_slope.reshape((2,) * ks + (tok_dev, 2 * HD)), seq_bits, list(range(ks)), bf16
            ),
            Scatter(
                cross_kv_slope.reshape((2,) * ky + (mem_dev, 2 * HD)),
                gy_bits,
                list(range(ky))[::-1],
                bf16,
                halves=True,
            ),
        ],
    )
    mem_slope = mem_slope.reshape(micro * mem_dev, 2 * HD)
    cross_kv_grad = t_dot(memory_own, mem_slope)
    memory_grad = dot_t(mem_slope, cross_kv)
    qkv_slope = jnp.concatenate([query_slope, kv_slope], axis=1)
    qkv_grad = t_dot(normed_self, qkv_slope)
    back_part, norm_self_grad = norm_back(resid0, norm_self, dot_t(qkv_slope, qkv_w))
    grad0 = grad1 + back_part
    (slopes,) = exchange(
        "row_slopes", 7, [Gather(grad0.astype(bf16), gy_bits, list(range(ky)))]
    )
    embed_part = t_dot(
        (local_ids[:, None] == columns[None, :]).astype(bf16), slopes.reshape(rows_total, width)
    ).astype(bf16)
    gain_grads = jnp.stack([norm_self_grad, norm_cross_grad, norm_ff_grad, norm_final_grad], axis=1)
    gain_grads = jnp.pad(gain_grads, ((0, 0), (0, GAIN_PAD - 4)))
    sums = (
        gate_up_grad.astype(bf16),
        jnp.concatenate([down_grad, cross_kv_grad, cross_out_grad], axis=1).astype(bf16),
        jnp.concatenate([qkv_grad, self_out_grad, cross_query_grad, gain_grads], axis=1).astype(bf16),
    )
    small = jnp.concatenate([bias_grad.reshape(-1), loss_part[None]])
    small = jnp.pad(small, (0, 1024 - small.shape[0])).reshape(8, 128)
    blocks = [
        part.reshape((2,) * (kx + ky) + packed_shape(part, n_gx * n_gy)) for part in sums
    ]
    grad_a, grad_b, grad_c, embedding_grad, small = exchange(
        "scatter_weights",
        8,
        [Scatter(part, all_bits, order[::-1]) for part, order in zip(blocks, orders)]
        + [
            Scatter(embed_part.reshape((2,) * kx + (voc_dev, width)), gx_bits, gx_order[::-1]),
            Gather(small, all_bits, orders[0]),
        ],
    )
    rows_dev = width // (n_gx * n_gy)
    grad_a, grad_b, grad_c = (
        grad.reshape(rows_dev, part.shape[1]) for grad, part in zip((grad_a, grad_b, grad_c), sums)
    )
    small = jnp.sum(small.reshape(n_gx * n_gy, 1024), axis=0)
    loss = small[HEADS * BUCKETS] / jnp.sum(lengths).astype(f32)
    bias_total = small[: HEADS * BUCKETS].reshape(HEADS, BUCKETS)
    gain_out = [grad_c[:, 5 * HD + number] for number in range(4)]
    return (
        loss,
        memory_grad.reshape(micro, 1, mem_dev, width),
        embedding_grad,
        head_grad,
        gain_out[0],
        grad_c[:, :HD],
        grad_c[:, HD : 2 * HD],
        grad_c[:, 2 * HD : 3 * HD],
        grad_c[:, 3 * HD : 4 * HD],
        bias_total,
        gain_out[1],
        grad_c[:, 4 * HD : 5 * HD],
        grad_b[:, ff : ff + HD],
        grad_b[:, ff + HD : ff + 2 * HD],
        grad_b[:, ff + 2 * HD :],
        gain_out[2],
        grad_a[:, :ff],
        grad_a[:, ff:],
        grad_b[:, :ff],
        gain_out[3],
    )


def packed_shape(part, count):
    rows, columns = part.shape[0] // count, part.shape[1]
    if rows % 16 == 0:
        return (rows, columns)
    return (16, rows * columns // 16)


def solution(mesh):
    placed = (
        P(None, "gx", "gy"),
        P(None, "gx", "gy"),
        P(),
        P(None, "gx", "gy", None),
        P(("gx", "gy"), None),
        P(("gx", "gy"), None),
        P(("gx", "gy")),
        P(("gx", "gy"), None),
        P(("gx", "gy"), None),
        P(("gx", "gy"), None),
        P(("gx", "gy"), None),
        P(),
        P(("gx", "gy")),
        P(("gx", "gy"), None),
        P(("gx", "gy"), None),
        P(("gx", "gy"), None),
        P(("gx", "gy"), None),
        P(("gx", "gy")),
        P(("gx", "gy"), None),
        P(("gx", "gy"), None),
        P(("gx", "gy"), None),
        P(("gx", "gy")),
    )
    return jax.shard_map(
        per_device,
        mesh=mesh,
        in_specs=placed,
        out_specs=(
            P(),
            P(None, "gx", "gy", None),
            P(("gx", "gy"), None),
            P(("gx", "gy"), None),
            P(("gx", "gy")),
            P(("gx", "gy"), None),
            P(("gx", "gy"), None),
            P(("gx", "gy"), None),
            P(("gx", "gy"), None),
            P(),
            P(("gx", "gy")),
            P(("gx", "gy"), None),
            P(("gx", "gy"), None),
            P(("gx", "gy"), None),
            P(("gx", "gy"), None),
            P(("gx", "gy")),
            P(("gx", "gy"), None),
            P(("gx", "gy"), None),
            P(("gx", "gy"), None),
            P(("gx", "gy")),
        ),
        check_vma=False,
    )
```

```python
import functools
import itertools
import math

import jax
import jax.numpy as jnp
from jax import lax
from jax.experimental import pallas as pl
from jax.experimental.pallas import tpu as pltpu
from jax.sharding import PartitionSpec as P

HEADS = 6
HEAD = 64
HD = HEADS * HEAD
BUCKETS = 32
GAIN_PAD = 128

eps = 1e-06
masked_score = -1000000000.0
bf16 = jnp.bfloat16
f32 = jnp.float32


def flip(position, offset):
    moved = position
    weight = 1
    while weight <= offset:
        if offset & weight:
            moved = moved + weight * (1 - 2 * ((position // weight) % 2))
        weight *= 2
    return moved


def coordinates():
    gx, gy = lax.axis_index("gx"), lax.axis_index("gy")
    return {"a": gx // 2, "c": gx % 2, "s": gy // 2, "h": gy % 2}


def peer_of(dim, offset):
    gx, gy = lax.axis_index("gx"), lax.axis_index("gy")
    if dim == "a":
        return {"gx": 2 * flip(gx // 2, offset) + gx % 2}
    if dim == "c":
        return {"gx": flip(gx, 1)}
    if dim == "s":
        return {"gy": 2 * flip(gy // 2, offset) + gy % 2}
    return {"gy": flip(gy, 1)}


def remote(source, target, send, recv, dim, offset):
    return pltpu.make_async_remote_copy(
        src_ref=source,
        dst_ref=target,
        send_sem=send,
        recv_sem=recv,
        device_id=peer_of(dim, offset),
        device_id_type=pl.DeviceIdType.MESH,
    )


def each_piece(rows, columns, body, width=16384):
    step = rows
    while step * columns > width and step % 32 == 0:
        step //= 2
    if step == rows:
        body(slice(None))
        return

    def piece(number, carry):
        body(pl.ds(pl.multiple_of(number * step, step), step))
        return carry

    lax.fori_loop(0, rows // step, piece, 0)


class Gather:
    def __init__(self, block, order, layout, sizes, merged=""):
        self.value = block
        self.order, self.layout, self.sizes, self.merged = order, layout, sizes, merged
        self.out = jax.ShapeDtypeStruct(tuple(sizes[d] for d in layout) + block.shape, block.dtype)
        self.in_spec = pl.BlockSpec(memory_space=pltpu.VMEM)
        self.out_spec = pl.BlockSpec(memory_space=pl.ANY)
        self.transfers = []
        for level, dim in enumerate(order):
            ranges = [(None,) if d in merged else range(sizes[d]) for d in order[:level]]
            for unit in itertools.product(*ranges):
                for offset in range(1, sizes[dim]):
                    self.transfers.append((level, unit, offset))
        self.index = {transfer: number for number, transfer in enumerate(self.transfers)}
        count = len(self.transfers)
        self.scratch = [
            pltpu.SemaphoreType.DMA((count,)),
            pltpu.SemaphoreType.DMA((count,)),
            pltpu.SemaphoreType.DMA,
        ]
        self.peers = [(d, offset) for d in order for offset in range(1, sizes[d])]

    def prepare(self, refs, place):
        self.source, self.target, self.send, self.recv, self.local_sem = refs
        self.place = place
        self.local = pltpu.make_async_copy(
            self.source, self.target.at[tuple(place[d] for d in self.layout)], self.local_sem
        )
        self.local.start()
        self.local_done = False
        self.arrived = set()
        self.sent = []

    def region(self, level, unit, offset):
        where = dict(self.place)
        for d, moved in zip(self.order[:level], unit):
            where[d] = slice(None) if moved is None else flip(self.place[d], moved)
        if offset:
            where[self.order[level]] = flip(self.place[self.order[level]], offset)
        return self.target.at[tuple(where[d] for d in self.layout)]

    def needs(self, level, unit):
        if level == 0:
            return []
        last, before = unit[-1], unit[:-1]
        if last is None:
            dim = self.order[level - 1]
            return self.needs(level - 1, before) + [
                (level - 1, before, offset) for offset in range(1, self.sizes[dim])
            ]
        if last == 0:
            return self.needs(level - 1, before)
        return [(level - 1, before, last)]

    def arrive(self, transfer):
        if transfer in self.arrived:
            return
        self.arrived.add(transfer)
        level, unit, offset = transfer
        number = self.index[transfer]
        there = self.region(level, unit, offset)
        remote(
            there, there, self.send.at[number], self.recv.at[number], self.order[level], offset
        ).wait_recv()

    def launch(self, transfer):
        level, unit, offset = transfer
        number = self.index[transfer]
        for need in self.needs(level, unit):
            self.arrive(need)
        target = self.region(level, unit, 0)
        own = all(moved == 0 for moved in unit)
        if None in unit and not self.local_done:
            self.local.wait()
            self.local_done = True
        copy = remote(
            self.source if own else target,
            target,
            self.send.at[number],
            self.recv.at[number],
            self.order[level],
            offset,
        )
        copy.start()
        self.sent.append(copy)

    def events(self):
        found = []
        for transfer in self.transfers:
            level, unit, offset = transfer
            key = 0.1 * level + 0.01 * offset
            for d, moved in zip(self.order, unit):
                key += self.sizes[d] - 1 if moved is None else moved
            found.append((key, functools.partial(self.launch, transfer)))
        return found

    def finish(self):
        if not self.local_done:
            self.local.wait()
        for transfer in self.transfers:
            self.arrive(transfer)
        for copy in self.sent:
            copy.wait_send()


class Scatter:
    def __init__(self, value, order, layout, sizes, merged="", out_dtype=f32):
        self.value = value
        self.order, self.layout, self.sizes, self.merged = order, layout, sizes, merged
        self.block = value.shape[len(layout) :]
        self.out = jax.ShapeDtypeStruct(self.block, out_dtype)
        self.in_spec = pl.BlockSpec(memory_space=pltpu.VMEM)
        self.out_spec = pl.BlockSpec(memory_space=pltpu.VMEM)
        self.levels = len(order)
        self.units = []
        self.scratch = []
        self.layouts = [layout]
        for level, dim in enumerate(order):
            later = order[level + 1 :]
            ranges = [(None,) if d in merged else range(sizes[d]) for d in later]
            units = sorted(
                itertools.product(*ranges), key=lambda unit: -sum(moved or 0 for moved in unit)
            )
            self.units.append(units)
            left = "".join(d for d in self.layouts[-1] if d != dim)
            self.layouts.append(left)
            self.scratch.append(
                pltpu.VMEM(
                    (sizes[dim] - 1,) + tuple(sizes[d] for d in left) + self.block, value.dtype
                )
            )
        self.index = {}
        for level, dim in enumerate(order):
            for unit in self.units[level]:
                for offset in range(1, sizes[dim]):
                    self.index[(level, unit, offset)] = len(self.index)
        count = len(self.index)
        self.scratch += [pltpu.SemaphoreType.DMA((count,)), pltpu.SemaphoreType.DMA((count,))]
        self.peers = [(d, offset) for d in order for offset in range(1, sizes[d])]

    def prepare(self, refs, place):
        self.source, self.target = refs[0], refs[1]
        self.landing = refs[2 : 2 + self.levels]
        self.send, self.recv = refs[2 + self.levels :]
        self.place = place
        self.sent = []

    def held(self, level):
        return self.source if level == 0 else self.landing[level - 1].at[0]

    def later(self, level, unit):
        where = {}
        for d, moved in zip(self.order[level + 1 :], unit):
            where[d] = slice(None) if moved is None else flip(self.place[d], moved)
        return where

    def copy(self, level, unit, offset):
        number = self.index[(level, unit, offset)]
        dim = self.order[level]
        where = self.later(level, unit)
        landed = self.landing[level].at[
            (offset - 1,) + tuple(where[d] for d in self.layouts[level + 1])
        ]
        where[dim] = flip(self.place[dim], offset)
        source = self.held(level).at[tuple(where[d] for d in self.layouts[level])]
        return remote(source, landed, self.send.at[number], self.recv.at[number], dim, offset)

    def launch(self, level, unit, offset):
        copy = self.copy(level, unit, offset)
        copy.start()
        self.sent.append(copy)

    def reduce(self, level, unit):
        dim = self.order[level]
        size = self.sizes[dim]
        for offset in range(1, size):
            self.copy(level, unit, offset).wait_recv()
        where = self.later(level, unit)
        free = [d for d in self.order[level + 1 :] if isinstance(where[d], slice)]
        total = math.prod(self.sizes[d] for d in free)
        rows, columns = self.block
        last = level == self.levels - 1

        def one(number, carry):
            at = dict(where)
            rest = number
            for d in free:
                at[d] = rest % self.sizes[d]
                rest = rest // self.sizes[d]
            spot = tuple(at[d] for d in self.layouts[level + 1])
            at[dim] = self.place[dim]
            mine = tuple(at[d] for d in self.layouts[level])

            def body(piece):
                result = self.held(level)[mine + (piece,)].astype(f32)
                for offset in range(1, size):
                    result = result + self.landing[level][(offset - 1,) + spot + (piece,)].astype(f32)
                if last:
                    self.target[(piece,)] = result.astype(self.target.dtype)
                else:
                    self.landing[level][(0,) + spot + (piece,)] = result.astype(self.landing[level].dtype)

            each_piece(rows, columns, body)
            return carry

        if total == 1:
            one(0, 0)
        else:
            lax.fori_loop(0, total, one, 0)
        if not last:
            ahead, rest = unit[0], unit[1:]
            if ahead is None:
                offsets = range(1, self.sizes[self.order[level + 1]])
            else:
                offsets = [ahead] if ahead else []
            for offset in offsets:
                self.launch(level + 1, rest, offset)

    def events(self):
        found = []
        for number, unit in enumerate(self.units[0]):
            for offset in range(1, self.sizes[self.order[0]]):
                found.append(
                    (-1 + 0.001 * number, functools.partial(self.launch, 0, unit, offset))
                )
        for level in range(self.levels):
            count = len(self.units[level])
            for number, unit in enumerate(self.units[level]):
                found.append(
                    (level + number / count, functools.partial(self.reduce, level, unit))
                )
        return found

    def finish(self):
        for copy in self.sent:
            copy.wait_send()


class MemoryGather:
    def __init__(self, memory, sizes):
        self.value = memory
        self.sizes = sizes
        self.out = jax.ShapeDtypeStruct((sizes["s"], 2) + memory.shape[1:], memory.dtype)
        self.in_spec = pl.BlockSpec(memory_space=pltpu.VMEM)
        self.out_spec = pl.BlockSpec(memory_space=pl.ANY)
        rows = sizes["s"]
        self.scratch = [
            pltpu.SemaphoreType.DMA((2, rows)),
            pltpu.SemaphoreType.DMA((2, rows)),
            pltpu.SemaphoreType.DMA((2, rows, 2)),
            pltpu.SemaphoreType.DMA,
        ]
        self.peers = [("s", offset) for offset in range(1, rows)] + [("h", 1), ("c", 1)]

    def prepare(self, refs, place):
        self.source, self.target, self.along, self.across, self.core, self.local = refs
        self.place = place
        self.mine = place["s"] % 2 == place["c"]

    def row(self, offset):
        return flip(self.place["s"], offset)

    def along_copy(self, offset, arriving):
        to = self.row(offset)
        spot = to if arriving else self.place["s"]
        return remote(
            self.source.at[self.place["s"] // 2 if arriving else to // 2],
            self.target.at[spot, self.place["h"]],
            self.along.at[0, offset],
            self.along.at[1, offset],
            "s",
            offset,
        )

    def across_copy(self, offset, arriving):
        h = self.place["h"]
        own = self.target.at[self.row(offset), 1 - h if arriving else h]
        if offset == 0 and not arriving:
            source = self.source.at[self.place["s"] // 2]
        else:
            source = own
        return remote(source, own, self.across.at[0, offset], self.across.at[1, offset], "h", 1)

    def core_copy(self, offset, other):
        h = self.place["h"]
        own = self.target.at[self.row(offset), 1 - h if other else h]
        source = self.source.at[self.place["s"] // 2] if offset == 0 and not other else own
        return remote(source, own, self.core.at[0, offset, other], self.core.at[1, offset, other], "c", 1)

    def events(self):
        rows = self.sizes["s"]

        def first():
            for offset in range(1, rows):
                @pl.when(self.row(offset) % 2 == self.place["c"])
                def _():
                    self.along_copy(offset, False).start()

            @pl.when(self.mine)
            def _():
                pltpu.make_async_copy(
                    self.source.at[self.place["s"] // 2],
                    self.target.at[self.place["s"], self.place["h"]],
                    self.local,
                ).start()
                self.across_copy(0, False).start()
                self.core_copy(0, 0).start()

        def arrival(offset):
            @pl.when(self.mine)
            def _():
                self.along_copy(offset, True).wait_recv()
                self.across_copy(offset, False).start()
                self.core_copy(offset, 0).start()

        def other(offset):
            @pl.when(self.mine)
            def _():
                self.across_copy(offset, True).wait_recv()
                self.core_copy(offset, 1).start()

        found = [(0.05, first)]
        for offset in range(1, rows):
            found.append((offset + 0.05, functools.partial(arrival, offset)))
        for offset in range(rows):
            found.append((rows + offset, functools.partial(other, offset)))
        return found

    def finish(self):
        rows = self.sizes["s"]
        for offset in range(1, rows):
            @pl.when(self.row(offset) % 2 == self.place["c"])
            def _():
                self.along_copy(offset, False).wait_send()

        @pl.when(self.mine)
        def _():
            pltpu.make_async_copy(
                self.source.at[self.place["s"] // 2],
                self.target.at[self.place["s"], self.place["h"]],
                self.local,
            ).wait()
            for offset in range(rows):
                self.across_copy(offset, False).wait_send()
                for other in range(2):
                    self.core_copy(offset, other).wait_send()

        @pl.when(jnp.logical_not(self.mine))
        def _():
            for offset in range(rows):
                for other in range(2):
                    self.core_copy(offset, other).wait_recv()


class MemoryScatter:
    def __init__(self, value, sizes):
        self.value = value
        self.sizes = sizes
        rows = sizes["s"]
        self.block = value.shape[2:]
        self.out = jax.ShapeDtypeStruct((2,) + self.block, f32)
        self.in_spec = pl.BlockSpec(memory_space=pltpu.VMEM)
        self.out_spec = pl.BlockSpec(memory_space=pltpu.VMEM)
        self.scratch = [
            pltpu.VMEM(value.shape, value.dtype),
            pltpu.VMEM((rows,) + self.block, value.dtype),
            pltpu.VMEM((2,) + self.block, value.dtype),
            pltpu.SemaphoreType.DMA((2, rows, 2)),
            pltpu.SemaphoreType.DMA((2, rows)),
            pltpu.SemaphoreType.DMA((2, rows)),
        ]
        self.peers = [("s", offset) for offset in range(1, rows)] + [("h", 1), ("c", 1)]

    def prepare(self, refs, place):
        self.source, self.target = refs[0], refs[1]
        self.summed, self.halved, self.landed, self.core, self.across, self.along = refs[2:]
        self.place = place
        self.mine = place["s"] % 2 == place["c"]

    def row(self, offset):
        return flip(self.place["s"], offset)

    def core_copy(self, offset, other):
        h = self.place["h"]
        spot = (self.row(offset), flip(h, 1) if other else h)
        return remote(
            self.source.at[spot],
            self.summed.at[spot],
            self.core.at[0, offset, other],
            self.core.at[1, offset, other],
            "c",
            1,
        )

    def across_copy(self, offset):
        row = self.row(offset)
        return remote(
            self.summed.at[row, flip(self.place["h"], 1)],
            self.halved.at[row],
            self.across.at[0, offset],
            self.across.at[1, offset],
            "h",
            1,
        )

    def along_copy(self, offset, arriving):
        to = self.row(offset)
        return remote(
            self.halved.at[to],
            self.landed.at[to // 2 if arriving else self.place["s"] // 2],
            self.along.at[0, offset],
            self.along.at[1, offset],
            "s",
            offset,
        )

    def events(self):
        rows = self.sizes["s"]
        high, wide = self.block
        orders = list(range(1, rows))[::-1] + [0]

        def first():
            @pl.when(jnp.logical_not(self.mine))
            def _():
                for other in (1, 0):
                    for offset in orders:
                        self.core_copy(offset, other).start()

        def level(offset, other):
            @pl.when(self.mine)
            def _():
                self.core_copy(offset, other).wait_recv()
                h = self.place["h"]
                spot = (self.row(offset), flip(h, 1) if other else h)

                def body(piece):
                    total = self.summed[spot + (piece,)].astype(f32) + self.source[
                        spot + (piece,)
                    ].astype(f32)
                    self.summed[spot + (piece,)] = total.astype(self.summed.dtype)

                each_piece(high, wide, body)
                if other:
                    self.across_copy(offset).start()

        def last(offset):
            @pl.when(self.mine)
            def _():
                self.across_copy(offset).wait_recv()
                row = self.row(offset)

                def body(piece):
                    total = self.halved[(row, piece)].astype(f32) + self.summed[
                        (row, self.place["h"], piece)
                    ].astype(f32)
                    self.halved[(row, piece)] = total.astype(self.halved.dtype)
                    if offset == 0:
                        self.target[(self.place["s"] // 2, piece)] = total

                each_piece(high, wide, body)
                if offset:
                    self.along_copy(offset, False).start()

        found = [(-0.95, first)]
        for number, offset in enumerate(orders):
            found.append((0.05 + 0.1 * number, functools.partial(level, offset, 1)))
        for number, offset in enumerate(orders):
            found.append((0.55 + 0.1 * number, functools.partial(level, offset, 0)))
        for number, offset in enumerate(orders):
            found.append((1.05 + 0.2 * number, functools.partial(last, offset)))
        return found

    def finish(self):
        rows = self.sizes["s"]
        high, wide = self.block
        for offset in range(1, rows):
            @pl.when(self.row(offset) % 2 == self.place["c"])
            def _():
                self.along_copy(offset, True).wait_recv()
                number = self.row(offset) // 2

                def body(piece):
                    self.target[(number, piece)] = self.landed[(number, piece)].astype(f32)

                each_piece(high, wide, body)

        @pl.when(self.mine)
        def _():
            for offset in range(rows):
                self.across_copy(offset).wait_send()
            for offset in range(1, rows):
                self.along_copy(offset, False).wait_send()

        @pl.when(jnp.logical_not(self.mine))
        def _():
            for offset in range(rows):
                for other in range(2):
                    self.core_copy(offset, other).wait_send()


def exchange(name, collective_id, jobs):
    sizes = [len(job.scratch) for job in jobs]
    peers = []
    for job in jobs:
        for peer in job.peers:
            if peer not in peers:
                peers.append(peer)

    def kernel(*refs):
        count = len(jobs)
        scratch = refs[2 * count :]
        offset = 0
        barrier = pltpu.get_barrier_semaphore()
        for peer in peers:
            pl.semaphore_signal(
                barrier, inc=1, device_id=peer_of(*peer), device_id_type=pl.DeviceIdType.MESH
            )
        place = coordinates()
        for number, job in enumerate(jobs):
            job.prepare(
                (refs[number], refs[count + number]) + tuple(scratch[offset : offset + sizes[number]]),
                place,
            )
            offset += sizes[number]
        pl.semaphore_wait(barrier, len(peers))
        events = [event for job in jobs for event in job.events()]
        for _, act in sorted(events, key=lambda event: event[0]):
            act()
        for job in jobs:
            job.finish()

    return pl.pallas_call(
        kernel,
        name=name,
        out_shape=tuple(job.out for job in jobs),
        in_specs=[job.in_spec for job in jobs],
        out_specs=tuple(job.out_spec for job in jobs),
        scratch_shapes=[item for job in jobs for item in job.scratch],
        compiler_params=pltpu.CompilerParams(
            collective_id=collective_id, has_side_effects=True, vmem_limit_bytes=60 * 1024 * 1024
        ),
    )(*[job.value for job in jobs])


def packed(block):
    rows, columns = block.shape
    if rows % 16 == 0:
        return block
    return block.reshape(16, rows * columns // 16)


def bucket_edges():
    edges = []
    for target in range(1, 32):
        if target < 16:
            edges.append(target)
        else:
            found = 0
            for distance in range(16, 4096):
                value = 16 + int(math.log(distance / 16.0) / math.log(8.0) * 16.0)
                if found == 0 and value >= target:
                    found = distance
            edges.append(found)
    return edges


def bucket_of(distance):
    edges = jnp.array(bucket_edges(), dtype=jnp.int32)
    return jnp.sum((distance[..., None] >= edges).astype(jnp.int32), axis=-1)


def rms_norm(rows, gain):
    return rows * lax.rsqrt(jnp.mean(rows * rows, axis=-1, keepdims=True) + eps) * gain


def gelu_tanh(value):
    return (
        0.5
        * value
        * (1.0 + jnp.tanh(0.7978845608028654 * (value + 0.044715 * value * value * value)))
    )


def norm_back(rows, gain, slope):
    _, pullback = jax.vjp(rms_norm, rows, gain)
    return pullback(slope)


def dot(left, right):
    return jnp.einsum("sd,df->sf", left, right, preferred_element_type=f32)


def dot_t(left, right):
    return jnp.einsum("sf,df->sd", left, right, preferred_element_type=f32)


def t_dot(left, right):
    return jnp.einsum("sd,sf->df", left, right, preferred_element_type=f32)


def heads_of(tensor):
    return tensor.reshape(tensor.shape[0], HEADS, HEAD)


def attend_scores(query, keys, bias, mask):
    scores = jnp.einsum("qhe,khe->hqk", heads_of(query), heads_of(keys), preferred_element_type=f32)
    if bias is not None:
        scores = jnp.where(mask[None], scores + bias, masked_score)
    return scores


def attend(query, keys, values, bias, mask):
    scores = attend_scores(query, keys, bias, mask)
    highest = jnp.max(scores, axis=-1, keepdims=True)
    log_total = highest + jnp.log(jnp.sum(jnp.exp(scores - highest), axis=-1, keepdims=True))
    shares = jnp.exp(scores - log_total).astype(bf16)
    output = jnp.einsum("hqk,khe->qhe", shares, heads_of(values), preferred_element_type=f32)
    return output.reshape(query.shape).astype(bf16), log_total


def attend_back(query, keys, values, bias, mask, log_total, out_slope):
    scores = attend_scores(query, keys, bias, mask)
    shares = jnp.exp(scores - log_total)
    out_heads = heads_of(out_slope)
    share_slope = jnp.einsum("qhe,khe->hqk", out_heads, heads_of(values), preferred_element_type=f32)
    inner = jnp.sum(shares * share_slope, axis=-1, keepdims=True)
    score_slope = (shares * (share_slope - inner)).astype(bf16)
    query_slope = jnp.einsum("hqk,khe->qhe", score_slope, heads_of(keys), preferred_element_type=f32)
    key_slope = jnp.einsum("hqk,qhe->khe", score_slope, heads_of(query), preferred_element_type=f32)
    value_slope = jnp.einsum("hqk,qhe->khe", shares.astype(bf16), out_heads, preferred_element_type=f32)
    return (
        query_slope.reshape(query.shape).astype(bf16),
        jnp.concatenate(
            [key_slope.reshape(keys.shape), value_slope.reshape(values.shape)], axis=1
        ).astype(bf16),
        score_slope,
    )


def per_device(
    target_ids,
    labels,
    lengths,
    memory,
    embedding,
    head,
    gain_self,
    w_query,
    w_key,
    w_value,
    w_out,
    relative_bias,
    gain_cross,
    c_query,
    c_key,
    c_value,
    c_out,
    gain_ff,
    w_gate,
    w_up,
    w_down,
    gain_final,
):
    micro = target_ids.shape[0]
    seq_dev = target_ids.shape[2]
    mem_dev = memory.shape[2]
    voc_dev, width = embedding.shape
    ff = w_gate.shape[1]
    n_gx = lax.axis_size("gx")
    n_gy = lax.axis_size("gy")
    column = lax.axis_index("gy")
    row_group = lax.axis_index("gx")
    devices = n_gx * n_gy
    sizes = {"a": n_gx // 2, "c": 2, "s": n_gy // 2, "h": 2}
    assert sizes["s"] == 2 * micro
    place = coordinates()
    seq = seq_dev * n_gy
    plane = sizes["s"] * seq
    tok_dev = seq // 4
    span = sizes["a"] * voc_dev
    merged = "" if sizes["a"] == 2 else "ashc"

    gains = jnp.stack([gain_self, gain_cross, gain_ff, gain_final], axis=1)
    gains = jnp.pad(gains, ((0, 0), (0, GAIN_PAD - 4)))
    shards = (
        jnp.concatenate([w_gate, w_up], axis=1),
        jnp.concatenate([w_down, c_key, c_value, c_out], axis=1),
        jnp.concatenate([w_query, w_key, w_value, w_out, c_query, gains], axis=1),
    )
    orders = ("shac", "sahc", "sahc")
    own_ids = jnp.stack([target_ids.reshape(-1), labels.reshape(-1)])
    part_a, part_b, part_c, embed_rows, ids, memory_all = exchange(
        "gather_weights",
        0,
        [
            Gather(packed(part), order, "acsh", sizes, merged)
            for part, order in zip(shards, orders)
        ]
        + [
            Gather(embedding, "a", "a", sizes),
            Gather(own_ids, "shc", "shc", sizes, "shc"),
            MemoryGather(memory.reshape(micro, mem_dev, width), sizes),
        ],
    )
    part_a, part_b, part_c = (
        full.reshape(devices * part.shape[0], part.shape[1])
        for full, part in zip((part_a, part_b, part_c), shards)
    )
    embed_rows = embed_rows.reshape(span, width)
    memory_all = memory_all.reshape(n_gy * mem_dev, width)
    ids = ids.reshape(n_gy // 2, 2, 2, 2, micro, seq_dev).transpose(3, 4, 2, 0, 1, 5).reshape(2, plane)

    def local_of(index):
        shard = index // voc_dev
        held = (shard % n_gy == column) & (shard // n_gy % 2 == place["c"])
        return jnp.where(held, shard // (2 * n_gy) * voc_dev + index % voc_dev, -1)

    local_ids = local_of(ids[0])
    targets = local_of(ids[1])
    columns = jnp.arange(span, dtype=jnp.int32)
    norm_self, norm_cross, norm_ff, norm_final = (
        part_c[:, 5 * HD + number].astype(f32) for number in range(4)
    )
    qkv_w = part_c[:, : 3 * HD]
    self_out = part_c[:, 3 * HD : 4 * HD]
    cross_query = part_c[:, 4 * HD : 5 * HD]
    down_full = part_b[:, :ff]
    cross_kv = part_b[:, ff : ff + 2 * HD]
    cross_out = part_b[:, ff + 2 * HD :]

    picked_rows = dot((local_ids[:, None] == columns[None, :]).astype(bf16), embed_rows).astype(bf16)
    tok_layout = (sizes["s"], 2, 2, tok_dev, width)
    resid0, head_rows = exchange(
        "rows",
        1,
        [
            Scatter(picked_rows.reshape(tok_layout), "chs", "shc", sizes),
            Gather(head, "a", "a", sizes),
        ],
    )
    head_rows = head_rows.reshape(span, width)
    mem_kv = dot(memory_all, cross_kv).astype(bf16)
    keys_cross, values_cross = mem_kv[:, :HD], mem_kv[:, HD:]

    plane_lengths = lax.dynamic_slice_in_dim(lengths, 2 * place["a"], 2, axis=1).reshape(-1)
    live_length = lax.dynamic_index_in_dim(plane_lengths, place["s"], keepdims=False)
    query_pos = (2 * place["h"] + place["c"]) * tok_dev + jnp.arange(tok_dev, dtype=jnp.int32)
    key_pos = jnp.arange(seq, dtype=jnp.int32)
    bucket = bucket_of(jnp.maximum(query_pos[:, None] - key_pos[None, :], 0))
    indicator = (bucket[None] == jnp.arange(BUCKETS, dtype=jnp.int32)[:, None, None]).astype(bf16)
    bias = jnp.einsum("som,ns->nom", indicator, relative_bias, preferred_element_type=f32)
    mask = (key_pos[None, :] <= query_pos[:, None]) & (key_pos[None, :] < live_length)

    normed_self = rms_norm(resid0, norm_self).astype(bf16)
    qkv = dot(normed_self, qkv_w).astype(bf16)
    query_self = qkv[:, :HD]
    (self_kv_all,) = exchange("self_keys", 2, [Gather(qkv[:, HD:], "hc", "hc", sizes)])
    self_kv_all = self_kv_all.reshape(seq, 2 * HD)
    keys_self, values_self = self_kv_all[:, :HD], self_kv_all[:, HD:]
    attn_self, total_self = attend(query_self, keys_self, values_self, bias, mask)
    resid1 = resid0 + dot_t(attn_self, self_out)
    normed_cross = rms_norm(resid1, norm_cross).astype(bf16)
    query_cross = dot(normed_cross, cross_query).astype(bf16)
    attn_cross, total_cross = attend(query_cross, keys_cross, values_cross, None, None)
    resid2 = resid1 + dot_t(attn_cross, cross_out)
    normed_ff = rms_norm(resid2, norm_ff).astype(bf16)
    gate_up = dot(normed_ff, part_a)
    gate_value, up_value = gate_up[:, :ff], gate_up[:, ff:]
    hidden = (gelu_tanh(gate_value) * up_value).astype(bf16)
    resid3 = resid2 + dot_t(hidden, down_full)
    final_rows = rms_norm(resid3, norm_final).astype(bf16)

    (states,) = exchange("final_rows", 3, [Gather(final_rows, "shc", "shc", sizes, merged)])
    states = states.reshape(plane, width)
    logits = dot_t(states, head_rows)
    highest = jnp.max(logits, axis=1)
    own_total = highest + jnp.log(jnp.sum(jnp.exp(logits - highest[:, None]), axis=1))
    (totals,) = exchange(
        "totals", 4, [Gather(own_total.reshape(plane // 128, 128), "shc", "shc", sizes, merged)]
    )
    totals = totals.reshape(2 * n_gy, plane)
    top = jnp.max(totals, axis=0)
    log_total = top + jnp.log(jnp.sum(jnp.exp(totals - top[None]), axis=0))
    index = jnp.arange(plane, dtype=jnp.int32)
    alive = (index % seq < jnp.repeat(plane_lengths, seq)).astype(f32)
    hit = columns[None, :] == targets[:, None]
    picked = jnp.sum(jnp.where(hit, logits, 0.0), axis=1)
    loss_part = -jnp.sum(alive * picked) + jnp.where(
        (column == 0) & (place["c"] == 0), jnp.sum(alive * log_total), 0.0
    )
    slope = ((jnp.exp(logits - log_total[:, None]) - hit.astype(f32)) * alive[:, None]).astype(bf16)
    head_part = t_dot(slope, states).astype(bf16)
    final_part = dot(slope, head_rows).astype(bf16)
    final_slope, head_grad = exchange(
        "final_slopes",
        5,
        [
            Scatter(final_part.reshape(tok_layout), "chs", "shc", sizes),
            Scatter(head_part.reshape(sizes["a"], voc_dev, width), "a", "a", sizes),
        ],
    )

    grad3, norm_final_grad = norm_back(resid3, norm_final, final_slope)
    down_in = grad3.astype(bf16)
    down_grad = t_dot(down_in, hidden)
    hidden_slope = dot(down_in, down_full)
    activated, gelu_pull = jax.vjp(gelu_tanh, gate_value)
    up_slope = (hidden_slope * activated).astype(bf16)
    gate_slope = gelu_pull(hidden_slope * up_value)[0].astype(bf16)
    gate_up_slope = jnp.concatenate([gate_slope, up_slope], axis=1)
    gate_up_grad = t_dot(normed_ff, gate_up_slope)
    back_part, norm_ff_grad = norm_back(resid2, norm_ff, dot_t(gate_up_slope, part_a))
    grad2 = grad3 + back_part
    cross_in = grad2.astype(bf16)
    cross_out_grad = t_dot(cross_in, attn_cross)
    attn_slope = dot(cross_in, cross_out).astype(bf16)
    cross_query_slope, cross_kv_slope, _ = attend_back(
        query_cross, keys_cross, values_cross, None, None, total_cross, attn_slope
    )
    cross_query_grad = t_dot(normed_cross, cross_query_slope)
    cross_kv_grad = t_dot(memory_all, cross_kv_slope)
    memory_part = dot_t(cross_kv_slope, cross_kv).astype(bf16)
    back_part, norm_cross_grad = norm_back(
        resid1, norm_cross, dot_t(cross_query_slope, cross_query)
    )
    grad1 = grad2 + back_part
    self_in = grad1.astype(bf16)
    self_out_grad = t_dot(self_in, attn_self)
    attn_slope = dot(self_in, self_out).astype(bf16)
    query_slope, kv_slope, score_slope = attend_back(
        query_self, keys_self, values_self, bias, mask, total_self, attn_slope
    )
    bias_grad = jnp.einsum("noj,soj->ns", score_slope, indicator, preferred_element_type=f32)
    (kv_slope,) = exchange(
        "key_slopes",
        6,
        [Scatter(kv_slope.reshape(2, 2, tok_dev, 2 * HD), "ch", "hc", sizes, "", bf16)],
    )
    qkv_slope = jnp.concatenate([query_slope, kv_slope], axis=1)
    qkv_grad = t_dot(normed_self, qkv_slope)
    back_part, norm_self_grad = norm_back(resid0, norm_self, dot_t(qkv_slope, qkv_w))
    grad0 = grad1 + back_part
    (slopes,) = exchange("row_slopes", 7, [Gather(grad0.astype(bf16), "shc", "shc", sizes, merged)])
    embed_part = t_dot(
        (local_ids[:, None] == columns[None, :]).astype(bf16), slopes.reshape(plane, width)
    ).astype(bf16)
    gain_grads = jnp.stack([norm_self_grad, norm_cross_grad, norm_ff_grad, norm_final_grad], axis=1)
    gain_grads = jnp.pad(gain_grads, ((0, 0), (0, GAIN_PAD - 4)))
    sums = (
        gate_up_grad.astype(bf16),
        jnp.concatenate([down_grad, cross_kv_grad, cross_out_grad], axis=1).astype(bf16),
        jnp.concatenate([qkv_grad, self_out_grad, cross_query_grad, gain_grads], axis=1).astype(bf16),
    )
    small = jnp.concatenate([bias_grad.reshape(-1), loss_part[None]])
    small = jnp.pad(small, (0, 1024 - small.shape[0])).reshape(8, 128)
    device_layout = (sizes["a"], 2, sizes["s"], 2)
    blocks = [part.reshape(device_layout + packed_shape(part, devices)) for part in sums]
    grad_a, grad_b, grad_c, embedding_grad, memory_grad, small = exchange(
        "scatter_weights",
        8,
        [
            Scatter(part, order[::-1], "acsh", sizes, merged)
            for part, order in zip(blocks, orders)
        ]
        + [
            Scatter(embed_part.reshape(sizes["a"], voc_dev, width), "a", "a", sizes),
            MemoryScatter(memory_part.reshape(sizes["s"], 2, mem_dev, width), sizes),
            Gather(small, "shac", "acsh", sizes, "ashc"),
        ],
    )
    rows_dev = width // devices
    grad_a, grad_b, grad_c = (
        grad.reshape(rows_dev, part.shape[1]) for grad, part in zip((grad_a, grad_b, grad_c), sums)
    )
    small = jnp.sum(small.reshape(devices, 1024), axis=0)
    loss = small[HEADS * BUCKETS] / jnp.sum(lengths).astype(f32)
    bias_total = small[: HEADS * BUCKETS].reshape(HEADS, BUCKETS)
    gain_out = [grad_c[:, 5 * HD + number] for number in range(4)]
    return (
        loss,
        memory_grad.reshape(micro, 1, mem_dev, width),
        embedding_grad,
        head_grad,
        gain_out[0],
        grad_c[:, :HD],
        grad_c[:, HD : 2 * HD],
        grad_c[:, 2 * HD : 3 * HD],
        grad_c[:, 3 * HD : 4 * HD],
        bias_total,
        gain_out[1],
        grad_c[:, 4 * HD : 5 * HD],
        grad_b[:, ff : ff + HD],
        grad_b[:, ff + HD : ff + 2 * HD],
        grad_b[:, ff + 2 * HD :],
        gain_out[2],
        grad_a[:, :ff],
        grad_a[:, ff:],
        grad_b[:, :ff],
        gain_out[3],
    )


def packed_shape(part, count):
    rows, columns = part.shape[0] // count, part.shape[1]
    if rows % 16 == 0:
        return (rows, columns)
    return (16, rows * columns // 16)


def solution(mesh):
    placed = (
        P(None, "gx", "gy"),
        P(None, "gx", "gy"),
        P(),
        P(None, "gx", "gy", None),
        P(("gx", "gy"), None),
        P(("gx", "gy"), None),
        P(("gx", "gy")),
        P(("gx", "gy"), None),
        P(("gx", "gy"), None),
        P(("gx", "gy"), None),
        P(("gx", "gy"), None),
        P(),
        P(("gx", "gy")),
        P(("gx", "gy"), None),
        P(("gx", "gy"), None),
        P(("gx", "gy"), None),
        P(("gx", "gy"), None),
        P(("gx", "gy")),
        P(("gx", "gy"), None),
        P(("gx", "gy"), None),
        P(("gx", "gy"), None),
        P(("gx", "gy")),
    )
    return jax.shard_map(
        per_device,
        mesh=mesh,
        in_specs=placed,
        out_specs=(
            P(),
            P(None, "gx", "gy", None),
            P(("gx", "gy"), None),
            P(("gx", "gy"), None),
            P(("gx", "gy")),
            P(("gx", "gy"), None),
            P(("gx", "gy"), None),
            P(("gx", "gy"), None),
            P(("gx", "gy"), None),
            P(),
            P(("gx", "gy")),
            P(("gx", "gy"), None),
            P(("gx", "gy"), None),
            P(("gx", "gy"), None),
            P(("gx", "gy"), None),
            P(("gx", "gy")),
            P(("gx", "gy"), None),
            P(("gx", "gy"), None),
            P(("gx", "gy"), None),
            P(("gx", "gy")),
        ),
        check_vma=False,
    )
```

```python
import functools
import itertools
import math

import jax
import jax.numpy as jnp
import numpy as np
from jax import lax
from jax.experimental import pallas as pl
from jax.experimental.pallas import tpu as pltpu
from jax.sharding import PartitionSpec as P

HEADS = 6
HEAD = 64
HD = HEADS * HEAD
BUCKETS = 32
GAIN_PAD = 128

eps = 1e-06
masked_score = -1000000000.0
bf16 = jnp.bfloat16
f32 = jnp.float32


def flip(position, offset):
    moved = position
    weight = 1
    while weight <= offset:
        if offset & weight:
            moved = moved + weight * (1 - 2 * ((position // weight) % 2))
        weight *= 2
    return moved


def coordinates():
    gx, gy = lax.axis_index("gx"), lax.axis_index("gy")
    return {"a": gx // 2, "c": gx % 2, "s": gy // 2, "h": gy % 2}


def peer_of(dim, offset):
    gx, gy = lax.axis_index("gx"), lax.axis_index("gy")
    if dim == "a":
        return {"gx": 2 * flip(gx // 2, offset) + gx % 2}
    if dim == "c":
        return {"gx": flip(gx, 1)}
    if dim == "plane":
        s, h, c = offset
        return {
            "gx": gx // 2 * 2 + flip(gx % 2, c),
            "gy": 2 * flip(gy // 2, s) + flip(gy % 2, h),
        }
    if dim == "s":
        return {"gy": 2 * flip(gy // 2, offset) + gy % 2}
    return {"gy": flip(gy, 1)}


def remote(source, target, send, recv, dim, offset):
    return pltpu.make_async_remote_copy(
        src_ref=source,
        dst_ref=target,
        send_sem=send,
        recv_sem=recv,
        device_id=peer_of(dim, offset),
        device_id_type=pl.DeviceIdType.MESH,
    )


def along_line(position, step):
    half = position // 2
    return (position, flip(position, 1), 2 - half, 3 - 3 * half)[step]


def is_middle(position):
    return (position + 1) // 2 == 1


def across_middle():
    gy = lax.axis_index("gy")
    return {"gy": 2 * (3 - gy // 2) + gy % 2}


def spot_of(dim, position, offset):
    return along_line(position, offset) if dim == "s" else flip(position, offset)


def remote_to(source, target, send, recv, device):
    return pltpu.make_async_remote_copy(
        src_ref=source,
        dst_ref=target,
        send_sem=send,
        recv_sem=recv,
        device_id=device,
        device_id_type=pl.DeviceIdType.MESH,
    )


def each_piece(rows, columns, body, width=16384):
    step = rows
    while step * columns > width and step % 32 == 0:
        step //= 2
    if step == rows:
        body(slice(None))
        return

    def piece(number, carry):
        body(pl.ds(pl.multiple_of(number * step, step), step))
        return carry

    lax.fori_loop(0, rows // step, piece, 0)


LINE_PEERS = [("s", 1), ("m", 1)]


class Gather:
    def __init__(self, block, order, layout, sizes, merged=""):
        self.value = block
        self.order, self.layout, self.sizes, self.merged = order, layout, sizes, merged
        self.out = jax.ShapeDtypeStruct(tuple(sizes[d] for d in layout) + block.shape, block.dtype)
        self.in_spec = pl.BlockSpec(memory_space=pltpu.VMEM)
        self.out_spec = pl.BlockSpec(memory_space=pl.ANY)
        self.transfers = []
        for level, dim in enumerate(order):
            ranges = [(None,) if d in merged else range(sizes[d]) for d in order[:level]]
            for unit in itertools.product(*ranges):
                for offset in range(1, sizes[dim]):
                    self.transfers.append((level, unit, offset))
        self.index = {transfer: number for number, transfer in enumerate(self.transfers)}
        count = len(self.transfers)
        self.line = order[0] == "s"
        self.scratch = [
            pltpu.SemaphoreType.DMA((count,)),
            pltpu.SemaphoreType.DMA((count,)),
            pltpu.SemaphoreType.DMA,
            pltpu.SemaphoreType.DMA((5,)),
        ]
        self.peers = [(d, offset) for d in order for offset in range(1, sizes[d]) if d != "s"]
        if self.line:
            self.peers += LINE_PEERS

    def prepare(self, refs, place):
        self.source, self.target, self.send, self.recv, self.local_sem, self.line_send = refs
        self.place = place
        self.local = pltpu.make_async_copy(
            self.source, self.target.at[tuple(place[d] for d in self.layout)], self.local_sem
        )
        self.local.start()
        self.local_done = False
        self.arrived = set()
        self.sent = []

    def region(self, level, unit, offset):
        where = dict(self.place)
        for d, moved in zip(self.order[:level], unit):
            where[d] = slice(None) if moved is None else spot_of(d, self.place[d], moved)
        if offset:
            dim = self.order[level]
            where[dim] = spot_of(dim, self.place[dim], offset)
        return self.target.at[tuple(where[d] for d in self.layout)]

    def needs(self, level, unit):
        if level == 0:
            return []
        last, before = unit[-1], unit[:-1]
        if last is None:
            dim = self.order[level - 1]
            return self.needs(level - 1, before) + [
                (level - 1, before, offset) for offset in range(1, self.sizes[dim])
            ]
        if last == 0:
            return self.needs(level - 1, before)
        return [(level - 1, before, last)]

    def arrive(self, transfer):
        if transfer in self.arrived:
            return
        self.arrived.add(transfer)
        level, unit, offset = transfer
        number = self.index[transfer]
        there = self.region(level, unit, offset)
        if self.line and level == 0:
            offset = 1
        remote(
            there, there, self.send.at[number], self.recv.at[number], self.order[level], offset
        ).wait_recv()

    def line_copy(self, number):
        held, there = ((0, 1), (0, 2), (1, 3), (2, 2), (3, 3))[number]
        target = self.region(0, (), held)
        device = peer_of("s", 1) if number in (0, 3, 4) else across_middle()
        recv = self.recv.at[self.index[(0, (), there)]]
        source = target if held else self.source
        return remote_to(source, target, self.line_send.at[number], recv, device)

    def line_first(self):
        self.line_copy(0).start()

        @pl.when(is_middle(self.place["s"]))
        def _():
            self.line_copy(1).start()

    def line_next(self, step):
        self.arrive((0, (), step))

        @pl.when(is_middle(self.place["s"]))
        def _():
            self.line_copy(step + 1).start()

    def launch(self, transfer):
        level, unit, offset = transfer
        number = self.index[transfer]
        for need in self.needs(level, unit):
            self.arrive(need)
        target = self.region(level, unit, 0)
        own = all(moved == 0 for moved in unit)
        if None in unit and not self.local_done:
            self.local.wait()
            self.local_done = True
        copy = remote(
            self.source if own else target,
            target,
            self.send.at[number],
            self.recv.at[number],
            self.order[level],
            offset,
        )
        copy.start()
        self.sent.append(copy)

    def events(self):
        found = []
        if self.line:
            found.append((0, self.line_first))
            for step in (1, 2, 3):
                found.append((step, functools.partial(self.line_next, step)))
        for transfer in self.transfers:
            level, unit, offset = transfer
            if self.line and level == 0:
                continue
            key = 0.1 * level + 0.01 * offset
            for d, moved in zip(self.order, unit):
                key += self.sizes[d] - 1 if moved is None else moved
            found.append((key, functools.partial(self.launch, transfer)))
        return found

    def finish(self):
        if not self.local_done:
            self.local.wait()
        for transfer in self.transfers:
            self.arrive(transfer)
        for copy in self.sent:
            copy.wait_send()
        if self.line:
            self.line_copy(0).wait_send()

            @pl.when(is_middle(self.place["s"]))
            def _():
                for number in range(1, 5):
                    self.line_copy(number).wait_send()


class DirectGather:
    def __init__(self, block, sizes):
        self.value = block
        shape = (sizes["s"], 2, 2)
        self.out = jax.ShapeDtypeStruct(shape + block.shape, block.dtype)
        self.in_spec = pl.BlockSpec(memory_space=pltpu.VMEM)
        self.out_spec = pl.BlockSpec(memory_space=pltpu.VMEM)
        self.offsets = list(itertools.product(*(range(size) for size in shape)))[1:]
        count = len(self.offsets)
        self.scratch = [pltpu.SemaphoreType.DMA((count,)), pltpu.SemaphoreType.DMA((count,))]
        self.peers = [("plane", offset) for offset in self.offsets]

    def prepare(self, refs, place):
        self.source, self.target, self.send, self.recv = refs
        self.place = place
        self.target[place["s"], place["h"], place["c"]] = self.source[...]

    def copy(self, number, arriving):
        offset = self.offsets[number]
        spot = tuple(
            flip(self.place[d], moved) if arriving else self.place[d] for d, moved in zip("shc", offset)
        )
        return remote_to(
            self.source,
            self.target.at[spot],
            self.send.at[number],
            self.recv.at[number],
            peer_of("plane", offset),
        )

    def events(self):
        return [(0, functools.partial(self.start, number)) for number in range(len(self.offsets))]

    def start(self, number):
        self.copy(number, False).start()

    def finish(self):
        for number in range(len(self.offsets)):
            self.copy(number, True).wait()


class Scatter:
    def __init__(self, value, order, layout, sizes, merged="", out_dtype=f32):
        self.value = value
        self.order, self.layout, self.sizes, self.merged = order, layout, sizes, merged
        self.block = value.shape[len(layout) :]
        self.out = jax.ShapeDtypeStruct(self.block, out_dtype)
        self.in_spec = pl.BlockSpec(memory_space=pltpu.VMEM)
        self.out_spec = pl.BlockSpec(memory_space=pltpu.VMEM)
        self.line = order[-1] == "s"
        self.levels = len(order)
        self.units = []
        self.scratch = []
        self.layouts = [layout]
        for level, dim in enumerate(order):
            later = order[level + 1 :]
            ranges = [(None,) if d in merged else range(sizes[d]) for d in later]
            units = sorted(
                itertools.product(*ranges),
                key=lambda unit: (-(unit[-1] or 0) if unit else 0, -sum(moved or 0 for moved in unit)),
            )
            self.units.append(units)
            left = "".join(d for d in self.layouts[-1] if d != dim)
            self.layouts.append(left)
            self.scratch.append(
                pltpu.VMEM(
                    (5 if dim == "s" else sizes[dim] - 1,)
                    + tuple(sizes[d] for d in left)
                    + self.block,
                    value.dtype,
                )
            )
        self.index = {}
        for level, dim in enumerate(order):
            for unit in self.units[level]:
                for offset in range(1, sizes[dim]):
                    self.index[(level, unit, offset)] = len(self.index)
        count = len(self.index)
        self.scratch += [
            pltpu.SemaphoreType.DMA((count,)),
            pltpu.SemaphoreType.DMA((count,)),
            pltpu.SemaphoreType.DMA((2, 5)),
        ]
        self.peers = [(d, offset) for d in order for offset in range(1, sizes[d]) if d != "s"]
        if self.line:
            self.peers += LINE_PEERS

    def prepare(self, refs, place):
        self.source, self.target = refs[0], refs[1]
        self.landing = refs[2 : 2 + self.levels]
        self.send, self.recv, self.line_sems = refs[2 + self.levels :]
        self.place = place
        self.sent = []

    def held(self, level):
        return self.source if level == 0 else self.landing[level - 1].at[0]

    def later(self, level, unit):
        where = {}
        for d, moved in zip(self.order[level + 1 :], unit):
            where[d] = slice(None) if moved is None else spot_of(d, self.place[d], moved)
        return where

    def copy(self, level, unit, offset):
        number = self.index[(level, unit, offset)]
        dim = self.order[level]
        where = self.later(level, unit)
        landed = self.landing[level].at[
            (offset - 1,) + tuple(where[d] for d in self.layouts[level + 1])
        ]
        where[dim] = flip(self.place[dim], offset)
        source = self.held(level).at[tuple(where[d] for d in self.layouts[level])]
        return remote(source, landed, self.send.at[number], self.recv.at[number], dim, offset)

    def launch(self, level, unit, offset):
        copy = self.copy(level, unit, offset)
        copy.start()
        self.sent.append(copy)

    def reduce(self, level, unit):
        dim = self.order[level]
        size = self.sizes[dim]
        for offset in range(1, size):
            self.copy(level, unit, offset).wait_recv()
        where = self.later(level, unit)
        free = [d for d in self.order[level + 1 :] if isinstance(where[d], slice)]
        total = math.prod(self.sizes[d] for d in free)
        rows, columns = self.block
        last = level == self.levels - 1

        def one(number, carry):
            at = dict(where)
            rest = number
            for d in free:
                at[d] = rest % self.sizes[d]
                rest = rest // self.sizes[d]
            spot = tuple(at[d] for d in self.layouts[level + 1])
            at[dim] = self.place[dim]
            mine = tuple(at[d] for d in self.layouts[level])

            def body(piece):
                if not last and size == 2:
                    self.landing[level][(0,) + spot + (piece,)] += self.held(level)[mine + (piece,)]
                    return
                result = self.held(level)[mine + (piece,)].astype(f32)
                for offset in range(1, size):
                    result = result + self.landing[level][(offset - 1,) + spot + (piece,)].astype(f32)
                if last:
                    self.target[(piece,)] = result.astype(self.target.dtype)
                else:
                    self.landing[level][(0,) + spot + (piece,)] = result.astype(self.landing[level].dtype)

            each_piece(rows, columns, body)
            return carry

        if total == 1:
            one(0, 0)
        else:
            lax.fori_loop(0, total, one, 0)
        if not last and not (self.line and level == self.levels - 2):
            ahead, rest = unit[0], unit[1:]
            if ahead is None:
                offsets = range(1, self.sizes[self.order[level + 1]])
            else:
                offsets = [ahead] if ahead else []
            for offset in offsets:
                self.launch(level + 1, rest, offset)

    def line_copy(self, number):
        step, slot = ((1, 0), (2, 1), (3, 2), (3, 3), (2, 4))[number]
        level = self.levels - 1
        block = self.held(level).at[along_line(self.place["s"], step)]
        landed = self.landing[level].at[slot]
        device = peer_of("s", 1) if number < 3 else across_middle()
        return remote_to(block, landed, self.line_sems.at[0, number], self.line_sems.at[1, number], device)

    def line_step(self, step):
        level = self.levels - 1
        middle = is_middle(self.place["s"])
        rows, columns = self.block
        held, landing = self.held(level), self.landing[level]
        position = along_line(self.place["s"], step)

        if step:
            @pl.when(jnp.logical_not(middle))
            def _():
                self.line_copy(step - 1).start()

            @pl.when(middle)
            def _():
                arrived = (0, 3, 1, 2)[step]
                self.line_copy(arrived).wait_recv()

                def body(piece):
                    held[(position, piece)] += landing[(arrived, piece)]

                each_piece(rows, columns, body)
                self.line_copy((0, 0, 4, 3)[step]).start()

            return

        self.line_copy(0).wait_recv()

        @pl.when(middle)
        def _():
            self.line_copy(4).wait_recv()

            def body(piece):
                result = held[(position, piece)].astype(f32) + landing[(0, piece)].astype(f32)
                self.target[(piece,)] = (result + landing[(4, piece)].astype(f32)).astype(
                    self.target.dtype
                )

            each_piece(rows, columns, body)

        @pl.when(jnp.logical_not(middle))
        def _():
            def body(piece):
                result = held[(position, piece)].astype(f32) + landing[(0, piece)].astype(f32)
                self.target[(piece,)] = result.astype(self.target.dtype)

            each_piece(rows, columns, body)

    def events(self):
        found = []
        for number, unit in enumerate(self.units[0]):
            for offset in range(1, self.sizes[self.order[0]]):
                found.append(
                    (-1 + 0.001 * number, functools.partial(self.launch, 0, unit, offset))
                )
        spread = 4 if self.line else 1
        for level in range(self.levels - self.line):
            count = len(self.units[level])
            for number, unit in enumerate(self.units[level]):
                found.append(
                    (level + spread * number / count, functools.partial(self.reduce, level, unit))
                )
        if self.line:
            for number, step in enumerate((3, 2, 1, 0)):
                found.append(
                    (self.levels - 1 + number + 0.5, functools.partial(self.line_step, step))
                )
        return found

    def finish(self):
        for copy in self.sent:
            copy.wait_send()
        if self.line:
            self.line_copy(0).wait_send()
            middle = is_middle(self.place["s"])

            @pl.when(middle)
            def _():
                for number in (3, 4):
                    self.line_copy(number).wait_send()

            @pl.when(jnp.logical_not(middle))
            def _():
                for number in (1, 2):
                    self.line_copy(number).wait_send()


class MemoryGather:
    def __init__(self, memory, sizes):
        self.value = memory
        self.sizes = sizes
        self.out = jax.ShapeDtypeStruct((sizes["s"], 2) + memory.shape[1:], memory.dtype)
        self.in_spec = pl.BlockSpec(memory_space=pltpu.VMEM)
        self.out_spec = pl.BlockSpec(memory_space=pl.ANY)
        rows = sizes["s"]
        self.scratch = [
            pltpu.SemaphoreType.DMA((2, rows)),
            pltpu.SemaphoreType.DMA((2, rows)),
            pltpu.SemaphoreType.DMA((2, rows, 2)),
            pltpu.SemaphoreType.DMA,
        ]
        self.peers = [("s", offset) for offset in range(1, rows)] + [("h", 1), ("c", 1)]

    def prepare(self, refs, place):
        self.source, self.target, self.along, self.across, self.core, self.local = refs
        self.place = place
        self.mine = place["s"] % 2 == place["c"]

    def row(self, offset):
        return flip(self.place["s"], offset)

    def along_copy(self, offset, arriving):
        to = self.row(offset)
        spot = to if arriving else self.place["s"]
        return remote(
            self.source.at[self.place["s"] // 2 if arriving else to // 2],
            self.target.at[spot, self.place["h"]],
            self.along.at[0, offset],
            self.along.at[1, offset],
            "s",
            offset,
        )

    def across_copy(self, offset, arriving):
        h = self.place["h"]
        own = self.target.at[self.row(offset), 1 - h if arriving else h]
        if offset == 0 and not arriving:
            source = self.source.at[self.place["s"] // 2]
        else:
            source = own
        return remote(source, own, self.across.at[0, offset], self.across.at[1, offset], "h", 1)

    def core_copy(self, offset, other):
        h = self.place["h"]
        own = self.target.at[self.row(offset), 1 - h if other else h]
        source = self.source.at[self.place["s"] // 2] if offset == 0 and not other else own
        return remote(source, own, self.core.at[0, offset, other], self.core.at[1, offset, other], "c", 1)

    def events(self):
        rows = self.sizes["s"]

        def first():
            for offset in range(1, rows):
                @pl.when(self.row(offset) % 2 == self.place["c"])
                def _():
                    self.along_copy(offset, False).start()

            @pl.when(self.mine)
            def _():
                pltpu.make_async_copy(
                    self.source.at[self.place["s"] // 2],
                    self.target.at[self.place["s"], self.place["h"]],
                    self.local,
                ).start()
                self.across_copy(0, False).start()
                self.core_copy(0, 0).start()

        def arrival(offset):
            @pl.when(self.mine)
            def _():
                self.along_copy(offset, True).wait_recv()
                self.across_copy(offset, False).start()
                self.core_copy(offset, 0).start()

        def other(offset):
            @pl.when(self.mine)
            def _():
                self.across_copy(offset, True).wait_recv()
                self.core_copy(offset, 1).start()

        found = [(0.05, first)]
        for offset in range(1, rows):
            found.append((offset + 0.05, functools.partial(arrival, offset)))
        for offset in range(rows):
            found.append((rows + offset, functools.partial(other, offset)))
        return found

    def finish(self):
        rows = self.sizes["s"]
        for offset in range(1, rows):
            @pl.when(self.row(offset) % 2 == self.place["c"])
            def _():
                self.along_copy(offset, False).wait_send()

        @pl.when(self.mine)
        def _():
            pltpu.make_async_copy(
                self.source.at[self.place["s"] // 2],
                self.target.at[self.place["s"], self.place["h"]],
                self.local,
            ).wait()
            for offset in range(rows):
                self.across_copy(offset, False).wait_send()
                for other in range(2):
                    self.core_copy(offset, other).wait_send()

        @pl.when(jnp.logical_not(self.mine))
        def _():
            for offset in range(rows):
                for other in range(2):
                    self.core_copy(offset, other).wait_recv()


class MemoryScatter:
    def __init__(self, value, sizes):
        self.value = value
        self.sizes = sizes
        rows = sizes["s"]
        self.block = value.shape[2:]
        self.out = jax.ShapeDtypeStruct((2,) + self.block, f32)
        self.in_spec = pl.BlockSpec(memory_space=pltpu.VMEM)
        self.out_spec = pl.BlockSpec(memory_space=pltpu.VMEM)
        self.scratch = [
            pltpu.VMEM(value.shape, value.dtype),
            pltpu.VMEM((rows,) + self.block, value.dtype),
            pltpu.VMEM((2,) + self.block, value.dtype),
            pltpu.SemaphoreType.DMA((2, rows, 2)),
            pltpu.SemaphoreType.DMA((2, rows)),
            pltpu.SemaphoreType.DMA((2, rows)),
        ]
        self.peers = [("s", offset) for offset in range(1, rows)] + [("h", 1), ("c", 1)]

    def prepare(self, refs, place):
        self.source, self.target = refs[0], refs[1]
        self.summed, self.halved, self.landed, self.core, self.across, self.along = refs[2:]
        self.place = place
        self.mine = place["s"] % 2 == place["c"]

    def row(self, offset):
        return flip(self.place["s"], offset)

    def core_copy(self, offset, other):
        h = self.place["h"]
        spot = (self.row(offset), flip(h, 1) if other else h)
        return remote(
            self.source.at[spot],
            self.summed.at[spot],
            self.core.at[0, offset, other],
            self.core.at[1, offset, other],
            "c",
            1,
        )

    def across_copy(self, offset):
        row = self.row(offset)
        return remote(
            self.summed.at[row, flip(self.place["h"], 1)],
            self.halved.at[row],
            self.across.at[0, offset],
            self.across.at[1, offset],
            "h",
            1,
        )

    def along_copy(self, offset, arriving):
        to = self.row(offset)
        return remote(
            self.halved.at[to],
            self.landed.at[to // 2 if arriving else self.place["s"] // 2],
            self.along.at[0, offset],
            self.along.at[1, offset],
            "s",
            offset,
        )

    def events(self):
        rows = self.sizes["s"]
        high, wide = self.block
        orders = list(range(1, rows))[::-1] + [0]

        def first():
            @pl.when(jnp.logical_not(self.mine))
            def _():
                for other in (1, 0):
                    for offset in orders:
                        self.core_copy(offset, other).start()

        def level(offset, other):
            @pl.when(self.mine)
            def _():
                self.core_copy(offset, other).wait_recv()
                h = self.place["h"]
                spot = (self.row(offset), flip(h, 1) if other else h)

                def body(piece):
                    total = self.summed[spot + (piece,)].astype(f32) + self.source[
                        spot + (piece,)
                    ].astype(f32)
                    self.summed[spot + (piece,)] = total.astype(self.summed.dtype)

                each_piece(high, wide, body)
                if other:
                    self.across_copy(offset).start()

        def last(offset):
            @pl.when(self.mine)
            def _():
                self.across_copy(offset).wait_recv()
                row = self.row(offset)

                def body(piece):
                    total = self.halved[(row, piece)].astype(f32) + self.summed[
                        (row, self.place["h"], piece)
                    ].astype(f32)
                    self.halved[(row, piece)] = total.astype(self.halved.dtype)
                    if offset == 0:
                        self.target[(self.place["s"] // 2, piece)] = total

                each_piece(high, wide, body)
                if offset:
                    self.along_copy(offset, False).start()

        found = [(-0.95, first)]
        for number, offset in enumerate(orders):
            found.append((0.05 + 0.1 * number, functools.partial(level, offset, 1)))
        for number, offset in enumerate(orders):
            found.append((0.55 + 0.1 * number, functools.partial(level, offset, 0)))
        for number, offset in enumerate(orders):
            found.append((1.05 + 0.2 * number, functools.partial(last, offset)))
        return found

    def finish(self):
        rows = self.sizes["s"]
        high, wide = self.block
        for offset in range(1, rows):
            @pl.when(self.row(offset) % 2 == self.place["c"])
            def _():
                self.along_copy(offset, True).wait_recv()
                number = self.row(offset) // 2

                def body(piece):
                    self.target[(number, piece)] = self.landed[(number, piece)].astype(f32)

                each_piece(high, wide, body)

        @pl.when(self.mine)
        def _():
            for offset in range(rows):
                self.across_copy(offset).wait_send()
            for offset in range(1, rows):
                self.along_copy(offset, False).wait_send()

        @pl.when(jnp.logical_not(self.mine))
        def _():
            for offset in range(rows):
                for other in range(2):
                    self.core_copy(offset, other).wait_send()


def exchange(name, collective_id, jobs):
    sizes = [len(job.scratch) for job in jobs]
    peers = []
    for job in jobs:
        for peer in job.peers:
            if peer not in peers:
                peers.append(peer)

    def kernel(*refs):
        count = len(jobs)
        scratch = refs[2 * count :]
        offset = 0
        barrier = pltpu.get_barrier_semaphore()
        place = coordinates()
        middle = is_middle(place["s"])
        awaited = 0
        for peer in peers:
            if peer[0] == "m":
                @pl.when(middle)
                def _():
                    pl.semaphore_signal(
                        barrier, inc=1, device_id=across_middle(), device_id_type=pl.DeviceIdType.MESH
                    )
                continue
            awaited += 1
            pl.semaphore_signal(
                barrier, inc=1, device_id=peer_of(*peer), device_id_type=pl.DeviceIdType.MESH
            )
        for number, job in enumerate(jobs):
            job.prepare(
                (refs[number], refs[count + number]) + tuple(scratch[offset : offset + sizes[number]]),
                place,
            )
            offset += sizes[number]
        if ("m", 1) in peers:
            @pl.when(middle)
            def _():
                pl.semaphore_wait(barrier, awaited + 1)

            @pl.when(jnp.logical_not(middle))
            def _():
                pl.semaphore_wait(barrier, awaited)
        else:
            pl.semaphore_wait(barrier, awaited)
        events = [event for job in jobs for event in job.events()]
        for _, act in sorted(events, key=lambda event: event[0]):
            act()
        for job in jobs:
            job.finish()

    return pl.pallas_call(
        kernel,
        name=name,
        out_shape=tuple(job.out for job in jobs),
        in_specs=[job.in_spec for job in jobs],
        out_specs=tuple(job.out_spec for job in jobs),
        scratch_shapes=[item for job in jobs for item in job.scratch],
        compiler_params=pltpu.CompilerParams(
            collective_id=collective_id, has_side_effects=True, vmem_limit_bytes=60 * 1024 * 1024
        ),
    )(*[job.value for job in jobs])


def packed(block):
    rows, columns = block.shape
    if rows % 16 == 0:
        return block
    return block.reshape(16, rows * columns // 16)


def bucket_edges():
    edges = []
    for target in range(1, 32):
        if target < 16:
            edges.append(target)
        else:
            found = 0
            for distance in range(16, 4096):
                value = 16 + int(math.log(distance / 16.0) / math.log(8.0) * 16.0)
                if found == 0 and value >= target:
                    found = distance
            edges.append(found)
    return edges


def gelu_tanh(value):
    return (
        0.5
        * value
        * (1.0 + jnp.tanh(0.7978845608028654 * (value + 0.044715 * value * value * value)))
    )


def dot(left, right):
    return jnp.einsum("sd,df->sf", left, right, preferred_element_type=f32)


def dot_t(left, right):
    return jnp.einsum("sf,df->sd", left, right, preferred_element_type=f32)


def t_dot(left, right):
    return jnp.einsum("sd,sf->df", left, right, preferred_element_type=f32)


def distance_table(seq):
    edges = np.array(bucket_edges())
    distance = (-np.arange(seq)) % seq
    bucket = (distance[:, None] >= edges[None, :]).sum(axis=1)
    return (np.arange(BUCKETS)[:, None] == bucket[None, :]).astype(np.float32)


def mm(left, right):
    return lax.dot_general(left, right, (((1,), (0,)), ((), ())), preferred_element_type=f32)


def mm_t(left, right):
    return lax.dot_general(left, right, (((1,), (1,)), ((), ())), preferred_element_type=f32)


def t_mm(left, right):
    return lax.dot_general(left, right, (((0,), (0,)), ((), ())), preferred_element_type=f32)


def inverse_rms(rows):
    return lax.rsqrt(jnp.mean(rows * rows, axis=-1, keepdims=True) + eps)


def rms_back(rows, gain, slope):
    inverse = inverse_rms(rows)
    unit = rows * inverse
    scaled = slope * gain
    back = inverse * (scaled - unit * jnp.mean(unit * scaled, axis=-1, keepdims=True))
    return back, jnp.sum(slope * unit, axis=0, keepdims=True)


def lanes_of(shape):
    return lax.broadcasted_iota(jnp.int32, shape, len(shape) - 1)


def one_half(pair, half):
    inside = (lanes_of(pair.shape) // HEAD) == half
    return jnp.where(inside, pair, jnp.zeros_like(pair))


def joined(first, second):
    return jnp.where(lanes_of(first.shape) < HEAD, first, second)


def pair_of(ref, start, pair):
    return ref[:, start + 2 * HEAD * pair : start + 2 * HEAD * (pair + 1)]


FF_STEP = 256


class Fetch:
    def __init__(self, sources, targets, sems):
        self.copies = [
            pltpu.make_async_copy(source, target, sems.at[number])
            for number, (source, target) in enumerate(zip(sources, targets))
        ]
        self.targets = targets
        self.ready = set()
        for copy in self.copies:
            copy.start()

    def __getitem__(self, number):
        if number not in self.ready:
            self.ready.add(number)
            self.copies[number].wait()
        return self.targets[number]


def enter_kernel(resid_ref, part_c_ref, query_ref, kv_ref, normed_ref, gains_ref):
    row = lax.broadcasted_iota(jnp.int32, (16, GAIN_PAD), 0)
    pick = (row == lanes_of((16, GAIN_PAD))).astype(bf16)
    gains = mm_t(pick, part_c_ref[:, 5 * HD : 5 * HD + GAIN_PAD])
    gains_ref[...] = gains
    resid = resid_ref[...]
    normed = (resid * inverse_rms(resid) * gains[0:1]).astype(bf16)
    normed_ref[...] = normed
    query_ref[...] = mm(normed, part_c_ref[:, :HD]).astype(bf16)
    kv_ref[...] = mm(normed, part_c_ref[:, HD : 3 * HD]).astype(bf16)


def biased_scores(scores, row, first, length):
    bias = pltpu.roll(jnp.broadcast_to(row, scores.shape), 0, 1, stride=1, stride_axis=0)
    query_pos = first + lax.broadcasted_iota(jnp.int32, scores.shape, 0)
    key_pos = lanes_of(scores.shape)
    mask = (key_pos <= query_pos) & (key_pos < length)
    return jnp.where(mask, scores + bias, masked_score)


def softmax_parts(scores):
    highest = jnp.max(scores, axis=-1, keepdims=True)
    total = highest + jnp.log(jnp.sum(jnp.exp(scores - highest), axis=-1, keepdims=True))
    return total, jnp.exp(scores - total)


def forward_kernel(
    scalars_ref,
    query_ref,
    kv_ref,
    resid0_ref,
    gains_ref,
    table_ref,
    bias_ref,
    memory_hbm,
    part_a_hbm,
    part_b_hbm,
    part_c_hbm,
    attn_self_ref,
    total_self_ref,
    resid1_ref,
    normed_cross_ref,
    query_cross_ref,
    mem_kv_ref,
    attn_cross_ref,
    total_cross_ref,
    resid2_ref,
    normed_ff_ref,
    gate_up_ref,
    hidden_ref,
    resid3_ref,
    final_ref,
    memory_ref,
    part_a_ref,
    part_b_ref,
    part_c_ref,
    sems,
):
    fetched = Fetch(
        (part_c_hbm, part_b_hbm, memory_hbm, part_a_hbm),
        (part_c_ref, part_b_ref, memory_ref, part_a_ref),
        sems,
    )
    first, length = scalars_ref[0], scalars_ref[1]
    ff = hidden_ref.shape[1]
    bias_rows = pltpu.roll(mm(bias_ref[...], table_ref[...]), first, 1)
    lanes = lanes_of(total_self_ref.shape)
    totals = jnp.zeros(total_self_ref.shape, f32)
    for pair in range(HEADS // 2):
        keys, values = pair_of(kv_ref, 0, pair), pair_of(kv_ref, HD, pair)
        outputs = []
        for half in range(2):
            number = 2 * pair + half
            scores = mm_t(one_half(pair_of(query_ref, 0, pair), half), keys)
            scores = biased_scores(scores, bias_rows[number : number + 1], first, length)
            total, shares = softmax_parts(scores)
            totals = jnp.where(lanes == number, total, totals)
            outputs.append(mm(shares.astype(bf16), values))
        attn_self_ref[:, 2 * HEAD * pair : 2 * HEAD * (pair + 1)] = joined(*outputs).astype(bf16)
    total_self_ref[...] = totals

    part_c = fetched[0]
    resid1 = resid0_ref[...] + mm_t(attn_self_ref[...], part_c[:, 3 * HD : 4 * HD])
    resid1_ref[...] = resid1
    normed = (resid1 * inverse_rms(resid1) * gains_ref[1:2]).astype(bf16)
    normed_cross_ref[...] = normed
    query_cross_ref[...] = mm(normed, part_c[:, 4 * HD : 5 * HD]).astype(bf16)

    part_b = fetched[1]
    memory = fetched[2]
    step = min(256, memory.shape[0])

    def project(number, carry):
        rows = pl.ds(pl.multiple_of(number * step, step), step)
        mem_kv_ref[rows, :] = mm(memory[rows, :], part_b[:, ff : ff + 2 * HD]).astype(bf16)
        return carry

    lax.fori_loop(0, memory.shape[0] // step, project, 0)
    totals = jnp.zeros(total_self_ref.shape, f32)
    for pair in range(HEADS // 2):
        keys, values = pair_of(mem_kv_ref, 0, pair), pair_of(mem_kv_ref, HD, pair)
        outputs = []
        for half in range(2):
            scores = mm_t(one_half(pair_of(query_cross_ref, 0, pair), half), keys)
            total, shares = softmax_parts(scores)
            totals = jnp.where(lanes == 2 * pair + half, total, totals)
            outputs.append(mm(shares.astype(bf16), values))
        attn_cross_ref[:, 2 * HEAD * pair : 2 * HEAD * (pair + 1)] = joined(*outputs).astype(bf16)
    total_cross_ref[...] = totals
    resid2 = resid1_ref[...] + mm_t(attn_cross_ref[...], part_b[:, ff + 2 * HD :])
    resid2_ref[...] = resid2
    normed_ff_ref[...] = (resid2 * inverse_rms(resid2) * gains_ref[2:3]).astype(bf16)

    part_a = fetched[3]
    for start in range(0, ff, FF_STEP):
        gate = mm(normed_ff_ref[...], part_a[:, start : start + FF_STEP])
        up = mm(normed_ff_ref[...], part_a[:, ff + start : ff + start + FF_STEP])
        gate_up_ref[:, start : start + FF_STEP] = gate
        gate_up_ref[:, ff + start : ff + start + FF_STEP] = up
        hidden_ref[:, start : start + FF_STEP] = (gelu_tanh(gate) * up).astype(bf16)
    resid3 = resid2_ref[...] + mm_t(hidden_ref[...], part_b[:, :ff])
    resid3_ref[...] = resid3
    final_ref[...] = (resid3 * inverse_rms(resid3) * gains_ref[3:4]).astype(bf16)


def attention_back(query, keys, values, scores, total, out_slope):
    shares = jnp.exp(scores - total)
    share_slope = mm_t(out_slope, values)
    inner = jnp.sum(shares * share_slope, axis=-1, keepdims=True)
    score_slope = shares * (share_slope - inner)
    rounded = score_slope.astype(bf16)
    return (
        rounded,
        mm(rounded, keys),
        t_mm(rounded, query),
        t_mm(shares.astype(bf16), out_slope),
    )


def backward_kernel(
    scalars_ref,
    slope_ref,
    resid3_ref,
    hidden_ref,
    gate_up_ref,
    normed_ff_ref,
    resid2_ref,
    attn_cross_ref,
    query_cross_ref,
    total_cross_ref,
    normed_cross_ref,
    resid1_ref,
    attn_self_ref,
    query_ref,
    kv_ref,
    total_self_ref,
    gains_ref,
    table_ref,
    bias_ref,
    mem_kv_hbm,
    memory_hbm,
    part_a_hbm,
    part_b_hbm,
    part_c_hbm,
    grad_a_hbm,
    grad_b_hbm,
    memory_part_hbm,
    grad_c_ref,
    query_slope_ref,
    kv_slope_ref,
    grad1_ref,
    norm_grads_ref,
    bias_grad_ref,
    mem_kv_ref,
    memory_ref,
    part_a_ref,
    part_b_ref,
    part_c_ref,
    grad_a_ref,
    grad_b_ref,
    memory_part_ref,
    gate_up_slope_ref,
    cross_query_slope_ref,
    cross_kv_slope_ref,
    sems,
    out_sems,
):
    fetched = Fetch(
        (part_b_hbm, part_a_hbm, mem_kv_hbm, memory_hbm, part_c_hbm),
        (part_b_ref, part_a_ref, mem_kv_ref, memory_ref, part_c_ref),
        sems,
    )
    first, length = scalars_ref[0], scalars_ref[1]
    ff = hidden_ref.shape[1]
    width = resid3_ref.shape[1]
    norm_grads_ref[...] = jnp.zeros_like(norm_grads_ref)

    grad3, norm_grad = rms_back(resid3_ref[...], gains_ref[3:4], slope_ref[...])
    norm_grads_ref[3:4] = norm_grad
    down_in = grad3.astype(bf16)
    part_b = fetched[0]
    for start in range(0, ff, FF_STEP):
        here, there = slice(start, start + FF_STEP), slice(ff + start, ff + start + FF_STEP)
        hidden_slope = mm(down_in, part_b[:, here])
        gate, up = gate_up_ref[:, here], gate_up_ref[:, there]
        inner = jnp.tanh(0.7978845608028654 * (gate + 0.044715 * gate * gate * gate))
        activated = 0.5 * gate * (1.0 + inner)
        steep = 0.5 * (1.0 + inner) + 0.5 * gate * (1.0 - inner * inner) * (
            0.7978845608028654 * (1.0 + 3.0 * 0.044715 * gate * gate)
        )
        gate_up_slope_ref[:, here] = (hidden_slope * up * steep).astype(bf16)
        gate_up_slope_ref[:, there] = (hidden_slope * activated).astype(bf16)
        grad_b_ref[:, here] = t_mm(down_in, hidden_ref[:, here]).astype(bf16)
    part_a = fetched[1]
    back, norm_grad = rms_back(
        resid2_ref[...], gains_ref[2:3], mm_t(gate_up_slope_ref[...], part_a[...])
    )
    norm_grads_ref[2:3] = norm_grad
    grad2 = grad3 + back
    for start in range(0, 2 * ff, 2 * FF_STEP):
        here = slice(start, start + 2 * FF_STEP)
        grad_a_ref[:, here] = t_mm(normed_ff_ref[...], gate_up_slope_ref[:, here]).astype(bf16)
    copy_a = pltpu.make_async_copy(grad_a_ref, grad_a_hbm, out_sems.at[0])
    copy_a.start()

    cross_in = grad2.astype(bf16)
    grad_b_ref[:, ff + 2 * HD :] = t_mm(cross_in, attn_cross_ref[...]).astype(bf16)
    out_slope = mm(cross_in, part_b[:, ff + 2 * HD :]).astype(bf16)
    mem_kv = fetched[2]
    for pair in range(HEADS // 2):
        place = slice(2 * HEAD * pair, 2 * HEAD * (pair + 1))
        place_v = slice(HD + 2 * HEAD * pair, HD + 2 * HEAD * (pair + 1))
        keys, values = mem_kv[:, place], mem_kv[:, place_v]
        parts = []
        for half in range(2):
            number = 2 * pair + half
            query = one_half(query_cross_ref[:, place], half)
            parts.append(
                attention_back(
                    query,
                    keys,
                    values,
                    mm_t(query, keys),
                    total_cross_ref[:, number : number + 1],
                    one_half(out_slope[:, place], half),
                )
            )
        cross_query_slope_ref[:, place] = joined(parts[0][1], parts[1][1]).astype(bf16)
        cross_kv_slope_ref[:, place] = (parts[0][2] + parts[1][2]).astype(bf16)
        cross_kv_slope_ref[:, place_v] = (parts[0][3] + parts[1][3]).astype(bf16)
    memory = fetched[3]
    for start in range(0, 2 * HD, 2 * HEAD):
        here = slice(start, start + 2 * HEAD)
        grad_b_ref[:, ff + start : ff + start + 2 * HEAD] = t_mm(
            memory[...], cross_kv_slope_ref[:, here]
        ).astype(bf16)
    copy_b = pltpu.make_async_copy(grad_b_ref, grad_b_hbm, out_sems.at[1])
    copy_b.start()
    step = min(256, memory.shape[0])

    def project(number, carry):
        rows = pl.ds(pl.multiple_of(number * step, step), step)
        memory_part_ref[rows, :] = mm_t(
            cross_kv_slope_ref[rows, :], part_b[:, ff : ff + 2 * HD]
        ).astype(bf16)
        return carry

    lax.fori_loop(0, memory.shape[0] // step, project, 0)
    copy_m = pltpu.make_async_copy(memory_part_ref, memory_part_hbm, out_sems.at[2])
    copy_m.start()
    part_c = fetched[4]
    query_slope = cross_query_slope_ref[...]
    grad_c_ref[:, HD : 2 * HD] = t_mm(normed_cross_ref[...], query_slope).astype(bf16)
    back, norm_grad = rms_back(
        resid1_ref[...], gains_ref[1:2], mm_t(query_slope, part_c[:, 4 * HD : 5 * HD])
    )
    norm_grads_ref[1:2] = norm_grad
    grad1 = grad2 + back
    grad1_ref[...] = grad1

    self_in = grad1.astype(bf16)
    grad_c_ref[:, :HD] = t_mm(self_in, attn_self_ref[...]).astype(bf16)
    out_slope = mm(self_in, part_c[:, 3 * HD : 4 * HD]).astype(bf16)
    bias_rows = pltpu.roll(mm(bias_ref[...], table_ref[...]), first, 1)
    bias_sums = jnp.zeros(bias_rows.shape, f32)
    rows, seq = query_ref.shape[0], kv_ref.shape[0]
    reverse = lax.broadcasted_iota(jnp.int32, (rows, rows), 0) + lanes_of((rows, rows)) == rows - 1
    reverse = reverse.astype(bf16)
    for pair in range(HEADS // 2):
        place = slice(2 * HEAD * pair, 2 * HEAD * (pair + 1))
        place_v = slice(HD + 2 * HEAD * pair, HD + 2 * HEAD * (pair + 1))
        keys, values = kv_ref[:, place], kv_ref[:, place_v]
        parts = []
        for half in range(2):
            number = 2 * pair + half
            query = one_half(query_ref[:, place], half)
            scores = biased_scores(
                mm_t(query, keys), bias_rows[number : number + 1], first, length
            )
            part = attention_back(
                query,
                keys,
                values,
                scores,
                total_self_ref[:, number : number + 1],
                one_half(out_slope[:, place], half),
            )
            parts.append(part)
            turned = pltpu.roll(mm(reverse, part[0]), 0, 1, stride=1, stride_axis=0)
            where = lax.broadcasted_iota(jnp.int32, bias_sums.shape, 0) == number
            bias_sums = jnp.where(where, jnp.sum(turned, axis=0, keepdims=True), bias_sums)
        query_slope_ref[:, place] = joined(parts[0][1], parts[1][1]).astype(bf16)
        kv_slope_ref[:, place] = (parts[0][2] + parts[1][2]).astype(bf16)
        kv_slope_ref[:, place_v] = (parts[0][3] + parts[1][3]).astype(bf16)
    bias_sums = pltpu.roll(bias_sums, 2 * seq + 1 - rows - first, 1)
    high = bias_sums.astype(bf16)
    rest = bias_sums - high.astype(f32)
    middle = rest.astype(bf16)
    low = (rest - middle.astype(f32)).astype(bf16)
    table = table_ref[...]
    bias_grad_ref[...] = mm_t(high, table) + (mm_t(middle, table) + mm_t(low, table))
    copy_a.wait()
    copy_b.wait()
    copy_m.wait()


def leave_kernel(
    query_slope_ref,
    kv_slope_ref,
    normed_ref,
    resid0_ref,
    grad1_ref,
    gains_ref,
    norm_grads_ref,
    part_grad_ref,
    part_c_ref,
    grad_c_ref,
    grad0_ref,
):
    normed = normed_ref[...]
    query_slope, kv_slope = query_slope_ref[...], kv_slope_ref[...]
    slope = mm_t(query_slope, part_c_ref[:, :HD]) + mm_t(kv_slope, part_c_ref[:, HD : 3 * HD])
    back, norm_grad = rms_back(resid0_ref[...], gains_ref[0:1], slope)
    grad0_ref[...] = (grad1_ref[...] + back).astype(bf16)
    grad_c_ref[:, :HD] = t_mm(normed, query_slope).astype(bf16)
    grad_c_ref[:, HD : 3 * HD] = t_mm(normed, kv_slope).astype(bf16)
    grad_c_ref[:, 3 * HD : 5 * HD] = part_grad_ref[...]
    where = lax.broadcasted_iota(jnp.int32, norm_grads_ref.shape, 0) == 0
    norm_grads = jnp.where(where, norm_grad, norm_grads_ref[...]).astype(bf16)
    row = lax.broadcasted_iota(jnp.int32, (norm_grads.shape[0], GAIN_PAD), 0)
    spread = (row == lanes_of(row.shape)).astype(bf16)
    grad_c_ref[:, 5 * HD :] = t_mm(norm_grads, spread).astype(bf16)


def local_kernel(name, kernel, outs, args, spaces="", out_spaces="", scratch=()):
    space = {"v": pltpu.VMEM, "s": pltpu.SMEM, "a": pl.ANY}
    spaces = spaces or "v" * len(args)
    out_spaces = out_spaces or "v" * len(outs)
    return pl.pallas_call(
        kernel,
        name=name,
        out_shape=tuple(jax.ShapeDtypeStruct(shape, dtype) for shape, dtype in outs),
        in_specs=[pl.BlockSpec(memory_space=space[letter]) for letter in spaces],
        out_specs=tuple(pl.BlockSpec(memory_space=space[letter]) for letter in out_spaces),
        scratch_shapes=list(scratch),
        compiler_params=pltpu.CompilerParams(vmem_limit_bytes=60 * 1024 * 1024),
    )(*args)


def per_device(
    target_ids,
    labels,
    lengths,
    memory,
    embedding,
    head,
    gain_self,
    w_query,
    w_key,
    w_value,
    w_out,
    relative_bias,
    gain_cross,
    c_query,
    c_key,
    c_value,
    c_out,
    gain_ff,
    w_gate,
    w_up,
    w_down,
    gain_final,
):
    micro = target_ids.shape[0]
    seq_dev = target_ids.shape[2]
    mem_dev = memory.shape[2]
    voc_dev, width = embedding.shape
    ff = w_gate.shape[1]
    n_gx = lax.axis_size("gx")
    n_gy = lax.axis_size("gy")
    column = lax.axis_index("gy")
    row_group = lax.axis_index("gx")
    devices = n_gx * n_gy
    sizes = {"a": n_gx // 2, "c": 2, "s": n_gy // 2, "h": 2}
    assert sizes["s"] == 2 * micro
    place = coordinates()
    seq = seq_dev * n_gy
    plane = sizes["s"] * seq
    tok_dev = seq // 4
    span = sizes["a"] * voc_dev
    merged = "" if sizes["a"] == 2 else "ashc"

    gains = jnp.stack([gain_self, gain_cross, gain_ff, gain_final], axis=1)
    gains = jnp.pad(gains, ((0, 0), (0, GAIN_PAD - 4)))
    shards = (
        jnp.concatenate([w_gate, w_up], axis=1),
        jnp.concatenate([w_down, c_key, c_value, c_out], axis=1),
        jnp.concatenate([w_query, w_key, w_value, w_out, c_query, gains], axis=1),
    )
    orders = ("shac", "sahc", "sahc")
    own_ids = jnp.stack([target_ids.reshape(-1), labels.reshape(-1)])
    part_a, part_b, part_c, embed_rows, ids, memory_all = exchange(
        "gather_weights",
        0,
        [
            Gather(packed(part), order, "acsh", sizes, merged)
            for part, order in zip(shards, orders)
        ]
        + [
            Gather(embedding, "a", "a", sizes),
            Gather(own_ids, "shc", "shc", sizes, "shc"),
            MemoryGather(memory.reshape(micro, mem_dev, width), sizes),
        ],
    )
    part_a, part_b, part_c = (
        full.reshape(devices * part.shape[0], part.shape[1])
        for full, part in zip((part_a, part_b, part_c), shards)
    )
    embed_rows = embed_rows.reshape(span, width)
    memory_all = memory_all.reshape(n_gy * mem_dev, width)
    ids = ids.reshape(n_gy // 2, 2, 2, 2, micro, seq_dev).transpose(3, 4, 2, 0, 1, 5).reshape(2, plane)

    def local_of(index):
        shard = index // voc_dev
        held = (shard % n_gy == column) & (shard // n_gy % 2 == place["c"])
        return jnp.where(held, shard // (2 * n_gy) * voc_dev + index % voc_dev, -1)

    local_ids = local_of(ids[0])
    targets = local_of(ids[1])
    columns = jnp.arange(span, dtype=jnp.int32)

    picked_rows = dot((local_ids[:, None] == columns[None, :]).astype(bf16), embed_rows).astype(bf16)
    tok_layout = (sizes["s"], 2, 2, tok_dev, width)
    resid0, head_rows = exchange(
        "rows",
        1,
        [
            Scatter(picked_rows.reshape(tok_layout), "chs", "shc", sizes),
            Gather(head, "a", "a", sizes),
        ],
    )
    head_rows = head_rows.reshape(span, width)

    plane_lengths = lax.dynamic_slice_in_dim(lengths, 2 * place["a"], 2, axis=1).reshape(-1)
    live_length = lax.dynamic_index_in_dim(plane_lengths, place["s"], keepdims=False)
    scalars = jnp.stack([(2 * place["h"] + place["c"]) * tok_dev, live_length])
    table = jnp.asarray(distance_table(seq), bf16)
    bias_pad = jnp.pad(relative_bias, ((0, 8 - HEADS), (0, 0)))
    query_self, own_kv, normed_self, gain_rows = local_kernel(
        "enter",
        enter_kernel,
        [((tok_dev, HD), bf16), ((tok_dev, 2 * HD), bf16), ((tok_dev, width), bf16), ((16, width), f32)],
        [resid0, part_c],
    )
    (self_kv_all,) = exchange("self_keys", 2, [Gather(own_kv, "hc", "hc", sizes)])
    self_kv_all = self_kv_all.reshape(seq, 2 * HD)
    rows_f32, rows_bf16, rows_heads = ((tok_dev, width), f32), ((tok_dev, width), bf16), ((tok_dev, HD), bf16)
    totals_shape = ((tok_dev, 128), f32)
    all_mem = n_gy * mem_dev
    (
        attn_self,
        total_self,
        resid1,
        normed_cross,
        query_cross,
        mem_kv,
        attn_cross,
        total_cross,
        resid2,
        normed_ff,
        gate_up,
        hidden,
        resid3,
        final_rows,
    ) = local_kernel(
        "forward",
        forward_kernel,
        [
            rows_heads,
            totals_shape,
            rows_f32,
            rows_bf16,
            rows_heads,
            ((all_mem, 2 * HD), bf16),
            rows_heads,
            totals_shape,
            rows_f32,
            rows_bf16,
            ((tok_dev, 2 * ff), f32),
            ((tok_dev, ff), bf16),
            rows_f32,
            rows_bf16,
        ],
        [scalars, query_self, self_kv_all, resid0, gain_rows, table, bias_pad]
        + [memory_all, part_a, part_b, part_c],
        "svvvvvvaaaa",
        scratch=[pltpu.VMEM(full.shape, bf16) for full in (memory_all, part_a, part_b, part_c)]
        + [pltpu.SemaphoreType.DMA((4,))],
    )

    (states,) = exchange("final_rows", 3, [Gather(final_rows, "shc", "shc", sizes, merged)])
    states = states.reshape(plane, width)
    logits = dot_t(states, head_rows)
    highest = jnp.max(logits, axis=1)
    own_total = highest + jnp.log(jnp.sum(jnp.exp(logits - highest[:, None]), axis=1))
    (totals,) = exchange(
        "totals", 4, [Gather(own_total.reshape(plane // 128, 128), "shc", "shc", sizes, "shc")]
    )
    totals = totals.reshape(2 * n_gy, plane)
    top = jnp.max(totals, axis=0)
    log_total = top + jnp.log(jnp.sum(jnp.exp(totals - top[None]), axis=0))
    index = jnp.arange(plane, dtype=jnp.int32)
    alive = (index % seq < jnp.repeat(plane_lengths, seq)).astype(f32)
    hit = columns[None, :] == targets[:, None]
    picked = jnp.sum(jnp.where(hit, logits, 0.0), axis=1)
    loss_part = -jnp.sum(alive * picked) + jnp.where(
        (column == 0) & (place["c"] == 0), jnp.sum(alive * log_total), 0.0
    )
    slope = ((jnp.exp(logits - log_total[:, None]) - hit.astype(f32)) * alive[:, None]).astype(bf16)
    head_part = t_dot(slope, states).astype(bf16)
    final_part = dot(slope, head_rows).astype(bf16)
    final_slope, head_grad = exchange(
        "final_slopes",
        5,
        [
            Scatter(final_part.reshape(tok_layout), "chs", "shc", sizes),
            Scatter(head_part.reshape(sizes["a"], voc_dev, width), "a", "a", sizes),
        ],
    )

    grad_a, grad_b, memory_part, part_grad_c, query_slope, kv_slope, grad1, norm_grads, bias_grad = (
        local_kernel(
            "backward",
            backward_kernel,
            [
                (part_a.shape, bf16),
                (part_b.shape, bf16),
                (memory_all.shape, bf16),
                ((width, 2 * HD), bf16),
                rows_heads,
                ((seq, 2 * HD), bf16),
                rows_f32,
                (gain_rows.shape, f32),
                ((8, BUCKETS), f32),
            ],
            [scalars, final_slope, resid3, hidden, gate_up, normed_ff, resid2, attn_cross]
            + [query_cross, total_cross, normed_cross, resid1, attn_self, query_self, self_kv_all]
            + [total_self, gain_rows, table, bias_pad, mem_kv, memory_all, part_a, part_b, part_c],
            "s" + "v" * 18 + "a" * 5,
            "aaa" + "v" * 6,
            [
                pltpu.VMEM(full.shape, bf16)
                for full in (mem_kv, memory_all, part_a, part_b, part_c, part_a, part_b, memory_all)
            ]
            + [
                pltpu.VMEM((tok_dev, 2 * ff), bf16),
                pltpu.VMEM((tok_dev, HD), bf16),
                pltpu.VMEM(mem_kv.shape, bf16),
                pltpu.SemaphoreType.DMA((5,)),
                pltpu.SemaphoreType.DMA((3,)),
            ],
        )
    )
    (kv_slope,) = exchange(
        "key_slopes",
        6,
        [Scatter(kv_slope.reshape(2, 2, tok_dev, 2 * HD), "ch", "hc", sizes, "", bf16)],
    )
    grad_c, grad0 = local_kernel(
        "leave",
        leave_kernel,
        [(part_c.shape, bf16), rows_bf16],
        [query_slope, kv_slope, normed_self, resid0, grad1, gain_rows, norm_grads, part_grad_c, part_c],
    )
    (slopes,) = exchange("row_slopes", 7, [Gather(grad0, "shc", "shc", sizes, merged)])
    embed_part = t_dot(
        (local_ids[:, None] == columns[None, :]).astype(bf16), slopes.reshape(plane, width)
    ).astype(bf16)
    sums = (grad_a, grad_b, grad_c)
    bias_grad = bias_grad[:HEADS]
    small = jnp.concatenate([bias_grad.reshape(-1), loss_part[None]])
    small = jnp.pad(small, (0, 1024 - small.shape[0])).reshape(8, 128)
    device_layout = (sizes["a"], 2, sizes["s"], 2)
    blocks = [part.reshape(device_layout + packed_shape(part, devices)) for part in sums]
    grad_a, grad_b, grad_c, embedding_grad, memory_grad, small = exchange(
        "scatter_weights",
        8,
        [
            Scatter(part, order[::-1], "acsh", sizes, merged)
            for part, order in zip(blocks, orders)
        ]
        + [
            Scatter(embed_part.reshape(sizes["a"], voc_dev, width), "a", "a", sizes),
            MemoryScatter(memory_part.reshape(sizes["s"], 2, mem_dev, width), sizes),
            Gather(small, "shac", "acsh", sizes, "ashc"),
        ],
    )
    rows_dev = width // devices
    grad_a, grad_b, grad_c = (
        grad.reshape(rows_dev, part.shape[1]) for grad, part in zip((grad_a, grad_b, grad_c), sums)
    )
    small = jnp.sum(small.reshape(devices, 1024), axis=0)
    loss = small[HEADS * BUCKETS] / jnp.sum(lengths).astype(f32)
    bias_total = small[: HEADS * BUCKETS].reshape(HEADS, BUCKETS)
    gain_out = [grad_c[:, 5 * HD + number] for number in range(4)]
    return (
        loss,
        memory_grad.reshape(micro, 1, mem_dev, width),
        embedding_grad,
        head_grad,
        gain_out[0],
        grad_c[:, :HD],
        grad_c[:, HD : 2 * HD],
        grad_c[:, 2 * HD : 3 * HD],
        grad_c[:, 3 * HD : 4 * HD],
        bias_total,
        gain_out[1],
        grad_c[:, 4 * HD : 5 * HD],
        grad_b[:, ff : ff + HD],
        grad_b[:, ff + HD : ff + 2 * HD],
        grad_b[:, ff + 2 * HD :],
        gain_out[2],
        grad_a[:, :ff],
        grad_a[:, ff:],
        grad_b[:, :ff],
        gain_out[3],
    )


def packed_shape(part, count):
    rows, columns = part.shape[0] // count, part.shape[1]
    if rows % 16 == 0:
        return (rows, columns)
    return (16, rows * columns // 16)


def solution(mesh):
    placed = (
        P(None, "gx", "gy"),
        P(None, "gx", "gy"),
        P(),
        P(None, "gx", "gy", None),
        P(("gx", "gy"), None),
        P(("gx", "gy"), None),
        P(("gx", "gy")),
        P(("gx", "gy"), None),
        P(("gx", "gy"), None),
        P(("gx", "gy"), None),
        P(("gx", "gy"), None),
        P(),
        P(("gx", "gy")),
        P(("gx", "gy"), None),
        P(("gx", "gy"), None),
        P(("gx", "gy"), None),
        P(("gx", "gy"), None),
        P(("gx", "gy")),
        P(("gx", "gy"), None),
        P(("gx", "gy"), None),
        P(("gx", "gy"), None),
        P(("gx", "gy")),
    )
    return jax.shard_map(
        per_device,
        mesh=mesh,
        in_specs=placed,
        out_specs=(
            P(),
            P(None, "gx", "gy", None),
            P(("gx", "gy"), None),
            P(("gx", "gy"), None),
            P(("gx", "gy")),
            P(("gx", "gy"), None),
            P(("gx", "gy"), None),
            P(("gx", "gy"), None),
            P(("gx", "gy"), None),
            P(),
            P(("gx", "gy")),
            P(("gx", "gy"), None),
            P(("gx", "gy"), None),
            P(("gx", "gy"), None),
            P(("gx", "gy"), None),
            P(("gx", "gy")),
            P(("gx", "gy"), None),
            P(("gx", "gy"), None),
            P(("gx", "gy"), None),
            P(("gx", "gy")),
        ),
        check_vma=False,
    )
```

```python
import functools
import itertools
import math

import jax
import jax.numpy as jnp
import numpy as np
from jax import lax
from jax.experimental import pallas as pl
from jax.experimental.pallas import tpu as pltpu
from jax.sharding import PartitionSpec as P

HEADS = 6
HEAD = 64
HD = HEADS * HEAD
BUCKETS = 32
GAIN_PAD = 128

eps = 1e-06
masked_score = -1000000000.0
bf16 = jnp.bfloat16
f32 = jnp.float32


def flip(position, offset):
    moved = position
    weight = 1
    while weight <= offset:
        if offset & weight:
            moved = moved + weight * (1 - 2 * ((position // weight) % 2))
        weight *= 2
    return moved


def coordinates():
    gx, gy = lax.axis_index("gx"), lax.axis_index("gy")
    return {"a": gx // 2, "c": gx % 2, "s": gy // 2, "h": gy % 2}


def peer_of(dim, offset):
    gx, gy = lax.axis_index("gx"), lax.axis_index("gy")
    if dim == "a":
        return {"gx": 2 * flip(gx // 2, offset) + gx % 2}
    if dim == "c":
        return {"gx": flip(gx, 1)}
    if dim == "plane":
        s, h = offset
        return {"gy": 2 * flip(gy // 2, s) + flip(gy % 2, h)}
    if dim == "s":
        return {"gy": 2 * flip(gy // 2, offset) + gy % 2}
    return {"gy": flip(gy, 1)}


def remote(source, target, send, recv, dim, offset):
    return pltpu.make_async_remote_copy(
        src_ref=source,
        dst_ref=target,
        send_sem=send,
        recv_sem=recv,
        device_id=peer_of(dim, offset),
        device_id_type=pl.DeviceIdType.MESH,
    )


def along_line(position, step):
    half = position // 2
    return (position, flip(position, 1), 2 - half, 3 - 3 * half)[step]


def is_middle(position):
    return (position + 1) // 2 == 1


def across_middle():
    gy = lax.axis_index("gy")
    return {"gy": 2 * (3 - gy // 2) + gy % 2}


def spot_of(dim, position, offset):
    return along_line(position, offset) if dim == "s" else flip(position, offset)


def remote_to(source, target, send, recv, device):
    return pltpu.make_async_remote_copy(
        src_ref=source,
        dst_ref=target,
        send_sem=send,
        recv_sem=recv,
        device_id=device,
        device_id_type=pl.DeviceIdType.MESH,
    )


def each_piece(rows, columns, body, width=16384):
    step = rows
    while step * columns > width and step % 32 == 0:
        step //= 2
    if step == rows:
        body(slice(None))
        return

    def piece(number, carry):
        body(pl.ds(pl.multiple_of(number * step, step), step))
        return carry

    lax.fori_loop(0, rows // step, piece, 0)


LINE_PEERS = [("s", 1), ("m", 1)]


class Gather:
    def __init__(self, block, order, layout, sizes, merged=""):
        self.value = block
        self.order, self.layout, self.sizes, self.merged = order, layout, sizes, merged
        self.out = jax.ShapeDtypeStruct(tuple(sizes[d] for d in layout) + block.shape, block.dtype)
        self.in_spec = pl.BlockSpec(memory_space=pltpu.VMEM)
        self.out_spec = pl.BlockSpec(memory_space=pl.ANY)
        self.transfers = []
        for level, dim in enumerate(order):
            ranges = [(None,) if d in merged else range(sizes[d]) for d in order[:level]]
            for unit in itertools.product(*ranges):
                for offset in range(1, sizes[dim]):
                    self.transfers.append((level, unit, offset))
        self.index = {transfer: number for number, transfer in enumerate(self.transfers)}
        count = len(self.transfers)
        self.line = order[0] == "s"
        self.scratch = [
            pltpu.SemaphoreType.DMA((count,)),
            pltpu.SemaphoreType.DMA((count,)),
            pltpu.SemaphoreType.DMA,
            pltpu.SemaphoreType.DMA((5,)),
        ]
        self.peers = [(d, offset) for d in order for offset in range(1, sizes[d]) if d != "s"]
        if self.line:
            self.peers += LINE_PEERS

    def prepare(self, refs, place):
        self.source, self.target, self.send, self.recv, self.local_sem, self.line_send = refs
        self.place = place
        self.local = pltpu.make_async_copy(
            self.source, self.target.at[tuple(place[d] for d in self.layout)], self.local_sem
        )
        self.local.start()
        self.local_done = False
        self.arrived = set()
        self.sent = []

    def region(self, level, unit, offset):
        where = dict(self.place)
        for d, moved in zip(self.order[:level], unit):
            where[d] = slice(None) if moved is None else spot_of(d, self.place[d], moved)
        if offset:
            dim = self.order[level]
            where[dim] = spot_of(dim, self.place[dim], offset)
        return self.target.at[tuple(where[d] for d in self.layout)]

    def needs(self, level, unit):
        if level == 0:
            return []
        last, before = unit[-1], unit[:-1]
        if last is None:
            dim = self.order[level - 1]
            return self.needs(level - 1, before) + [
                (level - 1, before, offset) for offset in range(1, self.sizes[dim])
            ]
        if last == 0:
            return self.needs(level - 1, before)
        return [(level - 1, before, last)]

    def arrive(self, transfer):
        if transfer in self.arrived:
            return
        self.arrived.add(transfer)
        level, unit, offset = transfer
        number = self.index[transfer]
        there = self.region(level, unit, offset)
        if self.line and level == 0:
            offset = 1
        remote(
            there, there, self.send.at[number], self.recv.at[number], self.order[level], offset
        ).wait_recv()

    def line_copy(self, number):
        held, there = ((0, 1), (0, 2), (1, 3), (2, 2), (3, 3))[number]
        target = self.region(0, (), held)
        device = peer_of("s", 1) if number in (0, 3, 4) else across_middle()
        recv = self.recv.at[self.index[(0, (), there)]]
        source = target if held else self.source
        return remote_to(source, target, self.line_send.at[number], recv, device)

    def line_first(self):
        self.line_copy(0).start()

        @pl.when(is_middle(self.place["s"]))
        def _():
            self.line_copy(1).start()

    def line_next(self, step):
        self.arrive((0, (), step))

        @pl.when(is_middle(self.place["s"]))
        def _():
            self.line_copy(step + 1).start()

    def launch(self, transfer):
        level, unit, offset = transfer
        number = self.index[transfer]
        for need in self.needs(level, unit):
            self.arrive(need)
        target = self.region(level, unit, 0)
        own = all(moved == 0 for moved in unit)
        if None in unit and not self.local_done:
            self.local.wait()
            self.local_done = True
        copy = remote(
            self.source if own else target,
            target,
            self.send.at[number],
            self.recv.at[number],
            self.order[level],
            offset,
        )
        copy.start()
        self.sent.append(copy)

    def events(self):
        found = []
        if self.line:
            found.append((0, self.line_first))
            for step in (1, 2, 3):
                found.append((step, functools.partial(self.line_next, step)))
        for transfer in self.transfers:
            level, unit, offset = transfer
            if self.line and level == 0:
                continue
            key = 0.1 * level + 0.01 * offset
            for d, moved in zip(self.order, unit):
                key += self.sizes[d] - 1 if moved is None else moved
            found.append((key, functools.partial(self.launch, transfer)))
        return found

    def finish(self):
        if not self.local_done:
            self.local.wait()
        for transfer in self.transfers:
            self.arrive(transfer)
        for copy in self.sent:
            copy.wait_send()
        if self.line:
            self.line_copy(0).wait_send()

            @pl.when(is_middle(self.place["s"]))
            def _():
                for number in range(1, 5):
                    self.line_copy(number).wait_send()


class PackedGather(Gather):
    def __init__(self, values, block, pack, *args):
        super().__init__(block, *args)
        self.values, self.pack = values, pack
        self.scratch = [pltpu.VMEM(block.shape, block.dtype)] + self.scratch


class DirectGather:
    def __init__(self, block, sizes):
        self.value = block
        shape = (sizes["s"], 2)
        self.out = jax.ShapeDtypeStruct(shape + block.shape, block.dtype)
        self.in_spec = pl.BlockSpec(memory_space=pltpu.VMEM)
        self.out_spec = pl.BlockSpec(memory_space=pltpu.VMEM)
        self.offsets = list(itertools.product(*(range(size) for size in shape)))[1:]
        count = len(self.offsets)
        self.scratch = [pltpu.SemaphoreType.DMA((count,)), pltpu.SemaphoreType.DMA((count,))]
        self.peers = [("plane", offset) for offset in self.offsets]

    def prepare(self, refs, place):
        self.source, self.target, self.send, self.recv = refs
        self.place = place
        self.target[place["s"], place["h"]] = self.source[...]

    def copy(self, number, arriving):
        offset = self.offsets[number]
        spot = tuple(
            flip(self.place[d], moved) if arriving else self.place[d] for d, moved in zip("sh", offset)
        )
        return remote_to(
            self.source,
            self.target.at[spot],
            self.send.at[number],
            self.recv.at[number],
            peer_of("plane", offset),
        )

    def events(self):
        return [(0, functools.partial(self.start, number)) for number in range(len(self.offsets))]

    def start(self, number):
        self.copy(number, False).start()

    def finish(self):
        for number in range(len(self.offsets)):
            self.copy(number, True).wait()


class Scatter:
    def __init__(self, value, order, layout, sizes, merged="", out_dtype=f32):
        self.value = value
        self.order, self.layout, self.sizes, self.merged = order, layout, sizes, merged
        self.block = value.shape[len(layout) :]
        self.out = jax.ShapeDtypeStruct(self.block, out_dtype)
        self.in_spec = pl.BlockSpec(memory_space=pltpu.VMEM)
        self.out_spec = pl.BlockSpec(memory_space=pltpu.VMEM)
        self.line = order[-1] == "s"
        self.levels = len(order)
        self.units = []
        self.scratch = []
        self.layouts = [layout]
        for level, dim in enumerate(order):
            later = order[level + 1 :]
            ranges = [(None,) if d in merged else range(sizes[d]) for d in later]
            units = sorted(
                itertools.product(*ranges),
                key=lambda unit: (-(unit[-1] or 0) if unit else 0, -sum(moved or 0 for moved in unit)),
            )
            self.units.append(units)
            left = "".join(d for d in self.layouts[-1] if d != dim)
            self.layouts.append(left)
            self.scratch.append(
                pltpu.VMEM(
                    (5 if dim == "s" else sizes[dim] - 1,)
                    + tuple(sizes[d] for d in left)
                    + self.block,
                    value.dtype,
                )
            )
        self.index = {}
        for level, dim in enumerate(order):
            for unit in self.units[level]:
                for offset in range(1, sizes[dim]):
                    self.index[(level, unit, offset)] = len(self.index)
        count = len(self.index)
        self.scratch += [
            pltpu.SemaphoreType.DMA((count,)),
            pltpu.SemaphoreType.DMA((count,)),
            pltpu.SemaphoreType.DMA((2, 5)),
        ]
        self.peers = [(d, offset) for d in order for offset in range(1, sizes[d]) if d != "s"]
        if self.line:
            self.peers += LINE_PEERS

    def prepare(self, refs, place):
        self.source, self.target = refs[0], refs[1]
        self.landing = refs[2 : 2 + self.levels]
        self.send, self.recv, self.line_sems = refs[2 + self.levels :]
        self.place = place
        self.sent = []

    def held(self, level):
        return self.source if level == 0 else self.landing[level - 1].at[0]

    def later(self, level, unit):
        where = {}
        for d, moved in zip(self.order[level + 1 :], unit):
            where[d] = slice(None) if moved is None else spot_of(d, self.place[d], moved)
        return where

    def copy(self, level, unit, offset):
        number = self.index[(level, unit, offset)]
        dim = self.order[level]
        where = self.later(level, unit)
        landed = self.landing[level].at[
            (offset - 1,) + tuple(where[d] for d in self.layouts[level + 1])
        ]
        where[dim] = flip(self.place[dim], offset)
        source = self.held(level).at[tuple(where[d] for d in self.layouts[level])]
        return remote(source, landed, self.send.at[number], self.recv.at[number], dim, offset)

    def launch(self, level, unit, offset):
        copy = self.copy(level, unit, offset)
        copy.start()
        self.sent.append(copy)

    def reduce(self, level, unit):
        dim = self.order[level]
        size = self.sizes[dim]
        for offset in range(1, size):
            self.copy(level, unit, offset).wait_recv()
        where = self.later(level, unit)
        free = [d for d in self.order[level + 1 :] if isinstance(where[d], slice)]
        total = math.prod(self.sizes[d] for d in free)
        rows, columns = self.block
        last = level == self.levels - 1

        def one(number, carry):
            at = dict(where)
            rest = number
            for d in free:
                at[d] = rest % self.sizes[d]
                rest = rest // self.sizes[d]
            spot = tuple(at[d] for d in self.layouts[level + 1])
            at[dim] = self.place[dim]
            mine = tuple(at[d] for d in self.layouts[level])

            def body(piece):
                if not last and size == 2:
                    self.landing[level][(0,) + spot + (piece,)] += self.held(level)[mine + (piece,)]
                    return
                result = self.held(level)[mine + (piece,)].astype(f32)
                for offset in range(1, size):
                    result = result + self.landing[level][(offset - 1,) + spot + (piece,)].astype(f32)
                if last:
                    self.target[(piece,)] = result.astype(self.target.dtype)
                else:
                    self.landing[level][(0,) + spot + (piece,)] = result.astype(self.landing[level].dtype)

            each_piece(rows, columns, body)
            return carry

        if total == 1:
            one(0, 0)
        else:
            lax.fori_loop(0, total, one, 0)
        if not last and not (self.line and level == self.levels - 2):
            ahead, rest = unit[0], unit[1:]
            if ahead is None:
                offsets = range(1, self.sizes[self.order[level + 1]])
            else:
                offsets = [ahead] if ahead else []
            for offset in offsets:
                self.launch(level + 1, rest, offset)

    def line_copy(self, number):
        step, slot = ((1, 0), (2, 1), (3, 2), (3, 3), (2, 4))[number]
        level = self.levels - 1
        block = self.held(level).at[along_line(self.place["s"], step)]
        landed = self.landing[level].at[slot]
        device = peer_of("s", 1) if number < 3 else across_middle()
        return remote_to(block, landed, self.line_sems.at[0, number], self.line_sems.at[1, number], device)

    def line_step(self, step):
        level = self.levels - 1
        middle = is_middle(self.place["s"])
        rows, columns = self.block
        held, landing = self.held(level), self.landing[level]
        position = along_line(self.place["s"], step)

        if step:
            @pl.when(jnp.logical_not(middle))
            def _():
                self.line_copy(step - 1).start()

            @pl.when(middle)
            def _():
                arrived = (0, 3, 1, 2)[step]
                self.line_copy(arrived).wait_recv()

                def body(piece):
                    held[(position, piece)] += landing[(arrived, piece)]

                each_piece(rows, columns, body)
                self.line_copy((0, 0, 4, 3)[step]).start()

            return

        self.line_copy(0).wait_recv()

        @pl.when(middle)
        def _():
            self.line_copy(4).wait_recv()

            def body(piece):
                result = held[(position, piece)].astype(f32) + landing[(0, piece)].astype(f32)
                self.target[(piece,)] = (result + landing[(4, piece)].astype(f32)).astype(
                    self.target.dtype
                )

            each_piece(rows, columns, body)

        @pl.when(jnp.logical_not(middle))
        def _():
            def body(piece):
                result = held[(position, piece)].astype(f32) + landing[(0, piece)].astype(f32)
                self.target[(piece,)] = result.astype(self.target.dtype)

            each_piece(rows, columns, body)

    def events(self):
        found = []
        for number, unit in enumerate(self.units[0]):
            for offset in range(1, self.sizes[self.order[0]]):
                found.append(
                    (-1 + 0.001 * number, functools.partial(self.launch, 0, unit, offset))
                )
        spread = 4 if self.line else 1
        for level in range(self.levels - self.line):
            count = len(self.units[level])
            for number, unit in enumerate(self.units[level]):
                late = 0
                if self.order[-1] == "a":
                    late = 20 if level == self.levels - 1 else 0.9
                found.append(
                    (late + level + spread * number / count, functools.partial(self.reduce, level, unit))
                )
        if self.line:
            for number, step in enumerate((3, 2, 1, 0)):
                found.append(
                    (self.levels - 1 + number + 0.5, functools.partial(self.line_step, step))
                )
        return found

    def finish(self):
        for copy in self.sent:
            copy.wait_send()
        if self.line:
            self.line_copy(0).wait_send()
            middle = is_middle(self.place["s"])

            @pl.when(middle)
            def _():
                for number in (3, 4):
                    self.line_copy(number).wait_send()

            @pl.when(jnp.logical_not(middle))
            def _():
                for number in (1, 2):
                    self.line_copy(number).wait_send()


class MemoryGather:
    def __init__(self, memory, sizes):
        self.value = memory
        self.sizes = sizes
        self.out = jax.ShapeDtypeStruct((sizes["s"], 2) + memory.shape[1:], memory.dtype)
        self.in_spec = pl.BlockSpec(memory_space=pltpu.VMEM)
        self.out_spec = pl.BlockSpec(memory_space=pl.ANY)
        rows = sizes["s"]
        self.scratch = [
            pltpu.SemaphoreType.DMA((2, rows)),
            pltpu.SemaphoreType.DMA((2, rows)),
            pltpu.SemaphoreType.DMA((2, rows, 2)),
            pltpu.SemaphoreType.DMA,
        ]
        self.peers = [("s", offset) for offset in range(1, rows)] + [("h", 1), ("c", 1)]

    def prepare(self, refs, place):
        self.source, self.target, self.along, self.across, self.core, self.local = refs
        self.place = place
        self.mine = place["s"] % 2 == place["c"]

    def row(self, offset):
        return flip(self.place["s"], offset)

    def along_copy(self, offset, arriving):
        to = self.row(offset)
        spot = to if arriving else self.place["s"]
        return remote(
            self.source.at[self.place["s"] // 2 if arriving else to // 2],
            self.target.at[spot, self.place["h"]],
            self.along.at[0, offset],
            self.along.at[1, offset],
            "s",
            offset,
        )

    def across_copy(self, offset, arriving):
        h = self.place["h"]
        own = self.target.at[self.row(offset), 1 - h if arriving else h]
        if offset == 0 and not arriving:
            source = self.source.at[self.place["s"] // 2]
        else:
            source = own
        return remote(source, own, self.across.at[0, offset], self.across.at[1, offset], "h", 1)

    def core_copy(self, offset, other):
        h = self.place["h"]
        own = self.target.at[self.row(offset), 1 - h if other else h]
        source = self.source.at[self.place["s"] // 2] if offset == 0 and not other else own
        return remote(source, own, self.core.at[0, offset, other], self.core.at[1, offset, other], "c", 1)

    def events(self):
        rows = self.sizes["s"]

        def first():
            for offset in range(1, rows):
                @pl.when(self.row(offset) % 2 == self.place["c"])
                def _():
                    self.along_copy(offset, False).start()

            @pl.when(self.mine)
            def _():
                pltpu.make_async_copy(
                    self.source.at[self.place["s"] // 2],
                    self.target.at[self.place["s"], self.place["h"]],
                    self.local,
                ).start()
                self.across_copy(0, False).start()
                self.core_copy(0, 0).start()

        def arrival(offset):
            @pl.when(self.mine)
            def _():
                self.along_copy(offset, True).wait_recv()
                self.across_copy(offset, False).start()
                self.core_copy(offset, 0).start()

        def other(offset):
            @pl.when(self.mine)
            def _():
                self.across_copy(offset, True).wait_recv()
                self.core_copy(offset, 1).start()

        found = [(0.05, first)]
        for offset in range(1, rows):
            found.append((offset + 0.05, functools.partial(arrival, offset)))
        for offset in range(rows):
            found.append((rows + offset, functools.partial(other, offset)))
        return found

    def finish(self):
        rows = self.sizes["s"]
        for offset in range(1, rows):
            @pl.when(self.row(offset) % 2 == self.place["c"])
            def _():
                self.along_copy(offset, False).wait_send()

        @pl.when(self.mine)
        def _():
            pltpu.make_async_copy(
                self.source.at[self.place["s"] // 2],
                self.target.at[self.place["s"], self.place["h"]],
                self.local,
            ).wait()
            for offset in range(rows):
                self.across_copy(offset, False).wait_send()
                for other in range(2):
                    self.core_copy(offset, other).wait_send()

        @pl.when(jnp.logical_not(self.mine))
        def _():
            for offset in range(rows):
                for other in range(2):
                    self.core_copy(offset, other).wait_recv()


class MemoryScatter:
    def __init__(self, value, sizes):
        self.value = value
        self.sizes = sizes
        rows = sizes["s"]
        self.block = value.shape[2:]
        self.out = jax.ShapeDtypeStruct((2,) + self.block, f32)
        self.in_spec = pl.BlockSpec(memory_space=pltpu.VMEM)
        self.out_spec = pl.BlockSpec(memory_space=pltpu.VMEM)
        self.scratch = [
            pltpu.VMEM(value.shape, value.dtype),
            pltpu.VMEM((rows,) + self.block, value.dtype),
            pltpu.VMEM((2,) + self.block, value.dtype),
            pltpu.SemaphoreType.DMA((2, rows, 2)),
            pltpu.SemaphoreType.DMA((2, rows)),
            pltpu.SemaphoreType.DMA((2, rows)),
        ]
        self.peers = [("s", offset) for offset in range(1, rows)] + [("h", 1), ("c", 1)]

    def prepare(self, refs, place):
        self.source, self.target = refs[0], refs[1]
        self.summed, self.halved, self.landed, self.core, self.across, self.along = refs[2:]
        self.place = place
        self.mine = place["s"] % 2 == place["c"]

    def row(self, offset):
        return flip(self.place["s"], offset)

    def core_copy(self, offset, other):
        h = self.place["h"]
        spot = (self.row(offset), flip(h, 1) if other else h)
        return remote(
            self.source.at[spot],
            self.summed.at[spot],
            self.core.at[0, offset, other],
            self.core.at[1, offset, other],
            "c",
            1,
        )

    def across_copy(self, offset):
        row = self.row(offset)
        return remote(
            self.summed.at[row, flip(self.place["h"], 1)],
            self.halved.at[row],
            self.across.at[0, offset],
            self.across.at[1, offset],
            "h",
            1,
        )

    def along_copy(self, offset, arriving):
        to = self.row(offset)
        return remote(
            self.halved.at[to],
            self.landed.at[to // 2 if arriving else self.place["s"] // 2],
            self.along.at[0, offset],
            self.along.at[1, offset],
            "s",
            offset,
        )

    def events(self):
        rows = self.sizes["s"]
        high, wide = self.block
        orders = list(range(1, rows))[::-1] + [0]

        def first():
            @pl.when(jnp.logical_not(self.mine))
            def _():
                for other in (1, 0):
                    for offset in orders:
                        self.core_copy(offset, other).start()

        def level(offset, other):
            @pl.when(self.mine)
            def _():
                self.core_copy(offset, other).wait_recv()
                h = self.place["h"]
                spot = (self.row(offset), flip(h, 1) if other else h)

                def body(piece):
                    total = self.summed[spot + (piece,)].astype(f32) + self.source[
                        spot + (piece,)
                    ].astype(f32)
                    self.summed[spot + (piece,)] = total.astype(self.summed.dtype)

                each_piece(high, wide, body)
                if other:
                    self.across_copy(offset).start()

        def last(offset):
            @pl.when(self.mine)
            def _():
                self.across_copy(offset).wait_recv()
                row = self.row(offset)

                def body(piece):
                    total = self.halved[(row, piece)].astype(f32) + self.summed[
                        (row, self.place["h"], piece)
                    ].astype(f32)
                    self.halved[(row, piece)] = total.astype(self.halved.dtype)
                    if offset == 0:
                        self.target[(self.place["s"] // 2, piece)] = total

                each_piece(high, wide, body)
                if offset:
                    self.along_copy(offset, False).start()

        found = [(-0.95, first)]
        for number, offset in enumerate(orders):
            found.append((0.05 + 0.1 * number, functools.partial(level, offset, 1)))
        for number, offset in enumerate(orders):
            found.append((0.55 + 0.1 * number, functools.partial(level, offset, 0)))
        for number, offset in enumerate(orders):
            found.append((1.05 + 0.2 * number, functools.partial(last, offset)))
        return found

    def finish(self):
        rows = self.sizes["s"]
        high, wide = self.block
        for offset in range(1, rows):
            @pl.when(self.row(offset) % 2 == self.place["c"])
            def _():
                self.along_copy(offset, True).wait_recv()
                number = self.row(offset) // 2

                def body(piece):
                    self.target[(number, piece)] = self.landed[(number, piece)].astype(f32)

                each_piece(high, wide, body)

        @pl.when(self.mine)
        def _():
            for offset in range(rows):
                self.across_copy(offset).wait_send()
            for offset in range(1, rows):
                self.along_copy(offset, False).wait_send()

        @pl.when(jnp.logical_not(self.mine))
        def _():
            for offset in range(rows):
                for other in range(2):
                    self.core_copy(offset, other).wait_send()


def exchange(name, collective_id, jobs):
    values = [getattr(job, "values", None) or [job.value] for job in jobs]
    peers = []
    for job in jobs:
        for peer in job.peers:
            if peer not in peers:
                peers.append(peer)

    def kernel(*refs):
        total = sum(len(held) for held in values)
        results = refs[total : total + len(jobs)]
        scratch = refs[total + len(jobs) :]
        begin = offset = 0
        barrier = pltpu.get_barrier_semaphore()
        place = coordinates()
        middle = is_middle(place["s"])
        awaited = 0
        for peer in peers:
            if peer[0] == "m":
                @pl.when(middle)
                def _():
                    pl.semaphore_signal(
                        barrier, inc=1, device_id=across_middle(), device_id_type=pl.DeviceIdType.MESH
                    )
                continue
            awaited += 1
            pl.semaphore_signal(
                barrier, inc=1, device_id=peer_of(*peer), device_id_type=pl.DeviceIdType.MESH
            )
        for number, job in enumerate(jobs):
            end = begin + len(values[number])
            ins = refs[begin:end]
            if hasattr(job, "pack"):
                job.pack(ins, scratch[offset])
                ins, offset = (scratch[offset],), offset + 1
            mine = len(job.scratch) - hasattr(job, "pack")
            job.prepare(tuple(ins) + (results[number],) + tuple(scratch[offset : offset + mine]), place)
            begin, offset = end, offset + mine
        if ("m", 1) in peers:
            @pl.when(middle)
            def _():
                pl.semaphore_wait(barrier, awaited + 1)

            @pl.when(jnp.logical_not(middle))
            def _():
                pl.semaphore_wait(barrier, awaited)
        else:
            pl.semaphore_wait(barrier, awaited)
        events = [event for job in jobs for event in job.events()]
        for _, act in sorted(events, key=lambda event: event[0]):
            act()
        for job in jobs:
            job.finish()

    return pl.pallas_call(
        kernel,
        name=name,
        out_shape=tuple(job.out for job in jobs),
        in_specs=[job.in_spec for job, held in zip(jobs, values) for _ in held],
        out_specs=tuple(job.out_spec for job in jobs),
        scratch_shapes=[item for job in jobs for item in job.scratch],
        compiler_params=pltpu.CompilerParams(
            collective_id=collective_id, has_side_effects=True, vmem_limit_bytes=60 * 1024 * 1024
        ),
    )(*[value for held in values for value in held])


def packed(block):
    rows, columns = block.shape
    if rows % 16 == 0:
        return block
    return block.reshape(16, rows * columns // 16)


def bucket_edges():
    edges = []
    for target in range(1, 32):
        if target < 16:
            edges.append(target)
        else:
            found = 0
            for distance in range(16, 4096):
                value = 16 + int(math.log(distance / 16.0) / math.log(8.0) * 16.0)
                if found == 0 and value >= target:
                    found = distance
            edges.append(found)
    return edges


def gelu_tanh(value):
    return (
        0.5
        * value
        * (1.0 + jnp.tanh(0.7978845608028654 * (value + 0.044715 * value * value * value)))
    )


def dot(left, right):
    return jnp.einsum("sd,df->sf", left, right, preferred_element_type=f32)


def dot_t(left, right):
    return jnp.einsum("sf,df->sd", left, right, preferred_element_type=f32)


def t_dot(left, right):
    return jnp.einsum("sd,sf->df", left, right, preferred_element_type=f32)


def distance_table(seq):
    edges = np.array(bucket_edges())
    distance = (-np.arange(seq)) % seq
    bucket = (distance[:, None] >= edges[None, :]).sum(axis=1)
    return (np.arange(128)[:, None] == bucket[None, :]).astype(np.float32)


def mm(left, right):
    return lax.dot_general(left, right, (((1,), (0,)), ((), ())), preferred_element_type=f32)


def mm_t(left, right):
    return lax.dot_general(left, right, (((1,), (1,)), ((), ())), preferred_element_type=f32)


def t_mm(left, right):
    return lax.dot_general(left, right, (((0,), (0,)), ((), ())), preferred_element_type=f32)


def inverse_rms(rows):
    return lax.rsqrt(jnp.mean(rows * rows, axis=-1, keepdims=True) + eps)


def rms_back(rows, gain, slope):
    inverse = inverse_rms(rows)
    unit = rows * inverse
    scaled = slope * gain
    back = inverse * (scaled - unit * jnp.mean(unit * scaled, axis=-1, keepdims=True))
    return back, jnp.sum(slope * unit, axis=0, keepdims=True)


def lanes_of(shape):
    return lax.broadcasted_iota(jnp.int32, shape, len(shape) - 1)


def one_half(pair, half):
    inside = (lanes_of(pair.shape) // HEAD) == half
    return jnp.where(inside, pair, jnp.zeros_like(pair))


def joined(first, second):
    return jnp.where(lanes_of(first.shape) < HEAD, first, second)


def pair_of(ref, start, pair):
    return ref[:, start + 2 * HEAD * pair : start + 2 * HEAD * (pair + 1)]


FF_STEP = 256


def in_steps(total, step, body, further=0):
    def one(number, carry):
        here = pl.ds(pl.multiple_of(number * step, step), step)
        if further:
            body(here, pl.ds(pl.multiple_of(number * step + further, step), step))
        else:
            body(here)
        return carry

    lax.fori_loop(0, total // step, one, 0)


class Fetch:
    def __init__(self, sources, targets, sems):
        self.copies = [
            pltpu.make_async_copy(source, target, sems.at[number])
            for number, (source, target) in enumerate(zip(sources, targets))
        ]
        self.targets = targets
        self.ready = set()
        for copy in self.copies:
            copy.start()

    def __getitem__(self, number):
        if number not in self.ready:
            self.ready.add(number)
            self.copies[number].wait()
        return self.targets[number]


def enter_kernel(resid_ref, part_c_ref, query_ref, kv_ref, normed_ref, gains_ref):
    row = lax.broadcasted_iota(jnp.int32, (16, GAIN_PAD), 0)
    pick = (row == lanes_of((16, GAIN_PAD))).astype(bf16)
    gains = mm_t(pick, part_c_ref[:, 5 * HD : 5 * HD + GAIN_PAD])
    gains_ref[...] = gains
    resid = resid_ref[...]
    normed = (resid * inverse_rms(resid) * gains[0:1]).astype(bf16)
    normed_ref[...] = normed
    query_ref[...] = mm(normed, part_c_ref[:, :HD]).astype(bf16)
    kv_ref[...] = mm(normed, part_c_ref[:, HD : 3 * HD]).astype(bf16)


def biased_scores(scores, row, first, length):
    bias = pltpu.roll(jnp.broadcast_to(row, scores.shape), 0, 1, stride=1, stride_axis=0)
    query_pos = first + lax.broadcasted_iota(jnp.int32, scores.shape, 0)
    key_pos = lanes_of(scores.shape)
    mask = (key_pos <= query_pos) & (key_pos < length)
    return jnp.where(mask, scores + bias, masked_score)


def softmax_parts(scores):
    highest = jnp.max(scores, axis=-1, keepdims=True)
    total = highest + jnp.log(jnp.sum(jnp.exp(scores - highest), axis=-1, keepdims=True))
    return total, jnp.exp(scores - total)


def forward_kernel(
    scalars_ref,
    query_ref,
    kv_ref,
    resid0_ref,
    gains_ref,
    table_ref,
    bias_ref,
    memory_hbm,
    part_a_hbm,
    part_b_hbm,
    part_c_hbm,
    attn_self_ref,
    total_self_ref,
    resid1_ref,
    normed_cross_ref,
    query_cross_ref,
    mem_kv_ref,
    attn_cross_ref,
    total_cross_ref,
    resid2_ref,
    normed_ff_ref,
    gate_up_ref,
    hidden_ref,
    resid3_ref,
    final_ref,
    memory_ref,
    part_a_ref,
    part_b_ref,
    part_c_ref,
    sems,
):
    fetched = Fetch(
        (part_c_hbm, part_b_hbm, memory_hbm, part_a_hbm),
        (part_c_ref, part_b_ref, memory_ref, part_a_ref),
        sems,
    )
    first, length = scalars_ref[0], scalars_ref[1]
    ff = hidden_ref.shape[1]
    bias_rows = pltpu.roll(mm(bias_ref[...], table_ref[...]), first, 1)
    lanes = lanes_of(total_self_ref.shape)
    totals = jnp.zeros(total_self_ref.shape, f32)
    for pair in range(HEADS // 2):
        keys, values = pair_of(kv_ref, 0, pair), pair_of(kv_ref, HD, pair)
        outputs = []
        for half in range(2):
            number = 2 * pair + half
            scores = mm_t(one_half(pair_of(query_ref, 0, pair), half), keys)
            scores = biased_scores(scores, bias_rows[number : number + 1], first, length)
            total, shares = softmax_parts(scores)
            totals = jnp.where(lanes == number, total, totals)
            outputs.append(mm(shares.astype(bf16), values))
        attn_self_ref[:, 2 * HEAD * pair : 2 * HEAD * (pair + 1)] = joined(*outputs).astype(bf16)
    total_self_ref[...] = totals

    part_c = fetched[0]
    resid1 = resid0_ref[...] + mm_t(attn_self_ref[...], part_c[:, 3 * HD : 4 * HD])
    resid1_ref[...] = resid1
    normed = (resid1 * inverse_rms(resid1) * gains_ref[1:2]).astype(bf16)
    normed_cross_ref[...] = normed
    query_cross_ref[...] = mm(normed, part_c[:, 4 * HD : 5 * HD]).astype(bf16)

    part_b = fetched[1]
    memory = fetched[2]
    step = min(256, memory.shape[0])

    def project(number, carry):
        rows = pl.ds(pl.multiple_of(number * step, step), step)
        mem_kv_ref[rows, :] = mm(memory[rows, :], part_b[:, ff : ff + 2 * HD]).astype(bf16)
        return carry

    lax.fori_loop(0, memory.shape[0] // step, project, 0)
    total_cross_ref[...] = jnp.zeros(total_cross_ref.shape, f32)

    def cross_pair(place, place_v):
        keys, values = mem_kv_ref[:, place], mem_kv_ref[:, place_v]
        outputs = []
        for half in range(2):
            scores = mm_t(one_half(query_cross_ref[:, place], half), keys)
            total, shares = softmax_parts(scores)
            number = place.start // HEAD + half
            total_cross_ref[...] = jnp.where(lanes == number, total, total_cross_ref[...])
            outputs.append(mm(shares.astype(bf16), values))
        attn_cross_ref[:, place] = joined(*outputs).astype(bf16)

    in_steps(HD, 2 * HEAD, cross_pair, HD)
    resid2 = resid1_ref[...] + mm_t(attn_cross_ref[...], part_b[:, ff + 2 * HD :])
    resid2_ref[...] = resid2
    normed_ff_ref[...] = (resid2 * inverse_rms(resid2) * gains_ref[2:3]).astype(bf16)

    part_a = fetched[3]

    def feed(here, there):
        gate = mm(normed_ff_ref[...], part_a[:, here])
        up = mm(normed_ff_ref[...], part_a[:, there])
        gate_up_ref[:, here] = gate
        gate_up_ref[:, there] = up
        hidden_ref[:, here] = (gelu_tanh(gate) * up).astype(bf16)

    in_steps(ff, FF_STEP, feed, ff)
    resid3 = resid2_ref[...] + mm_t(hidden_ref[...], part_b[:, :ff])
    resid3_ref[...] = resid3
    final_ref[...] = (resid3 * inverse_rms(resid3) * gains_ref[3:4]).astype(bf16)


def attention_back(query, keys, values, scores, total, out_slope):
    shares = jnp.exp(scores - total)
    share_slope = mm_t(out_slope, values)
    inner = jnp.sum(shares * share_slope, axis=-1, keepdims=True)
    score_slope = shares * (share_slope - inner)
    rounded = score_slope.astype(bf16)
    return (
        rounded,
        mm(rounded, keys),
        t_mm(rounded, query),
        t_mm(shares.astype(bf16), out_slope),
    )


def backward_kernel(
    scalars_ref,
    slope_ref,
    resid3_ref,
    hidden_ref,
    gate_up_ref,
    normed_ff_ref,
    resid2_ref,
    attn_cross_ref,
    query_cross_ref,
    total_cross_ref,
    normed_cross_ref,
    resid1_ref,
    attn_self_ref,
    query_ref,
    kv_ref,
    total_self_ref,
    gains_ref,
    table_ref,
    bias_ref,
    mem_kv_hbm,
    memory_hbm,
    part_a_hbm,
    part_b_hbm,
    part_c_hbm,
    grad_a_hbm,
    grad_b_hbm,
    memory_part_hbm,
    grad_c_ref,
    query_slope_ref,
    kv_slope_ref,
    grad1_ref,
    norm_grads_ref,
    bias_grad_ref,
    mem_kv_ref,
    memory_ref,
    part_a_ref,
    part_b_ref,
    part_c_ref,
    grad_a_ref,
    grad_b_ref,
    memory_part_ref,
    gate_up_slope_ref,
    cross_query_slope_ref,
    cross_kv_slope_ref,
    sems,
    out_sems,
):
    fetched = Fetch(
        (part_b_hbm, part_a_hbm, mem_kv_hbm, memory_hbm, part_c_hbm),
        (part_b_ref, part_a_ref, mem_kv_ref, memory_ref, part_c_ref),
        sems,
    )
    first, length = scalars_ref[0], scalars_ref[1]
    ff = hidden_ref.shape[1]
    width = resid3_ref.shape[1]
    norm_grads_ref[...] = jnp.zeros_like(norm_grads_ref)

    grad3, norm_grad = rms_back(resid3_ref[...], gains_ref[3:4], slope_ref[...])
    norm_grads_ref[3:4] = norm_grad
    down_in = grad3.astype(bf16)
    part_b = fetched[0]

    def feed_back(here, there):
        hidden_slope = mm(down_in, part_b[:, here])
        gate, up = gate_up_ref[:, here], gate_up_ref[:, there]
        inner = jnp.tanh(0.7978845608028654 * (gate + 0.044715 * gate * gate * gate))
        activated = 0.5 * gate * (1.0 + inner)
        steep = 0.5 * (1.0 + inner) + 0.5 * gate * (1.0 - inner * inner) * (
            0.7978845608028654 * (1.0 + 3.0 * 0.044715 * gate * gate)
        )
        gate_up_slope_ref[:, here] = (hidden_slope * up * steep).astype(bf16)
        gate_up_slope_ref[:, there] = (hidden_slope * activated).astype(bf16)
        grad_b_ref[:, here] = t_mm(down_in, hidden_ref[:, here]).astype(bf16)

    in_steps(ff, FF_STEP, feed_back, ff)
    part_a = fetched[1]
    back, norm_grad = rms_back(
        resid2_ref[...], gains_ref[2:3], mm_t(gate_up_slope_ref[...], part_a[...])
    )
    norm_grads_ref[2:3] = norm_grad
    grad2 = grad3 + back

    def gate_up_grad(here):
        grad_a_ref[:, here] = t_mm(normed_ff_ref[...], gate_up_slope_ref[:, here]).astype(bf16)

    in_steps(2 * ff, 2 * FF_STEP, gate_up_grad)
    copy_a = pltpu.make_async_copy(grad_a_ref, grad_a_hbm, out_sems.at[0])
    copy_a.start()

    cross_in = grad2.astype(bf16)
    grad_b_ref[:, ff + 2 * HD :] = t_mm(cross_in, attn_cross_ref[...]).astype(bf16)
    out_slope = mm(cross_in, part_b[:, ff + 2 * HD :]).astype(bf16)
    mem_kv = fetched[2]
    cross_query_slope_ref[...] = out_slope

    def cross_pair_back(place, place_v):
        keys, values = mem_kv[:, place], mem_kv[:, place_v]
        parts = []
        for half in range(2):
            lanes = lanes_of(total_cross_ref.shape)
            total = jnp.where(lanes == place.start // HEAD + half, total_cross_ref[...], 0.0)
            query = one_half(query_cross_ref[:, place], half)
            parts.append(
                attention_back(
                    query,
                    keys,
                    values,
                    mm_t(query, keys),
                    jnp.sum(total, axis=-1, keepdims=True),
                    one_half(cross_query_slope_ref[:, place], half),
                )
            )
        cross_query_slope_ref[:, place] = joined(parts[0][1], parts[1][1]).astype(bf16)
        cross_kv_slope_ref[:, place] = (parts[0][2] + parts[1][2]).astype(bf16)
        cross_kv_slope_ref[:, place_v] = (parts[0][3] + parts[1][3]).astype(bf16)

    in_steps(HD, 2 * HEAD, cross_pair_back, HD)
    memory = fetched[3]

    def memory_weights(here, there):
        grad_b_ref[:, there] = t_mm(memory[...], cross_kv_slope_ref[:, here]).astype(bf16)

    in_steps(2 * HD, FF_STEP, memory_weights, ff)
    copy_b = pltpu.make_async_copy(grad_b_ref, grad_b_hbm, out_sems.at[1])
    copy_b.start()
    step = min(256, memory.shape[0])

    def project(number, carry):
        rows = pl.ds(pl.multiple_of(number * step, step), step)
        memory_part_ref[rows, :] = mm_t(
            cross_kv_slope_ref[rows, :], part_b[:, ff : ff + 2 * HD]
        ).astype(bf16)
        return carry

    lax.fori_loop(0, memory.shape[0] // step, project, 0)
    copy_m = pltpu.make_async_copy(memory_part_ref, memory_part_hbm, out_sems.at[2])
    copy_m.start()
    part_c = fetched[4]
    query_slope = cross_query_slope_ref[...]
    grad_c_ref[:, HD : 2 * HD] = t_mm(normed_cross_ref[...], query_slope).astype(bf16)
    back, norm_grad = rms_back(
        resid1_ref[...], gains_ref[1:2], mm_t(query_slope, part_c[:, 4 * HD : 5 * HD])
    )
    norm_grads_ref[1:2] = norm_grad
    grad1 = grad2 + back
    grad1_ref[...] = grad1

    self_in = grad1.astype(bf16)
    grad_c_ref[:, :HD] = t_mm(self_in, attn_self_ref[...]).astype(bf16)
    out_slope = mm(self_in, part_c[:, 3 * HD : 4 * HD]).astype(bf16)
    bias_rows = pltpu.roll(mm(bias_ref[...], table_ref[...]), first, 1)
    bias_sums = jnp.zeros(bias_rows.shape, f32)
    rows, seq = query_ref.shape[0], kv_ref.shape[0]
    reverse = lax.broadcasted_iota(jnp.int32, (rows, rows), 0) + lanes_of((rows, rows)) == rows - 1
    reverse = reverse.astype(bf16)
    for pair in range(HEADS // 2):
        place = slice(2 * HEAD * pair, 2 * HEAD * (pair + 1))
        place_v = slice(HD + 2 * HEAD * pair, HD + 2 * HEAD * (pair + 1))
        keys, values = kv_ref[:, place], kv_ref[:, place_v]
        parts = []
        for half in range(2):
            number = 2 * pair + half
            query = one_half(query_ref[:, place], half)
            scores = biased_scores(
                mm_t(query, keys), bias_rows[number : number + 1], first, length
            )
            part = attention_back(
                query,
                keys,
                values,
                scores,
                total_self_ref[:, number : number + 1],
                one_half(out_slope[:, place], half),
            )
            parts.append(part)
            turned = pltpu.roll(mm(reverse, part[0]), 0, 1, stride=1, stride_axis=0)
            where = lax.broadcasted_iota(jnp.int32, bias_sums.shape, 0) == number
            bias_sums = jnp.where(where, jnp.sum(turned, axis=0, keepdims=True), bias_sums)
        query_slope_ref[:, place] = joined(parts[0][1], parts[1][1]).astype(bf16)
        kv_slope_ref[:, place] = (parts[0][2] + parts[1][2]).astype(bf16)
        kv_slope_ref[:, place_v] = (parts[0][3] + parts[1][3]).astype(bf16)
    bias_sums = pltpu.roll(bias_sums, 2 * seq + 1 - rows - first, 1)
    high = bias_sums.astype(bf16)
    rest = bias_sums - high.astype(f32)
    middle = rest.astype(bf16)
    low = (rest - middle.astype(f32)).astype(bf16)
    table = table_ref[...]
    bias_grad_ref[...] = mm_t(high, table) + (mm_t(middle, table) + mm_t(low, table))
    copy_a.wait()
    copy_b.wait()
    copy_m.wait()


def leave_kernel(
    query_slope_ref,
    kv_slope_ref,
    normed_ref,
    resid0_ref,
    grad1_ref,
    gains_ref,
    norm_grads_ref,
    part_grad_ref,
    part_c_ref,
    grad_c_ref,
    grad0_ref,
):
    normed = normed_ref[...]
    query_slope, kv_slope = query_slope_ref[...], kv_slope_ref[...]
    slope = mm_t(query_slope, part_c_ref[:, :HD]) + mm_t(kv_slope, part_c_ref[:, HD : 3 * HD])
    back, norm_grad = rms_back(resid0_ref[...], gains_ref[0:1], slope)
    grad0_ref[...] = (grad1_ref[...] + back).astype(bf16)
    grad_c_ref[:, :HD] = t_mm(normed, query_slope).astype(bf16)
    grad_c_ref[:, HD : 3 * HD] = t_mm(normed, kv_slope).astype(bf16)
    grad_c_ref[:, 3 * HD : 5 * HD] = part_grad_ref[...]
    where = lax.broadcasted_iota(jnp.int32, norm_grads_ref.shape, 0) == 0
    norm_grads = jnp.where(where, norm_grad, norm_grads_ref[...]).astype(bf16)
    row = lax.broadcasted_iota(jnp.int32, (norm_grads.shape[0], GAIN_PAD), 0)
    spread = (row == lanes_of(row.shape)).astype(bf16)
    grad_c_ref[:, 5 * HD :] = t_mm(norm_grads, spread).astype(bf16)


def local_kernel(name, kernel, outs, args, spaces="", out_spaces="", scratch=()):
    space = {"v": pltpu.VMEM, "s": pltpu.SMEM, "a": pl.ANY}
    spaces = spaces or "v" * len(args)
    out_spaces = out_spaces or "v" * len(outs)
    return pl.pallas_call(
        kernel,
        name=name,
        out_shape=tuple(jax.ShapeDtypeStruct(shape, dtype) for shape, dtype in outs),
        in_specs=[pl.BlockSpec(memory_space=space[letter]) for letter in spaces],
        out_specs=tuple(pl.BlockSpec(memory_space=space[letter]) for letter in out_spaces),
        scratch_shapes=list(scratch),
        compiler_params=pltpu.CompilerParams(vmem_limit_bytes=60 * 1024 * 1024),
    )(*args)


def pack_columns(pieces, block):
    start = 0
    for piece in pieces:
        if piece.shape[0] == 1:
            break
        block[:, start : start + piece.shape[1]] = piece[...]
        start += piece.shape[1]
    gains = pieces[-4:]
    if gains[0].shape[0] == 1:
        rows = gains[0].shape[1]
        where = lax.broadcasted_iota(jnp.int32, (16, rows), 0)
        stacked = jnp.zeros((16, rows), f32)
        for number, gain in enumerate(gains):
            stacked = jnp.where(where == number, gain[...].astype(f32), stacked)
        pick = lax.broadcasted_iota(jnp.int32, (16, GAIN_PAD), 0) == lanes_of((16, GAIN_PAD))
        block[:, start:] = t_mm(stacked.astype(bf16), pick.astype(bf16)).astype(bf16)


def pack_ids(pieces, block):
    block[...] = jnp.zeros_like(block)
    for number, piece in enumerate(pieces):
        micro, _, count = piece.shape
        for which in range(micro):
            block[micro * number + which : micro * number + which + 1, :count] = piece[which]


def tail_kernel(lengths_ref, *refs):
    (a_ref, b_ref, c_ref, small_ref, memory_ref, embedding_ref, head_ref), outs = refs[:7], refs[7:]
    (loss_ref, memory_out, embedding_out, head_out, bias_out), outs = outs[:5], outs[5:]
    memory_out[...] = memory_ref[...]
    embedding_out[...] = embedding_ref[...]
    head_out[...] = head_ref[...]
    total = jnp.sum(small_ref[...], axis=0)
    count = 0
    for first in range(lengths_ref.shape[0]):
        for second in range(lengths_ref.shape[1]):
            count = count + lengths_ref[first, second]
    loss_ref[...] = total[0:1, 64:65] / count.astype(f32)
    bias_out[...] = total[:HEADS, :BUCKETS]
    for ref, pieces in ((a_ref, outs[:2]), (b_ref, outs[2:6]), (c_ref, outs[6:11])):
        start = 0
        for piece in pieces:
            piece[...] = ref[:, start : start + piece.shape[1]]
            start += piece.shape[1]
    turned = jnp.transpose(c_ref[:, 5 * HD :])
    for number, piece in enumerate(outs[11:]):
        piece[...] = turned[number : number + 1]


def per_device(
    target_ids,
    labels,
    lengths,
    memory,
    embedding,
    head,
    gain_self,
    w_query,
    w_key,
    w_value,
    w_out,
    relative_bias,
    gain_cross,
    c_query,
    c_key,
    c_value,
    c_out,
    gain_ff,
    w_gate,
    w_up,
    w_down,
    gain_final,
):
    micro = target_ids.shape[0]
    seq_dev = target_ids.shape[2]
    mem_dev = memory.shape[2]
    voc_dev, width = embedding.shape
    ff = w_gate.shape[1]
    n_gx = lax.axis_size("gx")
    n_gy = lax.axis_size("gy")
    column = lax.axis_index("gy")
    row_group = lax.axis_index("gx")
    devices = n_gx * n_gy
    sizes = {"a": n_gx // 2, "c": 2, "s": n_gy // 2, "h": 2}
    assert sizes["s"] == 2 * micro
    place = coordinates()
    seq = seq_dev * n_gy
    plane = sizes["s"] * seq
    tok_dev = seq // 4
    tokens = plane // 2
    span = n_gx * voc_dev
    merged = "" if sizes["a"] == 2 else "ashc"

    rows_dev = width // devices
    whole_tiles = rows_dev % 16 == 0
    groups = (
        (w_gate, w_up),
        (w_down, c_key, c_value, c_out),
        (w_query, w_key, w_value, w_out, c_query),
    )
    gains = (gain_self, gain_cross, gain_ff, gain_final)
    widths = [sum(piece.shape[1] for piece in group) for group in groups]
    widths[2] += GAIN_PAD
    orders = ("shac", "sahc", "sahc")
    if whole_tiles:
        operands = list(groups)
        operands[2] += tuple(gain.reshape(1, rows_dev) for gain in gains)
        weights = [
            PackedGather(
                group,
                jax.ShapeDtypeStruct((rows_dev, count), bf16),
                pack_columns,
                order,
                "acsh",
                sizes,
                merged,
            )
            for group, count, order in zip(operands, widths, orders)
        ]
    else:
        shards = [jnp.concatenate(group, axis=1) for group in groups]
        columns_of = jnp.pad(jnp.stack(gains, axis=1), ((0, 0), (0, GAIN_PAD - 4)))
        shards[2] = jnp.concatenate([shards[2], columns_of], axis=1)
        weights = [
            Gather(packed(part), order, "acsh", sizes, merged) for part, order in zip(shards, orders)
        ]
    part_a, part_b, part_c, embed_rows, ids, memory_all = exchange(
        "gather_weights",
        0,
        weights
        + [
            Gather(embedding, "ac", "ac", sizes),
            PackedGather(
                (target_ids, labels),
                jax.ShapeDtypeStruct((8, 128), jnp.int32),
                pack_ids,
                "shc",
                "shc",
                sizes,
                "shc",
            ),
            MemoryGather(memory.reshape(micro, mem_dev, width), sizes),
        ],
    )
    part_a, part_b, part_c = (
        full.reshape(width, count) for full, count in zip((part_a, part_b, part_c), widths)
    )
    embed_rows = embed_rows.reshape(span, width)
    memory_all = memory_all.reshape(n_gy * mem_dev, width)
    ids = ids[..., : 2 * micro, :seq_dev].reshape(n_gy, 2, 2, micro, seq_dev)
    ids = ids.transpose(2, 3, 1, 0, 4).reshape(2, sizes["s"] * 2, 2, tok_dev)
    ids = lax.dynamic_index_in_dim(ids, place["c"], axis=2, keepdims=False).reshape(2, tokens)

    def local_of(index):
        shard = index // voc_dev
        return jnp.where(shard % n_gy == column, shard // n_gy * voc_dev + index % voc_dev, -1)

    local_ids = local_of(ids[0])
    targets = local_of(ids[1])
    columns = jnp.arange(span, dtype=jnp.int32)

    picked_rows = dot((local_ids[:, None] == columns[None, :]).astype(bf16), embed_rows).astype(bf16)
    tok_layout = (sizes["s"], 2, tok_dev, width)
    resid0, head_rows = exchange(
        "rows",
        1,
        [
            Scatter(picked_rows.reshape(tok_layout), "hs", "sh", sizes),
            Gather(head, "ac", "ac", sizes),
        ],
    )
    head_rows = head_rows.reshape(span, width)

    plane_lengths = lax.dynamic_slice_in_dim(lengths, 2 * place["a"], 2, axis=1).reshape(-1)
    live_length = lax.dynamic_index_in_dim(plane_lengths, place["s"], keepdims=False)
    scalars = jnp.stack([(2 * place["h"] + place["c"]) * tok_dev, live_length])
    table = jnp.asarray(distance_table(seq), bf16)
    bias_pad = jnp.pad(relative_bias, ((0, 8 - HEADS), (0, 128 - BUCKETS)))
    query_self, own_kv, normed_self, gain_rows = local_kernel(
        "enter",
        enter_kernel,
        [((tok_dev, HD), bf16), ((tok_dev, 2 * HD), bf16), ((tok_dev, width), bf16), ((16, width), f32)],
        [resid0, part_c],
    )
    (self_kv_all,) = exchange("self_keys", 2, [Gather(own_kv, "hc", "hc", sizes)])
    self_kv_all = self_kv_all.reshape(seq, 2 * HD)
    rows_f32, rows_bf16, rows_heads = ((tok_dev, width), f32), ((tok_dev, width), bf16), ((tok_dev, HD), bf16)
    totals_shape = ((tok_dev, 128), f32)
    all_mem = n_gy * mem_dev
    (
        attn_self,
        total_self,
        resid1,
        normed_cross,
        query_cross,
        mem_kv,
        attn_cross,
        total_cross,
        resid2,
        normed_ff,
        gate_up,
        hidden,
        resid3,
        final_rows,
    ) = local_kernel(
        "forward",
        forward_kernel,
        [
            rows_heads,
            totals_shape,
            rows_f32,
            rows_bf16,
            rows_heads,
            ((all_mem, 2 * HD), bf16),
            rows_heads,
            totals_shape,
            rows_f32,
            rows_bf16,
            ((tok_dev, 2 * ff), f32),
            ((tok_dev, ff), bf16),
            rows_f32,
            rows_bf16,
        ],
        [scalars, query_self, self_kv_all, resid0, gain_rows, table, bias_pad]
        + [memory_all, part_a, part_b, part_c],
        "svvvvvvaaaa",
        scratch=[pltpu.VMEM(full.shape, bf16) for full in (memory_all, part_a, part_b, part_c)]
        + [pltpu.SemaphoreType.DMA((4,))],
    )

    (states,) = exchange("final_rows", 3, [Gather(final_rows, "sh", "sh", sizes, merged)])
    states = states.reshape(tokens, width)
    logits = dot_t(states, head_rows)
    highest = jnp.max(logits, axis=1)
    own_total = highest + jnp.log(jnp.sum(jnp.exp(logits - highest[:, None]), axis=1))
    (totals,) = exchange("totals", 4, [DirectGather(own_total.reshape(tokens // 128, 128), sizes)])
    totals = totals.reshape(n_gy, tokens)
    top = jnp.max(totals, axis=0)
    log_total = top + jnp.log(jnp.sum(jnp.exp(totals - top[None]), axis=0))
    index = jnp.arange(tokens, dtype=jnp.int32)
    position = (2 * (index // tok_dev % 2) + place["c"]) * tok_dev + index % tok_dev
    alive = (position < jnp.repeat(plane_lengths, 2 * tok_dev)).astype(f32)
    hit = columns[None, :] == targets[:, None]
    picked = jnp.sum(jnp.where(hit, logits, 0.0), axis=1)
    loss_part = jnp.where(column == 0, jnp.sum(alive * log_total), 0.0) - jnp.sum(alive * picked)
    slope = ((jnp.exp(logits - log_total[:, None]) - hit.astype(f32)) * alive[:, None]).astype(bf16)
    head_part = t_dot(slope, states).astype(bf16)
    final_part = dot(slope, head_rows).astype(bf16)
    final_slope, head_grad = exchange(
        "final_slopes",
        5,
        [
            Scatter(final_part.reshape(tok_layout), "hs", "sh", sizes),
            Scatter(head_part.reshape(sizes["a"], 2, voc_dev, width), "ca", "ac", sizes),
        ],
    )

    grad_a, grad_b, memory_part, part_grad_c, query_slope, kv_slope, grad1, norm_grads, bias_grad = (
        local_kernel(
            "backward",
            backward_kernel,
            [
                (part_a.shape, bf16),
                (part_b.shape, bf16),
                (memory_all.shape, bf16),
                ((width, 2 * HD), bf16),
                rows_heads,
                ((seq, 2 * HD), bf16),
                rows_f32,
                (gain_rows.shape, f32),
                ((8, 128), f32),
            ],
            [scalars, final_slope, resid3, hidden, gate_up, normed_ff, resid2, attn_cross]
            + [query_cross, total_cross, normed_cross, resid1, attn_self, query_self, self_kv_all]
            + [total_self, gain_rows, table, bias_pad, mem_kv, memory_all, part_a, part_b, part_c],
            "s" + "v" * 18 + "a" * 5,
            "aaa" + "v" * 6,
            [
                pltpu.VMEM(full.shape, bf16)
                for full in (mem_kv, memory_all, part_a, part_b, part_c, part_a, part_b, memory_all)
            ]
            + [
                pltpu.VMEM((tok_dev, 2 * ff), bf16),
                pltpu.VMEM((tok_dev, HD), bf16),
                pltpu.VMEM(mem_kv.shape, bf16),
                pltpu.SemaphoreType.DMA((5,)),
                pltpu.SemaphoreType.DMA((3,)),
            ],
        )
    )
    (kv_slope,) = exchange(
        "key_slopes",
        6,
        [Scatter(kv_slope.reshape(2, 2, tok_dev, 2 * HD), "ch", "hc", sizes, "", bf16)],
    )
    grad_c, grad0 = local_kernel(
        "leave",
        leave_kernel,
        [(part_c.shape, bf16), rows_bf16],
        [query_slope, kv_slope, normed_self, resid0, grad1, gain_rows, norm_grads, part_grad_c, part_c],
    )
    (slopes,) = exchange("row_slopes", 7, [Gather(grad0, "sh", "sh", sizes, merged)])
    embed_part = t_dot(
        (local_ids[:, None] == columns[None, :]).astype(bf16), slopes.reshape(tokens, width)
    ).astype(bf16)
    sums = (grad_a, grad_b, grad_c)
    at_loss = (jnp.arange(8)[:, None] == 0) & (jnp.arange(128)[None, :] == 64)
    small = jnp.where(at_loss, loss_part, bias_grad)
    device_layout = (sizes["a"], 2, sizes["s"], 2)
    blocks = [part.reshape(device_layout + packed_shape(part, devices)) for part in sums]
    grad_a, grad_b, grad_c, embedding_grad, memory_grad, small = exchange(
        "scatter_weights",
        8,
        [
            Scatter(part, order[::-1], "acsh", sizes, merged)
            for part, order in zip(blocks, orders)
        ]
        + [
            Scatter(embed_part.reshape(sizes["a"], 2, voc_dev, width), "ca", "ac", sizes),
            MemoryScatter(memory_part.reshape(sizes["s"], 2, mem_dev, width), sizes),
            Gather(small, "shac", "acsh", sizes, "ashc"),
        ],
    )
    small = small.reshape(devices, 8, 128)
    memory_grad = memory_grad.reshape(micro, 1, mem_dev, width)
    if whole_tiles:
        pieces = [piece.shape[1] for group in groups for piece in group]
        outs = [
            ((1, 1), f32),
            (memory_grad.shape, f32),
            (embedding_grad.shape, f32),
            (head_grad.shape, f32),
            ((HEADS, BUCKETS), f32),
        ]
        outs += [((rows_dev, count), f32) for count in pieces] + [((1, rows_dev), f32)] * 4
        results = local_kernel(
            "tail",
            tail_kernel,
            outs,
            [lengths, grad_a, grad_b, grad_c, small, memory_grad, embedding_grad, head_grad],
            "s" + "v" * 7,
        )
        loss, memory_grad, embedding_grad, head_grad, bias_total = results[:5]
        loss = loss.reshape(())
        cut = results[5:16]
        gain_out = [gain.reshape(rows_dev) for gain in results[16:]]
    else:
        grad_a, grad_b, grad_c = (
            grad.reshape(rows_dev, count) for grad, count in zip((grad_a, grad_b, grad_c), widths)
        )
        small = jnp.sum(small, axis=0)
        loss = small[0, 64] / jnp.sum(lengths).astype(f32)
        bias_total = small[:HEADS, :BUCKETS]
        cut = []
        for grad, group in zip((grad_a, grad_b, grad_c), groups):
            start = 0
            for piece in group:
                cut.append(grad[:, start : start + piece.shape[1]])
                start += piece.shape[1]
        gain_out = [grad_c[:, 5 * HD + number] for number in range(4)]
    gate_grad, up_grad, down_grad, c_key_grad, c_value_grad, c_out_grad = cut[:6]
    query_grad, key_grad, value_grad, out_grad, c_query_grad = cut[6:]
    return (
        loss,
        memory_grad,
        embedding_grad,
        head_grad,
        gain_out[0],
        query_grad,
        key_grad,
        value_grad,
        out_grad,
        bias_total,
        gain_out[1],
        c_query_grad,
        c_key_grad,
        c_value_grad,
        c_out_grad,
        gain_out[2],
        gate_grad,
        up_grad,
        down_grad,
        gain_out[3],
    )


def packed_shape(part, count):
    rows, columns = part.shape[0] // count, part.shape[1]
    if rows % 16 == 0:
        return (rows, columns)
    return (16, rows * columns // 16)


def solution(mesh):
    placed = (
        P(None, "gx", "gy"),
        P(None, "gx", "gy"),
        P(),
        P(None, "gx", "gy", None),
        P(("gx", "gy"), None),
        P(("gx", "gy"), None),
        P(("gx", "gy")),
        P(("gx", "gy"), None),
        P(("gx", "gy"), None),
        P(("gx", "gy"), None),
        P(("gx", "gy"), None),
        P(),
        P(("gx", "gy")),
        P(("gx", "gy"), None),
        P(("gx", "gy"), None),
        P(("gx", "gy"), None),
        P(("gx", "gy"), None),
        P(("gx", "gy")),
        P(("gx", "gy"), None),
        P(("gx", "gy"), None),
        P(("gx", "gy"), None),
        P(("gx", "gy")),
    )
    return jax.shard_map(
        per_device,
        mesh=mesh,
        in_specs=placed,
        out_specs=(
            P(),
            P(None, "gx", "gy", None),
            P(("gx", "gy"), None),
            P(("gx", "gy"), None),
            P(("gx", "gy")),
            P(("gx", "gy"), None),
            P(("gx", "gy"), None),
            P(("gx", "gy"), None),
            P(("gx", "gy"), None),
            P(),
            P(("gx", "gy")),
            P(("gx", "gy"), None),
            P(("gx", "gy"), None),
            P(("gx", "gy"), None),
            P(("gx", "gy"), None),
            P(("gx", "gy")),
            P(("gx", "gy"), None),
            P(("gx", "gy"), None),
            P(("gx", "gy"), None),
            P(("gx", "gy")),
        ),
        check_vma=False,
    )
```

```python
import functools
import itertools
import math

import jax
import jax.numpy as jnp
import numpy as np
from jax import lax
from jax.experimental import pallas as pl
from jax.experimental.pallas import tpu as pltpu
from jax.sharding import PartitionSpec as P

HEADS = 6
HEAD = 64
HD = HEADS * HEAD
BUCKETS = 32
GAIN_PAD = 128

eps = 1e-06
masked_score = -1000000000.0
bf16 = jnp.bfloat16
f32 = jnp.float32


def flip(position, offset):
    moved = position
    weight = 1
    while weight <= offset:
        if offset & weight:
            moved = moved + weight * (1 - 2 * ((position // weight) % 2))
        weight *= 2
    return moved


def coordinates():
    gx, gy = lax.axis_index("gx"), lax.axis_index("gy")
    return {"a": gx // 2, "c": gx % 2, "s": gy // 2, "h": gy % 2}


def peer_of(dim, offset):
    gx, gy = lax.axis_index("gx"), lax.axis_index("gy")
    if dim == "a":
        return {"gx": 2 * flip(gx // 2, offset) + gx % 2}
    if dim == "c":
        return {"gx": flip(gx, 1)}
    if dim == "plane":
        s, h = offset
        return {"gy": 2 * flip(gy // 2, s) + flip(gy % 2, h)}
    if dim == "s":
        return {"gy": 2 * flip(gy // 2, offset) + gy % 2}
    return {"gy": flip(gy, 1)}


def remote(source, target, send, recv, dim, offset):
    return pltpu.make_async_remote_copy(
        src_ref=source,
        dst_ref=target,
        send_sem=send,
        recv_sem=recv,
        device_id=peer_of(dim, offset),
        device_id_type=pl.DeviceIdType.MESH,
    )


def along_line(position, step):
    half = position // 2
    return (position, flip(position, 1), 2 - half, 3 - 3 * half)[step]


def is_middle(position):
    return (position + 1) // 2 == 1


def across_middle():
    gy = lax.axis_index("gy")
    return {"gy": 2 * (3 - gy // 2) + gy % 2}


def spot_of(dim, position, offset):
    return along_line(position, offset) if dim == "s" else flip(position, offset)


def remote_to(source, target, send, recv, device):
    return pltpu.make_async_remote_copy(
        src_ref=source,
        dst_ref=target,
        send_sem=send,
        recv_sem=recv,
        device_id=device,
        device_id_type=pl.DeviceIdType.MESH,
    )


def each_piece(rows, columns, body, width=16384):
    step = rows
    while step * columns > width and step % 32 == 0:
        step //= 2
    if step == rows:
        body(slice(None))
        return

    def piece(number, carry):
        body(pl.ds(pl.multiple_of(number * step, step), step))
        return carry

    lax.fori_loop(0, rows // step, piece, 0)


LINE_PEERS = [("s", 1), ("m", 1)]


class Gather:
    def __init__(self, block, order, layout, sizes, merged="", late=0):
        self.value = block
        self.late = late
        self.order, self.layout, self.sizes, self.merged = order, layout, sizes, merged
        self.out = jax.ShapeDtypeStruct(tuple(sizes[d] for d in layout) + block.shape, block.dtype)
        self.in_spec = pl.BlockSpec(memory_space=pltpu.VMEM)
        self.out_spec = pl.BlockSpec(memory_space=pl.ANY)
        self.transfers = []
        for level, dim in enumerate(order):
            ranges = [(None,) if d in merged else range(sizes[d]) for d in order[:level]]
            for unit in itertools.product(*ranges):
                for offset in range(1, sizes[dim]):
                    self.transfers.append((level, unit, offset))
        self.index = {transfer: number for number, transfer in enumerate(self.transfers)}
        count = len(self.transfers)
        self.line = order[0] == "s"
        self.scratch = [
            pltpu.SemaphoreType.DMA((count,)),
            pltpu.SemaphoreType.DMA((count,)),
            pltpu.SemaphoreType.DMA,
            pltpu.SemaphoreType.DMA((5,)),
        ]
        self.peers = [(d, offset) for d in order for offset in range(1, sizes[d]) if d != "s"]
        if self.line:
            self.peers += LINE_PEERS

    def prepare(self, refs, place):
        self.source, self.target, self.send, self.recv, self.local_sem, self.line_send = refs
        self.place = place
        self.local = pltpu.make_async_copy(
            self.source, self.target.at[tuple(place[d] for d in self.layout)], self.local_sem
        )
        self.local.start()
        self.local_done = False
        self.arrived = set()
        self.sent = []

    def region(self, level, unit, offset):
        where = dict(self.place)
        for d, moved in zip(self.order[:level], unit):
            where[d] = slice(None) if moved is None else spot_of(d, self.place[d], moved)
        if offset:
            dim = self.order[level]
            where[dim] = spot_of(dim, self.place[dim], offset)
        return self.target.at[tuple(where[d] for d in self.layout)]

    def needs(self, level, unit):
        if level == 0:
            return []
        last, before = unit[-1], unit[:-1]
        if last is None:
            dim = self.order[level - 1]
            return self.needs(level - 1, before) + [
                (level - 1, before, offset) for offset in range(1, self.sizes[dim])
            ]
        if last == 0:
            return self.needs(level - 1, before)
        return [(level - 1, before, last)]

    def arrive(self, transfer):
        if transfer in self.arrived:
            return
        self.arrived.add(transfer)
        level, unit, offset = transfer
        number = self.index[transfer]
        there = self.region(level, unit, offset)
        if self.line and level == 0:
            offset = 1
        remote(
            there, there, self.send.at[number], self.recv.at[number], self.order[level], offset
        ).wait_recv()

    def line_copy(self, number):
        held, there = ((0, 1), (0, 2), (1, 3), (2, 2), (3, 3))[number]
        target = self.region(0, (), held)
        device = peer_of("s", 1) if number in (0, 3, 4) else across_middle()
        recv = self.recv.at[self.index[(0, (), there)]]
        source = target if held else self.source
        return remote_to(source, target, self.line_send.at[number], recv, device)

    def line_first(self):
        self.line_copy(0).start()

        @pl.when(is_middle(self.place["s"]))
        def _():
            self.line_copy(1).start()

    def line_next(self, step):
        self.arrive((0, (), step))

        @pl.when(is_middle(self.place["s"]))
        def _():
            self.line_copy(step + 1).start()

    def copy(self, transfer):
        level, unit, offset = transfer
        number = self.index[transfer]
        target = self.region(level, unit, 0)
        own = all(moved == 0 for moved in unit)
        return remote(
            self.source if own else target,
            target,
            self.send.at[number],
            self.recv.at[number],
            self.order[level],
            offset,
        )

    def launch(self, transfer):
        level, unit, offset = transfer
        for need in self.needs(level, unit):
            self.arrive(need)
        if None in unit and not self.local_done:
            self.local.wait()
            self.local_done = True
        self.copy(transfer).start()
        self.sent.append(transfer)

    def events(self):
        found = []
        if self.line:
            found.append((0, self.line_first))
            for step in (1, 2, 3):
                found.append((step, functools.partial(self.line_next, step)))
        for transfer in self.transfers:
            level, unit, offset = transfer
            if self.line and level == 0:
                continue
            key = 0.1 * level + 0.01 * offset
            for d, moved in zip(self.order, unit):
                key += self.sizes[d] - 1 if moved is None else moved
            if self.late and self.needs(level, unit):
                key += self.late
            found.append((key, functools.partial(self.launch, transfer)))
        return found

    def finish(self):
        if not self.local_done:
            self.local.wait()
        for transfer in self.transfers:
            self.arrive(transfer)
        for transfer in self.sent:
            self.copy(transfer).wait_send()
        if self.line:
            self.line_copy(0).wait_send()

            @pl.when(is_middle(self.place["s"]))
            def _():
                for number in range(1, 5):
                    self.line_copy(number).wait_send()


class PackedGather(Gather):
    def __init__(self, values, block, pack, *args):
        super().__init__(block, *args)
        self.values, self.pack = values, pack
        self.scratch = [pltpu.VMEM(block.shape, block.dtype)] + self.scratch


class DirectGather:
    def __init__(self, block, sizes):
        self.value = block
        shape = (sizes["s"], 2)
        self.out = jax.ShapeDtypeStruct(shape + block.shape, block.dtype)
        self.in_spec = pl.BlockSpec(memory_space=pltpu.VMEM)
        self.out_spec = pl.BlockSpec(memory_space=pltpu.VMEM)
        self.offsets = list(itertools.product(*(range(size) for size in shape)))[1:]
        count = len(self.offsets)
        self.scratch = [pltpu.SemaphoreType.DMA((count,)), pltpu.SemaphoreType.DMA((count,))]
        self.peers = [("plane", offset) for offset in self.offsets]

    def prepare(self, refs, place):
        self.source, self.target, self.send, self.recv = refs
        self.place = place

    def copy(self, number, arriving):
        offset = self.offsets[number]
        spot = tuple(
            flip(self.place[d], moved) if arriving else self.place[d] for d, moved in zip("sh", offset)
        )
        return remote_to(
            self.source,
            self.target.at[spot],
            self.send.at[number],
            self.recv.at[number],
            peer_of("plane", offset),
        )

    def events(self):
        return [(0, self.begin)]

    def begin(self):
        for number in range(len(self.offsets)):
            self.copy(number, False).start()
        self.target[self.place["s"], self.place["h"]] = self.source[...]

    def finish(self):
        self.receive()
        self.drain()

    def receive(self):
        for number in range(len(self.offsets)):
            self.copy(number, True).wait_recv()

    def drain(self):
        for number in range(len(self.offsets)):
            self.copy(number, False).wait_send()


class Scatter:
    def __init__(self, value, order, layout, sizes, merged="", out_dtype=f32):
        self.value = value
        self.order, self.layout, self.sizes, self.merged = order, layout, sizes, merged
        self.block = value.shape[len(layout) :]
        self.out = jax.ShapeDtypeStruct(self.block, out_dtype)
        self.in_spec = pl.BlockSpec(memory_space=pltpu.VMEM)
        self.out_spec = pl.BlockSpec(memory_space=pltpu.VMEM)
        self.line = order[-1] == "s"
        self.levels = len(order)
        self.units = []
        self.scratch = []
        self.layouts = [layout]
        for level, dim in enumerate(order):
            later = order[level + 1 :]
            ranges = [(None,) if d in merged else range(sizes[d]) for d in later]
            units = sorted(
                itertools.product(*ranges),
                key=lambda unit: (-(unit[-1] or 0) if unit else 0, -sum(moved or 0 for moved in unit)),
            )
            self.units.append(units)
            left = "".join(d for d in self.layouts[-1] if d != dim)
            self.layouts.append(left)
            self.scratch.append(
                pltpu.VMEM(
                    (5 if dim == "s" else sizes[dim] - 1,)
                    + tuple(sizes[d] for d in left)
                    + self.block,
                    value.dtype,
                )
            )
        self.index = {}
        for level, dim in enumerate(order):
            for unit in self.units[level]:
                for offset in range(1, sizes[dim]):
                    self.index[(level, unit, offset)] = len(self.index)
        count = len(self.index)
        self.scratch += [
            pltpu.SemaphoreType.DMA((count,)),
            pltpu.SemaphoreType.DMA((count,)),
            pltpu.SemaphoreType.DMA((2, 5)),
        ]
        self.peers = [(d, offset) for d in order for offset in range(1, sizes[d]) if d != "s"]
        if self.line:
            self.peers += LINE_PEERS

    def prepare(self, refs, place):
        self.source, self.target = refs[0], refs[1]
        self.landing = refs[2 : 2 + self.levels]
        self.send, self.recv, self.line_sems = refs[2 + self.levels :]
        self.place = place
        self.sent = []

    def held(self, level):
        return self.source if level == 0 else self.landing[level - 1].at[0]

    def later(self, level, unit):
        where = {}
        for d, moved in zip(self.order[level + 1 :], unit):
            where[d] = slice(None) if moved is None else spot_of(d, self.place[d], moved)
        return where

    def copy(self, level, unit, offset):
        number = self.index[(level, unit, offset)]
        dim = self.order[level]
        where = self.later(level, unit)
        landed = self.landing[level].at[
            (offset - 1,) + tuple(where[d] for d in self.layouts[level + 1])
        ]
        where[dim] = flip(self.place[dim], offset)
        source = self.held(level).at[tuple(where[d] for d in self.layouts[level])]
        return remote(source, landed, self.send.at[number], self.recv.at[number], dim, offset)

    def launch(self, level, unit, offset):
        self.copy(level, unit, offset).start()
        self.sent.append((level, unit, offset))

    def reduce(self, level, unit):
        dim = self.order[level]
        size = self.sizes[dim]
        for offset in range(1, size):
            self.copy(level, unit, offset).wait_recv()
        where = self.later(level, unit)
        free = [d for d in self.order[level + 1 :] if isinstance(where[d], slice)]
        total = math.prod(self.sizes[d] for d in free)
        rows, columns = self.block
        last = level == self.levels - 1

        def one(number, carry):
            at = dict(where)
            rest = number
            for d in free:
                at[d] = rest % self.sizes[d]
                rest = rest // self.sizes[d]
            spot = tuple(at[d] for d in self.layouts[level + 1])
            at[dim] = self.place[dim]
            mine = tuple(at[d] for d in self.layouts[level])

            def body(piece):
                if not last and size == 2:
                    self.landing[level][(0,) + spot + (piece,)] += self.held(level)[mine + (piece,)]
                    return
                result = self.held(level)[mine + (piece,)].astype(f32)
                for offset in range(1, size):
                    result = result + self.landing[level][(offset - 1,) + spot + (piece,)].astype(f32)
                if last:
                    self.target[(piece,)] = result.astype(self.target.dtype)
                else:
                    self.landing[level][(0,) + spot + (piece,)] = result.astype(self.landing[level].dtype)

            each_piece(rows, columns, body)
            return carry

        if total == 1:
            one(0, 0)
        else:
            lax.fori_loop(0, total, one, 0)
        if not last and not (self.line and level == self.levels - 2):
            ahead, rest = unit[0], unit[1:]
            if ahead is None:
                offsets = range(1, self.sizes[self.order[level + 1]])
            else:
                offsets = [ahead] if ahead else []
            for offset in offsets:
                self.launch(level + 1, rest, offset)

    def line_copy(self, number):
        step, slot = ((1, 0), (2, 1), (3, 2), (3, 3), (2, 4))[number]
        level = self.levels - 1
        block = self.held(level).at[along_line(self.place["s"], step)]
        landed = self.landing[level].at[slot]
        device = peer_of("s", 1) if number < 3 else across_middle()
        return remote_to(block, landed, self.line_sems.at[0, number], self.line_sems.at[1, number], device)

    def line_step(self, step, ends=True, middles=True):
        level = self.levels - 1
        middle = is_middle(self.place["s"])
        rows, columns = self.block
        held, landing = self.held(level), self.landing[level]
        position = along_line(self.place["s"], step)

        def pass_on():
            arrived = (0, 3, 1, 2)[step]
            self.line_copy(arrived).wait_recv()

            def body(piece):
                held[(position, piece)] += landing[(arrived, piece)]

            each_piece(rows, columns, body)
            self.line_copy((0, 0, 4, 3)[step]).start()

        if step:
            if ends:
                pl.when(jnp.logical_not(middle))(lambda: self.line_copy(step - 1).start())
            if middles:
                pl.when(middle)(pass_on)
            return

        self.line_copy(0).wait_recv()

        @pl.when(middle)
        def _():
            self.line_copy(4).wait_recv()

            def body(piece):
                result = held[(position, piece)].astype(f32) + landing[(0, piece)].astype(f32)
                self.target[(piece,)] = (result + landing[(4, piece)].astype(f32)).astype(
                    self.target.dtype
                )

            each_piece(rows, columns, body)

        @pl.when(jnp.logical_not(middle))
        def _():
            def body(piece):
                result = held[(position, piece)].astype(f32) + landing[(0, piece)].astype(f32)
                self.target[(piece,)] = result.astype(self.target.dtype)

            each_piece(rows, columns, body)

    def events(self):
        found = []
        for number, unit in enumerate(self.units[0]):
            for offset in range(1, self.sizes[self.order[0]]):
                found.append(
                    (-1 + 0.001 * number, functools.partial(self.launch, 0, unit, offset))
                )
        spread = 4 if self.line else 1
        for level in range(self.levels - self.line):
            count = len(self.units[level])
            for number, unit in enumerate(self.units[level]):
                late = 0
                if self.order[-1] == "a":
                    late = 20 if level == self.levels - 1 else 0.9
                found.append(
                    (late + level + spread * number / count, functools.partial(self.reduce, level, unit))
                )
        if self.line:
            for number, step in enumerate((3, 2, 1, 0)):
                found.append(
                    (self.levels - 1 + number + 0.5, functools.partial(self.line_step, step))
                )
        return found

    def finish(self):
        for transfer in self.sent:
            self.copy(*transfer).wait_send()
        if self.line:
            self.line_copy(0).wait_send()
            middle = is_middle(self.place["s"])

            @pl.when(middle)
            def _():
                for number in (3, 4):
                    self.line_copy(number).wait_send()

            @pl.when(jnp.logical_not(middle))
            def _():
                for number in (1, 2):
                    self.line_copy(number).wait_send()


class MemoryGather:
    def __init__(self, memory, sizes):
        self.value = memory
        self.sizes = sizes
        self.out = jax.ShapeDtypeStruct((sizes["s"], 2) + memory.shape[1:], memory.dtype)
        self.in_spec = pl.BlockSpec(memory_space=pltpu.VMEM)
        self.out_spec = pl.BlockSpec(memory_space=pl.ANY)
        rows = sizes["s"]
        self.scratch = [
            pltpu.SemaphoreType.DMA((2, rows)),
            pltpu.SemaphoreType.DMA((2, rows)),
            pltpu.SemaphoreType.DMA((2, rows, 2)),
            pltpu.SemaphoreType.DMA,
        ]
        self.peers = [("s", offset) for offset in range(1, rows)] + [("h", 1), ("c", 1)]

    def prepare(self, refs, place):
        self.source, self.target, self.along, self.across, self.core, self.local = refs
        self.place = place
        self.mine = place["s"] % 2 == place["c"]

    def row(self, offset):
        return flip(self.place["s"], offset)

    def along_copy(self, offset, arriving):
        to = self.row(offset)
        spot = to if arriving else self.place["s"]
        return remote(
            self.source.at[self.place["s"] // 2 if arriving else to // 2],
            self.target.at[spot, self.place["h"]],
            self.along.at[0, offset],
            self.along.at[1, offset],
            "s",
            offset,
        )

    def across_copy(self, offset, arriving):
        h = self.place["h"]
        own = self.target.at[self.row(offset), 1 - h if arriving else h]
        if offset == 0 and not arriving:
            source = self.source.at[self.place["s"] // 2]
        else:
            source = own
        return remote(source, own, self.across.at[0, offset], self.across.at[1, offset], "h", 1)

    def core_copy(self, offset, other):
        h = self.place["h"]
        own = self.target.at[self.row(offset), 1 - h if other else h]
        source = self.source.at[self.place["s"] // 2] if offset == 0 and not other else own
        return remote(source, own, self.core.at[0, offset, other], self.core.at[1, offset, other], "c", 1)

    def events(self):
        rows = self.sizes["s"]

        def first():
            for offset in range(1, rows):
                @pl.when(self.row(offset) % 2 == self.place["c"])
                def _():
                    self.along_copy(offset, False).start()

            @pl.when(self.mine)
            def _():
                pltpu.make_async_copy(
                    self.source.at[self.place["s"] // 2],
                    self.target.at[self.place["s"], self.place["h"]],
                    self.local,
                ).start()
                self.across_copy(0, False).start()
                self.core_copy(0, 0).start()

        def arrival(offset):
            @pl.when(self.mine)
            def _():
                self.along_copy(offset, True).wait_recv()
                self.across_copy(offset, False).start()
                self.core_copy(offset, 0).start()

        def other(offset):
            @pl.when(self.mine)
            def _():
                self.across_copy(offset, True).wait_recv()
                self.core_copy(offset, 1).start()

        found = [(0.05, first)]
        for offset in range(1, rows):
            found.append((offset + 0.05, functools.partial(arrival, offset)))
        for offset in range(rows):
            found.append((rows + offset, functools.partial(other, offset)))
        return found

    def finish(self):
        rows = self.sizes["s"]
        for offset in range(1, rows):
            @pl.when(self.row(offset) % 2 == self.place["c"])
            def _():
                self.along_copy(offset, False).wait_send()

        @pl.when(self.mine)
        def _():
            pltpu.make_async_copy(
                self.source.at[self.place["s"] // 2],
                self.target.at[self.place["s"], self.place["h"]],
                self.local,
            ).wait()
            for offset in range(rows):
                self.across_copy(offset, False).wait_send()
                for other in range(2):
                    self.core_copy(offset, other).wait_send()

        @pl.when(jnp.logical_not(self.mine))
        def _():
            for offset in range(rows):
                for other in range(2):
                    self.core_copy(offset, other).wait_recv()


class MemoryScatter:
    def __init__(self, value, sizes):
        self.value = value
        self.sizes = sizes
        rows = sizes["s"]
        self.block = value.shape[2:]
        self.out = jax.ShapeDtypeStruct((2,) + self.block, f32)
        self.in_spec = pl.BlockSpec(memory_space=pltpu.VMEM)
        self.out_spec = pl.BlockSpec(memory_space=pltpu.VMEM)
        self.scratch = [
            pltpu.VMEM(value.shape, value.dtype),
            pltpu.VMEM((rows,) + self.block, value.dtype),
            pltpu.VMEM((2,) + self.block, value.dtype),
            pltpu.SemaphoreType.DMA((2, rows, 2)),
            pltpu.SemaphoreType.DMA((2, rows)),
            pltpu.SemaphoreType.DMA((2, rows)),
        ]
        self.peers = [("s", offset) for offset in range(1, rows)] + [("h", 1), ("c", 1)]

    def prepare(self, refs, place):
        self.source, self.target = refs[0], refs[1]
        self.summed, self.halved, self.landed, self.core, self.across, self.along = refs[2:]
        self.place = place
        self.mine = place["s"] % 2 == place["c"]

    def row(self, offset):
        return flip(self.place["s"], offset)

    def core_copy(self, offset, other):
        h = self.place["h"]
        spot = (self.row(offset), flip(h, 1) if other else h)
        return remote(
            self.source.at[spot],
            self.summed.at[spot],
            self.core.at[0, offset, other],
            self.core.at[1, offset, other],
            "c",
            1,
        )

    def across_copy(self, offset):
        row = self.row(offset)
        return remote(
            self.summed.at[row, flip(self.place["h"], 1)],
            self.halved.at[row],
            self.across.at[0, offset],
            self.across.at[1, offset],
            "h",
            1,
        )

    def along_copy(self, offset, arriving):
        to = self.row(offset)
        return remote(
            self.halved.at[to],
            self.landed.at[to // 2 if arriving else self.place["s"] // 2],
            self.along.at[0, offset],
            self.along.at[1, offset],
            "s",
            offset,
        )

    def events(self):
        rows = self.sizes["s"]
        high, wide = self.block
        orders = list(range(1, rows))[::-1] + [0]

        def first():
            @pl.when(jnp.logical_not(self.mine))
            def _():
                for other in (1, 0):
                    for offset in orders:
                        self.core_copy(offset, other).start()

        def level(offset, other):
            @pl.when(self.mine)
            def _():
                self.core_copy(offset, other).wait_recv()
                h = self.place["h"]
                spot = (self.row(offset), flip(h, 1) if other else h)

                def body(piece):
                    total = self.summed[spot + (piece,)].astype(f32) + self.source[
                        spot + (piece,)
                    ].astype(f32)
                    self.summed[spot + (piece,)] = total.astype(self.summed.dtype)

                each_piece(high, wide, body)
                if other:
                    self.across_copy(offset).start()

        def last(offset):
            @pl.when(self.mine)
            def _():
                self.across_copy(offset).wait_recv()
                row = self.row(offset)

                def body(piece):
                    total = self.halved[(row, piece)].astype(f32) + self.summed[
                        (row, self.place["h"], piece)
                    ].astype(f32)
                    self.halved[(row, piece)] = total.astype(self.halved.dtype)
                    if offset == 0:
                        self.target[(self.place["s"] // 2, piece)] = total

                each_piece(high, wide, body)
                if offset:
                    self.along_copy(offset, False).start()

        found = [(-0.95, first)]
        for number, offset in enumerate(orders):
            found.append((0.05 + 0.1 * number, functools.partial(level, offset, 1)))
        for number, offset in enumerate(orders):
            found.append((0.55 + 0.1 * number, functools.partial(level, offset, 0)))
        for number, offset in enumerate(orders):
            found.append((1.05 + 0.2 * number, functools.partial(last, offset)))
        return found

    def finish(self):
        rows = self.sizes["s"]
        high, wide = self.block
        for offset in range(1, rows):
            @pl.when(self.row(offset) % 2 == self.place["c"])
            def _():
                self.along_copy(offset, True).wait_recv()
                number = self.row(offset) // 2

                def body(piece):
                    self.target[(number, piece)] = self.landed[(number, piece)].astype(f32)

                each_piece(high, wide, body)

        @pl.when(self.mine)
        def _():
            for offset in range(rows):
                self.across_copy(offset).wait_send()
            for offset in range(1, rows):
                self.along_copy(offset, False).wait_send()

        @pl.when(jnp.logical_not(self.mine))
        def _():
            for offset in range(rows):
                for other in range(2):
                    self.core_copy(offset, other).wait_send()


def peers_of(jobs):
    peers = []
    for job in jobs:
        for peer in job.peers:
            if peer not in peers:
                peers.append(peer)
    return peers


def greet(peers, place):
    barrier = pltpu.get_barrier_semaphore()
    middle = is_middle(place["s"])
    awaited = 0
    for peer in peers:
        if peer[0] == "m":
            @pl.when(middle)
            def _():
                pl.semaphore_signal(
                    barrier, inc=1, device_id=across_middle(), device_id_type=pl.DeviceIdType.MESH
                )
            continue
        awaited += 1
        pl.semaphore_signal(
            barrier, inc=1, device_id=peer_of(*peer), device_id_type=pl.DeviceIdType.MESH
        )
    return awaited


def welcome(peers, place, awaited):
    barrier = pltpu.get_barrier_semaphore()
    middle = is_middle(place["s"])
    if ("m", 1) in peers:
        @pl.when(middle)
        def _():
            pl.semaphore_wait(barrier, awaited + 1)

        @pl.when(jnp.logical_not(middle))
        def _():
            pl.semaphore_wait(barrier, awaited)
    else:
        pl.semaphore_wait(barrier, awaited)


def exchange(name, collective_id, jobs):
    values = [getattr(job, "values", None) or [job.value] for job in jobs]
    peers = peers_of(jobs)

    def kernel(*refs):
        total = sum(len(held) for held in values)
        results = refs[total : total + len(jobs)]
        scratch = refs[total + len(jobs) :]
        begin = offset = 0
        place = coordinates()
        awaited = greet(peers, place)
        for number, job in enumerate(jobs):
            end = begin + len(values[number])
            ins = refs[begin:end]
            if hasattr(job, "pack"):
                job.pack(ins, scratch[offset])
                ins, offset = (scratch[offset],), offset + 1
            mine = len(job.scratch) - hasattr(job, "pack")
            job.prepare(tuple(ins) + (results[number],) + tuple(scratch[offset : offset + mine]), place)
            begin, offset = end, offset + mine
        welcome(peers, place, awaited)
        events = [event for job in jobs for event in job.events()]
        for _, act in sorted(events, key=lambda event: event[0]):
            act()
        for job in jobs:
            job.finish()

    return pl.pallas_call(
        kernel,
        name=name,
        out_shape=tuple(job.out for job in jobs),
        in_specs=[job.in_spec for job, held in zip(jobs, values) for _ in held],
        out_specs=tuple(job.out_spec for job in jobs),
        scratch_shapes=[item for job in jobs for item in job.scratch],
        compiler_params=pltpu.CompilerParams(
            collective_id=collective_id, has_side_effects=True, vmem_limit_bytes=60 * 1024 * 1024
        ),
    )(*[value for held in values for value in held])


def packed(block):
    rows, columns = block.shape
    if rows % 16 == 0:
        return block
    return block.reshape(16, rows * columns // 16)


def bucket_edges():
    edges = []
    for target in range(1, 32):
        if target < 16:
            edges.append(target)
        else:
            found = 0
            for distance in range(16, 4096):
                value = 16 + int(math.log(distance / 16.0) / math.log(8.0) * 16.0)
                if found == 0 and value >= target:
                    found = distance
            edges.append(found)
    return edges


def gelu_tanh(value):
    return (
        0.5
        * value
        * (1.0 + jnp.tanh(0.7978845608028654 * (value + 0.044715 * value * value * value)))
    )


def dot(left, right):
    return jnp.einsum("sd,df->sf", left, right, preferred_element_type=f32)


def dot_t(left, right):
    return jnp.einsum("sf,df->sd", left, right, preferred_element_type=f32)


def t_dot(left, right):
    return jnp.einsum("sd,sf->df", left, right, preferred_element_type=f32)


def distance_table(seq):
    edges = np.array(bucket_edges())
    distance = (-np.arange(seq)) % seq
    bucket = (distance[:, None] >= edges[None, :]).sum(axis=1)
    return (np.arange(128)[:, None] == bucket[None, :]).astype(np.float32)


def mm(left, right):
    return lax.dot_general(left, right, (((1,), (0,)), ((), ())), preferred_element_type=f32)


def mm_t(left, right):
    return lax.dot_general(left, right, (((1,), (1,)), ((), ())), preferred_element_type=f32)


def t_mm(left, right):
    return lax.dot_general(left, right, (((0,), (0,)), ((), ())), preferred_element_type=f32)


def inverse_rms(rows):
    return lax.rsqrt(jnp.mean(rows * rows, axis=-1, keepdims=True) + eps)


def rms_back(rows, gain, slope):
    inverse = inverse_rms(rows)
    unit = rows * inverse
    scaled = slope * gain
    back = inverse * (scaled - unit * jnp.mean(unit * scaled, axis=-1, keepdims=True))
    return back, jnp.sum(slope * unit, axis=0, keepdims=True)


def lanes_of(shape):
    return lax.broadcasted_iota(jnp.int32, shape, len(shape) - 1)


def one_half(pair, half):
    inside = (lanes_of(pair.shape) // HEAD) == half
    return jnp.where(inside, pair, jnp.zeros_like(pair))


def joined(first, second):
    return jnp.where(lanes_of(first.shape) < HEAD, first, second)


def pair_of(ref, start, pair):
    return ref[:, start + 2 * HEAD * pair : start + 2 * HEAD * (pair + 1)]


FF_STEP = 256


def in_steps(total, step, body, further=0):
    def one(number, carry):
        here = pl.ds(pl.multiple_of(number * step, step), step)
        if further:
            body(here, pl.ds(pl.multiple_of(number * step + further, step), step))
        else:
            body(here)
        return carry

    lax.fori_loop(0, total // step, one, 0)


class Fetch:
    def __init__(self, sources, targets, sems):
        self.copies = [
            pltpu.make_async_copy(source, target, sems.at[number])
            for number, (source, target) in enumerate(zip(sources, targets))
        ]
        self.targets = targets
        self.ready = set()
        for copy in self.copies:
            copy.start()

    def __getitem__(self, number):
        if number not in self.ready:
            self.ready.add(number)
            self.copies[number].wait()
        return self.targets[number]


def enter_kernel(resid_ref, part_c_ref, query_ref, kv_ref, normed_ref, gains_ref):
    row = lax.broadcasted_iota(jnp.int32, (16, GAIN_PAD), 0)
    pick = (row == lanes_of((16, GAIN_PAD))).astype(bf16)
    gains = mm_t(pick, part_c_ref[:, 5 * HD : 5 * HD + GAIN_PAD])
    gains_ref[...] = gains
    resid = resid_ref[...]
    normed = (resid * inverse_rms(resid) * gains[0:1]).astype(bf16)
    normed_ref[...] = normed
    query_ref[...] = mm(normed, part_c_ref[:, :HD]).astype(bf16)
    kv_ref[...] = mm(normed, part_c_ref[:, HD : 3 * HD]).astype(bf16)


def biased_scores(scores, row, first, length):
    bias = pltpu.roll(jnp.broadcast_to(row, scores.shape), 0, 1, stride=1, stride_axis=0)
    query_pos = first + lax.broadcasted_iota(jnp.int32, scores.shape, 0)
    key_pos = lanes_of(scores.shape)
    mask = (key_pos <= query_pos) & (key_pos < length)
    return jnp.where(mask, scores + bias, masked_score)


def softmax_parts(scores):
    highest = jnp.max(scores, axis=-1, keepdims=True)
    total = highest + jnp.log(jnp.sum(jnp.exp(scores - highest), axis=-1, keepdims=True))
    return total, jnp.exp(scores - total)


def forward_kernel(
    scalars_ref,
    query_ref,
    kv_ref,
    resid0_ref,
    gains_ref,
    table_ref,
    bias_ref,
    memory_hbm,
    part_a_hbm,
    part_b_hbm,
    part_c_hbm,
    attn_self_ref,
    total_self_ref,
    resid1_ref,
    normed_cross_ref,
    query_cross_ref,
    mem_kv_ref,
    attn_cross_ref,
    total_cross_ref,
    resid2_ref,
    normed_ff_ref,
    gate_up_ref,
    hidden_ref,
    resid3_ref,
    final_ref,
    memory_ref,
    part_a_ref,
    part_b_ref,
    part_c_ref,
    sems,
):
    fetched = Fetch(
        (part_c_hbm, part_b_hbm, memory_hbm, part_a_hbm),
        (part_c_ref, part_b_ref, memory_ref, part_a_ref),
        sems,
    )
    first, length = scalars_ref[0], scalars_ref[1]
    ff = hidden_ref.shape[1]
    bias_rows = pltpu.roll(mm(bias_ref[...], table_ref[...]), first, 1)
    lanes = lanes_of(total_self_ref.shape)
    totals = jnp.zeros(total_self_ref.shape, f32)
    for pair in range(HEADS // 2):
        keys, values = pair_of(kv_ref, 0, pair), pair_of(kv_ref, HD, pair)
        outputs = []
        for half in range(2):
            number = 2 * pair + half
            scores = mm_t(one_half(pair_of(query_ref, 0, pair), half), keys)
            scores = biased_scores(scores, bias_rows[number : number + 1], first, length)
            total, shares = softmax_parts(scores)
            totals = jnp.where(lanes == number, total, totals)
            outputs.append(mm(shares.astype(bf16), values))
        attn_self_ref[:, 2 * HEAD * pair : 2 * HEAD * (pair + 1)] = joined(*outputs).astype(bf16)
    total_self_ref[...] = totals

    part_c = fetched[0]
    resid1 = resid0_ref[...] + mm_t(attn_self_ref[...], part_c[:, 3 * HD : 4 * HD])
    resid1_ref[...] = resid1
    normed = (resid1 * inverse_rms(resid1) * gains_ref[1:2]).astype(bf16)
    normed_cross_ref[...] = normed
    query_cross_ref[...] = mm(normed, part_c[:, 4 * HD : 5 * HD]).astype(bf16)

    part_b = fetched[1]
    memory = fetched[2]
    step = min(256, memory.shape[0])

    def project(number, carry):
        rows = pl.ds(pl.multiple_of(number * step, step), step)
        mem_kv_ref[rows, :] = mm(memory[rows, :], part_b[:, ff : ff + 2 * HD]).astype(bf16)
        return carry

    lax.fori_loop(0, memory.shape[0] // step, project, 0)
    total_cross_ref[...] = jnp.zeros(total_cross_ref.shape, f32)

    def cross_pair(place, place_v):
        keys, values = mem_kv_ref[:, place], mem_kv_ref[:, place_v]
        outputs = []
        for half in range(2):
            scores = mm_t(one_half(query_cross_ref[:, place], half), keys)
            total, shares = softmax_parts(scores)
            number = place.start // HEAD + half
            total_cross_ref[...] = jnp.where(lanes == number, total, total_cross_ref[...])
            outputs.append(mm(shares.astype(bf16), values))
        attn_cross_ref[:, place] = joined(*outputs).astype(bf16)

    in_steps(HD, 2 * HEAD, cross_pair, HD)
    resid2 = resid1_ref[...] + mm_t(attn_cross_ref[...], part_b[:, ff + 2 * HD :])
    resid2_ref[...] = resid2
    normed_ff_ref[...] = (resid2 * inverse_rms(resid2) * gains_ref[2:3]).astype(bf16)

    part_a = fetched[3]

    def feed(here, there):
        gate = mm(normed_ff_ref[...], part_a[:, here])
        up = mm(normed_ff_ref[...], part_a[:, there])
        gate_up_ref[:, here] = gate
        gate_up_ref[:, there] = up
        hidden_ref[:, here] = (gelu_tanh(gate) * up).astype(bf16)

    in_steps(ff, FF_STEP, feed, ff)
    resid3 = resid2_ref[...] + mm_t(hidden_ref[...], part_b[:, :ff])
    resid3_ref[...] = resid3
    final_ref[...] = (resid3 * inverse_rms(resid3) * gains_ref[3:4]).astype(bf16)


def attention_back(query, keys, values, scores, total, out_slope):
    shares = jnp.exp(scores - total)
    share_slope = mm_t(out_slope, values)
    inner = jnp.sum(shares * share_slope, axis=-1, keepdims=True)
    score_slope = shares * (share_slope - inner)
    rounded = score_slope.astype(bf16)
    return (
        rounded,
        mm(rounded, keys),
        t_mm(rounded, query),
        t_mm(shares.astype(bf16), out_slope),
    )


def backward_kernel(
    scalars_ref,
    slope_ref,
    resid3_ref,
    hidden_ref,
    gate_up_ref,
    normed_ff_ref,
    resid2_ref,
    attn_cross_ref,
    query_cross_ref,
    total_cross_ref,
    normed_cross_ref,
    resid1_ref,
    attn_self_ref,
    query_ref,
    kv_ref,
    total_self_ref,
    gains_ref,
    table_ref,
    bias_ref,
    mem_kv_hbm,
    memory_hbm,
    part_a_hbm,
    part_b_hbm,
    part_c_hbm,
    grad_a_hbm,
    grad_b_hbm,
    memory_part_hbm,
    grad_c_ref,
    query_slope_ref,
    kv_slope_ref,
    grad1_ref,
    norm_grads_ref,
    bias_grad_ref,
    mem_kv_ref,
    memory_ref,
    part_a_ref,
    part_b_ref,
    part_c_ref,
    grad_a_ref,
    grad_b_ref,
    memory_part_ref,
    gate_up_slope_ref,
    cross_query_slope_ref,
    cross_kv_slope_ref,
    sems,
    out_sems,
):
    fetched = Fetch(
        (part_b_hbm, part_a_hbm, mem_kv_hbm, memory_hbm, part_c_hbm),
        (part_b_ref, part_a_ref, mem_kv_ref, memory_ref, part_c_ref),
        sems,
    )
    first, length = scalars_ref[0], scalars_ref[1]
    ff = hidden_ref.shape[1]
    width = resid3_ref.shape[1]
    norm_grads_ref[...] = jnp.zeros_like(norm_grads_ref)

    grad3, norm_grad = rms_back(resid3_ref[...], gains_ref[3:4], slope_ref[...])
    norm_grads_ref[3:4] = norm_grad
    down_in = grad3.astype(bf16)
    part_b = fetched[0]

    def feed_back(here, there):
        hidden_slope = mm(down_in, part_b[:, here])
        gate, up = gate_up_ref[:, here], gate_up_ref[:, there]
        inner = jnp.tanh(0.7978845608028654 * (gate + 0.044715 * gate * gate * gate))
        activated = 0.5 * gate * (1.0 + inner)
        steep = 0.5 * (1.0 + inner) + 0.5 * gate * (1.0 - inner * inner) * (
            0.7978845608028654 * (1.0 + 3.0 * 0.044715 * gate * gate)
        )
        gate_up_slope_ref[:, here] = (hidden_slope * up * steep).astype(bf16)
        gate_up_slope_ref[:, there] = (hidden_slope * activated).astype(bf16)
        grad_b_ref[:, here] = t_mm(down_in, hidden_ref[:, here]).astype(bf16)

    in_steps(ff, FF_STEP, feed_back, ff)
    part_a = fetched[1]
    back, norm_grad = rms_back(
        resid2_ref[...], gains_ref[2:3], mm_t(gate_up_slope_ref[...], part_a[...])
    )
    norm_grads_ref[2:3] = norm_grad
    grad2 = grad3 + back

    def gate_up_grad(here):
        grad_a_ref[:, here] = t_mm(normed_ff_ref[...], gate_up_slope_ref[:, here]).astype(bf16)

    in_steps(2 * ff, 2 * FF_STEP, gate_up_grad)
    copy_a = pltpu.make_async_copy(grad_a_ref, grad_a_hbm, out_sems.at[0])
    copy_a.start()

    cross_in = grad2.astype(bf16)
    grad_b_ref[:, ff + 2 * HD :] = t_mm(cross_in, attn_cross_ref[...]).astype(bf16)
    out_slope = mm(cross_in, part_b[:, ff + 2 * HD :]).astype(bf16)
    mem_kv = fetched[2]
    cross_query_slope_ref[...] = out_slope

    def cross_pair_back(place, place_v):
        keys, values = mem_kv[:, place], mem_kv[:, place_v]
        parts = []
        for half in range(2):
            lanes = lanes_of(total_cross_ref.shape)
            total = jnp.where(lanes == place.start // HEAD + half, total_cross_ref[...], 0.0)
            query = one_half(query_cross_ref[:, place], half)
            parts.append(
                attention_back(
                    query,
                    keys,
                    values,
                    mm_t(query, keys),
                    jnp.sum(total, axis=-1, keepdims=True),
                    one_half(cross_query_slope_ref[:, place], half),
                )
            )
        cross_query_slope_ref[:, place] = joined(parts[0][1], parts[1][1]).astype(bf16)
        cross_kv_slope_ref[:, place] = (parts[0][2] + parts[1][2]).astype(bf16)
        cross_kv_slope_ref[:, place_v] = (parts[0][3] + parts[1][3]).astype(bf16)

    in_steps(HD, 2 * HEAD, cross_pair_back, HD)
    memory = fetched[3]

    def memory_weights(here, there):
        grad_b_ref[:, there] = t_mm(memory[...], cross_kv_slope_ref[:, here]).astype(bf16)

    in_steps(2 * HD, FF_STEP, memory_weights, ff)
    copy_b = pltpu.make_async_copy(grad_b_ref, grad_b_hbm, out_sems.at[1])
    copy_b.start()
    step = min(256, memory.shape[0])

    def project(number, carry):
        rows = pl.ds(pl.multiple_of(number * step, step), step)
        memory_part_ref[rows, :] = mm_t(
            cross_kv_slope_ref[rows, :], part_b[:, ff : ff + 2 * HD]
        ).astype(bf16)
        return carry

    lax.fori_loop(0, memory.shape[0] // step, project, 0)
    copy_m = pltpu.make_async_copy(memory_part_ref, memory_part_hbm, out_sems.at[2])
    copy_m.start()
    part_c = fetched[4]
    query_slope = cross_query_slope_ref[...]
    grad_c_ref[:, HD : 2 * HD] = t_mm(normed_cross_ref[...], query_slope).astype(bf16)
    back, norm_grad = rms_back(
        resid1_ref[...], gains_ref[1:2], mm_t(query_slope, part_c[:, 4 * HD : 5 * HD])
    )
    norm_grads_ref[1:2] = norm_grad
    grad1 = grad2 + back
    grad1_ref[...] = grad1

    self_in = grad1.astype(bf16)
    grad_c_ref[:, :HD] = t_mm(self_in, attn_self_ref[...]).astype(bf16)
    out_slope = mm(self_in, part_c[:, 3 * HD : 4 * HD]).astype(bf16)
    bias_rows = pltpu.roll(mm(bias_ref[...], table_ref[...]), first, 1)
    bias_sums = jnp.zeros(bias_rows.shape, f32)
    rows, seq = query_ref.shape[0], kv_ref.shape[0]
    reverse = lax.broadcasted_iota(jnp.int32, (rows, rows), 0) + lanes_of((rows, rows)) == rows - 1
    reverse = reverse.astype(bf16)
    for pair in range(HEADS // 2):
        place = slice(2 * HEAD * pair, 2 * HEAD * (pair + 1))
        place_v = slice(HD + 2 * HEAD * pair, HD + 2 * HEAD * (pair + 1))
        keys, values = kv_ref[:, place], kv_ref[:, place_v]
        parts = []
        for half in range(2):
            number = 2 * pair + half
            query = one_half(query_ref[:, place], half)
            scores = biased_scores(
                mm_t(query, keys), bias_rows[number : number + 1], first, length
            )
            part = attention_back(
                query,
                keys,
                values,
                scores,
                total_self_ref[:, number : number + 1],
                one_half(out_slope[:, place], half),
            )
            parts.append(part)
            turned = pltpu.roll(mm(reverse, part[0]), 0, 1, stride=1, stride_axis=0)
            where = lax.broadcasted_iota(jnp.int32, bias_sums.shape, 0) == number
            bias_sums = jnp.where(where, jnp.sum(turned, axis=0, keepdims=True), bias_sums)
        query_slope_ref[:, place] = joined(parts[0][1], parts[1][1]).astype(bf16)
        kv_slope_ref[:, place] = (parts[0][2] + parts[1][2]).astype(bf16)
        kv_slope_ref[:, place_v] = (parts[0][3] + parts[1][3]).astype(bf16)
    bias_sums = pltpu.roll(bias_sums, 2 * seq + 1 - rows - first, 1)
    high = bias_sums.astype(bf16)
    rest = bias_sums - high.astype(f32)
    middle = rest.astype(bf16)
    low = (rest - middle.astype(f32)).astype(bf16)
    table = table_ref[...]
    bias_grad_ref[...] = mm_t(high, table) + (mm_t(middle, table) + mm_t(low, table))
    copy_a.wait()
    copy_b.wait()
    copy_m.wait()


def leave_kernel(
    query_slope_ref,
    kv_slope_ref,
    normed_ref,
    resid0_ref,
    grad1_ref,
    gains_ref,
    norm_grads_ref,
    part_grad_ref,
    part_c_ref,
    grad_c_ref,
    grad0_ref,
):
    normed = normed_ref[...]
    query_slope, kv_slope = query_slope_ref[...], kv_slope_ref[...]
    slope = mm_t(query_slope, part_c_ref[:, :HD]) + mm_t(kv_slope, part_c_ref[:, HD : 3 * HD])
    back, norm_grad = rms_back(resid0_ref[...], gains_ref[0:1], slope)
    grad0_ref[...] = (grad1_ref[...] + back).astype(bf16)
    grad_c_ref[:, :HD] = t_mm(normed, query_slope).astype(bf16)
    grad_c_ref[:, HD : 3 * HD] = t_mm(normed, kv_slope).astype(bf16)
    grad_c_ref[:, 3 * HD : 5 * HD] = part_grad_ref[...]
    where = lax.broadcasted_iota(jnp.int32, norm_grads_ref.shape, 0) == 0
    norm_grads = jnp.where(where, norm_grad, norm_grads_ref[...]).astype(bf16)
    row = lax.broadcasted_iota(jnp.int32, (norm_grads.shape[0], GAIN_PAD), 0)
    spread = (row == lanes_of(row.shape)).astype(bf16)
    grad_c_ref[:, 5 * HD :] = t_mm(norm_grads, spread).astype(bf16)


def local_kernel(name, kernel, outs, args, spaces="", out_spaces="", scratch=()):
    space = {"v": pltpu.VMEM, "s": pltpu.SMEM, "a": pl.ANY}
    spaces = spaces or "v" * len(args)
    out_spaces = out_spaces or "v" * len(outs)
    return pl.pallas_call(
        kernel,
        name=name,
        out_shape=tuple(jax.ShapeDtypeStruct(shape, dtype) for shape, dtype in outs),
        in_specs=[pl.BlockSpec(memory_space=space[letter]) for letter in spaces],
        out_specs=tuple(pl.BlockSpec(memory_space=space[letter]) for letter in out_spaces),
        scratch_shapes=list(scratch),
        compiler_params=pltpu.CompilerParams(vmem_limit_bytes=60 * 1024 * 1024),
    )(*args)


def pack_columns(pieces, block):
    start = 0
    for piece in pieces:
        if piece.shape[0] == 1:
            break
        block[:, start : start + piece.shape[1]] = piece[...]
        start += piece.shape[1]
    gains = pieces[-4:]
    if gains[0].shape[0] == 1:
        rows = gains[0].shape[1]
        where = lax.broadcasted_iota(jnp.int32, (16, rows), 0)
        stacked = jnp.zeros((16, rows), f32)
        for number, gain in enumerate(gains):
            stacked = jnp.where(where == number, gain[...].astype(f32), stacked)
        pick = lax.broadcasted_iota(jnp.int32, (16, GAIN_PAD), 0) == lanes_of((16, GAIN_PAD))
        block[:, start:] = t_mm(stacked.astype(bf16), pick.astype(bf16)).astype(bf16)


def pack_ids(pieces, block):
    block[...] = jnp.zeros_like(block)
    for number, piece in enumerate(pieces):
        micro, _, count = piece.shape
        for which in range(micro):
            block[micro * number + which : micro * number + which + 1, :count] = piece[which]


def tail_kernel(lengths_ref, *refs):
    (a_ref, b_ref, c_ref, small_ref, memory_ref, embedding_ref, head_ref), outs = refs[:7], refs[7:]
    (loss_ref, memory_out, embedding_out, head_out, bias_out), outs = outs[:5], outs[5:]
    memory_out[...] = memory_ref[...]
    embedding_out[...] = embedding_ref[...]
    head_out[...] = head_ref[...]
    total = jnp.sum(small_ref[...], axis=0)
    count = 0
    for first in range(lengths_ref.shape[0]):
        for second in range(lengths_ref.shape[1]):
            count = count + lengths_ref[first, second]
    loss_ref[...] = total[0:1, 64:65] / count.astype(f32)
    bias_out[...] = total[:HEADS, :BUCKETS]
    for ref, pieces in ((a_ref, outs[:2]), (b_ref, outs[2:6]), (c_ref, outs[6:11])):
        start = 0
        for piece in pieces:
            piece[...] = ref[:, start : start + piece.shape[1]]
            start += piece.shape[1]
    turned = jnp.transpose(c_ref[:, 5 * HD :])
    for number, piece in enumerate(outs[11:]):
        piece[...] = turned[number : number + 1]


def vocabulary(name, collective_id, final_rows, head_rows, targets, alive, sizes):
    span, width = head_rows.shape
    tok_dev = final_rows.shape[0]
    lines = sizes["s"]
    blocks = 2 * lines
    step_rows = min(512, span)
    gather = Gather(final_rows, "sh", "sh", sizes)
    direct = DirectGather(jax.ShapeDtypeStruct((blocks, tok_dev), f32), sizes)
    scatter = Scatter(jax.ShapeDtypeStruct((lines, 2, tok_dev, width), bf16), "hs", "sh", sizes)
    jobs = (gather, direct, scatter)
    peers = peers_of(jobs)

    def kernel(*refs):
        final_ref, head_ref, targets_ref, alive_ref = refs[:4]
        slope_ref, head_part_ref, picked_ref, log_total_ref = refs[4:8]
        states, totals, own_total, logits, turned, value = refs[8:14]
        rest = refs[14:]
        place = coordinates()
        awaited = greet(peers, place)
        counts = [len(job.scratch) for job in jobs]
        gather.prepare((final_ref, states) + rest[: counts[0]], place)
        direct.prepare((own_total, totals) + rest[counts[0] : counts[0] + counts[1]], place)
        scatter.prepare((value, slope_ref) + rest[counts[0] + counts[1] :], place)
        welcome(peers, place, awaited)
        position = place["s"]
        half = position // 2

        def spot(token, other):
            far, second = token // 2, token % 2
            near_row = position + second * (1 - 2 * (position % 2))
            far_row = 2 - half + second * (1 - 2 * half)
            row = near_row + far * (far_row - near_row)
            side = place["h"] + other * (1 - 2 * place["h"])
            return row, side, 2 * row + side

        def chunk_of(number):
            return pl.ds(pl.multiple_of(number * step_rows, step_rows), step_rows)

        def hits(number, target):
            rows = lax.broadcasted_iota(jnp.int32, (step_rows, tok_dev), 0) + number * step_rows
            return rows == target

        def bring(step):
            token, other = step // 2, step % 2
            if step == 0:
                gather.line_first()
                gather.launch((1, (0,), 1))
                gather.local.wait()
                gather.local_done = True
            if other:
                gather.arrive((1, (token,), 1))
                if token + 1 < lines:
                    gather.line_next(token + 1)
                    gather.launch((1, (token + 1,), 1))

        def forward_step(step, carry):
            for number in range(blocks):
                pl.when(step == number)(functools.partial(bring, number))
            row, side, number = spot(step // 2, step % 2)
            block = states[row, side]
            target = targets_ref[pl.ds(number, 1), :]

            def scores(chunk, best):
                found = mm_t(head_ref[chunk_of(chunk), :], block)
                logits[number, chunk_of(chunk), :] = found
                return jnp.maximum(best, jnp.max(found, axis=0, keepdims=True))

            count = span // step_rows
            best = lax.fori_loop(0, count, scores, jnp.full((1, tok_dev), -3.0e38, f32))

            def spread(chunk, sums):
                found = logits[number, chunk_of(chunk), :]
                hit = hits(chunk, target)
                return (
                    sums[0] + jnp.sum(jnp.exp(found - best), axis=0, keepdims=True),
                    sums[1] + jnp.sum(jnp.where(hit, found, 0.0), axis=0, keepdims=True),
                )

            zero = jnp.zeros((1, tok_dev), f32)
            total, picked = lax.fori_loop(0, count, spread, (zero, zero))
            own_total[pl.ds(number, 1), :] = best + jnp.log(total)
            picked_ref[pl.ds(number, 1), :] = picked
            return carry

        lax.fori_loop(0, blocks, forward_step, 0)
        direct.begin()
        direct.receive()
        parts = totals[...].reshape((blocks,) + own_total.shape)
        top = jnp.max(parts, axis=0)
        log_total_ref[...] = top + jnp.log(jnp.sum(jnp.exp(parts - top[None]), axis=0))

        def backward_step(step, carry):
            row, side, number = spot(lines - 1 - step // 2, 1 - step % 2)
            lanes = pl.ds(pl.multiple_of(number * tok_dev, tok_dev), tok_dev)
            target = targets_ref[pl.ds(number, 1), :]
            live = alive_ref[pl.ds(number, 1), :]
            log_total = log_total_ref[pl.ds(number, 1), :]

            def slopes(chunk, inner):
                share = jnp.exp(logits[number, chunk_of(chunk), :] - log_total)
                slope = (share - jnp.where(hits(chunk, target), 1.0, 0.0)) * live
                turned[chunk_of(chunk), lanes] = slope.astype(bf16)
                return inner

            lax.fori_loop(0, span // step_rows, slopes, 0)
            value[row, side] = t_mm(turned[:, lanes], head_ref[...]).astype(bf16)
            for which in range(lines):
                pl.when(step == 2 * which)(
                    functools.partial(scatter.launch, 0, (lines - 1 - which,), 1)
                )
            return carry

        lax.fori_loop(0, blocks, backward_step, 0)
        for token in (3, 2):
            scatter.reduce(0, (token,))
            scatter.line_step(token, middles=False)

        def head_chunk(number, carry):
            rows = pl.ds(pl.multiple_of(number * 256, 256), 256)
            every = states[...].reshape(blocks * tok_dev, width)
            head_part_ref[rows, :] = mm(turned[rows, :], every).astype(bf16)
            return carry

        lax.fori_loop(0, span // 256, head_chunk, 0)
        scatter.line_step(3, ends=False)
        scatter.line_step(2, ends=False)
        for token in (1, 0):
            scatter.reduce(0, (token,))
            scatter.line_step(token)
        gather.finish()
        direct.drain()
        scatter.finish()

    vmem = pl.BlockSpec(memory_space=pltpu.VMEM)
    rows = jax.ShapeDtypeStruct((blocks, tok_dev), f32)
    return pl.pallas_call(
        kernel,
        name=name,
        out_shape=(scatter.out, jax.ShapeDtypeStruct(head_rows.shape, bf16), rows, rows),
        in_specs=[vmem] * 4,
        out_specs=(vmem,) * 4,
        scratch_shapes=[
            pltpu.VMEM(gather.out.shape, bf16),
            pltpu.VMEM(direct.out.shape, f32),
            pltpu.VMEM((blocks, tok_dev), f32),
            pltpu.VMEM((blocks, span, tok_dev), f32),
            pltpu.VMEM((span, blocks * tok_dev), bf16),
            pltpu.VMEM(scatter.value.shape, bf16),
        ]
        + [item for job in jobs for item in job.scratch],
        compiler_params=pltpu.CompilerParams(
            collective_id=collective_id, has_side_effects=True, vmem_limit_bytes=60 * 1024 * 1024
        ),
    )(final_rows, head_rows, targets, alive)


def per_device(
    target_ids,
    labels,
    lengths,
    memory,
    embedding,
    head,
    gain_self,
    w_query,
    w_key,
    w_value,
    w_out,
    relative_bias,
    gain_cross,
    c_query,
    c_key,
    c_value,
    c_out,
    gain_ff,
    w_gate,
    w_up,
    w_down,
    gain_final,
):
    micro = target_ids.shape[0]
    seq_dev = target_ids.shape[2]
    mem_dev = memory.shape[2]
    voc_dev, width = embedding.shape
    ff = w_gate.shape[1]
    n_gx = lax.axis_size("gx")
    n_gy = lax.axis_size("gy")
    column = lax.axis_index("gy")
    row_group = lax.axis_index("gx")
    devices = n_gx * n_gy
    sizes = {"a": n_gx // 2, "c": 2, "s": n_gy // 2, "h": 2}
    assert sizes["s"] == 2 * micro
    place = coordinates()
    seq = seq_dev * n_gy
    plane = sizes["s"] * seq
    tok_dev = seq // 4
    tokens = plane // 2
    span = n_gx * voc_dev
    merged = "" if sizes["a"] == 2 else "ashc"

    rows_dev = width // devices
    whole_tiles = rows_dev % 16 == 0
    groups = (
        (w_gate, w_up),
        (w_down, c_key, c_value, c_out),
        (w_query, w_key, w_value, w_out, c_query),
    )
    gains = (gain_self, gain_cross, gain_ff, gain_final)
    widths = [sum(piece.shape[1] for piece in group) for group in groups]
    widths[2] += GAIN_PAD
    orders = ("shac", "sahc", "sahc")
    if whole_tiles:
        operands = list(groups)
        operands[2] += tuple(gain.reshape(1, rows_dev) for gain in gains)
        weights = [
            PackedGather(
                group,
                jax.ShapeDtypeStruct((rows_dev, count), bf16),
                pack_columns,
                order,
                "acsh",
                sizes,
                merged,
            )
            for group, count, order in zip(operands, widths, orders)
        ]
    else:
        shards = [jnp.concatenate(group, axis=1) for group in groups]
        columns_of = jnp.pad(jnp.stack(gains, axis=1), ((0, 0), (0, GAIN_PAD - 4)))
        shards[2] = jnp.concatenate([shards[2], columns_of], axis=1)
        weights = [
            Gather(packed(part), order, "acsh", sizes, merged) for part, order in zip(shards, orders)
        ]
    part_a, part_b, part_c, embed_rows, ids, memory_all = exchange(
        "gather_weights",
        0,
        weights
        + [
            Gather(embedding, "ac", "ac", sizes, "", 20),
            PackedGather(
                (target_ids, labels),
                jax.ShapeDtypeStruct((8, 128), jnp.int32),
                pack_ids,
                "shc",
                "shc",
                sizes,
                "shc",
            ),
            MemoryGather(memory.reshape(micro, mem_dev, width), sizes),
        ],
    )
    part_a, part_b, part_c = (
        full.reshape(width, count) for full, count in zip((part_a, part_b, part_c), widths)
    )
    embed_rows = embed_rows.reshape(span, width)
    memory_all = memory_all.reshape(n_gy * mem_dev, width)
    ids = ids[..., : 2 * micro, :seq_dev].reshape(n_gy, 2, 2, micro, seq_dev)
    ids = ids.transpose(2, 3, 1, 0, 4).reshape(2, sizes["s"] * 2, 2, tok_dev)
    ids = lax.dynamic_index_in_dim(ids, place["c"], axis=2, keepdims=False).reshape(2, tokens)

    def local_of(index):
        shard = index // voc_dev
        return jnp.where(shard % n_gy == column, shard // n_gy * voc_dev + index % voc_dev, -1)

    local_ids = local_of(ids[0])
    targets = local_of(ids[1])
    columns = jnp.arange(span, dtype=jnp.int32)

    picked_rows = dot((local_ids[:, None] == columns[None, :]).astype(bf16), embed_rows).astype(bf16)
    tok_layout = (sizes["s"], 2, tok_dev, width)
    resid0, head_rows = exchange(
        "rows",
        1,
        [
            Scatter(picked_rows.reshape(tok_layout), "hs", "sh", sizes),
            Gather(head, "ac", "ac", sizes, "", 20),
        ],
    )
    head_rows = head_rows.reshape(span, width)

    plane_lengths = lax.dynamic_slice_in_dim(lengths, 2 * place["a"], 2, axis=1).reshape(-1)
    live_length = lax.dynamic_index_in_dim(plane_lengths, place["s"], keepdims=False)
    scalars = jnp.stack([(2 * place["h"] + place["c"]) * tok_dev, live_length])
    table = jnp.asarray(distance_table(seq), bf16)
    bias_pad = jnp.pad(relative_bias, ((0, 8 - HEADS), (0, 128 - BUCKETS)))
    query_self, own_kv, normed_self, gain_rows = local_kernel(
        "enter",
        enter_kernel,
        [((tok_dev, HD), bf16), ((tok_dev, 2 * HD), bf16), ((tok_dev, width), bf16), ((16, width), f32)],
        [resid0, part_c],
    )
    (self_kv_all,) = exchange("self_keys", 2, [Gather(own_kv, "hc", "hc", sizes)])
    self_kv_all = self_kv_all.reshape(seq, 2 * HD)
    rows_f32, rows_bf16, rows_heads = ((tok_dev, width), f32), ((tok_dev, width), bf16), ((tok_dev, HD), bf16)
    totals_shape = ((tok_dev, 128), f32)
    all_mem = n_gy * mem_dev
    (
        attn_self,
        total_self,
        resid1,
        normed_cross,
        query_cross,
        mem_kv,
        attn_cross,
        total_cross,
        resid2,
        normed_ff,
        gate_up,
        hidden,
        resid3,
        final_rows,
    ) = local_kernel(
        "forward",
        forward_kernel,
        [
            rows_heads,
            totals_shape,
            rows_f32,
            rows_bf16,
            rows_heads,
            ((all_mem, 2 * HD), bf16),
            rows_heads,
            totals_shape,
            rows_f32,
            rows_bf16,
            ((tok_dev, 2 * ff), f32),
            ((tok_dev, ff), bf16),
            rows_f32,
            rows_bf16,
        ],
        [scalars, query_self, self_kv_all, resid0, gain_rows, table, bias_pad]
        + [memory_all, part_a, part_b, part_c],
        "svvvvvvaaaa",
        scratch=[pltpu.VMEM(full.shape, bf16) for full in (memory_all, part_a, part_b, part_c)]
        + [pltpu.SemaphoreType.DMA((4,))],
    )

    index = jnp.arange(tokens, dtype=jnp.int32)
    position = (2 * (index // tok_dev % 2) + place["c"]) * tok_dev + index % tok_dev
    alive = (position < jnp.repeat(plane_lengths, 2 * tok_dev)).astype(f32)
    if span <= 2048 and tok_dev == 128:
        by_block = (n_gy, tok_dev)
        final_slope, head_part, picked, log_total = vocabulary(
            "vocabulary", 3, final_rows, head_rows, targets.reshape(by_block), alive.reshape(by_block), sizes
        )
        picked, log_total = picked.reshape(tokens), log_total.reshape(tokens)
    else:
        (states,) = exchange("final_rows", 3, [Gather(final_rows, "sh", "sh", sizes, merged)])
        states = states.reshape(tokens, width)
        logits = dot_t(states, head_rows)
        highest = jnp.max(logits, axis=1)
        own_total = highest + jnp.log(jnp.sum(jnp.exp(logits - highest[:, None]), axis=1))
        (totals,) = exchange("totals", 4, [DirectGather(own_total.reshape(tokens // 128, 128), sizes)])
        totals = totals.reshape(n_gy, tokens)
        top = jnp.max(totals, axis=0)
        log_total = top + jnp.log(jnp.sum(jnp.exp(totals - top[None]), axis=0))
        hit = columns[None, :] == targets[:, None]
        picked = jnp.sum(jnp.where(hit, logits, 0.0), axis=1)
        slope = jnp.exp(logits - log_total[:, None]) - hit.astype(f32)
        slope = (slope * alive[:, None]).astype(bf16)
        head_part = t_dot(slope, states).astype(bf16)
        final_part = dot(slope, head_rows).astype(bf16)
        (final_slope,) = exchange(
            "final_slopes", 5, [Scatter(final_part.reshape(tok_layout), "hs", "sh", sizes)]
        )
    loss_part = jnp.where(column == 0, jnp.sum(alive * log_total), 0.0) - jnp.sum(alive * picked)

    grad_a, grad_b, memory_part, part_grad_c, query_slope, kv_slope, grad1, norm_grads, bias_grad = (
        local_kernel(
            "backward",
            backward_kernel,
            [
                (part_a.shape, bf16),
                (part_b.shape, bf16),
                (memory_all.shape, bf16),
                ((width, 2 * HD), bf16),
                rows_heads,
                ((seq, 2 * HD), bf16),
                rows_f32,
                (gain_rows.shape, f32),
                ((8, 128), f32),
            ],
            [scalars, final_slope, resid3, hidden, gate_up, normed_ff, resid2, attn_cross]
            + [query_cross, total_cross, normed_cross, resid1, attn_self, query_self, self_kv_all]
            + [total_self, gain_rows, table, bias_pad, mem_kv, memory_all, part_a, part_b, part_c],
            "s" + "v" * 18 + "a" * 5,
            "aaa" + "v" * 6,
            [
                pltpu.VMEM(full.shape, bf16)
                for full in (mem_kv, memory_all, part_a, part_b, part_c, part_a, part_b, memory_all)
            ]
            + [
                pltpu.VMEM((tok_dev, 2 * ff), bf16),
                pltpu.VMEM((tok_dev, HD), bf16),
                pltpu.VMEM(mem_kv.shape, bf16),
                pltpu.SemaphoreType.DMA((5,)),
                pltpu.SemaphoreType.DMA((3,)),
            ],
        )
    )
    (kv_slope,) = exchange(
        "key_slopes",
        6,
        [Scatter(kv_slope.reshape(2, 2, tok_dev, 2 * HD), "ch", "hc", sizes, "", bf16)],
    )
    grad_c, grad0 = local_kernel(
        "leave",
        leave_kernel,
        [(part_c.shape, bf16), rows_bf16],
        [query_slope, kv_slope, normed_self, resid0, grad1, gain_rows, norm_grads, part_grad_c, part_c],
    )
    slopes, head_grad = exchange(
        "row_slopes",
        7,
        [
            Gather(grad0, "sh", "sh", sizes, merged),
            Scatter(head_part.reshape(sizes["a"], 2, voc_dev, width), "ca", "ac", sizes),
        ],
    )
    embed_part = t_dot(
        (local_ids[:, None] == columns[None, :]).astype(bf16), slopes.reshape(tokens, width)
    ).astype(bf16)
    sums = (grad_a, grad_b, grad_c)
    at_loss = (jnp.arange(8)[:, None] == 0) & (jnp.arange(128)[None, :] == 64)
    small = jnp.where(at_loss, loss_part, bias_grad)
    device_layout = (sizes["a"], 2, sizes["s"], 2)
    blocks = [part.reshape(device_layout + packed_shape(part, devices)) for part in sums]
    grad_a, grad_b, grad_c, embedding_grad, memory_grad, small = exchange(
        "scatter_weights",
        8,
        [
            Scatter(part, order[::-1], "acsh", sizes, merged)
            for part, order in zip(blocks, orders)
        ]
        + [
            Scatter(embed_part.reshape(sizes["a"], 2, voc_dev, width), "ca", "ac", sizes),
            MemoryScatter(memory_part.reshape(sizes["s"], 2, mem_dev, width), sizes),
            Gather(small, "shac", "acsh", sizes, "ashc"),
        ],
    )
    small = small.reshape(devices, 8, 128)
    memory_grad = memory_grad.reshape(micro, 1, mem_dev, width)
    if whole_tiles:
        pieces = [piece.shape[1] for group in groups for piece in group]
        outs = [
            ((1, 1), f32),
            (memory_grad.shape, f32),
            (embedding_grad.shape, f32),
            (head_grad.shape, f32),
            ((HEADS, BUCKETS), f32),
        ]
        outs += [((rows_dev, count), f32) for count in pieces] + [((1, rows_dev), f32)] * 4
        results = local_kernel(
            "tail",
            tail_kernel,
            outs,
            [lengths, grad_a, grad_b, grad_c, small, memory_grad, embedding_grad, head_grad],
            "s" + "v" * 7,
        )
        loss, memory_grad, embedding_grad, head_grad, bias_total = results[:5]
        loss = loss.reshape(())
        cut = results[5:16]
        gain_out = [gain.reshape(rows_dev) for gain in results[16:]]
    else:
        grad_a, grad_b, grad_c = (
            grad.reshape(rows_dev, count) for grad, count in zip((grad_a, grad_b, grad_c), widths)
        )
        small = jnp.sum(small, axis=0)
        loss = small[0, 64] / jnp.sum(lengths).astype(f32)
        bias_total = small[:HEADS, :BUCKETS]
        cut = []
        for grad, group in zip((grad_a, grad_b, grad_c), groups):
            start = 0
            for piece in group:
                cut.append(grad[:, start : start + piece.shape[1]])
                start += piece.shape[1]
        gain_out = [grad_c[:, 5 * HD + number] for number in range(4)]
    gate_grad, up_grad, down_grad, c_key_grad, c_value_grad, c_out_grad = cut[:6]
    query_grad, key_grad, value_grad, out_grad, c_query_grad = cut[6:]
    return (
        loss,
        memory_grad,
        embedding_grad,
        head_grad,
        gain_out[0],
        query_grad,
        key_grad,
        value_grad,
        out_grad,
        bias_total,
        gain_out[1],
        c_query_grad,
        c_key_grad,
        c_value_grad,
        c_out_grad,
        gain_out[2],
        gate_grad,
        up_grad,
        down_grad,
        gain_out[3],
    )


def packed_shape(part, count):
    rows, columns = part.shape[0] // count, part.shape[1]
    if rows % 16 == 0:
        return (rows, columns)
    return (16, rows * columns // 16)


def solution(mesh):
    placed = (
        P(None, "gx", "gy"),
        P(None, "gx", "gy"),
        P(),
        P(None, "gx", "gy", None),
        P(("gx", "gy"), None),
        P(("gx", "gy"), None),
        P(("gx", "gy")),
        P(("gx", "gy"), None),
        P(("gx", "gy"), None),
        P(("gx", "gy"), None),
        P(("gx", "gy"), None),
        P(),
        P(("gx", "gy")),
        P(("gx", "gy"), None),
        P(("gx", "gy"), None),
        P(("gx", "gy"), None),
        P(("gx", "gy"), None),
        P(("gx", "gy")),
        P(("gx", "gy"), None),
        P(("gx", "gy"), None),
        P(("gx", "gy"), None),
        P(("gx", "gy")),
    )
    return jax.shard_map(
        per_device,
        mesh=mesh,
        in_specs=placed,
        out_specs=(
            P(),
            P(None, "gx", "gy", None),
            P(("gx", "gy"), None),
            P(("gx", "gy"), None),
            P(("gx", "gy")),
            P(("gx", "gy"), None),
            P(("gx", "gy"), None),
            P(("gx", "gy"), None),
            P(("gx", "gy"), None),
            P(),
            P(("gx", "gy")),
            P(("gx", "gy"), None),
            P(("gx", "gy"), None),
            P(("gx", "gy"), None),
            P(("gx", "gy"), None),
            P(("gx", "gy")),
            P(("gx", "gy"), None),
            P(("gx", "gy"), None),
            P(("gx", "gy"), None),
            P(("gx", "gy")),
        ),
        check_vma=False,
    )
```

```python
import functools
import itertools
import math

import jax
import jax.numpy as jnp
import numpy as np
from jax import lax
from jax.experimental import pallas as pl
from jax.experimental.pallas import tpu as pltpu
from jax.sharding import PartitionSpec as P

HEADS = 6
HEAD = 64
HD = HEADS * HEAD
BUCKETS = 32
GAIN_PAD = 128

eps = 1e-06
masked_score = -1000000000.0
bf16 = jnp.bfloat16
f32 = jnp.float32


def flip(position, offset):
    moved = position
    weight = 1
    while weight <= offset:
        if offset & weight:
            moved = moved + weight * (1 - 2 * ((position // weight) % 2))
        weight *= 2
    return moved


def coordinates():
    gx, gy = lax.axis_index("gx"), lax.axis_index("gy")
    return {"a": gx // 2, "c": gx % 2, "s": gy // 2, "h": gy % 2}


def peer_of(dim, offset):
    gx, gy = lax.axis_index("gx"), lax.axis_index("gy")
    if dim == "a":
        return {"gx": 2 * flip(gx // 2, offset) + gx % 2}
    if dim == "c":
        return {"gx": flip(gx, 1)}
    if dim == "plane":
        s, h, c = offset + (0,) * (3 - len(offset))
        there = {"gy": 2 * flip(gy // 2, s) + flip(gy % 2, h)}
        if c:
            there["gx"] = flip(gx, 1)
        return there
    if dim == "s":
        return {"gy": 2 * flip(gy // 2, offset) + gy % 2}
    return {"gy": flip(gy, 1)}


def remote(source, target, send, recv, dim, offset):
    return pltpu.make_async_remote_copy(
        src_ref=source,
        dst_ref=target,
        send_sem=send,
        recv_sem=recv,
        device_id=peer_of(dim, offset),
        device_id_type=pl.DeviceIdType.MESH,
    )


def along_line(position, step):
    half = position // 2
    return (position, flip(position, 1), 2 - half, 3 - 3 * half)[step]


def is_middle(position):
    return (position + 1) // 2 == 1


def across_middle():
    gy = lax.axis_index("gy")
    return {"gy": 2 * (3 - gy // 2) + gy % 2}


def spot_of(dim, position, offset):
    return along_line(position, offset) if dim == "s" else flip(position, offset)


def remote_to(source, target, send, recv, device):
    return pltpu.make_async_remote_copy(
        src_ref=source,
        dst_ref=target,
        send_sem=send,
        recv_sem=recv,
        device_id=device,
        device_id_type=pl.DeviceIdType.MESH,
    )


def each_piece(rows, columns, body, width=16384):
    step = rows
    while step * columns > width and step % 32 == 0:
        step //= 2
    if step == rows:
        body(slice(None))
        return

    def piece(number, carry):
        body(pl.ds(pl.multiple_of(number * step, step), step))
        return carry

    lax.fori_loop(0, rows // step, piece, 0)


LINE_PEERS = [("s", 1), ("m", 1)]


class Gather:
    def __init__(self, block, order, layout, sizes, merged="", late=0):
        self.value = block
        self.late = late
        self.order, self.layout, self.sizes, self.merged = order, layout, sizes, merged
        self.out = jax.ShapeDtypeStruct(tuple(sizes[d] for d in layout) + block.shape, block.dtype)
        self.in_spec = pl.BlockSpec(memory_space=pltpu.VMEM)
        self.out_spec = pl.BlockSpec(memory_space=pl.ANY)
        self.transfers = []
        for level, dim in enumerate(order):
            ranges = [(None,) if d in merged else range(sizes[d]) for d in order[:level]]
            for unit in itertools.product(*ranges):
                for offset in range(1, sizes[dim]):
                    self.transfers.append((level, unit, offset))
        self.index = {transfer: number for number, transfer in enumerate(self.transfers)}
        count = len(self.transfers)
        self.line = order[0] == "s"
        self.scratch = [
            pltpu.SemaphoreType.DMA((count,)),
            pltpu.SemaphoreType.DMA((count,)),
            pltpu.SemaphoreType.DMA,
            pltpu.SemaphoreType.DMA((5,)),
        ]
        self.peers = [(d, offset) for d in order for offset in range(1, sizes[d]) if d != "s"]
        if self.line:
            self.peers += LINE_PEERS

    def prepare(self, refs, place):
        self.source, self.target, self.send, self.recv, self.local_sem, self.line_send = refs
        self.place = place
        self.local = pltpu.make_async_copy(
            self.source, self.target.at[tuple(place[d] for d in self.layout)], self.local_sem
        )
        self.local.start()
        self.local_done = False
        self.arrived = set()
        self.sent = []

    def region(self, level, unit, offset):
        where = dict(self.place)
        for d, moved in zip(self.order[:level], unit):
            where[d] = slice(None) if moved is None else spot_of(d, self.place[d], moved)
        if offset:
            dim = self.order[level]
            where[dim] = spot_of(dim, self.place[dim], offset)
        return self.target.at[tuple(where[d] for d in self.layout)]

    def needs(self, level, unit):
        if level == 0:
            return []
        last, before = unit[-1], unit[:-1]
        if last is None:
            dim = self.order[level - 1]
            return self.needs(level - 1, before) + [
                (level - 1, before, offset) for offset in range(1, self.sizes[dim])
            ]
        if last == 0:
            return self.needs(level - 1, before)
        return [(level - 1, before, last)]

    def arrive(self, transfer):
        if transfer in self.arrived:
            return
        self.arrived.add(transfer)
        level, unit, offset = transfer
        number = self.index[transfer]
        there = self.region(level, unit, offset)
        if self.line and level == 0:
            offset = 1
        remote(
            there, there, self.send.at[number], self.recv.at[number], self.order[level], offset
        ).wait_recv()

    def line_copy(self, number):
        held, there = ((0, 1), (0, 2), (1, 3), (2, 2), (3, 3))[number]
        target = self.region(0, (), held)
        device = peer_of("s", 1) if number in (0, 3, 4) else across_middle()
        recv = self.recv.at[self.index[(0, (), there)]]
        source = target if held else self.source
        return remote_to(source, target, self.line_send.at[number], recv, device)

    def line_first(self):
        self.line_copy(0).start()

        @pl.when(is_middle(self.place["s"]))
        def _():
            self.line_copy(1).start()

    def line_next(self, step):
        self.arrive((0, (), step))

        @pl.when(is_middle(self.place["s"]))
        def _():
            self.line_copy(step + 1).start()

    def copy(self, transfer):
        level, unit, offset = transfer
        number = self.index[transfer]
        target = self.region(level, unit, 0)
        own = all(moved == 0 for moved in unit)
        return remote(
            self.source if own else target,
            target,
            self.send.at[number],
            self.recv.at[number],
            self.order[level],
            offset,
        )

    def launch(self, transfer):
        level, unit, offset = transfer
        for need in self.needs(level, unit):
            self.arrive(need)
        if None in unit and not self.local_done:
            self.local.wait()
            self.local_done = True
        self.copy(transfer).start()
        self.sent.append(transfer)

    def events(self):
        found = []
        if self.line:
            found.append((0, self.line_first))
            for step in (1, 2, 3):
                found.append((step, functools.partial(self.line_next, step)))
        for transfer in self.transfers:
            level, unit, offset = transfer
            if self.line and level == 0:
                continue
            key = 0.1 * level + 0.01 * offset
            for d, moved in zip(self.order, unit):
                key += self.sizes[d] - 1 if moved is None else moved
            if self.late and self.needs(level, unit):
                key += self.late
            found.append((key, functools.partial(self.launch, transfer)))
        return found

    def finish(self):
        if not self.local_done:
            self.local.wait()
        for transfer in self.transfers:
            self.arrive(transfer)
        for transfer in self.sent:
            self.copy(transfer).wait_send()
        if self.line:
            self.line_copy(0).wait_send()

            @pl.when(is_middle(self.place["s"]))
            def _():
                for number in range(1, 5):
                    self.line_copy(number).wait_send()


class PackedGather(Gather):
    def __init__(self, values, block, pack, *args):
        super().__init__(block, *args)
        self.values, self.pack = values, pack
        self.scratch = [pltpu.VMEM(block.shape, block.dtype)] + self.scratch


class DirectGather:
    def __init__(self, block, sizes, dims="sh"):
        self.value = block
        self.dims = dims
        shape = tuple(sizes[d] for d in dims)
        self.out = jax.ShapeDtypeStruct(shape + block.shape, block.dtype)
        self.in_spec = pl.BlockSpec(memory_space=pltpu.VMEM)
        self.out_spec = pl.BlockSpec(memory_space=pltpu.VMEM)
        self.offsets = list(itertools.product(*(range(size) for size in shape)))[1:]
        count = len(self.offsets)
        self.scratch = [pltpu.SemaphoreType.DMA((count,)), pltpu.SemaphoreType.DMA((count,))]
        self.peers = [("plane", offset) for offset in self.offsets]

    def prepare(self, refs, place):
        self.source, self.target, self.send, self.recv = refs
        self.place = place

    def copy(self, number, arriving):
        offset = self.offsets[number]
        spot = tuple(
            flip(self.place[d], moved) if arriving else self.place[d] for d, moved in zip(self.dims, offset)
        )
        return remote_to(
            self.source,
            self.target.at[spot],
            self.send.at[number],
            self.recv.at[number],
            peer_of("plane", offset),
        )

    def events(self):
        return [(0, self.begin)]

    def begin(self):
        for number in range(len(self.offsets)):
            self.copy(number, False).start()
        self.target[tuple(self.place[d] for d in self.dims)] = self.source[...]

    def finish(self):
        self.receive()
        self.drain()

    def receive(self):
        for number in range(len(self.offsets)):
            self.copy(number, True).wait_recv()

    def drain(self):
        for number in range(len(self.offsets)):
            self.copy(number, False).wait_send()


class Scatter:
    def __init__(self, value, order, layout, sizes, merged="", out_dtype=f32):
        self.value = value
        self.order, self.layout, self.sizes, self.merged = order, layout, sizes, merged
        self.block = value.shape[len(layout) :]
        self.out = jax.ShapeDtypeStruct(self.block, out_dtype)
        self.in_spec = pl.BlockSpec(memory_space=pltpu.VMEM)
        self.out_spec = pl.BlockSpec(memory_space=pltpu.VMEM)
        self.line = order[-1] == "s"
        self.levels = len(order)
        self.units = []
        self.scratch = []
        self.layouts = [layout]
        for level, dim in enumerate(order):
            later = order[level + 1 :]
            ranges = [(None,) if d in merged else range(sizes[d]) for d in later]
            units = sorted(
                itertools.product(*ranges),
                key=lambda unit: (-(unit[-1] or 0) if unit else 0, -sum(moved or 0 for moved in unit)),
            )
            self.units.append(units)
            left = "".join(d for d in self.layouts[-1] if d != dim)
            self.layouts.append(left)
            self.scratch.append(
                pltpu.VMEM(
                    (5 if dim == "s" else sizes[dim] - 1,)
                    + tuple(sizes[d] for d in left)
                    + self.block,
                    value.dtype,
                )
            )
        self.index = {}
        for level, dim in enumerate(order):
            for unit in self.units[level]:
                for offset in range(1, sizes[dim]):
                    self.index[(level, unit, offset)] = len(self.index)
        count = len(self.index)
        self.scratch += [
            pltpu.SemaphoreType.DMA((count,)),
            pltpu.SemaphoreType.DMA((count,)),
            pltpu.SemaphoreType.DMA((2, 5)),
        ]
        self.peers = [(d, offset) for d in order for offset in range(1, sizes[d]) if d != "s"]
        if self.line:
            self.peers += LINE_PEERS

    def prepare(self, refs, place):
        self.source, self.target = refs[0], refs[1]
        self.landing = refs[2 : 2 + self.levels]
        self.send, self.recv, self.line_sems = refs[2 + self.levels :]
        self.place = place
        self.sent = []

    def held(self, level):
        return self.source if level == 0 else self.landing[level - 1].at[0]

    def later(self, level, unit):
        where = {}
        for d, moved in zip(self.order[level + 1 :], unit):
            where[d] = slice(None) if moved is None else spot_of(d, self.place[d], moved)
        return where

    def copy(self, level, unit, offset):
        number = self.index[(level, unit, offset)]
        dim = self.order[level]
        where = self.later(level, unit)
        landed = self.landing[level].at[
            (offset - 1,) + tuple(where[d] for d in self.layouts[level + 1])
        ]
        where[dim] = flip(self.place[dim], offset)
        source = self.held(level).at[tuple(where[d] for d in self.layouts[level])]
        return remote(source, landed, self.send.at[number], self.recv.at[number], dim, offset)

    def launch(self, level, unit, offset):
        self.copy(level, unit, offset).start()
        self.sent.append((level, unit, offset))

    def reduce(self, level, unit):
        dim = self.order[level]
        size = self.sizes[dim]
        for offset in range(1, size):
            self.copy(level, unit, offset).wait_recv()
        where = self.later(level, unit)
        free = [d for d in self.order[level + 1 :] if isinstance(where[d], slice)]
        total = math.prod(self.sizes[d] for d in free)
        rows, columns = self.block
        last = level == self.levels - 1

        def one(number, carry):
            at = dict(where)
            rest = number
            for d in free:
                at[d] = rest % self.sizes[d]
                rest = rest // self.sizes[d]
            spot = tuple(at[d] for d in self.layouts[level + 1])
            at[dim] = self.place[dim]
            mine = tuple(at[d] for d in self.layouts[level])

            def body(piece):
                if not last and size == 2:
                    self.landing[level][(0,) + spot + (piece,)] += self.held(level)[mine + (piece,)]
                    return
                result = self.held(level)[mine + (piece,)].astype(f32)
                for offset in range(1, size):
                    result = result + self.landing[level][(offset - 1,) + spot + (piece,)].astype(f32)
                if last:
                    self.target[(piece,)] = result.astype(self.target.dtype)
                else:
                    self.landing[level][(0,) + spot + (piece,)] = result.astype(self.landing[level].dtype)

            each_piece(rows, columns, body)
            return carry

        if total == 1:
            one(0, 0)
        else:
            lax.fori_loop(0, total, one, 0)
        if not last and not (self.line and level == self.levels - 2):
            ahead, rest = unit[0], unit[1:]
            if ahead is None:
                offsets = range(1, self.sizes[self.order[level + 1]])
            else:
                offsets = [ahead] if ahead else []
            for offset in offsets:
                self.launch(level + 1, rest, offset)

    def line_copy(self, number):
        step, slot = ((1, 0), (2, 1), (3, 2), (3, 3), (2, 4))[number]
        level = self.levels - 1
        block = self.held(level).at[along_line(self.place["s"], step)]
        landed = self.landing[level].at[slot]
        device = peer_of("s", 1) if number < 3 else across_middle()
        return remote_to(block, landed, self.line_sems.at[0, number], self.line_sems.at[1, number], device)

    def line_step(self, step, ends=True, middles=True):
        level = self.levels - 1
        middle = is_middle(self.place["s"])
        rows, columns = self.block
        held, landing = self.held(level), self.landing[level]
        position = along_line(self.place["s"], step)

        def pass_on():
            arrived = (0, 3, 1, 2)[step]
            self.line_copy(arrived).wait_recv()

            def body(piece):
                held[(position, piece)] += landing[(arrived, piece)]

            each_piece(rows, columns, body)
            self.line_copy((0, 0, 4, 3)[step]).start()

        if step:
            if ends:
                pl.when(jnp.logical_not(middle))(lambda: self.line_copy(step - 1).start())
            if middles:
                pl.when(middle)(pass_on)
            return

        self.line_copy(0).wait_recv()

        @pl.when(middle)
        def _():
            self.line_copy(4).wait_recv()

            def body(piece):
                result = held[(position, piece)].astype(f32) + landing[(0, piece)].astype(f32)
                self.target[(piece,)] = (result + landing[(4, piece)].astype(f32)).astype(
                    self.target.dtype
                )

            each_piece(rows, columns, body)

        @pl.when(jnp.logical_not(middle))
        def _():
            def body(piece):
                result = held[(position, piece)].astype(f32) + landing[(0, piece)].astype(f32)
                self.target[(piece,)] = result.astype(self.target.dtype)

            each_piece(rows, columns, body)

    def events(self):
        found = []
        for number, unit in enumerate(self.units[0]):
            for offset in range(1, self.sizes[self.order[0]]):
                found.append(
                    (-1 + 0.001 * number, functools.partial(self.launch, 0, unit, offset))
                )
        spread = 4 if self.line else 1
        for level in range(self.levels - self.line):
            count = len(self.units[level])
            for number, unit in enumerate(self.units[level]):
                late = 0
                if self.order[-1] == "a":
                    late = 20 if level == self.levels - 1 else 0.9
                found.append(
                    (late + level + spread * number / count, functools.partial(self.reduce, level, unit))
                )
        if self.line:
            for number, step in enumerate((3, 2, 1, 0)):
                found.append(
                    (self.levels - 1 + number + 0.5, functools.partial(self.line_step, step))
                )
        return found

    def finish(self):
        for transfer in self.sent:
            self.copy(*transfer).wait_send()
        if self.line:
            self.line_copy(0).wait_send()
            middle = is_middle(self.place["s"])

            @pl.when(middle)
            def _():
                for number in (3, 4):
                    self.line_copy(number).wait_send()

            @pl.when(jnp.logical_not(middle))
            def _():
                for number in (1, 2):
                    self.line_copy(number).wait_send()


class MemoryGather:
    def __init__(self, memory, sizes):
        self.value = memory
        self.sizes = sizes
        self.out = jax.ShapeDtypeStruct((sizes["s"], 2) + memory.shape[1:], memory.dtype)
        self.in_spec = pl.BlockSpec(memory_space=pltpu.VMEM)
        self.out_spec = pl.BlockSpec(memory_space=pl.ANY)
        rows = sizes["s"]
        self.scratch = [
            pltpu.SemaphoreType.DMA((2, rows)),
            pltpu.SemaphoreType.DMA((2, rows)),
            pltpu.SemaphoreType.DMA((2, rows, 2)),
            pltpu.SemaphoreType.DMA,
        ]
        self.peers = [("s", offset) for offset in range(1, rows)] + [("h", 1), ("c", 1)]

    def prepare(self, refs, place):
        self.source, self.target, self.along, self.across, self.core, self.local = refs
        self.place = place
        self.mine = place["s"] % 2 == place["c"]

    def row(self, offset):
        return flip(self.place["s"], offset)

    def along_copy(self, offset, arriving):
        to = self.row(offset)
        spot = to if arriving else self.place["s"]
        return remote(
            self.source.at[self.place["s"] // 2 if arriving else to // 2],
            self.target.at[spot, self.place["h"]],
            self.along.at[0, offset],
            self.along.at[1, offset],
            "s",
            offset,
        )

    def across_copy(self, offset, arriving):
        h = self.place["h"]
        own = self.target.at[self.row(offset), 1 - h if arriving else h]
        if offset == 0 and not arriving:
            source = self.source.at[self.place["s"] // 2]
        else:
            source = own
        return remote(source, own, self.across.at[0, offset], self.across.at[1, offset], "h", 1)

    def core_copy(self, offset, other):
        h = self.place["h"]
        own = self.target.at[self.row(offset), 1 - h if other else h]
        source = self.source.at[self.place["s"] // 2] if offset == 0 and not other else own
        return remote(source, own, self.core.at[0, offset, other], self.core.at[1, offset, other], "c", 1)

    def events(self):
        rows = self.sizes["s"]

        def first():
            for offset in range(1, rows):
                @pl.when(self.row(offset) % 2 == self.place["c"])
                def _():
                    self.along_copy(offset, False).start()

            @pl.when(self.mine)
            def _():
                pltpu.make_async_copy(
                    self.source.at[self.place["s"] // 2],
                    self.target.at[self.place["s"], self.place["h"]],
                    self.local,
                ).start()
                self.across_copy(0, False).start()
                self.core_copy(0, 0).start()

        def arrival(offset):
            @pl.when(self.mine)
            def _():
                self.along_copy(offset, True).wait_recv()
                self.across_copy(offset, False).start()
                self.core_copy(offset, 0).start()

        def other(offset):
            @pl.when(self.mine)
            def _():
                self.across_copy(offset, True).wait_recv()
                self.core_copy(offset, 1).start()

        found = [(0.05, first)]
        for offset in range(1, rows):
            found.append((offset + 0.05, functools.partial(arrival, offset)))
        for offset in range(rows):
            found.append((rows + offset, functools.partial(other, offset)))
        return found

    def finish(self):
        rows = self.sizes["s"]
        for offset in range(1, rows):
            @pl.when(self.row(offset) % 2 == self.place["c"])
            def _():
                self.along_copy(offset, False).wait_send()

        @pl.when(self.mine)
        def _():
            pltpu.make_async_copy(
                self.source.at[self.place["s"] // 2],
                self.target.at[self.place["s"], self.place["h"]],
                self.local,
            ).wait()
            for offset in range(rows):
                self.across_copy(offset, False).wait_send()
                for other in range(2):
                    self.core_copy(offset, other).wait_send()

        @pl.when(jnp.logical_not(self.mine))
        def _():
            for offset in range(rows):
                for other in range(2):
                    self.core_copy(offset, other).wait_recv()


class MemoryScatter:
    def __init__(self, value, sizes):
        self.value = value
        self.sizes = sizes
        rows = sizes["s"]
        self.block = value.shape[2:]
        self.out = jax.ShapeDtypeStruct((2,) + self.block, f32)
        self.in_spec = pl.BlockSpec(memory_space=pltpu.VMEM)
        self.out_spec = pl.BlockSpec(memory_space=pltpu.VMEM)
        self.scratch = [
            pltpu.VMEM(value.shape, value.dtype),
            pltpu.VMEM((rows,) + self.block, value.dtype),
            pltpu.VMEM((2,) + self.block, value.dtype),
            pltpu.SemaphoreType.DMA((2, rows, 2)),
            pltpu.SemaphoreType.DMA((2, rows)),
            pltpu.SemaphoreType.DMA((2, rows)),
        ]
        self.peers = [("s", offset) for offset in range(1, rows)] + [("h", 1), ("c", 1)]

    def prepare(self, refs, place):
        self.source, self.target = refs[0], refs[1]
        self.summed, self.halved, self.landed, self.core, self.across, self.along = refs[2:]
        self.place = place
        self.mine = place["s"] % 2 == place["c"]

    def row(self, offset):
        return flip(self.place["s"], offset)

    def core_copy(self, offset, other):
        h = self.place["h"]
        spot = (self.row(offset), flip(h, 1) if other else h)
        return remote(
            self.source.at[spot],
            self.summed.at[spot],
            self.core.at[0, offset, other],
            self.core.at[1, offset, other],
            "c",
            1,
        )

    def across_copy(self, offset):
        row = self.row(offset)
        return remote(
            self.summed.at[row, flip(self.place["h"], 1)],
            self.halved.at[row],
            self.across.at[0, offset],
            self.across.at[1, offset],
            "h",
            1,
        )

    def along_copy(self, offset, arriving):
        to = self.row(offset)
        return remote(
            self.halved.at[to],
            self.landed.at[to // 2 if arriving else self.place["s"] // 2],
            self.along.at[0, offset],
            self.along.at[1, offset],
            "s",
            offset,
        )

    def events(self):
        rows = self.sizes["s"]
        high, wide = self.block
        orders = list(range(1, rows))[::-1] + [0]

        def first():
            @pl.when(jnp.logical_not(self.mine))
            def _():
                for other in (1, 0):
                    for offset in orders:
                        self.core_copy(offset, other).start()

        def level(offset, other):
            @pl.when(self.mine)
            def _():
                self.core_copy(offset, other).wait_recv()
                h = self.place["h"]
                spot = (self.row(offset), flip(h, 1) if other else h)

                def body(piece):
                    total = self.summed[spot + (piece,)].astype(f32) + self.source[
                        spot + (piece,)
                    ].astype(f32)
                    self.summed[spot + (piece,)] = total.astype(self.summed.dtype)

                each_piece(high, wide, body)
                if other:
                    self.across_copy(offset).start()

        def last(offset):
            @pl.when(self.mine)
            def _():
                self.across_copy(offset).wait_recv()
                row = self.row(offset)

                def body(piece):
                    total = self.halved[(row, piece)].astype(f32) + self.summed[
                        (row, self.place["h"], piece)
                    ].astype(f32)
                    self.halved[(row, piece)] = total.astype(self.halved.dtype)
                    if offset == 0:
                        self.target[(self.place["s"] // 2, piece)] = total

                each_piece(high, wide, body)
                if offset:
                    self.along_copy(offset, False).start()

        found = [(-0.95, first)]
        for number, offset in enumerate(orders):
            found.append((0.05 + 0.1 * number, functools.partial(level, offset, 1)))
        for number, offset in enumerate(orders):
            found.append((0.55 + 0.1 * number, functools.partial(level, offset, 0)))
        for number, offset in enumerate(orders):
            found.append((1.05 + 0.2 * number, functools.partial(last, offset)))
        return found

    def finish(self):
        rows = self.sizes["s"]
        high, wide = self.block
        for offset in range(1, rows):
            @pl.when(self.row(offset) % 2 == self.place["c"])
            def _():
                self.along_copy(offset, True).wait_recv()
                number = self.row(offset) // 2

                def body(piece):
                    self.target[(number, piece)] = self.landed[(number, piece)].astype(f32)

                each_piece(high, wide, body)

        @pl.when(self.mine)
        def _():
            for offset in range(rows):
                self.across_copy(offset).wait_send()
            for offset in range(1, rows):
                self.along_copy(offset, False).wait_send()

        @pl.when(jnp.logical_not(self.mine))
        def _():
            for offset in range(rows):
                for other in range(2):
                    self.core_copy(offset, other).wait_send()


def peers_of(jobs):
    peers = []
    for job in jobs:
        for peer in job.peers:
            if peer not in peers:
                peers.append(peer)
    return peers


def greet(peers, place):
    barrier = pltpu.get_barrier_semaphore()
    middle = is_middle(place["s"])
    awaited = 0
    for peer in peers:
        if peer[0] == "m":
            @pl.when(middle)
            def _():
                pl.semaphore_signal(
                    barrier, inc=1, device_id=across_middle(), device_id_type=pl.DeviceIdType.MESH
                )
            continue
        awaited += 1
        pl.semaphore_signal(
            barrier, inc=1, device_id=peer_of(*peer), device_id_type=pl.DeviceIdType.MESH
        )
    return awaited


def welcome(peers, place, awaited):
    barrier = pltpu.get_barrier_semaphore()
    middle = is_middle(place["s"])
    if ("m", 1) in peers:
        @pl.when(middle)
        def _():
            pl.semaphore_wait(barrier, awaited + 1)

        @pl.when(jnp.logical_not(middle))
        def _():
            pl.semaphore_wait(barrier, awaited)
    else:
        pl.semaphore_wait(barrier, awaited)


def exchange(name, collective_id, jobs):
    values = [getattr(job, "values", None) or [job.value] for job in jobs]
    peers = peers_of(jobs)

    def kernel(*refs):
        total = sum(len(held) for held in values)
        results = refs[total : total + len(jobs)]
        scratch = refs[total + len(jobs) :]
        begin = offset = 0
        place = coordinates()
        awaited = greet(peers, place)
        for number, job in enumerate(jobs):
            end = begin + len(values[number])
            ins = refs[begin:end]
            if hasattr(job, "pack"):
                job.pack(ins, scratch[offset])
                ins, offset = (scratch[offset],), offset + 1
            mine = len(job.scratch) - hasattr(job, "pack")
            job.prepare(tuple(ins) + (results[number],) + tuple(scratch[offset : offset + mine]), place)
            begin, offset = end, offset + mine
        welcome(peers, place, awaited)
        events = [event for job in jobs for event in job.events()]
        for _, act in sorted(events, key=lambda event: event[0]):
            act()
        for job in jobs:
            job.finish()

    return pl.pallas_call(
        kernel,
        name=name,
        out_shape=tuple(job.out for job in jobs),
        in_specs=[job.in_spec for job, held in zip(jobs, values) for _ in held],
        out_specs=tuple(job.out_spec for job in jobs),
        scratch_shapes=[item for job in jobs for item in job.scratch],
        compiler_params=pltpu.CompilerParams(
            collective_id=collective_id, has_side_effects=True, vmem_limit_bytes=60 * 1024 * 1024
        ),
    )(*[value for held in values for value in held])


def packed(block):
    rows, columns = block.shape
    if rows % 16 == 0:
        return block
    return block.reshape(16, rows * columns // 16)


def bucket_edges():
    edges = []
    for target in range(1, 32):
        if target < 16:
            edges.append(target)
        else:
            found = 0
            for distance in range(16, 4096):
                value = 16 + int(math.log(distance / 16.0) / math.log(8.0) * 16.0)
                if found == 0 and value >= target:
                    found = distance
            edges.append(found)
    return edges


def gelu_tanh(value):
    return (
        0.5
        * value
        * (1.0 + jnp.tanh(0.7978845608028654 * (value + 0.044715 * value * value * value)))
    )


def dot(left, right):
    return jnp.einsum("sd,df->sf", left, right, preferred_element_type=f32)


def dot_t(left, right):
    return jnp.einsum("sf,df->sd", left, right, preferred_element_type=f32)


def t_dot(left, right):
    return jnp.einsum("sd,sf->df", left, right, preferred_element_type=f32)


def distance_table(seq):
    edges = np.array(bucket_edges())
    distance = (-np.arange(seq)) % seq
    bucket = (distance[:, None] >= edges[None, :]).sum(axis=1)
    return (np.arange(128)[:, None] == bucket[None, :]).astype(np.float32)


def mm(left, right):
    return lax.dot_general(left, right, (((1,), (0,)), ((), ())), preferred_element_type=f32)


def mm_t(left, right):
    return lax.dot_general(left, right, (((1,), (1,)), ((), ())), preferred_element_type=f32)


def t_mm(left, right):
    return lax.dot_general(left, right, (((0,), (0,)), ((), ())), preferred_element_type=f32)


def inverse_rms(rows):
    return lax.rsqrt(jnp.mean(rows * rows, axis=-1, keepdims=True) + eps)


def rms_back(rows, gain, slope):
    inverse = inverse_rms(rows)
    unit = rows * inverse
    scaled = slope * gain
    back = inverse * (scaled - unit * jnp.mean(unit * scaled, axis=-1, keepdims=True))
    return back, jnp.sum(slope * unit, axis=0, keepdims=True)


def lanes_of(shape):
    return lax.broadcasted_iota(jnp.int32, shape, len(shape) - 1)


def one_half(pair, half):
    inside = (lanes_of(pair.shape) // HEAD) == half
    return jnp.where(inside, pair, jnp.zeros_like(pair))


def both_halves(pair):
    return jnp.concatenate([one_half(pair, 0), one_half(pair, 1)], axis=0)


def joined_rows(stacked):
    rows = stacked.shape[0] // 2
    return joined(stacked[:rows], stacked[rows:])


def joined(first, second):
    return jnp.where(lanes_of(first.shape) < HEAD, first, second)


def pair_of(ref, start, pair):
    return ref[:, start + 2 * HEAD * pair : start + 2 * HEAD * (pair + 1)]


FF_STEP = 256


def in_steps(total, step, body, further=0):
    def one(number, carry):
        here = pl.ds(pl.multiple_of(number * step, step), step)
        if further:
            body(here, pl.ds(pl.multiple_of(number * step + further, step), step))
        else:
            body(here)
        return carry

    lax.fori_loop(0, total // step, one, 0)


class Fetch:
    def __init__(self, sources, targets, sems):
        self.copies = [
            pltpu.make_async_copy(source, target, sems.at[number])
            for number, (source, target) in enumerate(zip(sources, targets))
        ]
        self.targets = targets
        self.ready = set()
        for copy in self.copies:
            copy.start()

    def __getitem__(self, number):
        if number not in self.ready:
            self.ready.add(number)
            self.copies[number].wait()
        return self.targets[number]


def enter_kernel(resid_ref, part_c_ref, query_ref, kv_ref, normed_ref, gains_ref):
    row = lax.broadcasted_iota(jnp.int32, (16, GAIN_PAD), 0)
    pick = (row == lanes_of((16, GAIN_PAD))).astype(bf16)
    gains = mm_t(pick, part_c_ref[:, 5 * HD : 5 * HD + GAIN_PAD])
    gains_ref[...] = gains
    resid = resid_ref[...]
    normed = (resid * inverse_rms(resid) * gains[0:1]).astype(bf16)
    normed_ref[...] = normed
    query_ref[...] = mm(normed, part_c_ref[:, :HD]).astype(bf16)
    kv_ref[...] = mm(normed, part_c_ref[:, HD : 3 * HD]).astype(bf16)


def biased_scores(scores, row, first, length):
    bias = pltpu.roll(jnp.broadcast_to(row, scores.shape), 0, 1, stride=1, stride_axis=0)
    query_pos = first + lax.broadcasted_iota(jnp.int32, scores.shape, 0)
    key_pos = lanes_of(scores.shape)
    mask = (key_pos <= query_pos) & (key_pos < length)
    return jnp.where(mask, scores + bias, masked_score)


def softmax_parts(scores):
    highest = jnp.max(scores, axis=-1, keepdims=True)
    total = highest + jnp.log(jnp.sum(jnp.exp(scores - highest), axis=-1, keepdims=True))
    return total, jnp.exp(scores - total)


def forward_kernel(
    scalars_ref,
    query_ref,
    kv_ref,
    resid0_ref,
    gains_ref,
    table_ref,
    bias_ref,
    memory_hbm,
    part_a_hbm,
    part_b_hbm,
    part_c_hbm,
    attn_self_ref,
    total_self_ref,
    resid1_ref,
    normed_cross_ref,
    query_cross_ref,
    mem_kv_ref,
    attn_cross_ref,
    total_cross_ref,
    resid2_ref,
    normed_ff_ref,
    gate_up_ref,
    hidden_ref,
    resid3_ref,
    final_ref,
    memory_ref,
    part_a_ref,
    part_b_ref,
    part_c_ref,
    sems,
):
    fetched = Fetch(
        (part_c_hbm, part_b_hbm, memory_hbm, part_a_hbm),
        (part_c_ref, part_b_ref, memory_ref, part_a_ref),
        sems,
    )
    first, length = scalars_ref[0], scalars_ref[1]
    ff = hidden_ref.shape[1]
    bias_rows = pltpu.roll(mm(bias_ref[...], table_ref[...]), first, 1)
    lanes = lanes_of(total_self_ref.shape)
    totals = jnp.zeros(total_self_ref.shape, f32)
    for pair in range(HEADS // 2):
        keys, values = pair_of(kv_ref, 0, pair), pair_of(kv_ref, HD, pair)
        outputs = []
        for half in range(2):
            number = 2 * pair + half
            scores = mm_t(one_half(pair_of(query_ref, 0, pair), half), keys)
            scores = biased_scores(scores, bias_rows[number : number + 1], first, length)
            total, shares = softmax_parts(scores)
            totals = jnp.where(lanes == number, total, totals)
            outputs.append(mm(shares.astype(bf16), values))
        attn_self_ref[:, 2 * HEAD * pair : 2 * HEAD * (pair + 1)] = joined(*outputs).astype(bf16)
    total_self_ref[...] = totals

    part_c = fetched[0]
    resid1 = resid0_ref[...] + mm_t(attn_self_ref[...], part_c[:, 3 * HD : 4 * HD])
    resid1_ref[...] = resid1
    normed = (resid1 * inverse_rms(resid1) * gains_ref[1:2]).astype(bf16)
    normed_cross_ref[...] = normed
    query_cross_ref[...] = mm(normed, part_c[:, 4 * HD : 5 * HD]).astype(bf16)

    part_b = fetched[1]
    memory = fetched[2]
    step = min(256, memory.shape[0])

    def project(number, carry):
        rows = pl.ds(pl.multiple_of(number * step, step), step)
        mem_kv_ref[rows, :] = mm(memory[rows, :], part_b[:, ff : ff + 2 * HD]).astype(bf16)
        return carry

    lax.fori_loop(0, memory.shape[0] // step, project, 0)
    total_cross_ref[...] = jnp.zeros(total_cross_ref.shape, f32)

    def cross_pair(place, place_v):
        keys, values = mem_kv_ref[:, place], mem_kv_ref[:, place_v]
        outputs = []
        for half in range(2):
            scores = mm_t(one_half(query_cross_ref[:, place], half), keys)
            total, shares = softmax_parts(scores)
            number = place.start // HEAD + half
            total_cross_ref[...] = jnp.where(lanes == number, total, total_cross_ref[...])
            outputs.append(mm(shares.astype(bf16), values))
        attn_cross_ref[:, place] = joined(*outputs).astype(bf16)

    in_steps(HD, 2 * HEAD, cross_pair, HD)
    resid2 = resid1_ref[...] + mm_t(attn_cross_ref[...], part_b[:, ff + 2 * HD :])
    resid2_ref[...] = resid2
    normed_ff_ref[...] = (resid2 * inverse_rms(resid2) * gains_ref[2:3]).astype(bf16)

    part_a = fetched[3]

    def feed(here, there):
        gate = mm(normed_ff_ref[...], part_a[:, here])
        up = mm(normed_ff_ref[...], part_a[:, there])
        gate_up_ref[:, here] = gate
        gate_up_ref[:, there] = up
        hidden_ref[:, here] = (gelu_tanh(gate) * up).astype(bf16)

    in_steps(ff, FF_STEP, feed, ff)
    resid3 = resid2_ref[...] + mm_t(hidden_ref[...], part_b[:, :ff])
    resid3_ref[...] = resid3
    final_ref[...] = (resid3 * inverse_rms(resid3) * gains_ref[3:4]).astype(bf16)


def attention_back(query, keys, values, scores, total, out_slope):
    shares = jnp.exp(scores - total)
    share_slope = mm_t(out_slope, values)
    inner = jnp.sum(shares * share_slope, axis=-1, keepdims=True)
    score_slope = shares * (share_slope - inner)
    rounded = score_slope.astype(bf16)
    return (
        rounded,
        mm(rounded, keys),
        t_mm(rounded, query),
        t_mm(shares.astype(bf16), out_slope),
    )


def backward_kernel(
    scalars_ref,
    slope_ref,
    resid3_ref,
    hidden_ref,
    gate_up_ref,
    normed_ff_ref,
    resid2_ref,
    attn_cross_ref,
    query_cross_ref,
    total_cross_ref,
    normed_cross_ref,
    resid1_ref,
    attn_self_ref,
    query_ref,
    kv_ref,
    total_self_ref,
    gains_ref,
    table_ref,
    bias_ref,
    mem_kv_hbm,
    memory_hbm,
    part_a_hbm,
    part_b_hbm,
    part_c_hbm,
    grad_a_hbm,
    grad_b_hbm,
    memory_part_hbm,
    grad_c_ref,
    query_slope_ref,
    kv_slope_ref,
    grad1_ref,
    norm_grads_ref,
    bias_grad_ref,
    mem_kv_ref,
    memory_ref,
    part_a_ref,
    part_b_ref,
    part_c_ref,
    grad_a_ref,
    grad_b_ref,
    memory_part_ref,
    gate_up_slope_ref,
    cross_query_slope_ref,
    cross_kv_slope_ref,
    sems,
    out_sems,
):
    fetched = Fetch(
        (part_b_hbm, part_a_hbm, mem_kv_hbm, memory_hbm, part_c_hbm),
        (part_b_ref, part_a_ref, mem_kv_ref, memory_ref, part_c_ref),
        sems,
    )
    first, length = scalars_ref[0], scalars_ref[1]
    ff = hidden_ref.shape[1]
    width = resid3_ref.shape[1]
    norm_grads_ref[...] = jnp.zeros_like(norm_grads_ref)

    grad3, norm_grad = rms_back(resid3_ref[...], gains_ref[3:4], slope_ref[...])
    norm_grads_ref[3:4] = norm_grad
    down_in = grad3.astype(bf16)
    part_b = fetched[0]

    def feed_back(here, there):
        hidden_slope = mm(down_in, part_b[:, here])
        gate, up = gate_up_ref[:, here], gate_up_ref[:, there]
        inner = jnp.tanh(0.7978845608028654 * (gate + 0.044715 * gate * gate * gate))
        activated = 0.5 * gate * (1.0 + inner)
        steep = 0.5 * (1.0 + inner) + 0.5 * gate * (1.0 - inner * inner) * (
            0.7978845608028654 * (1.0 + 3.0 * 0.044715 * gate * gate)
        )
        gate_up_slope_ref[:, here] = (hidden_slope * up * steep).astype(bf16)
        gate_up_slope_ref[:, there] = (hidden_slope * activated).astype(bf16)
        grad_b_ref[:, here] = t_mm(down_in, hidden_ref[:, here]).astype(bf16)

    in_steps(ff, FF_STEP, feed_back, ff)
    part_a = fetched[1]
    back, norm_grad = rms_back(
        resid2_ref[...], gains_ref[2:3], mm_t(gate_up_slope_ref[...], part_a[...])
    )
    norm_grads_ref[2:3] = norm_grad
    grad2 = grad3 + back

    def gate_up_grad(here):
        grad_a_ref[:, here] = t_mm(normed_ff_ref[...], gate_up_slope_ref[:, here]).astype(bf16)

    in_steps(2 * ff, 2 * FF_STEP, gate_up_grad)
    copy_a = pltpu.make_async_copy(grad_a_ref, grad_a_hbm, out_sems.at[0])
    copy_a.start()

    cross_in = grad2.astype(bf16)
    grad_b_ref[:, ff + 2 * HD :] = t_mm(cross_in, attn_cross_ref[...]).astype(bf16)
    out_slope = mm(cross_in, part_b[:, ff + 2 * HD :]).astype(bf16)
    mem_kv = fetched[2]
    cross_query_slope_ref[...] = out_slope

    def cross_pair_back(place, place_v):
        keys, values = mem_kv[:, place], mem_kv[:, place_v]
        lanes = lanes_of(total_cross_ref.shape)
        totals = [
            jnp.sum(
                jnp.where(lanes == place.start // HEAD + half, total_cross_ref[...], 0.0),
                axis=-1,
                keepdims=True,
            )
            for half in range(2)
        ]
        query = both_halves(query_cross_ref[:, place])
        part = attention_back(
            query,
            keys,
            values,
            mm_t(query, keys),
            jnp.concatenate(totals, axis=0),
            both_halves(cross_query_slope_ref[:, place]),
        )
        cross_query_slope_ref[:, place] = joined_rows(part[1]).astype(bf16)
        cross_kv_slope_ref[:, place] = part[2].astype(bf16)
        cross_kv_slope_ref[:, place_v] = part[3].astype(bf16)

    in_steps(HD, 2 * HEAD, cross_pair_back, HD)
    memory = fetched[3]

    def memory_weights(here, there):
        grad_b_ref[:, there] = t_mm(memory[...], cross_kv_slope_ref[:, here]).astype(bf16)

    in_steps(2 * HD, FF_STEP, memory_weights, ff)
    copy_b = pltpu.make_async_copy(grad_b_ref, grad_b_hbm, out_sems.at[1])
    copy_b.start()
    step = min(256, memory.shape[0])

    def project(number, carry):
        rows = pl.ds(pl.multiple_of(number * step, step), step)
        memory_part_ref[rows, :] = mm_t(
            cross_kv_slope_ref[rows, :], part_b[:, ff : ff + 2 * HD]
        ).astype(bf16)
        return carry

    lax.fori_loop(0, memory.shape[0] // step, project, 0)
    copy_m = pltpu.make_async_copy(memory_part_ref, memory_part_hbm, out_sems.at[2])
    copy_m.start()
    part_c = fetched[4]
    query_slope = cross_query_slope_ref[...]
    grad_c_ref[:, HD : 2 * HD] = t_mm(normed_cross_ref[...], query_slope).astype(bf16)
    back, norm_grad = rms_back(
        resid1_ref[...], gains_ref[1:2], mm_t(query_slope, part_c[:, 4 * HD : 5 * HD])
    )
    norm_grads_ref[1:2] = norm_grad
    grad1 = grad2 + back
    grad1_ref[...] = grad1

    self_in = grad1.astype(bf16)
    grad_c_ref[:, :HD] = t_mm(self_in, attn_self_ref[...]).astype(bf16)
    out_slope = mm(self_in, part_c[:, 3 * HD : 4 * HD]).astype(bf16)
    bias_rows = pltpu.roll(mm(bias_ref[...], table_ref[...]), first, 1)
    bias_sums = jnp.zeros(bias_rows.shape, f32)
    rows, seq = query_ref.shape[0], kv_ref.shape[0]
    reverse = lax.broadcasted_iota(jnp.int32, (rows, rows), 0) + lanes_of((rows, rows)) == rows - 1
    reverse = reverse.astype(bf16)
    for pair in range(HEADS // 2):
        place = slice(2 * HEAD * pair, 2 * HEAD * (pair + 1))
        place_v = slice(HD + 2 * HEAD * pair, HD + 2 * HEAD * (pair + 1))
        keys, values = kv_ref[:, place], kv_ref[:, place_v]
        query = both_halves(query_ref[:, place])
        products = mm_t(query, keys)
        scores, totals = [], []
        for half in range(2):
            number = 2 * pair + half
            scores.append(
                biased_scores(
                    products[half * rows : (half + 1) * rows],
                    bias_rows[number : number + 1],
                    first,
                    length,
                )
            )
            totals.append(total_self_ref[:, number : number + 1])
        part = attention_back(
            query,
            keys,
            values,
            jnp.concatenate(scores, axis=0),
            jnp.concatenate(totals, axis=0),
            both_halves(out_slope[:, place]),
        )
        for half in range(2):
            turned = mm(reverse, part[0][half * rows : (half + 1) * rows])
            turned = pltpu.roll(turned, 0, 1, stride=1, stride_axis=0)
            where = lax.broadcasted_iota(jnp.int32, bias_sums.shape, 0) == 2 * pair + half
            bias_sums = jnp.where(where, jnp.sum(turned, axis=0, keepdims=True), bias_sums)
        query_slope_ref[:, place] = joined_rows(part[1]).astype(bf16)
        kv_slope_ref[:, place] = part[2].astype(bf16)
        kv_slope_ref[:, place_v] = part[3].astype(bf16)
    bias_sums = pltpu.roll(bias_sums, 2 * seq + 1 - rows - first, 1)
    high = bias_sums.astype(bf16)
    rest = bias_sums - high.astype(f32)
    middle = rest.astype(bf16)
    low = (rest - middle.astype(f32)).astype(bf16)
    table = table_ref[...]
    bias_grad_ref[...] = mm_t(high, table) + (mm_t(middle, table) + mm_t(low, table))
    copy_a.wait()
    copy_b.wait()
    copy_m.wait()


def leave_kernel(
    query_slope_ref,
    kv_slope_ref,
    normed_ref,
    resid0_ref,
    grad1_ref,
    gains_ref,
    norm_grads_ref,
    part_grad_ref,
    part_c_ref,
    grad_c_ref,
    grad0_ref,
):
    normed = normed_ref[...]
    query_slope, kv_slope = query_slope_ref[...], kv_slope_ref[...]
    slope = mm_t(query_slope, part_c_ref[:, :HD]) + mm_t(kv_slope, part_c_ref[:, HD : 3 * HD])
    back, norm_grad = rms_back(resid0_ref[...], gains_ref[0:1], slope)
    grad0_ref[...] = (grad1_ref[...] + back).astype(bf16)
    grad_c_ref[:, :HD] = t_mm(normed, query_slope).astype(bf16)
    grad_c_ref[:, HD : 3 * HD] = t_mm(normed, kv_slope).astype(bf16)
    grad_c_ref[:, 3 * HD : 5 * HD] = part_grad_ref[...]
    where = lax.broadcasted_iota(jnp.int32, norm_grads_ref.shape, 0) == 0
    norm_grads = jnp.where(where, norm_grad, norm_grads_ref[...]).astype(bf16)
    row = lax.broadcasted_iota(jnp.int32, (norm_grads.shape[0], GAIN_PAD), 0)
    spread = (row == lanes_of(row.shape)).astype(bf16)
    grad_c_ref[:, 5 * HD :] = t_mm(norm_grads, spread).astype(bf16)


def local_kernel(name, kernel, outs, args, spaces="", out_spaces="", scratch=()):
    space = {"v": pltpu.VMEM, "s": pltpu.SMEM, "a": pl.ANY}
    spaces = spaces or "v" * len(args)
    out_spaces = out_spaces or "v" * len(outs)
    return pl.pallas_call(
        kernel,
        name=name,
        out_shape=tuple(jax.ShapeDtypeStruct(shape, dtype) for shape, dtype in outs),
        in_specs=[pl.BlockSpec(memory_space=space[letter]) for letter in spaces],
        out_specs=tuple(pl.BlockSpec(memory_space=space[letter]) for letter in out_spaces),
        scratch_shapes=list(scratch),
        compiler_params=pltpu.CompilerParams(vmem_limit_bytes=60 * 1024 * 1024),
    )(*args)


def pack_columns(pieces, block):
    start = 0
    for piece in pieces:
        if piece.shape[0] == 1:
            break
        block[:, start : start + piece.shape[1]] = piece[...]
        start += piece.shape[1]
    gains = pieces[-4:]
    if gains[0].shape[0] == 1:
        rows = gains[0].shape[1]
        where = lax.broadcasted_iota(jnp.int32, (16, rows), 0)
        stacked = jnp.zeros((16, rows), f32)
        for number, gain in enumerate(gains):
            stacked = jnp.where(where == number, gain[...].astype(f32), stacked)
        pick = lax.broadcasted_iota(jnp.int32, (16, GAIN_PAD), 0) == lanes_of((16, GAIN_PAD))
        block[:, start:] = t_mm(stacked.astype(bf16), pick.astype(bf16)).astype(bf16)


def pack_ids(pieces, block):
    block[...] = jnp.zeros_like(block)
    for number, piece in enumerate(pieces):
        micro, _, count = piece.shape
        for which in range(micro):
            block[micro * number + which : micro * number + which + 1, :count] = piece[which]


def tail_kernel(lengths_ref, *refs):
    (a_ref, b_ref, c_ref, small_ref, memory_ref, embedding_ref, head_ref), outs = refs[:7], refs[7:]
    (loss_ref, memory_out, embedding_out, head_out, bias_out), outs = outs[:5], outs[5:]
    memory_out[...] = memory_ref[...]
    embedding_out[...] = embedding_ref[...]
    head_out[...] = head_ref[...]
    total = jnp.sum(small_ref[...], axis=0)
    count = 0
    for first in range(lengths_ref.shape[0]):
        for second in range(lengths_ref.shape[1]):
            count = count + lengths_ref[first, second]
    loss_ref[...] = total[0:1, 64:65] / count.astype(f32)
    bias_out[...] = total[:HEADS, :BUCKETS]
    for ref, pieces in ((a_ref, outs[:2]), (b_ref, outs[2:6]), (c_ref, outs[6:11])):
        start = 0
        for piece in pieces:
            piece[...] = ref[:, start : start + piece.shape[1]]
            start += piece.shape[1]
    turned = jnp.transpose(c_ref[:, 5 * HD :])
    for number, piece in enumerate(outs[11:]):
        piece[...] = turned[number : number + 1]


def vocabulary(name, collective_id, final_rows, head_rows, targets, alive, sizes):
    span, width = head_rows.shape
    tok_dev = final_rows.shape[0]
    lines = sizes["s"]
    blocks = 2 * lines
    step_rows = min(512, span)
    gather = Gather(final_rows, "sh", "sh", sizes)
    direct = DirectGather(jax.ShapeDtypeStruct((blocks, tok_dev), f32), sizes)
    scatter = Scatter(jax.ShapeDtypeStruct((lines, 2, tok_dev, width), bf16), "hs", "sh", sizes)
    jobs = (gather, direct, scatter)
    peers = peers_of(jobs)

    def kernel(*refs):
        final_ref, head_ref, targets_ref, alive_ref = refs[:4]
        slope_ref, head_part_ref, picked_ref, log_total_ref = refs[4:8]
        states, totals, own_total, logits, turned, value = refs[8:14]
        rest = refs[14:]
        place = coordinates()
        awaited = greet(peers, place)
        counts = [len(job.scratch) for job in jobs]
        gather.prepare((final_ref, states) + rest[: counts[0]], place)
        direct.prepare((own_total, totals) + rest[counts[0] : counts[0] + counts[1]], place)
        scatter.prepare((value, slope_ref) + rest[counts[0] + counts[1] :], place)
        welcome(peers, place, awaited)
        position = place["s"]
        half = position // 2

        def spot(token, other):
            far, second = token // 2, token % 2
            near_row = position + second * (1 - 2 * (position % 2))
            far_row = 2 - half + second * (1 - 2 * half)
            row = near_row + far * (far_row - near_row)
            side = place["h"] + other * (1 - 2 * place["h"])
            return row, side, 2 * row + side

        def chunk_of(number):
            return pl.ds(pl.multiple_of(number * step_rows, step_rows), step_rows)

        def hits(number, target):
            rows = lax.broadcasted_iota(jnp.int32, (step_rows, tok_dev), 0) + number * step_rows
            return rows == target

        def bring(step):
            token, other = step // 2, step % 2
            if step == 0:
                gather.line_first()
                gather.launch((1, (0,), 1))
                gather.local.wait()
                gather.local_done = True
            if other:
                gather.arrive((1, (token,), 1))
                if token + 1 < lines:
                    gather.line_next(token + 1)
                    gather.launch((1, (token + 1,), 1))

        def forward_step(step, carry):
            for number in range(blocks):
                pl.when(step == number)(functools.partial(bring, number))
            row, side, number = spot(step // 2, step % 2)
            block = states[row, side]
            target = targets_ref[pl.ds(number, 1), :]

            def scores(chunk, best):
                found = mm_t(head_ref[chunk_of(chunk), :], block)
                logits[number, chunk_of(chunk), :] = found
                return jnp.maximum(best, jnp.max(found, axis=0, keepdims=True))

            count = span // step_rows
            best = lax.fori_loop(0, count, scores, jnp.full((1, tok_dev), -3.0e38, f32))

            def spread(chunk, sums):
                found = logits[number, chunk_of(chunk), :]
                hit = hits(chunk, target)
                return (
                    sums[0] + jnp.sum(jnp.exp(found - best), axis=0, keepdims=True),
                    sums[1] + jnp.sum(jnp.where(hit, found, 0.0), axis=0, keepdims=True),
                )

            zero = jnp.zeros((1, tok_dev), f32)
            total, picked = lax.fori_loop(0, count, spread, (zero, zero))
            own_total[pl.ds(number, 1), :] = best + jnp.log(total)
            picked_ref[pl.ds(number, 1), :] = picked
            return carry

        lax.fori_loop(0, blocks, forward_step, 0)
        direct.begin()
        direct.receive()
        parts = totals[...].reshape((blocks,) + own_total.shape)
        top = jnp.max(parts, axis=0)
        log_total_ref[...] = top + jnp.log(jnp.sum(jnp.exp(parts - top[None]), axis=0))

        def backward_step(step, carry):
            row, side, number = spot(lines - 1 - step // 2, 1 - step % 2)
            lanes = pl.ds(pl.multiple_of(number * tok_dev, tok_dev), tok_dev)
            target = targets_ref[pl.ds(number, 1), :]
            live = alive_ref[pl.ds(number, 1), :]
            log_total = log_total_ref[pl.ds(number, 1), :]

            def slopes(chunk, inner):
                share = jnp.exp(logits[number, chunk_of(chunk), :] - log_total)
                slope = (share - jnp.where(hits(chunk, target), 1.0, 0.0)) * live
                turned[chunk_of(chunk), lanes] = slope.astype(bf16)
                return inner

            lax.fori_loop(0, span // step_rows, slopes, 0)
            value[row, side] = t_mm(turned[:, lanes], head_ref[...]).astype(bf16)
            for which in range(lines):
                pl.when(step == 2 * which)(
                    functools.partial(scatter.launch, 0, (lines - 1 - which,), 1)
                )
            return carry

        lax.fori_loop(0, blocks, backward_step, 0)
        for token in (3, 2):
            scatter.reduce(0, (token,))
            scatter.line_step(token, middles=False)

        def head_chunk(number, carry):
            rows = pl.ds(pl.multiple_of(number * 256, 256), 256)
            every = states[...].reshape(blocks * tok_dev, width)
            head_part_ref[rows, :] = mm(turned[rows, :], every).astype(bf16)
            return carry

        lax.fori_loop(0, span // 256, head_chunk, 0)
        scatter.line_step(3, ends=False)
        scatter.line_step(2, ends=False)
        for token in (1, 0):
            scatter.reduce(0, (token,))
            scatter.line_step(token)
        gather.finish()
        direct.drain()
        scatter.finish()

    vmem = pl.BlockSpec(memory_space=pltpu.VMEM)
    rows = jax.ShapeDtypeStruct((blocks, tok_dev), f32)
    return pl.pallas_call(
        kernel,
        name=name,
        out_shape=(scatter.out, jax.ShapeDtypeStruct(head_rows.shape, bf16), rows, rows),
        in_specs=[vmem] * 4,
        out_specs=(vmem,) * 4,
        scratch_shapes=[
            pltpu.VMEM(gather.out.shape, bf16),
            pltpu.VMEM(direct.out.shape, f32),
            pltpu.VMEM((blocks, tok_dev), f32),
            pltpu.VMEM((blocks, span, tok_dev), f32),
            pltpu.VMEM((span, blocks * tok_dev), bf16),
            pltpu.VMEM(scatter.value.shape, bf16),
        ]
        + [item for job in jobs for item in job.scratch],
        compiler_params=pltpu.CompilerParams(
            collective_id=collective_id, has_side_effects=True, vmem_limit_bytes=60 * 1024 * 1024
        ),
    )(final_rows, head_rows, targets, alive)


def opening(name, collective_id, weights, embedding, ids, memory, head, sizes):
    voc_dev, width = embedding.shape
    n_gy = 2 * sizes["s"]
    n_gx = 2 * sizes["a"]
    span = n_gx * voc_dev
    lines = sizes["s"]
    micro, _, seq_dev = ids[0].shape
    tok_dev = 2 * seq_dev
    table = Gather(embedding, "ac", "ac", sizes)
    codes = DirectGather(jax.ShapeDtypeStruct((8, 128), jnp.int32), sizes, "shc")
    memories = MemoryGather(memory, sizes)
    heads = Gather(head, "ac", "ac", sizes, "", 20)
    sums = Scatter(jax.ShapeDtypeStruct((lines, 2, tok_dev, width), bf16), "hs", "sh", sizes)
    jobs = list(weights) + [table, codes, memories, heads, sums]
    peers = peers_of(jobs)
    operands = [list(job.values) for job in weights] + [[embedding], list(ids), [memory], [head]]
    flat = [value for group in operands for value in group]

    def kernel(*refs):
        ins = list(refs[: len(flat)])
        outs = list(refs[len(flat) : len(flat) + 7])
        rest = list(refs[len(flat) + 7 :])
        place = coordinates()
        awaited = greet(peers, place)

        def take(source, count):
            taken = tuple(source[:count])
            del source[:count]
            return taken

        rows_ref, value, code = rest.pop(0), rest.pop(0), rest.pop(0)
        for job in weights:
            pieces = take(ins, len(job.values))
            block = rest.pop(0)
            job.pack(pieces, block)
            job.prepare((block, outs.pop(0)) + take(rest, len(job.scratch) - 1), place)
        table.prepare((ins.pop(0), rows_ref) + take(rest, len(table.scratch)), place)
        pack_ids(take(ins, 2), code)
        ids_ref = outs.pop(0)
        codes.prepare((code, ids_ref) + take(rest, len(codes.scratch)), place)
        memories.prepare((ins.pop(0), outs.pop(0)) + take(rest, len(memories.scratch)), place)
        heads.prepare((ins.pop(0), outs.pop(0)) + take(rest, len(heads.scratch)), place)
        sums.prepare((value, outs.pop(0)) + take(rest, len(sums.scratch)), place)
        welcome(peers, place, awaited)

        def tables_here():
            codes.receive()
            table.local.wait()
            table.local_done = True
            for transfer in table.transfers:
                table.arrive(transfer)

        def pick(token):
            row = along_line(place["s"], token)

            def one(other, carry):
                side = place["h"] + (1 - other) * (1 - 2 * place["h"])
                index = jnp.concatenate(
                    [
                        ids_ref[2 * side + place["c"], which, row % 2, pl.ds(row // 2, 1), :][:, :seq_dev]
                        for which in range(2)
                    ],
                    axis=1,
                )
                shard = index // voc_dev
                held = shard % n_gy == 2 * place["s"] + place["h"]
                index = jnp.where(held, shard // n_gy * voc_dev + index % voc_dev, -1)
                at = lax.broadcasted_iota(jnp.int32, (span, tok_dev), 0) == index
                every = rows_ref[...].reshape(span, width)
                value[row, side] = t_mm(jnp.where(at, 1.0, 0.0).astype(bf16), every).astype(bf16)
                pl.when(other == 0)(functools.partial(sums.launch, 0, (token,), 1))
                return carry

            lax.fori_loop(0, 2, one, 0)

        events = [event for job in list(weights) + [memories, heads] for event in job.events()]
        events.append((-2, codes.begin))
        for transfer in table.transfers:
            level, unit, _ = transfer
            key = -1 if level == 0 else TABLE_KEY if unit[0] else 0.1
            events.append((key, functools.partial(table.launch, transfer)))
        events.append((TABLE_KEY + 0.05, tables_here))
        for number, token in enumerate((3, 2, 1, 0)):
            events.append((PICK_KEY + PICK_STEP * number, functools.partial(pick, token)))
            key = SUM_KEY + SUM_STEP * number
            events.append((key, functools.partial(sums.reduce, 0, (token,))))
            if token:
                events.append((key + 0.01, functools.partial(sums.line_step, token, middles=False)))
                events.append((LINE_KEY + SUM_STEP * number, functools.partial(sums.line_step, token, ends=False)))
            else:
                events.append((LINE_KEY + SUM_STEP * number, functools.partial(sums.line_step, token)))
        for _, act in sorted(events, key=lambda event: event[0]):
            act()
        for job in jobs:
            if job is codes:
                job.drain()
            else:
                job.finish()

    vmem = pl.BlockSpec(memory_space=pltpu.VMEM)
    anywhere = pl.BlockSpec(memory_space=pl.ANY)
    scratch = [
        pltpu.VMEM(table.out.shape, bf16),
        pltpu.VMEM(sums.value.shape, bf16),
        pltpu.VMEM((8, 128), jnp.int32),
    ]
    return pl.pallas_call(
        kernel,
        name=name,
        out_shape=tuple(job.out for job in weights)
        + (codes.out, memories.out, heads.out, sums.out),
        in_specs=[vmem] * len(flat),
        out_specs=(anywhere,) * 3 + (vmem, anywhere, anywhere, vmem),
        scratch_shapes=scratch + [item for job in jobs for item in job.scratch],
        compiler_params=pltpu.CompilerParams(
            collective_id=collective_id, has_side_effects=True, vmem_limit_bytes=60 * 1024 * 1024
        ),
    )(*flat)


TABLE_KEY, PICK_KEY, PICK_STEP, SUM_KEY, SUM_STEP, LINE_KEY = 0.55, 0.65, 0.05, 1.3, 0.3, 1.9


def per_device(
    target_ids,
    labels,
    lengths,
    memory,
    embedding,
    head,
    gain_self,
    w_query,
    w_key,
    w_value,
    w_out,
    relative_bias,
    gain_cross,
    c_query,
    c_key,
    c_value,
    c_out,
    gain_ff,
    w_gate,
    w_up,
    w_down,
    gain_final,
):
    micro = target_ids.shape[0]
    seq_dev = target_ids.shape[2]
    mem_dev = memory.shape[2]
    voc_dev, width = embedding.shape
    ff = w_gate.shape[1]
    n_gx = lax.axis_size("gx")
    n_gy = lax.axis_size("gy")
    column = lax.axis_index("gy")
    row_group = lax.axis_index("gx")
    devices = n_gx * n_gy
    sizes = {"a": n_gx // 2, "c": 2, "s": n_gy // 2, "h": 2}
    assert sizes["s"] == 2 * micro
    place = coordinates()
    seq = seq_dev * n_gy
    plane = sizes["s"] * seq
    tok_dev = seq // 4
    tokens = plane // 2
    span = n_gx * voc_dev
    merged = "" if sizes["a"] == 2 else "ashc"

    rows_dev = width // devices
    whole_tiles = rows_dev % 16 == 0
    groups = (
        (w_gate, w_up),
        (w_down, c_key, c_value, c_out),
        (w_query, w_key, w_value, w_out, c_query),
    )
    gains = (gain_self, gain_cross, gain_ff, gain_final)
    widths = [sum(piece.shape[1] for piece in group) for group in groups]
    widths[2] += GAIN_PAD
    orders = ("shac", "shac", "sahc")
    ways_back = ("cahs", "chas", "chas")
    if whole_tiles:
        operands = list(groups)
        operands[2] += tuple(gain.reshape(1, rows_dev) for gain in gains)
        weights = [
            PackedGather(
                group,
                jax.ShapeDtypeStruct((rows_dev, count), bf16),
                pack_columns,
                order,
                "acsh",
                sizes,
                merged,
            )
            for group, count, order in zip(operands, widths, orders)
        ]
    else:
        shards = [jnp.concatenate(group, axis=1) for group in groups]
        columns_of = jnp.pad(jnp.stack(gains, axis=1), ((0, 0), (0, GAIN_PAD - 4)))
        shards[2] = jnp.concatenate([shards[2], columns_of], axis=1)
        weights = [
            Gather(packed(part), order, "acsh", sizes, merged) for part, order in zip(shards, orders)
        ]
    small_tables = whole_tiles and span <= 2048 and tok_dev == 128
    if small_tables:
        part_a, part_b, part_c, ids, memory_all, head_rows, resid0 = opening(
            "start",
            0,
            weights,
            embedding,
            (target_ids, labels),
            memory.reshape(micro, mem_dev, width),
            head,
            sizes,
        )
    else:
        part_a, part_b, part_c, embed_rows, ids, memory_all = exchange(
            "gather_weights",
            0,
            weights
            + [
                Gather(embedding, "ac", "ac", sizes, "", 20),
                PackedGather(
                    (target_ids, labels),
                    jax.ShapeDtypeStruct((8, 128), jnp.int32),
                    pack_ids,
                    "shc",
                    "shc",
                    sizes,
                    "shc",
                ),
                MemoryGather(memory.reshape(micro, mem_dev, width), sizes),
            ],
        )
    part_a, part_b, part_c = (
        full.reshape(width, count) for full, count in zip((part_a, part_b, part_c), widths)
    )
    memory_all = memory_all.reshape(n_gy * mem_dev, width)
    ids = ids[..., : 2 * micro, :seq_dev].reshape(n_gy, 2, 2, micro, seq_dev)
    ids = ids.transpose(2, 3, 1, 0, 4).reshape(2, sizes["s"] * 2, 2, tok_dev)
    ids = lax.dynamic_index_in_dim(ids, place["c"], axis=2, keepdims=False).reshape(2, tokens)

    def local_of(index):
        shard = index // voc_dev
        return jnp.where(shard % n_gy == column, shard // n_gy * voc_dev + index % voc_dev, -1)

    local_ids = local_of(ids[0])
    targets = local_of(ids[1])
    columns = jnp.arange(span, dtype=jnp.int32)

    tok_layout = (sizes["s"], 2, tok_dev, width)
    if not small_tables:
        chosen = (local_ids[:, None] == columns[None, :]).astype(bf16)
        picked_rows = dot(chosen, embed_rows.reshape(span, width)).astype(bf16)
        resid0, head_rows = exchange(
            "rows",
            1,
            [
                Scatter(picked_rows.reshape(tok_layout), "hs", "sh", sizes),
                Gather(head, "ac", "ac", sizes, "", 20),
            ],
        )
    head_rows = head_rows.reshape(span, width)

    plane_lengths = lax.dynamic_slice_in_dim(lengths, 2 * place["a"], 2, axis=1).reshape(-1)
    live_length = lax.dynamic_index_in_dim(plane_lengths, place["s"], keepdims=False)
    scalars = jnp.stack([(2 * place["h"] + place["c"]) * tok_dev, live_length])
    table = jnp.asarray(distance_table(seq), bf16)
    bias_pad = jnp.pad(relative_bias, ((0, 8 - HEADS), (0, 128 - BUCKETS)))
    query_self, own_kv, normed_self, gain_rows = local_kernel(
        "enter",
        enter_kernel,
        [((tok_dev, HD), bf16), ((tok_dev, 2 * HD), bf16), ((tok_dev, width), bf16), ((16, width), f32)],
        [resid0, part_c],
    )
    (self_kv_all,) = exchange("self_keys", 2, [Gather(own_kv, "hc", "hc", sizes)])
    self_kv_all = self_kv_all.reshape(seq, 2 * HD)
    rows_f32, rows_bf16, rows_heads = ((tok_dev, width), f32), ((tok_dev, width), bf16), ((tok_dev, HD), bf16)
    totals_shape = ((tok_dev, 128), f32)
    all_mem = n_gy * mem_dev
    (
        attn_self,
        total_self,
        resid1,
        normed_cross,
        query_cross,
        mem_kv,
        attn_cross,
        total_cross,
        resid2,
        normed_ff,
        gate_up,
        hidden,
        resid3,
        final_rows,
    ) = local_kernel(
        "forward",
        forward_kernel,
        [
            rows_heads,
            totals_shape,
            rows_f32,
            rows_bf16,
            rows_heads,
            ((all_mem, 2 * HD), bf16),
            rows_heads,
            totals_shape,
            rows_f32,
            rows_bf16,
            ((tok_dev, 2 * ff), f32),
            ((tok_dev, ff), bf16),
            rows_f32,
            rows_bf16,
        ],
        [scalars, query_self, self_kv_all, resid0, gain_rows, table, bias_pad]
        + [memory_all, part_a, part_b, part_c],
        "svvvvvvaaaa",
        scratch=[pltpu.VMEM(full.shape, bf16) for full in (memory_all, part_a, part_b, part_c)]
        + [pltpu.SemaphoreType.DMA((4,))],
    )

    index = jnp.arange(tokens, dtype=jnp.int32)
    position = (2 * (index // tok_dev % 2) + place["c"]) * tok_dev + index % tok_dev
    alive = (position < jnp.repeat(plane_lengths, 2 * tok_dev)).astype(f32)
    if small_tables:
        by_block = (n_gy, tok_dev)
        final_slope, head_part, picked, log_total = vocabulary(
            "vocabulary", 3, final_rows, head_rows, targets.reshape(by_block), alive.reshape(by_block), sizes
        )
        picked, log_total = picked.reshape(tokens), log_total.reshape(tokens)
    else:
        (states,) = exchange("final_rows", 3, [Gather(final_rows, "sh", "sh", sizes, merged)])
        states = states.reshape(tokens, width)
        logits = dot_t(states, head_rows)
        highest = jnp.max(logits, axis=1)
        own_total = highest + jnp.log(jnp.sum(jnp.exp(logits - highest[:, None]), axis=1))
        (totals,) = exchange("totals", 4, [DirectGather(own_total.reshape(tokens // 128, 128), sizes)])
        totals = totals.reshape(n_gy, tokens)
        top = jnp.max(totals, axis=0)
        log_total = top + jnp.log(jnp.sum(jnp.exp(totals - top[None]), axis=0))
        hit = columns[None, :] == targets[:, None]
        picked = jnp.sum(jnp.where(hit, logits, 0.0), axis=1)
        slope = jnp.exp(logits - log_total[:, None]) - hit.astype(f32)
        slope = (slope * alive[:, None]).astype(bf16)
        head_part = t_dot(slope, states).astype(bf16)
        final_part = dot(slope, head_rows).astype(bf16)
        (final_slope,) = exchange(
            "final_slopes", 5, [Scatter(final_part.reshape(tok_layout), "hs", "sh", sizes)]
        )
    loss_part = jnp.where(column == 0, jnp.sum(alive * log_total), 0.0) - jnp.sum(alive * picked)

    grad_a, grad_b, memory_part, part_grad_c, query_slope, kv_slope, grad1, norm_grads, bias_grad = (
        local_kernel(
            "backward",
            backward_kernel,
            [
                (part_a.shape, bf16),
                (part_b.shape, bf16),
                (memory_all.shape, bf16),
                ((width, 2 * HD), bf16),
                rows_heads,
                ((seq, 2 * HD), bf16),
                rows_f32,
                (gain_rows.shape, f32),
                ((8, 128), f32),
            ],
            [scalars, final_slope, resid3, hidden, gate_up, normed_ff, resid2, attn_cross]
            + [query_cross, total_cross, normed_cross, resid1, attn_self, query_self, self_kv_all]
            + [total_self, gain_rows, table, bias_pad, mem_kv, memory_all, part_a, part_b, part_c],
            "s" + "v" * 18 + "a" * 5,
            "aaa" + "v" * 6,
            [
                pltpu.VMEM(full.shape, bf16)
                for full in (mem_kv, memory_all, part_a, part_b, part_c, part_a, part_b, memory_all)
            ]
            + [
                pltpu.VMEM((tok_dev, 2 * ff), bf16),
                pltpu.VMEM((tok_dev, HD), bf16),
                pltpu.VMEM(mem_kv.shape, bf16),
                pltpu.SemaphoreType.DMA((5,)),
                pltpu.SemaphoreType.DMA((3,)),
            ],
        )
    )
    (kv_slope,) = exchange(
        "key_slopes",
        6,
        [Scatter(kv_slope.reshape(2, 2, tok_dev, 2 * HD), "ch", "hc", sizes, "", bf16)],
    )
    grad_c, grad0 = local_kernel(
        "leave",
        leave_kernel,
        [(part_c.shape, bf16), rows_bf16],
        [query_slope, kv_slope, normed_self, resid0, grad1, gain_rows, norm_grads, part_grad_c, part_c],
    )
    slopes, head_grad = exchange(
        "row_slopes",
        7,
        [
            Gather(grad0, "sh", "sh", sizes, merged),
            Scatter(head_part.reshape(sizes["a"], 2, voc_dev, width), "ca", "ac", sizes),
        ],
    )
    embed_part = t_dot(
        (local_ids[:, None] == columns[None, :]).astype(bf16), slopes.reshape(tokens, width)
    ).astype(bf16)
    sums = (grad_a, grad_b, grad_c)
    at_loss = (jnp.arange(8)[:, None] == 0) & (jnp.arange(128)[None, :] == 64)
    small = jnp.where(at_loss, loss_part, bias_grad)
    device_layout = (sizes["a"], 2, sizes["s"], 2)
    blocks = [part.reshape(device_layout + packed_shape(part, devices)) for part in sums]
    grad_a, grad_b, grad_c, embedding_grad, memory_grad, small = exchange(
        "scatter_weights",
        8,
        [
            Scatter(part, order, "acsh", sizes, merged)
            for part, order in zip(blocks, ways_back)
        ]
        + [
            Scatter(embed_part.reshape(sizes["a"], 2, voc_dev, width), "ca", "ac", sizes),
            MemoryScatter(memory_part.reshape(sizes["s"], 2, mem_dev, width), sizes),
            Gather(small, "shac", "acsh", sizes, "ashc"),
        ],
    )
    small = small.reshape(devices, 8, 128)
    memory_grad = memory_grad.reshape(micro, 1, mem_dev, width)
    if whole_tiles:
        pieces = [piece.shape[1] for group in groups for piece in group]
        outs = [
            ((1, 1), f32),
            (memory_grad.shape, f32),
            (embedding_grad.shape, f32),
            (head_grad.shape, f32),
            ((HEADS, BUCKETS), f32),
        ]
        outs += [((rows_dev, count), f32) for count in pieces] + [((1, rows_dev), f32)] * 4
        results = local_kernel(
            "tail",
            tail_kernel,
            outs,
            [lengths, grad_a, grad_b, grad_c, small, memory_grad, embedding_grad, head_grad],
            "s" + "v" * 7,
        )
        loss, memory_grad, embedding_grad, head_grad, bias_total = results[:5]
        loss = loss.reshape(())
        cut = results[5:16]
        gain_out = [gain.reshape(rows_dev) for gain in results[16:]]
    else:
        grad_a, grad_b, grad_c = (
            grad.reshape(rows_dev, count) for grad, count in zip((grad_a, grad_b, grad_c), widths)
        )
        small = jnp.sum(small, axis=0)
        loss = small[0, 64] / jnp.sum(lengths).astype(f32)
        bias_total = small[:HEADS, :BUCKETS]
        cut = []
        for grad, group in zip((grad_a, grad_b, grad_c), groups):
            start = 0
            for piece in group:
                cut.append(grad[:, start : start + piece.shape[1]])
                start += piece.shape[1]
        gain_out = [grad_c[:, 5 * HD + number] for number in range(4)]
    gate_grad, up_grad, down_grad, c_key_grad, c_value_grad, c_out_grad = cut[:6]
    query_grad, key_grad, value_grad, out_grad, c_query_grad = cut[6:]
    return (
        loss,
        memory_grad,
        embedding_grad,
        head_grad,
        gain_out[0],
        query_grad,
        key_grad,
        value_grad,
        out_grad,
        bias_total,
        gain_out[1],
        c_query_grad,
        c_key_grad,
        c_value_grad,
        c_out_grad,
        gain_out[2],
        gate_grad,
        up_grad,
        down_grad,
        gain_out[3],
    )


def packed_shape(part, count):
    rows, columns = part.shape[0] // count, part.shape[1]
    if rows % 16 == 0:
        return (rows, columns)
    return (16, rows * columns // 16)


def solution(mesh):
    placed = (
        P(None, "gx", "gy"),
        P(None, "gx", "gy"),
        P(),
        P(None, "gx", "gy", None),
        P(("gx", "gy"), None),
        P(("gx", "gy"), None),
        P(("gx", "gy")),
        P(("gx", "gy"), None),
        P(("gx", "gy"), None),
        P(("gx", "gy"), None),
        P(("gx", "gy"), None),
        P(),
        P(("gx", "gy")),
        P(("gx", "gy"), None),
        P(("gx", "gy"), None),
        P(("gx", "gy"), None),
        P(("gx", "gy"), None),
        P(("gx", "gy")),
        P(("gx", "gy"), None),
        P(("gx", "gy"), None),
        P(("gx", "gy"), None),
        P(("gx", "gy")),
    )
    return jax.shard_map(
        per_device,
        mesh=mesh,
        in_specs=placed,
        out_specs=(
            P(),
            P(None, "gx", "gy", None),
            P(("gx", "gy"), None),
            P(("gx", "gy"), None),
            P(("gx", "gy")),
            P(("gx", "gy"), None),
            P(("gx", "gy"), None),
            P(("gx", "gy"), None),
            P(("gx", "gy"), None),
            P(),
            P(("gx", "gy")),
            P(("gx", "gy"), None),
            P(("gx", "gy"), None),
            P(("gx", "gy"), None),
            P(("gx", "gy"), None),
            P(("gx", "gy")),
            P(("gx", "gy"), None),
            P(("gx", "gy"), None),
            P(("gx", "gy"), None),
            P(("gx", "gy")),
        ),
        check_vma=False,
    )
```

```python
import functools
import itertools
import math

import jax
import jax.numpy as jnp
import numpy as np
from jax import lax
from jax.experimental import pallas as pl
from jax.experimental.pallas import tpu as pltpu
from jax.sharding import PartitionSpec as P

HEADS = 6
HEAD = 64
HD = HEADS * HEAD
BUCKETS = 32
GAIN_PAD = 128

eps = 1e-06
masked_score = -1000000000.0
bf16 = jnp.bfloat16
f32 = jnp.float32


def flip(position, offset):
    moved = position
    weight = 1
    while weight <= offset:
        if offset & weight:
            moved = moved + weight * (1 - 2 * ((position // weight) % 2))
        weight *= 2
    return moved


def coordinates():
    gx, gy = lax.axis_index("gx"), lax.axis_index("gy")
    return {"a": gx // 2, "c": gx % 2, "s": gy // 2, "h": gy % 2}


def peer_of(dim, offset):
    gx, gy = lax.axis_index("gx"), lax.axis_index("gy")
    if dim == "a":
        return {"gx": 2 * flip(gx // 2, offset) + gx % 2}
    if dim == "c":
        return {"gx": flip(gx, 1)}
    if dim == "plane":
        s, h, c = offset + (0,) * (3 - len(offset))
        there = {"gy": 2 * flip(gy // 2, s) + flip(gy % 2, h)}
        if c:
            there["gx"] = flip(gx, 1)
        return there
    if dim == "s":
        return {"gy": 2 * flip(gy // 2, offset) + gy % 2}
    return {"gy": flip(gy, 1)}


def remote(source, target, send, recv, dim, offset):
    return pltpu.make_async_remote_copy(
        src_ref=source,
        dst_ref=target,
        send_sem=send,
        recv_sem=recv,
        device_id=peer_of(dim, offset),
        device_id_type=pl.DeviceIdType.MESH,
    )


def along_line(position, step):
    half = position // 2
    return (position, flip(position, 1), 2 - half, 3 - 3 * half)[step]


def is_middle(position):
    return (position + 1) // 2 == 1


def across_middle():
    gy = lax.axis_index("gy")
    return {"gy": 2 * (3 - gy // 2) + gy % 2}


def spot_of(dim, position, offset):
    return along_line(position, offset) if dim == "s" else flip(position, offset)


def remote_to(source, target, send, recv, device):
    return pltpu.make_async_remote_copy(
        src_ref=source,
        dst_ref=target,
        send_sem=send,
        recv_sem=recv,
        device_id=device,
        device_id_type=pl.DeviceIdType.MESH,
    )


def each_piece(rows, columns, body, width=16384):
    step = rows
    while step * columns > width and step % 32 == 0:
        step //= 2
    if step == rows:
        body(slice(None))
        return

    def piece(number, carry):
        body(pl.ds(pl.multiple_of(number * step, step), step))
        return carry

    lax.fori_loop(0, rows // step, piece, 0)


LINE_PEERS = [("s", 1), ("m", 1)]


class Gather:
    def __init__(self, block, order, layout, sizes, merged="", late=0):
        self.value = block
        self.late = late
        self.order, self.layout, self.sizes, self.merged = order, layout, sizes, merged
        self.out = jax.ShapeDtypeStruct(tuple(sizes[d] for d in layout) + block.shape, block.dtype)
        self.in_spec = pl.BlockSpec(memory_space=pltpu.VMEM)
        self.out_spec = pl.BlockSpec(memory_space=pl.ANY)
        self.transfers = []
        for level, dim in enumerate(order):
            ranges = [(None,) if d in merged else range(sizes[d]) for d in order[:level]]
            for unit in itertools.product(*ranges):
                for offset in range(1, sizes[dim]):
                    self.transfers.append((level, unit, offset))
        self.index = {transfer: number for number, transfer in enumerate(self.transfers)}
        count = len(self.transfers)
        self.line = order[0] == "s"
        self.scratch = [
            pltpu.SemaphoreType.DMA((count,)),
            pltpu.SemaphoreType.DMA((count,)),
            pltpu.SemaphoreType.DMA,
            pltpu.SemaphoreType.DMA((5,)),
        ]
        self.peers = [(d, offset) for d in order for offset in range(1, sizes[d]) if d != "s"]
        if self.line:
            self.peers += LINE_PEERS

    def prepare(self, refs, place):
        self.source, self.target, self.send, self.recv, self.local_sem, self.line_send = refs
        self.place = place
        self.local = pltpu.make_async_copy(
            self.source, self.target.at[tuple(place[d] for d in self.layout)], self.local_sem
        )
        self.local.start()
        self.local_done = False
        self.arrived = set()
        self.sent = []

    def region(self, level, unit, offset):
        where = dict(self.place)
        for d, moved in zip(self.order[:level], unit):
            where[d] = slice(None) if moved is None else spot_of(d, self.place[d], moved)
        if offset:
            dim = self.order[level]
            where[dim] = spot_of(dim, self.place[dim], offset)
        return self.target.at[tuple(where[d] for d in self.layout)]

    def needs(self, level, unit):
        if level == 0:
            return []
        last, before = unit[-1], unit[:-1]
        if last is None:
            dim = self.order[level - 1]
            return self.needs(level - 1, before) + [
                (level - 1, before, offset) for offset in range(1, self.sizes[dim])
            ]
        if last == 0:
            return self.needs(level - 1, before)
        return [(level - 1, before, last)]

    def arrive(self, transfer):
        if transfer in self.arrived:
            return
        self.arrived.add(transfer)
        level, unit, offset = transfer
        number = self.index[transfer]
        there = self.region(level, unit, offset)
        if self.line and level == 0:
            offset = 1
        remote(
            there, there, self.send.at[number], self.recv.at[number], self.order[level], offset
        ).wait_recv()

    def line_copy(self, number):
        held, there = ((0, 1), (0, 2), (1, 3), (2, 2), (3, 3))[number]
        target = self.region(0, (), held)
        device = peer_of("s", 1) if number in (0, 3, 4) else across_middle()
        recv = self.recv.at[self.index[(0, (), there)]]
        source = target if held else self.source
        return remote_to(source, target, self.line_send.at[number], recv, device)

    def line_first(self):
        self.line_copy(0).start()

        @pl.when(is_middle(self.place["s"]))
        def _():
            self.line_copy(1).start()

    def line_next(self, step):
        self.arrive((0, (), step))

        @pl.when(is_middle(self.place["s"]))
        def _():
            self.line_copy(step + 1).start()

    def copy(self, transfer):
        level, unit, offset = transfer
        number = self.index[transfer]
        target = self.region(level, unit, 0)
        own = all(moved == 0 for moved in unit)
        return remote(
            self.source if own else target,
            target,
            self.send.at[number],
            self.recv.at[number],
            self.order[level],
            offset,
        )

    def launch(self, transfer):
        level, unit, offset = transfer
        for need in self.needs(level, unit):
            self.arrive(need)
        if None in unit and not self.local_done:
            self.local.wait()
            self.local_done = True
        self.copy(transfer).start()
        self.sent.append(transfer)

    def events(self):
        found = []
        if self.line:
            found.append((0, self.line_first))
            for step in (1, 2, 3):
                found.append((step, functools.partial(self.line_next, step)))
        for transfer in self.transfers:
            level, unit, offset = transfer
            if self.line and level == 0:
                continue
            key = 0.1 * level + 0.01 * offset
            for d, moved in zip(self.order, unit):
                key += self.sizes[d] - 1 if moved is None else moved
            if self.late and self.needs(level, unit):
                key += self.late
            found.append((key, functools.partial(self.launch, transfer)))
        return found

    def finish(self):
        if not self.local_done:
            self.local.wait()
        for transfer in self.transfers:
            self.arrive(transfer)
        for transfer in self.sent:
            self.copy(transfer).wait_send()
        if self.line:
            self.line_copy(0).wait_send()

            @pl.when(is_middle(self.place["s"]))
            def _():
                for number in range(1, 5):
                    self.line_copy(number).wait_send()


class PackedGather(Gather):
    def __init__(self, values, block, pack, *args):
        super().__init__(block, *args)
        self.values, self.pack = values, pack
        self.scratch = [pltpu.VMEM(block.shape, block.dtype)] + self.scratch


class DirectGather:
    def __init__(self, block, sizes, dims="sh"):
        self.value = block
        self.dims = dims
        shape = tuple(sizes[d] for d in dims)
        self.out = jax.ShapeDtypeStruct(shape + block.shape, block.dtype)
        self.in_spec = pl.BlockSpec(memory_space=pltpu.VMEM)
        self.out_spec = pl.BlockSpec(memory_space=pltpu.VMEM)
        self.offsets = list(itertools.product(*(range(size) for size in shape)))[1:]
        count = len(self.offsets)
        self.scratch = [pltpu.SemaphoreType.DMA((count,)), pltpu.SemaphoreType.DMA((count,))]
        self.peers = [("plane", offset) for offset in self.offsets]

    def prepare(self, refs, place):
        self.source, self.target, self.send, self.recv = refs
        self.place = place

    def copy(self, number, arriving):
        offset = self.offsets[number]
        spot = tuple(
            flip(self.place[d], moved) if arriving else self.place[d] for d, moved in zip(self.dims, offset)
        )
        return remote_to(
            self.source,
            self.target.at[spot],
            self.send.at[number],
            self.recv.at[number],
            peer_of("plane", offset),
        )

    def events(self):
        return [(0, self.begin)]

    def begin(self):
        for number in range(len(self.offsets)):
            self.copy(number, False).start()
        self.target[tuple(self.place[d] for d in self.dims)] = self.source[...]

    def finish(self):
        self.receive()
        self.drain()

    def receive(self):
        for number in range(len(self.offsets)):
            self.copy(number, True).wait_recv()

    def drain(self):
        for number in range(len(self.offsets)):
            self.copy(number, False).wait_send()


class Scatter:
    def __init__(self, value, order, layout, sizes, merged="", out_dtype=f32):
        self.value = value
        self.order, self.layout, self.sizes, self.merged = order, layout, sizes, merged
        self.block = value.shape[len(layout) :]
        self.out = jax.ShapeDtypeStruct(self.block, out_dtype)
        self.in_spec = pl.BlockSpec(memory_space=pltpu.VMEM)
        self.out_spec = pl.BlockSpec(memory_space=pltpu.VMEM)
        self.line = order[-1] == "s"
        self.levels = len(order)
        self.units = []
        self.scratch = []
        self.layouts = [layout]
        for level, dim in enumerate(order):
            later = order[level + 1 :]
            ranges = [(None,) if d in merged else range(sizes[d]) for d in later]
            units = sorted(
                itertools.product(*ranges),
                key=lambda unit: (-(unit[-1] or 0) if unit else 0, -sum(moved or 0 for moved in unit)),
            )
            self.units.append(units)
            left = "".join(d for d in self.layouts[-1] if d != dim)
            self.layouts.append(left)
            self.scratch.append(
                pltpu.VMEM(
                    (5 if dim == "s" else sizes[dim] - 1,)
                    + tuple(sizes[d] for d in left)
                    + self.block,
                    value.dtype,
                )
            )
        self.index = {}
        for level, dim in enumerate(order):
            for unit in self.units[level]:
                for offset in range(1, sizes[dim]):
                    self.index[(level, unit, offset)] = len(self.index)
        count = len(self.index)
        self.scratch += [
            pltpu.SemaphoreType.DMA((count,)),
            pltpu.SemaphoreType.DMA((count,)),
            pltpu.SemaphoreType.DMA((2, 5)),
        ]
        self.peers = [(d, offset) for d in order for offset in range(1, sizes[d]) if d != "s"]
        if self.line:
            self.peers += LINE_PEERS

    def prepare(self, refs, place):
        self.source, self.target = refs[0], refs[1]
        self.landing = refs[2 : 2 + self.levels]
        self.send, self.recv, self.line_sems = refs[2 + self.levels :]
        self.place = place
        self.sent = []

    def held(self, level):
        return self.source if level == 0 else self.landing[level - 1].at[0]

    def later(self, level, unit):
        where = {}
        for d, moved in zip(self.order[level + 1 :], unit):
            where[d] = slice(None) if moved is None else spot_of(d, self.place[d], moved)
        return where

    def copy(self, level, unit, offset):
        number = self.index[(level, unit, offset)]
        dim = self.order[level]
        where = self.later(level, unit)
        landed = self.landing[level].at[
            (offset - 1,) + tuple(where[d] for d in self.layouts[level + 1])
        ]
        where[dim] = flip(self.place[dim], offset)
        source = self.held(level).at[tuple(where[d] for d in self.layouts[level])]
        return remote(source, landed, self.send.at[number], self.recv.at[number], dim, offset)

    def launch(self, level, unit, offset):
        self.copy(level, unit, offset).start()
        self.sent.append((level, unit, offset))

    def reduce(self, level, unit):
        dim = self.order[level]
        size = self.sizes[dim]
        for offset in range(1, size):
            self.copy(level, unit, offset).wait_recv()
        where = self.later(level, unit)
        free = [d for d in self.order[level + 1 :] if isinstance(where[d], slice)]
        total = math.prod(self.sizes[d] for d in free)
        rows, columns = self.block
        last = level == self.levels - 1

        def one(number, carry):
            at = dict(where)
            rest = number
            for d in free:
                at[d] = rest % self.sizes[d]
                rest = rest // self.sizes[d]
            spot = tuple(at[d] for d in self.layouts[level + 1])
            at[dim] = self.place[dim]
            mine = tuple(at[d] for d in self.layouts[level])

            def body(piece):
                if not last and size == 2:
                    self.landing[level][(0,) + spot + (piece,)] += self.held(level)[mine + (piece,)]
                    return
                result = self.held(level)[mine + (piece,)].astype(f32)
                for offset in range(1, size):
                    result = result + self.landing[level][(offset - 1,) + spot + (piece,)].astype(f32)
                if last:
                    self.target[(piece,)] = result.astype(self.target.dtype)
                else:
                    self.landing[level][(0,) + spot + (piece,)] = result.astype(self.landing[level].dtype)

            each_piece(rows, columns, body)
            return carry

        if total == 1:
            one(0, 0)
        else:
            lax.fori_loop(0, total, one, 0)
        if not last and not (self.line and level == self.levels - 2):
            ahead, rest = unit[0], unit[1:]
            if ahead is None:
                offsets = range(1, self.sizes[self.order[level + 1]])
            else:
                offsets = [ahead] if ahead else []
            for offset in offsets:
                self.launch(level + 1, rest, offset)

    def line_copy(self, number):
        step, slot = ((1, 0), (2, 1), (3, 2), (3, 3), (2, 4))[number]
        level = self.levels - 1
        block = self.held(level).at[along_line(self.place["s"], step)]
        landed = self.landing[level].at[slot]
        device = peer_of("s", 1) if number < 3 else across_middle()
        return remote_to(block, landed, self.line_sems.at[0, number], self.line_sems.at[1, number], device)

    def line_step(self, step, ends=True, middles=True):
        level = self.levels - 1
        middle = is_middle(self.place["s"])
        rows, columns = self.block
        held, landing = self.held(level), self.landing[level]
        position = along_line(self.place["s"], step)

        def pass_on():
            arrived = (0, 3, 1, 2)[step]
            self.line_copy(arrived).wait_recv()

            def body(piece):
                held[(position, piece)] += landing[(arrived, piece)]

            each_piece(rows, columns, body)
            self.line_copy((0, 0, 4, 3)[step]).start()

        if step:
            if ends:
                pl.when(jnp.logical_not(middle))(lambda: self.line_copy(step - 1).start())
            if middles:
                pl.when(middle)(pass_on)
            return

        self.line_copy(0).wait_recv()

        @pl.when(middle)
        def _():
            self.line_copy(4).wait_recv()

            def body(piece):
                result = held[(position, piece)].astype(f32) + landing[(0, piece)].astype(f32)
                self.target[(piece,)] = (result + landing[(4, piece)].astype(f32)).astype(
                    self.target.dtype
                )

            each_piece(rows, columns, body)

        @pl.when(jnp.logical_not(middle))
        def _():
            def body(piece):
                result = held[(position, piece)].astype(f32) + landing[(0, piece)].astype(f32)
                self.target[(piece,)] = result.astype(self.target.dtype)

            each_piece(rows, columns, body)

    def events(self):
        found = []
        for number, unit in enumerate(self.units[0]):
            for offset in range(1, self.sizes[self.order[0]]):
                found.append(
                    (-1 + 0.001 * number, functools.partial(self.launch, 0, unit, offset))
                )
        spread = 4 if self.line else 1
        for level in range(self.levels - self.line):
            count = len(self.units[level])
            for number, unit in enumerate(self.units[level]):
                late = 0
                if self.order[-1] == "a":
                    late = 20 if level == self.levels - 1 else 0.9
                found.append(
                    (late + level + spread * number / count, functools.partial(self.reduce, level, unit))
                )
        if self.line:
            for number, step in enumerate((3, 2, 1, 0)):
                found.append(
                    (self.levels - 1 + number + 0.5, functools.partial(self.line_step, step))
                )
        return found

    def finish(self):
        for transfer in self.sent:
            self.copy(*transfer).wait_send()
        if self.line:
            self.line_copy(0).wait_send()
            middle = is_middle(self.place["s"])

            @pl.when(middle)
            def _():
                for number in (3, 4):
                    self.line_copy(number).wait_send()

            @pl.when(jnp.logical_not(middle))
            def _():
                for number in (1, 2):
                    self.line_copy(number).wait_send()


class MemoryGather:
    def __init__(self, memory, sizes):
        self.value = memory
        self.sizes = sizes
        self.out = jax.ShapeDtypeStruct((sizes["s"], 2) + memory.shape[1:], memory.dtype)
        self.in_spec = pl.BlockSpec(memory_space=pltpu.VMEM)
        self.out_spec = pl.BlockSpec(memory_space=pl.ANY)
        rows = sizes["s"]
        self.scratch = [
            pltpu.SemaphoreType.DMA((2, rows)),
            pltpu.SemaphoreType.DMA((2, rows)),
            pltpu.SemaphoreType.DMA((2, rows, 2)),
            pltpu.SemaphoreType.DMA,
        ]
        self.peers = [("s", offset) for offset in range(1, rows)] + [("h", 1), ("c", 1)]

    def prepare(self, refs, place):
        self.source, self.target, self.along, self.across, self.core, self.local = refs
        self.place = place
        self.mine = place["s"] % 2 == place["c"]

    def row(self, offset):
        return flip(self.place["s"], offset)

    def along_copy(self, offset, arriving):
        to = self.row(offset)
        spot = to if arriving else self.place["s"]
        return remote(
            self.source.at[self.place["s"] // 2 if arriving else to // 2],
            self.target.at[spot, self.place["h"]],
            self.along.at[0, offset],
            self.along.at[1, offset],
            "s",
            offset,
        )

    def across_copy(self, offset, arriving):
        h = self.place["h"]
        own = self.target.at[self.row(offset), 1 - h if arriving else h]
        if offset == 0 and not arriving:
            source = self.source.at[self.place["s"] // 2]
        else:
            source = own
        return remote(source, own, self.across.at[0, offset], self.across.at[1, offset], "h", 1)

    def core_copy(self, offset, other):
        h = self.place["h"]
        own = self.target.at[self.row(offset), 1 - h if other else h]
        source = self.source.at[self.place["s"] // 2] if offset == 0 and not other else own
        return remote(source, own, self.core.at[0, offset, other], self.core.at[1, offset, other], "c", 1)

    def events(self):
        rows = self.sizes["s"]

        def first():
            for offset in range(1, rows):
                @pl.when(self.row(offset) % 2 == self.place["c"])
                def _():
                    self.along_copy(offset, False).start()

            @pl.when(self.mine)
            def _():
                pltpu.make_async_copy(
                    self.source.at[self.place["s"] // 2],
                    self.target.at[self.place["s"], self.place["h"]],
                    self.local,
                ).start()
                self.across_copy(0, False).start()
                self.core_copy(0, 0).start()

        def arrival(offset):
            @pl.when(self.mine)
            def _():
                self.along_copy(offset, True).wait_recv()
                self.across_copy(offset, False).start()
                self.core_copy(offset, 0).start()

        def other(offset):
            @pl.when(self.mine)
            def _():
                self.across_copy(offset, True).wait_recv()
                self.core_copy(offset, 1).start()

        found = [(0.05, first)]
        for offset in range(1, rows):
            found.append((offset + 0.05, functools.partial(arrival, offset)))
        for offset in range(rows):
            found.append((rows + offset, functools.partial(other, offset)))
        return found

    def finish(self):
        rows = self.sizes["s"]
        for offset in range(1, rows):
            @pl.when(self.row(offset) % 2 == self.place["c"])
            def _():
                self.along_copy(offset, False).wait_send()

        @pl.when(self.mine)
        def _():
            pltpu.make_async_copy(
                self.source.at[self.place["s"] // 2],
                self.target.at[self.place["s"], self.place["h"]],
                self.local,
            ).wait()
            for offset in range(rows):
                self.across_copy(offset, False).wait_send()
                for other in range(2):
                    self.core_copy(offset, other).wait_send()

        @pl.when(jnp.logical_not(self.mine))
        def _():
            for offset in range(rows):
                for other in range(2):
                    self.core_copy(offset, other).wait_recv()


class MemoryScatter:
    def __init__(self, value, sizes):
        self.value = value
        self.sizes = sizes
        rows = sizes["s"]
        self.block = value.shape[2:]
        self.out = jax.ShapeDtypeStruct((2,) + self.block, f32)
        self.in_spec = pl.BlockSpec(memory_space=pltpu.VMEM)
        self.out_spec = pl.BlockSpec(memory_space=pltpu.VMEM)
        self.scratch = [
            pltpu.VMEM(value.shape, value.dtype),
            pltpu.VMEM((rows,) + self.block, value.dtype),
            pltpu.VMEM((2,) + self.block, value.dtype),
            pltpu.SemaphoreType.DMA((2, rows, 2)),
            pltpu.SemaphoreType.DMA((2, rows)),
            pltpu.SemaphoreType.DMA((2, rows)),
        ]
        self.peers = [("s", offset) for offset in range(1, rows)] + [("h", 1), ("c", 1)]

    def prepare(self, refs, place):
        self.source, self.target = refs[0], refs[1]
        self.summed, self.halved, self.landed, self.core, self.across, self.along = refs[2:]
        self.place = place
        self.mine = place["s"] % 2 == place["c"]

    def row(self, offset):
        return flip(self.place["s"], offset)

    def core_copy(self, offset, other):
        h = self.place["h"]
        spot = (self.row(offset), flip(h, 1) if other else h)
        return remote(
            self.source.at[spot],
            self.summed.at[spot],
            self.core.at[0, offset, other],
            self.core.at[1, offset, other],
            "c",
            1,
        )

    def across_copy(self, offset):
        row = self.row(offset)
        return remote(
            self.summed.at[row, flip(self.place["h"], 1)],
            self.halved.at[row],
            self.across.at[0, offset],
            self.across.at[1, offset],
            "h",
            1,
        )

    def along_copy(self, offset, arriving):
        to = self.row(offset)
        return remote(
            self.halved.at[to],
            self.landed.at[to // 2 if arriving else self.place["s"] // 2],
            self.along.at[0, offset],
            self.along.at[1, offset],
            "s",
            offset,
        )

    def events(self):
        rows = self.sizes["s"]
        high, wide = self.block
        orders = list(range(1, rows))[::-1] + [0]

        def first():
            @pl.when(jnp.logical_not(self.mine))
            def _():
                for other in (1, 0):
                    for offset in orders:
                        self.core_copy(offset, other).start()

        def level(offset, other):
            @pl.when(self.mine)
            def _():
                self.core_copy(offset, other).wait_recv()
                h = self.place["h"]
                spot = (self.row(offset), flip(h, 1) if other else h)

                def body(piece):
                    total = self.summed[spot + (piece,)].astype(f32) + self.source[
                        spot + (piece,)
                    ].astype(f32)
                    self.summed[spot + (piece,)] = total.astype(self.summed.dtype)

                each_piece(high, wide, body)
                if other:
                    self.across_copy(offset).start()

        def last(offset):
            @pl.when(self.mine)
            def _():
                self.across_copy(offset).wait_recv()
                row = self.row(offset)

                def body(piece):
                    total = self.halved[(row, piece)].astype(f32) + self.summed[
                        (row, self.place["h"], piece)
                    ].astype(f32)
                    self.halved[(row, piece)] = total.astype(self.halved.dtype)
                    if offset == 0:
                        self.target[(self.place["s"] // 2, piece)] = total

                each_piece(high, wide, body)
                if offset:
                    self.along_copy(offset, False).start()

        found = [(-0.95, first)]
        for number, offset in enumerate(orders):
            found.append((0.05 + 0.1 * number, functools.partial(level, offset, 1)))
        for number, offset in enumerate(orders):
            found.append((0.55 + 0.1 * number, functools.partial(level, offset, 0)))
        for number, offset in enumerate(orders):
            found.append((1.05 + 0.2 * number, functools.partial(last, offset)))
        return found

    def finish(self):
        rows = self.sizes["s"]
        high, wide = self.block
        for offset in range(1, rows):
            @pl.when(self.row(offset) % 2 == self.place["c"])
            def _():
                self.along_copy(offset, True).wait_recv()
                number = self.row(offset) // 2

                def body(piece):
                    self.target[(number, piece)] = self.landed[(number, piece)].astype(f32)

                each_piece(high, wide, body)

        @pl.when(self.mine)
        def _():
            for offset in range(rows):
                self.across_copy(offset).wait_send()
            for offset in range(1, rows):
                self.along_copy(offset, False).wait_send()

        @pl.when(jnp.logical_not(self.mine))
        def _():
            for offset in range(rows):
                for other in range(2):
                    self.core_copy(offset, other).wait_send()


def peers_of(jobs):
    peers = []
    for job in jobs:
        for peer in job.peers:
            if peer not in peers:
                peers.append(peer)
    return peers


def greet(peers, place):
    barrier = pltpu.get_barrier_semaphore()
    middle = is_middle(place["s"])
    awaited = 0
    for peer in peers:
        if peer[0] == "m":
            @pl.when(middle)
            def _():
                pl.semaphore_signal(
                    barrier, inc=1, device_id=across_middle(), device_id_type=pl.DeviceIdType.MESH
                )
            continue
        awaited += 1
        pl.semaphore_signal(
            barrier, inc=1, device_id=peer_of(*peer), device_id_type=pl.DeviceIdType.MESH
        )
    return awaited


def welcome(peers, place, awaited):
    barrier = pltpu.get_barrier_semaphore()
    middle = is_middle(place["s"])
    if ("m", 1) in peers:
        @pl.when(middle)
        def _():
            pl.semaphore_wait(barrier, awaited + 1)

        @pl.when(jnp.logical_not(middle))
        def _():
            pl.semaphore_wait(barrier, awaited)
    else:
        pl.semaphore_wait(barrier, awaited)


def exchange(name, collective_id, jobs):
    values = [getattr(job, "values", None) or [job.value] for job in jobs]
    peers = peers_of(jobs)

    def kernel(*refs):
        total = sum(len(held) for held in values)
        results = refs[total : total + len(jobs)]
        scratch = refs[total + len(jobs) :]
        begin = offset = 0
        place = coordinates()
        awaited = greet(peers, place)
        for number, job in enumerate(jobs):
            end = begin + len(values[number])
            ins = refs[begin:end]
            if hasattr(job, "pack"):
                job.pack(ins, scratch[offset])
                ins, offset = (scratch[offset],), offset + 1
            mine = len(job.scratch) - hasattr(job, "pack")
            job.prepare(tuple(ins) + (results[number],) + tuple(scratch[offset : offset + mine]), place)
            begin, offset = end, offset + mine
        welcome(peers, place, awaited)
        events = [event for job in jobs for event in job.events()]
        for _, act in sorted(events, key=lambda event: event[0]):
            act()
        for job in jobs:
            job.finish()

    return pl.pallas_call(
        kernel,
        name=name,
        out_shape=tuple(job.out for job in jobs),
        in_specs=[job.in_spec for job, held in zip(jobs, values) for _ in held],
        out_specs=tuple(job.out_spec for job in jobs),
        scratch_shapes=[item for job in jobs for item in job.scratch],
        compiler_params=pltpu.CompilerParams(
            collective_id=collective_id, has_side_effects=True, vmem_limit_bytes=60 * 1024 * 1024
        ),
    )(*[value for held in values for value in held])


def packed(block):
    rows, columns = block.shape
    if rows % 16 == 0:
        return block
    return block.reshape(16, rows * columns // 16)


def bucket_edges():
    edges = []
    for target in range(1, 32):
        if target < 16:
            edges.append(target)
        else:
            found = 0
            for distance in range(16, 4096):
                value = 16 + int(math.log(distance / 16.0) / math.log(8.0) * 16.0)
                if found == 0 and value >= target:
                    found = distance
            edges.append(found)
    return edges


def gelu_tanh(value):
    return (
        0.5
        * value
        * (1.0 + jnp.tanh(0.7978845608028654 * (value + 0.044715 * value * value * value)))
    )


def dot(left, right):
    return jnp.einsum("sd,df->sf", left, right, preferred_element_type=f32)


def dot_t(left, right):
    return jnp.einsum("sf,df->sd", left, right, preferred_element_type=f32)


def t_dot(left, right):
    return jnp.einsum("sd,sf->df", left, right, preferred_element_type=f32)


def distance_table(seq):
    edges = np.array(bucket_edges())
    distance = (-np.arange(seq)) % seq
    bucket = (distance[:, None] >= edges[None, :]).sum(axis=1)
    return (np.arange(128)[:, None] == bucket[None, :]).astype(np.float32)


def mm(left, right):
    return lax.dot_general(left, right, (((1,), (0,)), ((), ())), preferred_element_type=f32)


def mm_t(left, right):
    return lax.dot_general(left, right, (((1,), (1,)), ((), ())), preferred_element_type=f32)


def t_mm(left, right):
    return lax.dot_general(left, right, (((0,), (0,)), ((), ())), preferred_element_type=f32)


def inverse_rms(rows):
    return lax.rsqrt(jnp.mean(rows * rows, axis=-1, keepdims=True) + eps)


def rms_back(rows, gain, slope):
    inverse = inverse_rms(rows)
    unit = rows * inverse
    scaled = slope * gain
    back = inverse * (scaled - unit * jnp.mean(unit * scaled, axis=-1, keepdims=True))
    return back, jnp.sum(slope * unit, axis=0, keepdims=True)


def lanes_of(shape):
    return lax.broadcasted_iota(jnp.int32, shape, len(shape) - 1)


def one_half(pair, half):
    inside = (lanes_of(pair.shape) // HEAD) == half
    return jnp.where(inside, pair, jnp.zeros_like(pair))


def both_halves(pair):
    return jnp.concatenate([one_half(pair, 0), one_half(pair, 1)], axis=0)


def joined_rows(stacked):
    rows = stacked.shape[0] // 2
    return joined(stacked[:rows], stacked[rows:])


def joined(first, second):
    return jnp.where(lanes_of(first.shape) < HEAD, first, second)


def pair_of(ref, start, pair):
    return ref[:, start + 2 * HEAD * pair : start + 2 * HEAD * (pair + 1)]


FF_STEP = 256


def in_steps(total, step, body, further=0):
    def one(number, carry):
        here = pl.ds(pl.multiple_of(number * step, step), step)
        if further:
            body(here, pl.ds(pl.multiple_of(number * step + further, step), step))
        else:
            body(here)
        return carry

    lax.fori_loop(0, total // step, one, 0)


class Fetch:
    def __init__(self, sources, targets, sems):
        self.copies = [
            pltpu.make_async_copy(source, target, sems.at[number])
            for number, (source, target) in enumerate(zip(sources, targets))
        ]
        self.targets = targets
        self.ready = set()
        for copy in self.copies:
            copy.start()

    def __getitem__(self, number):
        if number not in self.ready:
            self.ready.add(number)
            self.copies[number].wait()
        return self.targets[number]


def enter_kernel(resid_ref, part_c_ref, query_ref, kv_ref, normed_ref, gains_ref):
    row = lax.broadcasted_iota(jnp.int32, (16, GAIN_PAD), 0)
    pick = (row == lanes_of((16, GAIN_PAD))).astype(bf16)
    gains = mm_t(pick, part_c_ref[:, 5 * HD : 5 * HD + GAIN_PAD])
    gains_ref[...] = gains
    resid = resid_ref[...]
    normed = (resid * inverse_rms(resid) * gains[0:1]).astype(bf16)
    normed_ref[...] = normed
    query_ref[...] = mm(normed, part_c_ref[:, :HD]).astype(bf16)
    kv_ref[...] = mm(normed, part_c_ref[:, HD : 3 * HD]).astype(bf16)


def biased_scores(scores, row, first, length):
    bias = pltpu.roll(jnp.broadcast_to(row, scores.shape), 0, 1, stride=1, stride_axis=0)
    query_pos = first + lax.broadcasted_iota(jnp.int32, scores.shape, 0)
    key_pos = lanes_of(scores.shape)
    mask = (key_pos <= query_pos) & (key_pos < length)
    return jnp.where(mask, scores + bias, masked_score)


def softmax_parts(scores):
    highest = jnp.max(scores, axis=-1, keepdims=True)
    total = highest + jnp.log(jnp.sum(jnp.exp(scores - highest), axis=-1, keepdims=True))
    return total, jnp.exp(scores - total)


def query_span(lengths_ref, rows):
    place = coordinates()
    length = lengths_ref[place["s"] // 2, 2 * place["a"] + place["s"] % 2]
    return (2 * place["h"] + place["c"]) * rows, length


def forward_kernel(
    lengths_ref,
    query_ref,
    kv_ref,
    resid0_ref,
    gains_ref,
    table_ref,
    bias_ref,
    memory_hbm,
    part_a_hbm,
    part_b_hbm,
    part_c_hbm,
    attn_self_ref,
    total_self_ref,
    resid1_ref,
    normed_cross_ref,
    query_cross_ref,
    mem_kv_ref,
    attn_cross_ref,
    total_cross_ref,
    resid2_ref,
    normed_ff_ref,
    gate_up_ref,
    hidden_ref,
    resid3_ref,
    final_ref,
    memory_ref,
    part_a_ref,
    part_b_ref,
    part_c_ref,
    sems,
):
    fetched = Fetch(
        (part_c_hbm, part_b_hbm, memory_hbm, part_a_hbm),
        (part_c_ref, part_b_ref, memory_ref, part_a_ref),
        sems,
    )
    first, length = query_span(lengths_ref, query_ref.shape[0])
    ff = hidden_ref.shape[1]
    bias_rows = pltpu.roll(mm(bias_ref[...], table_ref[:BUCKETS, :]), first, 1)
    lanes = lanes_of(total_self_ref.shape)
    totals = jnp.zeros(total_self_ref.shape, f32)
    for pair in range(HEADS // 2):
        keys, values = pair_of(kv_ref, 0, pair), pair_of(kv_ref, HD, pair)
        outputs = []
        for half in range(2):
            number = 2 * pair + half
            scores = mm_t(one_half(pair_of(query_ref, 0, pair), half), keys)
            scores = biased_scores(scores, bias_rows[number : number + 1], first, length)
            total, shares = softmax_parts(scores)
            totals = jnp.where(lanes == number, total, totals)
            outputs.append(mm(shares.astype(bf16), values))
        attn_self_ref[:, 2 * HEAD * pair : 2 * HEAD * (pair + 1)] = joined(*outputs).astype(bf16)
    total_self_ref[...] = totals

    part_c = fetched[0]
    resid1 = resid0_ref[...] + mm_t(attn_self_ref[...], part_c[:, 3 * HD : 4 * HD])
    resid1_ref[...] = resid1
    normed = (resid1 * inverse_rms(resid1) * gains_ref[1:2]).astype(bf16)
    normed_cross_ref[...] = normed
    query_cross_ref[...] = mm(normed, part_c[:, 4 * HD : 5 * HD]).astype(bf16)

    part_b = fetched[1]
    memory = fetched[2]
    step = min(256, memory.shape[0])

    def project(number, carry):
        rows = pl.ds(pl.multiple_of(number * step, step), step)
        mem_kv_ref[rows, :] = mm(memory[rows, :], part_b[:, ff : ff + 2 * HD]).astype(bf16)
        return carry

    lax.fori_loop(0, memory.shape[0] // step, project, 0)
    total_cross_ref[...] = jnp.zeros(total_cross_ref.shape, f32)

    def cross_pair(place, place_v):
        keys, values = mem_kv_ref[:, place], mem_kv_ref[:, place_v]
        outputs = []
        for half in range(2):
            scores = mm_t(one_half(query_cross_ref[:, place], half), keys)
            total, shares = softmax_parts(scores)
            number = place.start // HEAD + half
            total_cross_ref[...] = jnp.where(lanes == number, total, total_cross_ref[...])
            outputs.append(mm(shares.astype(bf16), values))
        attn_cross_ref[:, place] = joined(*outputs).astype(bf16)

    in_steps(HD, 2 * HEAD, cross_pair, HD)
    resid2 = resid1_ref[...] + mm_t(attn_cross_ref[...], part_b[:, ff + 2 * HD :])
    resid2_ref[...] = resid2
    normed_ff_ref[...] = (resid2 * inverse_rms(resid2) * gains_ref[2:3]).astype(bf16)

    part_a = fetched[3]

    def feed(here, there):
        gate = mm(normed_ff_ref[...], part_a[:, here])
        up = mm(normed_ff_ref[...], part_a[:, there])
        gate_up_ref[:, here] = gate
        gate_up_ref[:, there] = up
        hidden_ref[:, here] = (gelu_tanh(gate) * up).astype(bf16)

    in_steps(ff, FF_STEP, feed, ff)
    resid3 = resid2_ref[...] + mm_t(hidden_ref[...], part_b[:, :ff])
    resid3_ref[...] = resid3
    final_ref[...] = (resid3 * inverse_rms(resid3) * gains_ref[3:4]).astype(bf16)


def attention_back(query, keys, values, scores, total, out_slope):
    shares = jnp.exp(scores - total)
    share_slope = mm_t(out_slope, values)
    inner = jnp.sum(shares * share_slope, axis=-1, keepdims=True)
    score_slope = shares * (share_slope - inner)
    rounded = score_slope.astype(bf16)
    return (
        rounded,
        mm(rounded, keys),
        t_mm(rounded, query),
        t_mm(shares.astype(bf16), out_slope),
    )


def backward_kernel(
    lengths_ref,
    slope_ref,
    resid3_ref,
    hidden_ref,
    gate_up_ref,
    normed_ff_ref,
    resid2_ref,
    attn_cross_ref,
    query_cross_ref,
    total_cross_ref,
    normed_cross_ref,
    resid1_ref,
    attn_self_ref,
    query_ref,
    kv_ref,
    total_self_ref,
    gains_ref,
    table_ref,
    bias_ref,
    mem_kv_hbm,
    memory_hbm,
    part_a_hbm,
    part_b_hbm,
    part_c_hbm,
    grad_a_hbm,
    grad_b_hbm,
    memory_part_hbm,
    grad_c_ref,
    query_slope_ref,
    kv_slope_ref,
    grad1_ref,
    norm_grads_ref,
    bias_grad_ref,
    mem_kv_ref,
    memory_ref,
    part_a_ref,
    part_b_ref,
    part_c_ref,
    grad_a_ref,
    grad_b_ref,
    memory_part_ref,
    gate_up_slope_ref,
    cross_query_slope_ref,
    cross_kv_slope_ref,
    sems,
    out_sems,
):
    fetched = Fetch(
        (part_b_hbm, part_a_hbm, mem_kv_hbm, memory_hbm, part_c_hbm),
        (part_b_ref, part_a_ref, mem_kv_ref, memory_ref, part_c_ref),
        sems,
    )
    first, length = query_span(lengths_ref, query_ref.shape[0])
    ff = hidden_ref.shape[1]
    width = resid3_ref.shape[1]
    norm_grads_ref[...] = jnp.zeros_like(norm_grads_ref)

    grad3, norm_grad = rms_back(resid3_ref[...], gains_ref[3:4], slope_ref[...])
    norm_grads_ref[3:4] = norm_grad
    down_in = grad3.astype(bf16)
    part_b = fetched[0]

    def feed_back(here, there):
        hidden_slope = mm(down_in, part_b[:, here])
        gate, up = gate_up_ref[:, here], gate_up_ref[:, there]
        inner = jnp.tanh(0.7978845608028654 * (gate + 0.044715 * gate * gate * gate))
        activated = 0.5 * gate * (1.0 + inner)
        steep = 0.5 * (1.0 + inner) + 0.5 * gate * (1.0 - inner * inner) * (
            0.7978845608028654 * (1.0 + 3.0 * 0.044715 * gate * gate)
        )
        gate_up_slope_ref[:, here] = (hidden_slope * up * steep).astype(bf16)
        gate_up_slope_ref[:, there] = (hidden_slope * activated).astype(bf16)
        grad_b_ref[:, here] = t_mm(down_in, hidden_ref[:, here]).astype(bf16)

    in_steps(ff, FF_STEP, feed_back, ff)
    part_a = fetched[1]
    back, norm_grad = rms_back(
        resid2_ref[...], gains_ref[2:3], mm_t(gate_up_slope_ref[...], part_a[...])
    )
    norm_grads_ref[2:3] = norm_grad
    grad2 = grad3 + back

    def gate_up_grad(here):
        grad_a_ref[:, here] = t_mm(normed_ff_ref[...], gate_up_slope_ref[:, here]).astype(bf16)

    in_steps(2 * ff, 2 * FF_STEP, gate_up_grad)
    copy_a = pltpu.make_async_copy(grad_a_ref, grad_a_hbm, out_sems.at[0])
    copy_a.start()

    cross_in = grad2.astype(bf16)
    grad_b_ref[:, ff + 2 * HD :] = t_mm(cross_in, attn_cross_ref[...]).astype(bf16)
    out_slope = mm(cross_in, part_b[:, ff + 2 * HD :]).astype(bf16)
    mem_kv = fetched[2]
    cross_query_slope_ref[...] = out_slope

    def cross_pair_back(place, place_v):
        keys, values = mem_kv[:, place], mem_kv[:, place_v]
        lanes = lanes_of(total_cross_ref.shape)
        totals = [
            jnp.sum(
                jnp.where(lanes == place.start // HEAD + half, total_cross_ref[...], 0.0),
                axis=-1,
                keepdims=True,
            )
            for half in range(2)
        ]
        query = both_halves(query_cross_ref[:, place])
        part = attention_back(
            query,
            keys,
            values,
            mm_t(query, keys),
            jnp.concatenate(totals, axis=0),
            both_halves(cross_query_slope_ref[:, place]),
        )
        cross_query_slope_ref[:, place] = joined_rows(part[1]).astype(bf16)
        cross_kv_slope_ref[:, place] = part[2].astype(bf16)
        cross_kv_slope_ref[:, place_v] = part[3].astype(bf16)

    in_steps(HD, 2 * HEAD, cross_pair_back, HD)
    memory = fetched[3]

    def memory_weights(here, there):
        grad_b_ref[:, there] = t_mm(memory[...], cross_kv_slope_ref[:, here]).astype(bf16)

    in_steps(2 * HD, FF_STEP, memory_weights, ff)
    copy_b = pltpu.make_async_copy(grad_b_ref, grad_b_hbm, out_sems.at[1])
    copy_b.start()
    step = min(256, memory.shape[0])

    def project(number, carry):
        rows = pl.ds(pl.multiple_of(number * step, step), step)
        memory_part_ref[rows, :] = mm_t(
            cross_kv_slope_ref[rows, :], part_b[:, ff : ff + 2 * HD]
        ).astype(bf16)
        return carry

    lax.fori_loop(0, memory.shape[0] // step, project, 0)
    copy_m = pltpu.make_async_copy(memory_part_ref, memory_part_hbm, out_sems.at[2])
    copy_m.start()
    part_c = fetched[4]
    query_slope = cross_query_slope_ref[...]
    grad_c_ref[:, HD : 2 * HD] = t_mm(normed_cross_ref[...], query_slope).astype(bf16)
    back, norm_grad = rms_back(
        resid1_ref[...], gains_ref[1:2], mm_t(query_slope, part_c[:, 4 * HD : 5 * HD])
    )
    norm_grads_ref[1:2] = norm_grad
    grad1 = grad2 + back
    grad1_ref[...] = grad1

    self_in = grad1.astype(bf16)
    grad_c_ref[:, :HD] = t_mm(self_in, attn_self_ref[...]).astype(bf16)
    out_slope = mm(self_in, part_c[:, 3 * HD : 4 * HD]).astype(bf16)
    bias_rows = pltpu.roll(mm(bias_ref[...], table_ref[:BUCKETS, :]), first, 1)
    bias_sums = jnp.zeros((8, bias_rows.shape[1]), f32)
    rows, seq = query_ref.shape[0], kv_ref.shape[0]
    reverse = lax.broadcasted_iota(jnp.int32, (rows, rows), 0) + lanes_of((rows, rows)) == rows - 1
    reverse = reverse.astype(bf16)
    for pair in range(HEADS // 2):
        place = slice(2 * HEAD * pair, 2 * HEAD * (pair + 1))
        place_v = slice(HD + 2 * HEAD * pair, HD + 2 * HEAD * (pair + 1))
        keys, values = kv_ref[:, place], kv_ref[:, place_v]
        query = both_halves(query_ref[:, place])
        products = mm_t(query, keys)
        scores, totals = [], []
        for half in range(2):
            number = 2 * pair + half
            scores.append(
                biased_scores(
                    products[half * rows : (half + 1) * rows],
                    bias_rows[number : number + 1],
                    first,
                    length,
                )
            )
            totals.append(total_self_ref[:, number : number + 1])
        part = attention_back(
            query,
            keys,
            values,
            jnp.concatenate(scores, axis=0),
            jnp.concatenate(totals, axis=0),
            both_halves(out_slope[:, place]),
        )
        for half in range(2):
            turned = mm(reverse, part[0][half * rows : (half + 1) * rows])
            turned = pltpu.roll(turned, 0, 1, stride=1, stride_axis=0)
            where = lax.broadcasted_iota(jnp.int32, bias_sums.shape, 0) == 2 * pair + half
            bias_sums = jnp.where(where, jnp.sum(turned, axis=0, keepdims=True), bias_sums)
        query_slope_ref[:, place] = joined_rows(part[1]).astype(bf16)
        kv_slope_ref[:, place] = part[2].astype(bf16)
        kv_slope_ref[:, place_v] = part[3].astype(bf16)
    bias_sums = pltpu.roll(bias_sums, 2 * seq + 1 - rows - first, 1)
    high = bias_sums.astype(bf16)
    rest = bias_sums - high.astype(f32)
    middle = rest.astype(bf16)
    low = (rest - middle.astype(f32)).astype(bf16)
    table = table_ref[...]
    bias_grad_ref[...] = mm_t(high, table) + (mm_t(middle, table) + mm_t(low, table))
    copy_a.wait()
    copy_b.wait()
    copy_m.wait()


def leave_kernel(
    query_slope_ref,
    kv_slope_ref,
    normed_ref,
    resid0_ref,
    grad1_ref,
    gains_ref,
    norm_grads_ref,
    part_grad_ref,
    part_c_ref,
    grad_c_ref,
    grad0_ref,
):
    normed = normed_ref[...]
    query_slope, kv_slope = query_slope_ref[...], kv_slope_ref[...]
    slope = mm_t(query_slope, part_c_ref[:, :HD]) + mm_t(kv_slope, part_c_ref[:, HD : 3 * HD])
    back, norm_grad = rms_back(resid0_ref[...], gains_ref[0:1], slope)
    grad0_ref[...] = (grad1_ref[...] + back).astype(bf16)
    grad_c_ref[:, :HD] = t_mm(normed, query_slope).astype(bf16)
    grad_c_ref[:, HD : 3 * HD] = t_mm(normed, kv_slope).astype(bf16)
    grad_c_ref[:, 3 * HD : 5 * HD] = part_grad_ref[...]
    where = lax.broadcasted_iota(jnp.int32, norm_grads_ref.shape, 0) == 0
    norm_grads = jnp.where(where, norm_grad, norm_grads_ref[...]).astype(bf16)
    row = lax.broadcasted_iota(jnp.int32, (norm_grads.shape[0], GAIN_PAD), 0)
    spread = (row == lanes_of(row.shape)).astype(bf16)
    grad_c_ref[:, 5 * HD :] = t_mm(norm_grads, spread).astype(bf16)


def local_kernel(name, kernel, outs, args, spaces="", out_spaces="", scratch=()):
    space = {"v": pltpu.VMEM, "s": pltpu.SMEM, "a": pl.ANY}
    spaces = spaces or "v" * len(args)
    out_spaces = out_spaces or "v" * len(outs)
    return pl.pallas_call(
        kernel,
        name=name,
        out_shape=tuple(jax.ShapeDtypeStruct(shape, dtype) for shape, dtype in outs),
        in_specs=[pl.BlockSpec(memory_space=space[letter]) for letter in spaces],
        out_specs=tuple(pl.BlockSpec(memory_space=space[letter]) for letter in out_spaces),
        scratch_shapes=list(scratch),
        compiler_params=pltpu.CompilerParams(vmem_limit_bytes=60 * 1024 * 1024),
    )(*args)


def pack_columns(pieces, block):
    start = 0
    for piece in pieces:
        if piece.shape[0] == 1:
            break
        block[:, start : start + piece.shape[1]] = piece[...]
        start += piece.shape[1]
    gains = pieces[-4:]
    if gains[0].shape[0] == 1:
        rows = gains[0].shape[1]
        where = lax.broadcasted_iota(jnp.int32, (16, rows), 0)
        stacked = jnp.zeros((16, rows), f32)
        for number, gain in enumerate(gains):
            stacked = jnp.where(where == number, gain[...].astype(f32), stacked)
        pick = lax.broadcasted_iota(jnp.int32, (16, GAIN_PAD), 0) == lanes_of((16, GAIN_PAD))
        block[:, start:] = t_mm(stacked.astype(bf16), pick.astype(bf16)).astype(bf16)


def pack_rows(pieces, block):
    start = 0
    for piece in pieces:
        block[start : start + piece.shape[0], :] = piece[...]
        start += piece.shape[0]


def pack_ids(pieces, block):
    block[...] = jnp.zeros_like(block)
    for number, piece in enumerate(pieces):
        micro, _, count = piece.shape
        for which in range(micro):
            block[micro * number + which : micro * number + which + 1, :count] = piece[which]


def tail_kernel(lengths_ref, *refs):
    (a_ref, b_ref, c_ref, small_ref, memory_ref, embedding_ref, head_ref), outs = refs[:7], refs[7:]
    (loss_ref, memory_out, embedding_out, head_out, bias_out), outs = outs[:5], outs[5:]
    memory_out[...] = memory_ref[...]
    embedding_out[...] = embedding_ref[...]
    head_out[...] = head_ref[...]
    total = jnp.sum(small_ref[...], axis=0)
    count = 0
    for first in range(lengths_ref.shape[0]):
        for second in range(lengths_ref.shape[1]):
            count = count + lengths_ref[first, second]
    loss_ref[...] = jnp.sum(total[8:], keepdims=True) / count.astype(f32)
    bias_out[...] = total[:HEADS, :BUCKETS]
    for ref, pieces in ((a_ref, outs[:2]), (b_ref, outs[2:6]), (c_ref, outs[6:11])):
        start = 0
        for piece in pieces:
            piece[...] = ref[:, start : start + piece.shape[1]]
            start += piece.shape[1]
    turned = jnp.transpose(c_ref[:, 5 * HD :])
    for number, piece in enumerate(outs[11:]):
        piece[...] = turned[number : number + 1]


def vocabulary(name, collective_id, final_rows, head_rows, targets, lengths, sizes):
    span, width = head_rows.shape
    tok_dev = final_rows.shape[0]
    lines = sizes["s"]
    blocks = 2 * lines
    step_rows = min(512, span)
    gather = Gather(final_rows, "sh", "sh", sizes)
    direct = DirectGather(jax.ShapeDtypeStruct((blocks, tok_dev), f32), sizes)
    scatter = Scatter(jax.ShapeDtypeStruct((lines, 2, tok_dev, width), bf16), "hs", "sh", sizes)
    jobs = (gather, direct, scatter)
    peers = peers_of(jobs)

    def kernel(*refs):
        final_ref, head_ref, targets_ref, lengths_ref = refs[:4]
        slope_ref, head_part_ref, loss_ref = refs[4:7]
        states, totals, own_total, logits, turned, value, picked_ref, log_total_ref = refs[7:15]
        rest = refs[15:]
        place = coordinates()
        awaited = greet(peers, place)
        counts = [len(job.scratch) for job in jobs]
        gather.prepare((final_ref, states) + rest[: counts[0]], place)
        direct.prepare((own_total, totals) + rest[counts[0] : counts[0] + counts[1]], place)
        scatter.prepare((value, slope_ref) + rest[counts[0] + counts[1] :], place)
        welcome(peers, place, awaited)
        position = place["s"]
        half = position // 2

        def spot(token, other):
            far, second = token // 2, token % 2
            near_row = position + second * (1 - 2 * (position % 2))
            far_row = 2 - half + second * (1 - 2 * half)
            row = near_row + far * (far_row - near_row)
            side = place["h"] + other * (1 - 2 * place["h"])
            return row, side, 2 * row + side

        def chunk_of(number):
            return pl.ds(pl.multiple_of(number * step_rows, step_rows), step_rows)

        def hits(number, target):
            rows = lax.broadcasted_iota(jnp.int32, (step_rows, tok_dev), 0) + number * step_rows
            return rows == target

        def bring(step):
            token, other = step // 2, step % 2
            if step == 0:
                gather.line_first()
                gather.launch((1, (0,), 1))
                gather.local.wait()
                gather.local_done = True
            if other:
                gather.arrive((1, (token,), 1))
                if token + 1 < lines:
                    gather.line_next(token + 1)
                    gather.launch((1, (token + 1,), 1))

        def forward_step(step, carry):
            for number in range(blocks):
                pl.when(step == number)(functools.partial(bring, number))
            row, side, number = spot(step // 2, step % 2)
            block = states[row, side]
            target = targets_ref[pl.ds(number, 1), :]

            def scores(chunk, best):
                found = mm_t(head_ref[chunk_of(chunk), :], block)
                logits[number, chunk_of(chunk), :] = found
                return jnp.maximum(best, jnp.max(found, axis=0, keepdims=True))

            count = span // step_rows
            best = lax.fori_loop(0, count, scores, jnp.full((1, tok_dev), -3.0e38, f32))

            def spread(chunk, sums):
                found = logits[number, chunk_of(chunk), :]
                hit = hits(chunk, target)
                return (
                    sums[0] + jnp.sum(jnp.exp(found - best), axis=0, keepdims=True),
                    sums[1] + jnp.sum(jnp.where(hit, found, 0.0), axis=0, keepdims=True),
                )

            zero = jnp.zeros((1, tok_dev), f32)
            total, picked = lax.fori_loop(0, count, spread, (zero, zero))
            own_total[pl.ds(number, 1), :] = best + jnp.log(total)
            picked_ref[pl.ds(number, 1), :] = picked
            return carry

        lax.fori_loop(0, blocks, forward_step, 0)
        direct.begin()
        direct.receive()
        parts = totals[...].reshape((blocks,) + own_total.shape)
        top = jnp.max(parts, axis=0)
        log_total_ref[...] = top + jnp.log(jnp.sum(jnp.exp(parts - top[None]), axis=0))

        def backward_step(step, carry):
            row, side, number = spot(lines - 1 - step // 2, 1 - step % 2)
            lanes = pl.ds(pl.multiple_of(number * tok_dev, tok_dev), tok_dev)
            target = targets_ref[pl.ds(number, 1), :]
            log_total = log_total_ref[pl.ds(number, 1), :]
            length = lengths_ref[row // 2, 2 * place["a"] + row % 2]
            spots = (2 * side + place["c"]) * tok_dev + lax.broadcasted_iota(jnp.int32, (1, tok_dev), 1)
            live = jnp.where(spots < length, 1.0, 0.0)
            shown = log_total * (1 - jnp.minimum(2 * position + place["h"], 1)).astype(f32)
            loss_ref[pl.ds(number, 1), :] = live * (shown - picked_ref[pl.ds(number, 1), :])

            def slopes(chunk, inner):
                share = jnp.exp(logits[number, chunk_of(chunk), :] - log_total)
                slope = (share - jnp.where(hits(chunk, target), 1.0, 0.0)) * live
                turned[chunk_of(chunk), lanes] = slope.astype(bf16)
                return inner

            lax.fori_loop(0, span // step_rows, slopes, 0)
            value[row, side] = t_mm(turned[:, lanes], head_ref[...]).astype(bf16)
            for which in range(lines):
                pl.when(step == 2 * which)(
                    functools.partial(scatter.launch, 0, (lines - 1 - which,), 1)
                )
            return carry

        lax.fori_loop(0, blocks, backward_step, 0)
        for token in (3, 2):
            scatter.reduce(0, (token,))
            scatter.line_step(token, middles=False)

        def head_chunk(number, carry):
            rows = pl.ds(pl.multiple_of(number * 256, 256), 256)
            every = states[...].reshape(blocks * tok_dev, width)
            head_part_ref[rows, :] = mm(turned[rows, :], every).astype(bf16)
            return carry

        lax.fori_loop(0, span // 256, head_chunk, 0)
        scatter.line_step(3, ends=False)
        scatter.line_step(2, ends=False)
        for token in (1, 0):
            scatter.reduce(0, (token,))
            scatter.line_step(token)
        gather.finish()
        direct.drain()
        scatter.finish()

    vmem = pl.BlockSpec(memory_space=pltpu.VMEM)
    rows = jax.ShapeDtypeStruct((blocks, tok_dev), f32)
    return pl.pallas_call(
        kernel,
        name=name,
        out_shape=(scatter.out, jax.ShapeDtypeStruct(head_rows.shape, bf16), rows),
        in_specs=[vmem] * 3 + [pl.BlockSpec(memory_space=pltpu.SMEM)],
        out_specs=(vmem,) * 3,
        scratch_shapes=[
            pltpu.VMEM(gather.out.shape, bf16),
            pltpu.VMEM(direct.out.shape, f32),
            pltpu.VMEM((blocks, tok_dev), f32),
            pltpu.VMEM((blocks, span, tok_dev), f32),
            pltpu.VMEM((span, blocks * tok_dev), bf16),
            pltpu.VMEM(scatter.value.shape, bf16),
            pltpu.VMEM((blocks, tok_dev), f32),
            pltpu.VMEM((blocks, tok_dev), f32),
        ]
        + [item for job in jobs for item in job.scratch],
        compiler_params=pltpu.CompilerParams(
            collective_id=collective_id, has_side_effects=True, vmem_limit_bytes=60 * 1024 * 1024
        ),
    )(final_rows, head_rows, targets, lengths)


def opening(name, collective_id, weights, embedding, ids, memory, head, sizes):
    voc_dev, width = embedding.shape
    n_gy = 2 * sizes["s"]
    n_gx = 2 * sizes["a"]
    span = n_gx * voc_dev
    lines = sizes["s"]
    micro, _, seq_dev = ids[0].shape
    tok_dev = 2 * seq_dev
    table = Gather(embedding, "ac", "ac", sizes)
    codes = DirectGather(jax.ShapeDtypeStruct((8, 128), jnp.int32), sizes, "shc")
    memories = MemoryGather(memory, sizes)
    heads = Gather(head, "ac", "ac", sizes, "", 20)
    sums = Scatter(jax.ShapeDtypeStruct((lines, 2, tok_dev, width), bf16), "hs", "sh", sizes)
    jobs = list(weights) + [table, codes, memories, heads, sums]
    peers = peers_of(jobs)
    operands = [list(job.values) for job in weights] + [[embedding], list(ids), [memory], [head]]
    flat = [value for group in operands for value in group]

    def kernel(*refs):
        ins = list(refs[: len(flat)])
        outs = list(refs[len(flat) : len(flat) + 8])
        rest = list(refs[len(flat) + 8 :])
        place = coordinates()
        awaited = greet(peers, place)

        def take(source, count):
            taken = tuple(source[:count])
            del source[:count]
            return taken

        rows_ref, value, code, ids_ref = (rest.pop(0) for _ in range(4))
        for job in weights:
            pieces = take(ins, len(job.values))
            block = rest.pop(0)
            job.pack(pieces, block)
            job.prepare((block, outs.pop(0)) + take(rest, len(job.scratch) - 1), place)
        table.prepare((ins.pop(0), rows_ref) + take(rest, len(table.scratch)), place)
        pack_ids(take(ins, 2), code)
        local_ref, target_ref = outs.pop(0), outs.pop(0)
        codes.prepare((code, ids_ref) + take(rest, len(codes.scratch)), place)
        memories.prepare((ins.pop(0), outs.pop(0)) + take(rest, len(memories.scratch)), place)
        heads.prepare((ins.pop(0), outs.pop(0)) + take(rest, len(heads.scratch)), place)
        sums.prepare((value, outs.pop(0)) + take(rest, len(sums.scratch)), place)
        welcome(peers, place, awaited)

        def tables_here():
            codes.receive()
            table.local.wait()
            table.local_done = True
            for transfer in table.transfers:
                table.arrive(transfer)

        def pick(token):
            row = along_line(place["s"], token)

            def one(other, carry):
                side = place["h"] + (1 - other) * (1 - 2 * place["h"])
                indices = []
                for kind, ref in enumerate((local_ref, target_ref)):
                    line = pl.ds(micro * kind + row // 2, 1)
                    index = jnp.concatenate(
                        [
                            ids_ref[2 * side + place["c"], which, row % 2, line, :][:, :seq_dev]
                            for which in range(2)
                        ],
                        axis=1,
                    )
                    shard = index // voc_dev
                    held = shard % n_gy == 2 * place["s"] + place["h"]
                    index = jnp.where(held, shard // n_gy * voc_dev + index % voc_dev, -1)
                    ref[pl.ds(2 * row + side, 1), :] = index
                    indices.append(index)
                index = indices[0]
                at = lax.broadcasted_iota(jnp.int32, (span, tok_dev), 0) == index
                every = rows_ref[...].reshape(span, width)
                value[row, side] = t_mm(jnp.where(at, 1.0, 0.0).astype(bf16), every).astype(bf16)
                pl.when(other == 0)(functools.partial(sums.launch, 0, (token,), 1))
                return carry

            lax.fori_loop(0, 2, one, 0)

        events = [event for job in list(weights) + [memories, heads] for event in job.events()]
        events.append((-2, codes.begin))
        for transfer in table.transfers:
            level, unit, _ = transfer
            key = -1 if level == 0 else TABLE_KEY if unit[0] else 0.1
            events.append((key, functools.partial(table.launch, transfer)))
        events.append((TABLE_KEY + 0.05, tables_here))
        for number, token in enumerate((3, 2, 1, 0)):
            events.append((PICK_KEY + PICK_STEP * number, functools.partial(pick, token)))
            key = SUM_KEY + SUM_STEP * number
            events.append((key, functools.partial(sums.reduce, 0, (token,))))
            if token:
                events.append((key + 0.01, functools.partial(sums.line_step, token, middles=False)))
                events.append((LINE_KEY + SUM_STEP * number, functools.partial(sums.line_step, token, ends=False)))
            else:
                events.append((LINE_KEY + SUM_STEP * number, functools.partial(sums.line_step, token)))
        for _, act in sorted(events, key=lambda event: event[0]):
            act()
        for job in jobs:
            if job is codes:
                job.drain()
            else:
                job.finish()

    vmem = pl.BlockSpec(memory_space=pltpu.VMEM)
    anywhere = pl.BlockSpec(memory_space=pl.ANY)
    scratch = [
        pltpu.VMEM(table.out.shape, bf16),
        pltpu.VMEM(sums.value.shape, bf16),
        pltpu.VMEM((8, 128), jnp.int32),
        pltpu.VMEM(codes.out.shape, jnp.int32),
    ]
    places = jax.ShapeDtypeStruct((n_gy, tok_dev), jnp.int32)
    return pl.pallas_call(
        kernel,
        name=name,
        out_shape=tuple(job.out for job in weights)
        + (places, places, memories.out, heads.out, sums.out),
        in_specs=[vmem] * len(flat),
        out_specs=(anywhere,) * 3 + (vmem, vmem, anywhere, anywhere, vmem),
        scratch_shapes=scratch + [item for job in jobs for item in job.scratch],
        compiler_params=pltpu.CompilerParams(
            collective_id=collective_id, has_side_effects=True, vmem_limit_bytes=60 * 1024 * 1024
        ),
    )(*flat)


TABLE_KEY, PICK_KEY, PICK_STEP, SUM_KEY, SUM_STEP, LINE_KEY = 0.55, 0.65, 0.05, 1.3, 0.3, 1.9


def per_device(
    target_ids,
    labels,
    lengths,
    memory,
    embedding,
    head,
    gain_self,
    w_query,
    w_key,
    w_value,
    w_out,
    relative_bias,
    gain_cross,
    c_query,
    c_key,
    c_value,
    c_out,
    gain_ff,
    w_gate,
    w_up,
    w_down,
    gain_final,
):
    micro = target_ids.shape[0]
    seq_dev = target_ids.shape[2]
    mem_dev = memory.shape[2]
    voc_dev, width = embedding.shape
    ff = w_gate.shape[1]
    n_gx = lax.axis_size("gx")
    n_gy = lax.axis_size("gy")
    column = lax.axis_index("gy")
    row_group = lax.axis_index("gx")
    devices = n_gx * n_gy
    sizes = {"a": n_gx // 2, "c": 2, "s": n_gy // 2, "h": 2}
    assert sizes["s"] == 2 * micro
    place = coordinates()
    seq = seq_dev * n_gy
    plane = sizes["s"] * seq
    tok_dev = seq // 4
    tokens = plane // 2
    span = n_gx * voc_dev
    merged = "" if sizes["a"] == 2 else "ashc"

    rows_dev = width // devices
    whole_tiles = rows_dev % 16 == 0
    groups = (
        (w_gate, w_up),
        (w_down, c_key, c_value, c_out),
        (w_query, w_key, w_value, w_out, c_query),
    )
    gains = (gain_self, gain_cross, gain_ff, gain_final)
    widths = [sum(piece.shape[1] for piece in group) for group in groups]
    widths[2] += GAIN_PAD
    orders = ("shac", "shac", "sahc")
    ways_back = ("cahs", "chas", "chas")
    if whole_tiles:
        operands = list(groups)
        operands[2] += tuple(gain.reshape(1, rows_dev) for gain in gains)
        weights = [
            PackedGather(
                group,
                jax.ShapeDtypeStruct((rows_dev, count), bf16),
                pack_columns,
                order,
                "acsh",
                sizes,
                merged,
            )
            for group, count, order in zip(operands, widths, orders)
        ]
    else:
        shards = [jnp.concatenate(group, axis=1) for group in groups]
        columns_of = jnp.pad(jnp.stack(gains, axis=1), ((0, 0), (0, GAIN_PAD - 4)))
        shards[2] = jnp.concatenate([shards[2], columns_of], axis=1)
        weights = [
            Gather(packed(part), order, "acsh", sizes, merged) for part, order in zip(shards, orders)
        ]
    small_tables = whole_tiles and span <= 2048 and tok_dev == 128
    if small_tables:
        part_a, part_b, part_c, local_ids, targets, memory_all, head_rows, resid0 = opening(
            "start",
            0,
            weights,
            embedding,
            (target_ids, labels),
            memory.reshape(micro, mem_dev, width),
            head,
            sizes,
        )
    else:
        part_a, part_b, part_c, embed_rows, ids, memory_all = exchange(
            "gather_weights",
            0,
            weights
            + [
                Gather(embedding, "ac", "ac", sizes, "", 20),
                PackedGather(
                    (target_ids, labels),
                    jax.ShapeDtypeStruct((8, 128), jnp.int32),
                    pack_ids,
                    "shc",
                    "shc",
                    sizes,
                    "shc",
                ),
                MemoryGather(memory.reshape(micro, mem_dev, width), sizes),
            ],
        )
    part_a, part_b, part_c = (
        full.reshape(width, count) for full, count in zip((part_a, part_b, part_c), widths)
    )
    memory_all = memory_all.reshape(n_gy * mem_dev, width)
    if small_tables:
        local_ids = local_ids.reshape(tokens)
    else:
        ids = ids[..., : 2 * micro, :seq_dev].reshape(n_gy, 2, 2, micro, seq_dev)
        ids = ids.transpose(2, 3, 1, 0, 4).reshape(2, sizes["s"] * 2, 2, tok_dev)
        ids = lax.dynamic_index_in_dim(ids, place["c"], axis=2, keepdims=False).reshape(2, tokens)

        def local_of(index):
            shard = index // voc_dev
            return jnp.where(shard % n_gy == column, shard // n_gy * voc_dev + index % voc_dev, -1)

        local_ids = local_of(ids[0])
        targets = local_of(ids[1])
    columns = jnp.arange(span, dtype=jnp.int32)

    tok_layout = (sizes["s"], 2, tok_dev, width)
    if not small_tables:
        chosen = (local_ids[:, None] == columns[None, :]).astype(bf16)
        picked_rows = dot(chosen, embed_rows.reshape(span, width)).astype(bf16)
        resid0, head_rows = exchange(
            "rows",
            1,
            [
                Scatter(picked_rows.reshape(tok_layout), "hs", "sh", sizes),
                Gather(head, "ac", "ac", sizes, "", 20),
            ],
        )
    head_rows = head_rows.reshape(span, width)

    plane_lengths = lax.dynamic_slice_in_dim(lengths, 2 * place["a"], 2, axis=1).reshape(-1)
    table = jnp.asarray(distance_table(seq), bf16)
    query_self, own_kv, normed_self, gain_rows = local_kernel(
        "enter",
        enter_kernel,
        [((tok_dev, HD), bf16), ((tok_dev, 2 * HD), bf16), ((tok_dev, width), bf16), ((16, width), f32)],
        [resid0, part_c],
    )
    (self_kv_all,) = exchange("self_keys", 2, [Gather(own_kv, "hc", "hc", sizes)])
    self_kv_all = self_kv_all.reshape(seq, 2 * HD)
    rows_f32, rows_bf16, rows_heads = ((tok_dev, width), f32), ((tok_dev, width), bf16), ((tok_dev, HD), bf16)
    totals_shape = ((tok_dev, 128), f32)
    all_mem = n_gy * mem_dev
    (
        attn_self,
        total_self,
        resid1,
        normed_cross,
        query_cross,
        mem_kv,
        attn_cross,
        total_cross,
        resid2,
        normed_ff,
        gate_up,
        hidden,
        resid3,
        final_rows,
    ) = local_kernel(
        "forward",
        forward_kernel,
        [
            rows_heads,
            totals_shape,
            rows_f32,
            rows_bf16,
            rows_heads,
            ((all_mem, 2 * HD), bf16),
            rows_heads,
            totals_shape,
            rows_f32,
            rows_bf16,
            ((tok_dev, 2 * ff), f32),
            ((tok_dev, ff), bf16),
            rows_f32,
            rows_bf16,
        ],
        [lengths, query_self, self_kv_all, resid0, gain_rows, table, relative_bias]
        + [memory_all, part_a, part_b, part_c],
        "svvvvvvaaaa",
        scratch=[pltpu.VMEM(full.shape, bf16) for full in (memory_all, part_a, part_b, part_c)]
        + [pltpu.SemaphoreType.DMA((4,))],
    )

    if small_tables:
        final_slope, head_part, loss_rows = vocabulary(
            "vocabulary", 3, final_rows, head_rows, targets, lengths, sizes
        )
    else:
        index = jnp.arange(tokens, dtype=jnp.int32)
        position = (2 * (index // tok_dev % 2) + place["c"]) * tok_dev + index % tok_dev
        alive = (position < jnp.repeat(plane_lengths, 2 * tok_dev)).astype(f32)
        (states,) = exchange("final_rows", 3, [Gather(final_rows, "sh", "sh", sizes, merged)])
        states = states.reshape(tokens, width)
        logits = dot_t(states, head_rows)
        highest = jnp.max(logits, axis=1)
        own_total = highest + jnp.log(jnp.sum(jnp.exp(logits - highest[:, None]), axis=1))
        (totals,) = exchange("totals", 4, [DirectGather(own_total.reshape(tokens // 128, 128), sizes)])
        totals = totals.reshape(n_gy, tokens)
        top = jnp.max(totals, axis=0)
        log_total = top + jnp.log(jnp.sum(jnp.exp(totals - top[None]), axis=0))
        hit = columns[None, :] == targets[:, None]
        picked = jnp.sum(jnp.where(hit, logits, 0.0), axis=1)
        slope = jnp.exp(logits - log_total[:, None]) - hit.astype(f32)
        slope = (slope * alive[:, None]).astype(bf16)
        head_part = t_dot(slope, states).astype(bf16)
        final_part = dot(slope, head_rows).astype(bf16)
        (final_slope,) = exchange(
            "final_slopes", 5, [Scatter(final_part.reshape(tok_layout), "hs", "sh", sizes)]
        )
        loss_rows = alive * (jnp.where(column == 0, log_total, 0.0) - picked)
        loss_rows = loss_rows.reshape(tokens // 128, 128)

    grad_a, grad_b, memory_part, part_grad_c, query_slope, kv_slope, grad1, norm_grads, bias_grad = (
        local_kernel(
            "backward",
            backward_kernel,
            [
                (part_a.shape, bf16),
                (part_b.shape, bf16),
                (memory_all.shape, bf16),
                ((width, 2 * HD), bf16),
                rows_heads,
                ((seq, 2 * HD), bf16),
                rows_f32,
                (gain_rows.shape, f32),
                ((8, 128), f32),
            ],
            [lengths, final_slope, resid3, hidden, gate_up, normed_ff, resid2, attn_cross]
            + [query_cross, total_cross, normed_cross, resid1, attn_self, query_self, self_kv_all]
            + [total_self, gain_rows, table, relative_bias, mem_kv, memory_all, part_a, part_b, part_c],
            "s" + "v" * 18 + "a" * 5,
            "aaa" + "v" * 6,
            [
                pltpu.VMEM(full.shape, bf16)
                for full in (mem_kv, memory_all, part_a, part_b, part_c, part_a, part_b, memory_all)
            ]
            + [
                pltpu.VMEM((tok_dev, 2 * ff), bf16),
                pltpu.VMEM((tok_dev, HD), bf16),
                pltpu.VMEM(mem_kv.shape, bf16),
                pltpu.SemaphoreType.DMA((5,)),
                pltpu.SemaphoreType.DMA((3,)),
            ],
        )
    )
    (kv_slope,) = exchange(
        "key_slopes",
        6,
        [Scatter(kv_slope.reshape(2, 2, tok_dev, 2 * HD), "ch", "hc", sizes, "", bf16)],
    )
    grad_c, grad0 = local_kernel(
        "leave",
        leave_kernel,
        [(part_c.shape, bf16), rows_bf16],
        [query_slope, kv_slope, normed_self, resid0, grad1, gain_rows, norm_grads, part_grad_c, part_c],
    )
    slopes, head_grad = exchange(
        "row_slopes",
        7,
        [
            Gather(grad0, "sh", "sh", sizes, merged),
            Scatter(head_part.reshape(sizes["a"], 2, voc_dev, width), "ca", "ac", sizes),
        ],
    )
    embed_part = t_dot(
        (local_ids[:, None] == columns[None, :]).astype(bf16), slopes.reshape(tokens, width)
    ).astype(bf16)
    sums = (grad_a, grad_b, grad_c)
    device_layout = (sizes["a"], 2, sizes["s"], 2)
    blocks = [part.reshape(device_layout + packed_shape(part, devices)) for part in sums]
    grad_a, grad_b, grad_c, embedding_grad, memory_grad, small = exchange(
        "scatter_weights",
        8,
        [
            Scatter(part, order, "acsh", sizes, merged)
            for part, order in zip(blocks, ways_back)
        ]
        + [
            Scatter(embed_part.reshape(sizes["a"], 2, voc_dev, width), "ca", "ac", sizes),
            MemoryScatter(memory_part.reshape(sizes["s"], 2, mem_dev, width), sizes),
            PackedGather(
                (bias_grad, loss_rows),
                jax.ShapeDtypeStruct((16, 128), f32),
                pack_rows,
                "shac",
                "acsh",
                sizes,
                "ashc",
            ),
        ],
    )
    small = small.reshape(devices, 16, 128)
    memory_grad = memory_grad.reshape(micro, 1, mem_dev, width)
    if whole_tiles:
        pieces = [piece.shape[1] for group in groups for piece in group]
        outs = [
            ((1, 1), f32),
            (memory_grad.shape, f32),
            (embedding_grad.shape, f32),
            (head_grad.shape, f32),
            ((HEADS, BUCKETS), f32),
        ]
        outs += [((rows_dev, count), f32) for count in pieces] + [((1, rows_dev), f32)] * 4
        results = local_kernel(
            "tail",
            tail_kernel,
            outs,
            [lengths, grad_a, grad_b, grad_c, small, memory_grad, embedding_grad, head_grad],
            "s" + "v" * 7,
        )
        loss, memory_grad, embedding_grad, head_grad, bias_total = results[:5]
        loss = loss.reshape(())
        cut = results[5:16]
        gain_out = [gain.reshape(rows_dev) for gain in results[16:]]
    else:
        grad_a, grad_b, grad_c = (
            grad.reshape(rows_dev, count) for grad, count in zip((grad_a, grad_b, grad_c), widths)
        )
        small = jnp.sum(small, axis=0)
        loss = jnp.sum(small[8:]) / jnp.sum(lengths).astype(f32)
        bias_total = small[:HEADS, :BUCKETS]
        cut = []
        for grad, group in zip((grad_a, grad_b, grad_c), groups):
            start = 0
            for piece in group:
                cut.append(grad[:, start : start + piece.shape[1]])
                start += piece.shape[1]
        gain_out = [grad_c[:, 5 * HD + number] for number in range(4)]
    gate_grad, up_grad, down_grad, c_key_grad, c_value_grad, c_out_grad = cut[:6]
    query_grad, key_grad, value_grad, out_grad, c_query_grad = cut[6:]
    return (
        loss,
        memory_grad,
        embedding_grad,
        head_grad,
        gain_out[0],
        query_grad,
        key_grad,
        value_grad,
        out_grad,
        bias_total,
        gain_out[1],
        c_query_grad,
        c_key_grad,
        c_value_grad,
        c_out_grad,
        gain_out[2],
        gate_grad,
        up_grad,
        down_grad,
        gain_out[3],
    )


def packed_shape(part, count):
    rows, columns = part.shape[0] // count, part.shape[1]
    if rows % 16 == 0:
        return (rows, columns)
    return (16, rows * columns // 16)


def solution(mesh):
    placed = (
        P(None, "gx", "gy"),
        P(None, "gx", "gy"),
        P(),
        P(None, "gx", "gy", None),
        P(("gx", "gy"), None),
        P(("gx", "gy"), None),
        P(("gx", "gy")),
        P(("gx", "gy"), None),
        P(("gx", "gy"), None),
        P(("gx", "gy"), None),
        P(("gx", "gy"), None),
        P(),
        P(("gx", "gy")),
        P(("gx", "gy"), None),
        P(("gx", "gy"), None),
        P(("gx", "gy"), None),
        P(("gx", "gy"), None),
        P(("gx", "gy")),
        P(("gx", "gy"), None),
        P(("gx", "gy"), None),
        P(("gx", "gy"), None),
        P(("gx", "gy")),
    )
    return jax.shard_map(
        per_device,
        mesh=mesh,
        in_specs=placed,
        out_specs=(
            P(),
            P(None, "gx", "gy", None),
            P(("gx", "gy"), None),
            P(("gx", "gy"), None),
            P(("gx", "gy")),
            P(("gx", "gy"), None),
            P(("gx", "gy"), None),
            P(("gx", "gy"), None),
            P(("gx", "gy"), None),
            P(),
            P(("gx", "gy")),
            P(("gx", "gy"), None),
            P(("gx", "gy"), None),
            P(("gx", "gy"), None),
            P(("gx", "gy"), None),
            P(("gx", "gy")),
            P(("gx", "gy"), None),
            P(("gx", "gy"), None),
            P(("gx", "gy"), None),
            P(("gx", "gy")),
        ),
        check_vma=False,
    )
```

```python
import functools
import itertools
import math

import jax
import jax.numpy as jnp
import numpy as np
from jax import lax
from jax.experimental import pallas as pl
from jax.experimental.pallas import tpu as pltpu
from jax.sharding import PartitionSpec as P

HEADS = 6
HEAD = 64
HD = HEADS * HEAD
BUCKETS = 32
GAIN_PAD = 128

eps = 1e-06
masked_score = -1000000000.0
bf16 = jnp.bfloat16
f32 = jnp.float32


def flip(position, offset):
    moved = position
    weight = 1
    while weight <= offset:
        if offset & weight:
            moved = moved + weight * (1 - 2 * ((position // weight) % 2))
        weight *= 2
    return moved


def coordinates():
    gx, gy = lax.axis_index("gx"), lax.axis_index("gy")
    return {"a": gx // 2, "c": gx % 2, "s": gy // 2, "h": gy % 2}


def peer_of(dim, offset):
    gx, gy = lax.axis_index("gx"), lax.axis_index("gy")
    if dim == "a":
        return {"gx": 2 * flip(gx // 2, offset) + gx % 2}
    if dim == "c":
        return {"gx": flip(gx, 1)}
    if dim == "plane":
        s, h, c = offset + (0,) * (3 - len(offset))
        there = {"gy": 2 * flip(gy // 2, s) + flip(gy % 2, h)}
        if c:
            there["gx"] = flip(gx, 1)
        return there
    if dim == "s":
        return {"gy": 2 * flip(gy // 2, offset) + gy % 2}
    return {"gy": flip(gy, 1)}


def remote(source, target, send, recv, dim, offset):
    return pltpu.make_async_remote_copy(
        src_ref=source,
        dst_ref=target,
        send_sem=send,
        recv_sem=recv,
        device_id=peer_of(dim, offset),
        device_id_type=pl.DeviceIdType.MESH,
    )


def along_line(position, step):
    half = position // 2
    return (position, flip(position, 1), 2 - half, 3 - 3 * half)[step]


def is_middle(position):
    return (position + 1) // 2 == 1


def across_middle():
    gy = lax.axis_index("gy")
    return {"gy": 2 * (3 - gy // 2) + gy % 2}


def spot_of(dim, position, offset):
    return along_line(position, offset) if dim == "s" else flip(position, offset)


def remote_to(source, target, send, recv, device):
    return pltpu.make_async_remote_copy(
        src_ref=source,
        dst_ref=target,
        send_sem=send,
        recv_sem=recv,
        device_id=device,
        device_id_type=pl.DeviceIdType.MESH,
    )


def each_piece(rows, columns, body, width=16384):
    step = rows
    while step * columns > width and step % 32 == 0:
        step //= 2
    if step == rows:
        body(slice(None))
        return

    def piece(number, carry):
        body(pl.ds(pl.multiple_of(number * step, step), step))
        return carry

    lax.fori_loop(0, rows // step, piece, 0)


LINE_PEERS = [("s", 1), ("m", 1)]


class Gather:
    def __init__(self, block, order, layout, sizes, merged="", late=0):
        self.value = block
        self.late = late
        self.order, self.layout, self.sizes, self.merged = order, layout, sizes, merged
        self.out = jax.ShapeDtypeStruct(tuple(sizes[d] for d in layout) + block.shape, block.dtype)
        self.in_spec = pl.BlockSpec(memory_space=pltpu.VMEM)
        self.out_spec = pl.BlockSpec(memory_space=pl.ANY)
        self.transfers = []
        for level, dim in enumerate(order):
            ranges = [(None,) if d in merged else range(sizes[d]) for d in order[:level]]
            for unit in itertools.product(*ranges):
                for offset in range(1, sizes[dim]):
                    self.transfers.append((level, unit, offset))
        self.index = {transfer: number for number, transfer in enumerate(self.transfers)}
        count = len(self.transfers)
        self.line = order[0] == "s"
        self.scratch = [
            pltpu.SemaphoreType.DMA((count,)),
            pltpu.SemaphoreType.DMA((count,)),
            pltpu.SemaphoreType.DMA,
            pltpu.SemaphoreType.DMA((5,)),
        ]
        self.peers = [(d, offset) for d in order for offset in range(1, sizes[d]) if d != "s"]
        if self.line:
            self.peers += LINE_PEERS

    def prepare(self, refs, place):
        self.source, self.target, self.send, self.recv, self.local_sem, self.line_send = refs
        self.place = place
        self.local = pltpu.make_async_copy(
            self.source, self.target.at[tuple(place[d] for d in self.layout)], self.local_sem
        )
        self.local.start()
        self.local_done = False
        self.arrived = set()
        self.sent = []

    def region(self, level, unit, offset):
        where = dict(self.place)
        for d, moved in zip(self.order[:level], unit):
            where[d] = slice(None) if moved is None else spot_of(d, self.place[d], moved)
        if offset:
            dim = self.order[level]
            where[dim] = spot_of(dim, self.place[dim], offset)
        return self.target.at[tuple(where[d] for d in self.layout)]

    def needs(self, level, unit):
        if level == 0:
            return []
        last, before = unit[-1], unit[:-1]
        if last is None:
            dim = self.order[level - 1]
            return self.needs(level - 1, before) + [
                (level - 1, before, offset) for offset in range(1, self.sizes[dim])
            ]
        if last == 0:
            return self.needs(level - 1, before)
        return [(level - 1, before, last)]

    def arrive(self, transfer):
        if transfer in self.arrived:
            return
        self.arrived.add(transfer)
        level, unit, offset = transfer
        number = self.index[transfer]
        there = self.region(level, unit, offset)
        if self.line and level == 0:
            offset = 1
        remote(
            there, there, self.send.at[number], self.recv.at[number], self.order[level], offset
        ).wait_recv()

    def line_copy(self, number):
        held, there = ((0, 1), (0, 2), (1, 3), (2, 2), (3, 3))[number]
        target = self.region(0, (), held)
        device = peer_of("s", 1) if number in (0, 3, 4) else across_middle()
        recv = self.recv.at[self.index[(0, (), there)]]
        source = target if held else self.source
        return remote_to(source, target, self.line_send.at[number], recv, device)

    def line_first(self):
        self.line_copy(0).start()

        @pl.when(is_middle(self.place["s"]))
        def _():
            self.line_copy(1).start()

    def line_next(self, step):
        self.arrive((0, (), step))

        @pl.when(is_middle(self.place["s"]))
        def _():
            self.line_copy(step + 1).start()

    def copy(self, transfer):
        level, unit, offset = transfer
        number = self.index[transfer]
        target = self.region(level, unit, 0)
        own = all(moved == 0 for moved in unit)
        return remote(
            self.source if own else target,
            target,
            self.send.at[number],
            self.recv.at[number],
            self.order[level],
            offset,
        )

    def launch(self, transfer):
        level, unit, offset = transfer
        for need in self.needs(level, unit):
            self.arrive(need)
        if None in unit and not self.local_done:
            self.local.wait()
            self.local_done = True
        self.copy(transfer).start()
        self.sent.append(transfer)

    def events(self):
        found = []
        if self.line:
            found.append((0, self.line_first))
            for step in (1, 2, 3):
                found.append((step, functools.partial(self.line_next, step)))
        for transfer in self.transfers:
            level, unit, offset = transfer
            if self.line and level == 0:
                continue
            key = 0.1 * level + 0.01 * offset
            for d, moved in zip(self.order, unit):
                key += self.sizes[d] - 1 if moved is None else moved
            if self.late and self.needs(level, unit):
                key += self.late
            found.append((key, functools.partial(self.launch, transfer)))
        return found

    def finish(self):
        if not self.local_done:
            self.local.wait()
        for transfer in self.transfers:
            self.arrive(transfer)
        for transfer in self.sent:
            self.copy(transfer).wait_send()
        if self.line:
            self.line_copy(0).wait_send()

            @pl.when(is_middle(self.place["s"]))
            def _():
                for number in range(1, 5):
                    self.line_copy(number).wait_send()


class Work:
    def __init__(self, values, out, act, key, columns=None):
        self.values, self.act, self.key = list(values), act, key
        self.columns = columns or [None] * len(self.values)
        self.out = jax.ShapeDtypeStruct(*out)
        self.in_spec = self.out_spec = pl.BlockSpec(memory_space=pl.ANY)
        shapes = [
            value.shape if cut is None else (value.shape[0], cut[1])
            for value, cut in zip(self.values, self.columns)
        ]
        self.scratch = [pltpu.VMEM(shape, value.dtype) for shape, value in zip(shapes, self.values)]
        self.scratch += [pltpu.VMEM(*out), pltpu.SemaphoreType.DMA((len(shapes) + 1,))]
        self.peers = []

    def prepare(self, refs, place):
        count = len(self.values)
        self.held, self.result, sems = refs[count + 1 : 2 * count + 1], refs[-2], refs[-1]
        self.copies = []
        for number, (source, cut, held) in enumerate(zip(refs, self.columns, self.held)):
            source = source if cut is None else source.at[:, cut[0] : cut[0] + cut[1]]
            self.copies.append(pltpu.make_async_copy(source, held, sems.at[number]))
            self.copies[-1].start()
        self.back = pltpu.make_async_copy(self.result, refs[count], sems.at[count])

    def events(self):
        return [(self.key, self.run)]

    def run(self):
        for copy in self.copies:
            copy.wait()
        self.act(self.held, self.result)
        self.back.start()

    def finish(self):
        self.back.wait()


class PackedGather(Gather):
    def __init__(self, values, block, pack, *args):
        super().__init__(block, *args)
        self.values, self.pack = values, pack
        self.scratch = [pltpu.VMEM(block.shape, block.dtype)] + self.scratch


class DirectGather:
    def __init__(self, block, sizes, dims="sh"):
        self.value = block
        self.dims = dims
        shape = tuple(sizes[d] for d in dims)
        self.out = jax.ShapeDtypeStruct(shape + block.shape, block.dtype)
        self.in_spec = pl.BlockSpec(memory_space=pltpu.VMEM)
        self.out_spec = pl.BlockSpec(memory_space=pltpu.VMEM)
        self.offsets = list(itertools.product(*(range(size) for size in shape)))[1:]
        count = len(self.offsets)
        self.scratch = [pltpu.SemaphoreType.DMA((count,)), pltpu.SemaphoreType.DMA((count,))]
        self.peers = [("plane", offset) for offset in self.offsets]

    def prepare(self, refs, place):
        self.source, self.target, self.send, self.recv = refs
        self.place = place

    def copy(self, number, arriving):
        offset = self.offsets[number]
        spot = tuple(
            flip(self.place[d], moved) if arriving else self.place[d] for d, moved in zip(self.dims, offset)
        )
        return remote_to(
            self.source,
            self.target.at[spot],
            self.send.at[number],
            self.recv.at[number],
            peer_of("plane", offset),
        )

    def events(self):
        return [(0, self.begin)]

    def begin(self):
        for number in range(len(self.offsets)):
            self.copy(number, False).start()
        self.target[tuple(self.place[d] for d in self.dims)] = self.source[...]

    def finish(self):
        self.receive()
        self.drain()

    def receive(self):
        for number in range(len(self.offsets)):
            self.copy(number, True).wait_recv()

    def drain(self):
        for number in range(len(self.offsets)):
            self.copy(number, False).wait_send()


class Scatter:
    def __init__(self, value, order, layout, sizes, merged="", out_dtype=f32):
        self.value = value
        self.order, self.layout, self.sizes, self.merged = order, layout, sizes, merged
        self.block = value.shape[len(layout) :]
        self.out = jax.ShapeDtypeStruct(self.block, out_dtype)
        self.in_spec = pl.BlockSpec(memory_space=pltpu.VMEM)
        self.out_spec = pl.BlockSpec(memory_space=pltpu.VMEM)
        self.line = order[-1] == "s"
        self.levels = len(order)
        self.units = []
        self.scratch = []
        self.layouts = [layout]
        for level, dim in enumerate(order):
            later = order[level + 1 :]
            ranges = [(None,) if d in merged else range(sizes[d]) for d in later]
            units = sorted(
                itertools.product(*ranges),
                key=lambda unit: (-(unit[-1] or 0) if unit else 0, -sum(moved or 0 for moved in unit)),
            )
            self.units.append(units)
            left = "".join(d for d in self.layouts[-1] if d != dim)
            self.layouts.append(left)
            self.scratch.append(
                pltpu.VMEM(
                    (5 if dim == "s" else sizes[dim] - 1,)
                    + tuple(sizes[d] for d in left)
                    + self.block,
                    value.dtype,
                )
            )
        self.index = {}
        for level, dim in enumerate(order):
            for unit in self.units[level]:
                for offset in range(1, sizes[dim]):
                    self.index[(level, unit, offset)] = len(self.index)
        count = len(self.index)
        self.scratch += [
            pltpu.SemaphoreType.DMA((count,)),
            pltpu.SemaphoreType.DMA((count,)),
            pltpu.SemaphoreType.DMA((2, 5)),
        ]
        self.peers = [(d, offset) for d in order for offset in range(1, sizes[d]) if d != "s"]
        if self.line:
            self.peers += LINE_PEERS

    def prepare(self, refs, place):
        self.source, self.target = refs[0], refs[1]
        self.landing = refs[2 : 2 + self.levels]
        self.send, self.recv, self.line_sems = refs[2 + self.levels :]
        self.place = place
        self.sent = []

    def held(self, level):
        return self.source if level == 0 else self.landing[level - 1].at[0]

    def later(self, level, unit):
        where = {}
        for d, moved in zip(self.order[level + 1 :], unit):
            where[d] = slice(None) if moved is None else spot_of(d, self.place[d], moved)
        return where

    def copy(self, level, unit, offset):
        number = self.index[(level, unit, offset)]
        dim = self.order[level]
        where = self.later(level, unit)
        landed = self.landing[level].at[
            (offset - 1,) + tuple(where[d] for d in self.layouts[level + 1])
        ]
        where[dim] = flip(self.place[dim], offset)
        source = self.held(level).at[tuple(where[d] for d in self.layouts[level])]
        return remote(source, landed, self.send.at[number], self.recv.at[number], dim, offset)

    def launch(self, level, unit, offset):
        self.copy(level, unit, offset).start()
        self.sent.append((level, unit, offset))

    def reduce(self, level, unit):
        dim = self.order[level]
        size = self.sizes[dim]
        for offset in range(1, size):
            self.copy(level, unit, offset).wait_recv()
        where = self.later(level, unit)
        free = [d for d in self.order[level + 1 :] if isinstance(where[d], slice)]
        total = math.prod(self.sizes[d] for d in free)
        rows, columns = self.block
        last = level == self.levels - 1

        def one(number, carry):
            at = dict(where)
            rest = number
            for d in free:
                at[d] = rest % self.sizes[d]
                rest = rest // self.sizes[d]
            spot = tuple(at[d] for d in self.layouts[level + 1])
            at[dim] = self.place[dim]
            mine = tuple(at[d] for d in self.layouts[level])

            def body(piece):
                if not last and size == 2:
                    self.landing[level][(0,) + spot + (piece,)] += self.held(level)[mine + (piece,)]
                    return
                result = self.held(level)[mine + (piece,)].astype(f32)
                for offset in range(1, size):
                    result = result + self.landing[level][(offset - 1,) + spot + (piece,)].astype(f32)
                if last:
                    self.target[(piece,)] = result.astype(self.target.dtype)
                else:
                    self.landing[level][(0,) + spot + (piece,)] = result.astype(self.landing[level].dtype)

            each_piece(rows, columns, body)
            return carry

        if total == 1:
            one(0, 0)
        else:
            lax.fori_loop(0, total, one, 0)
        if not last and not (self.line and level == self.levels - 2):
            ahead, rest = unit[0], unit[1:]
            if ahead is None:
                offsets = range(1, self.sizes[self.order[level + 1]])
            else:
                offsets = [ahead] if ahead else []
            for offset in offsets:
                self.launch(level + 1, rest, offset)

    def line_copy(self, number):
        step, slot = ((1, 0), (2, 1), (3, 2), (3, 3), (2, 4))[number]
        level = self.levels - 1
        block = self.held(level).at[along_line(self.place["s"], step)]
        landed = self.landing[level].at[slot]
        device = peer_of("s", 1) if number < 3 else across_middle()
        return remote_to(block, landed, self.line_sems.at[0, number], self.line_sems.at[1, number], device)

    def line_step(self, step, ends=True, middles=True):
        level = self.levels - 1
        middle = is_middle(self.place["s"])
        rows, columns = self.block
        held, landing = self.held(level), self.landing[level]
        position = along_line(self.place["s"], step)

        def pass_on():
            arrived = (0, 3, 1, 2)[step]
            self.line_copy(arrived).wait_recv()

            def body(piece):
                held[(position, piece)] += landing[(arrived, piece)]

            each_piece(rows, columns, body)
            self.line_copy((0, 0, 4, 3)[step]).start()

        if step:
            if ends:
                pl.when(jnp.logical_not(middle))(lambda: self.line_copy(step - 1).start())
            if middles:
                pl.when(middle)(pass_on)
            return

        self.line_copy(0).wait_recv()

        @pl.when(middle)
        def _():
            self.line_copy(4).wait_recv()

            def body(piece):
                result = held[(position, piece)].astype(f32) + landing[(0, piece)].astype(f32)
                self.target[(piece,)] = (result + landing[(4, piece)].astype(f32)).astype(
                    self.target.dtype
                )

            each_piece(rows, columns, body)

        @pl.when(jnp.logical_not(middle))
        def _():
            def body(piece):
                result = held[(position, piece)].astype(f32) + landing[(0, piece)].astype(f32)
                self.target[(piece,)] = result.astype(self.target.dtype)

            each_piece(rows, columns, body)

    def events(self):
        found = []
        for number, unit in enumerate(self.units[0]):
            for offset in range(1, self.sizes[self.order[0]]):
                found.append(
                    (-1 + 0.001 * number, functools.partial(self.launch, 0, unit, offset))
                )
        spread = 4 if self.line else 1
        for level in range(self.levels - self.line):
            count = len(self.units[level])
            for number, unit in enumerate(self.units[level]):
                late = 0
                if self.order[-1] == "a":
                    late = 20 if level == self.levels - 1 else 0.9
                found.append(
                    (late + level + spread * number / count, functools.partial(self.reduce, level, unit))
                )
        if self.line:
            for number, step in enumerate((3, 2, 1, 0)):
                found.append(
                    (self.levels - 1 + number + 0.5, functools.partial(self.line_step, step))
                )
        return found

    def finish(self):
        for transfer in self.sent:
            self.copy(*transfer).wait_send()
        if self.line:
            self.line_copy(0).wait_send()
            middle = is_middle(self.place["s"])

            @pl.when(middle)
            def _():
                for number in (3, 4):
                    self.line_copy(number).wait_send()

            @pl.when(jnp.logical_not(middle))
            def _():
                for number in (1, 2):
                    self.line_copy(number).wait_send()


class MemoryGather:
    def __init__(self, memory, sizes):
        self.value = memory
        self.sizes = sizes
        self.out = jax.ShapeDtypeStruct((sizes["s"], 2) + memory.shape[1:], memory.dtype)
        self.in_spec = pl.BlockSpec(memory_space=pltpu.VMEM)
        self.out_spec = pl.BlockSpec(memory_space=pl.ANY)
        rows = sizes["s"]
        self.scratch = [
            pltpu.SemaphoreType.DMA((2, rows)),
            pltpu.SemaphoreType.DMA((2, rows)),
            pltpu.SemaphoreType.DMA((2, rows, 2)),
            pltpu.SemaphoreType.DMA,
        ]
        self.peers = [("s", offset) for offset in range(1, rows)] + [("h", 1), ("c", 1)]

    def prepare(self, refs, place):
        self.source, self.target, self.along, self.across, self.core, self.local = refs
        self.place = place
        self.mine = place["s"] % 2 == place["c"]

    def row(self, offset):
        return flip(self.place["s"], offset)

    def along_copy(self, offset, arriving):
        to = self.row(offset)
        spot = to if arriving else self.place["s"]
        return remote(
            self.source.at[self.place["s"] // 2 if arriving else to // 2],
            self.target.at[spot, self.place["h"]],
            self.along.at[0, offset],
            self.along.at[1, offset],
            "s",
            offset,
        )

    def across_copy(self, offset, arriving):
        h = self.place["h"]
        own = self.target.at[self.row(offset), 1 - h if arriving else h]
        if offset == 0 and not arriving:
            source = self.source.at[self.place["s"] // 2]
        else:
            source = own
        return remote(source, own, self.across.at[0, offset], self.across.at[1, offset], "h", 1)

    def core_copy(self, offset, other):
        h = self.place["h"]
        own = self.target.at[self.row(offset), 1 - h if other else h]
        source = self.source.at[self.place["s"] // 2] if offset == 0 and not other else own
        return remote(source, own, self.core.at[0, offset, other], self.core.at[1, offset, other], "c", 1)

    def events(self):
        rows = self.sizes["s"]

        def first():
            for offset in range(1, rows):
                @pl.when(self.row(offset) % 2 == self.place["c"])
                def _():
                    self.along_copy(offset, False).start()

            @pl.when(self.mine)
            def _():
                pltpu.make_async_copy(
                    self.source.at[self.place["s"] // 2],
                    self.target.at[self.place["s"], self.place["h"]],
                    self.local,
                ).start()
                self.across_copy(0, False).start()
                self.core_copy(0, 0).start()

        def arrival(offset):
            @pl.when(self.mine)
            def _():
                self.along_copy(offset, True).wait_recv()
                self.across_copy(offset, False).start()
                self.core_copy(offset, 0).start()

        def other(offset):
            @pl.when(self.mine)
            def _():
                self.across_copy(offset, True).wait_recv()
                self.core_copy(offset, 1).start()

        found = [(0.05, first)]
        for offset in range(1, rows):
            found.append((offset + 0.05, functools.partial(arrival, offset)))
        for offset in range(rows):
            found.append((rows + offset, functools.partial(other, offset)))
        return found

    def finish(self):
        rows = self.sizes["s"]
        for offset in range(1, rows):
            @pl.when(self.row(offset) % 2 == self.place["c"])
            def _():
                self.along_copy(offset, False).wait_send()

        @pl.when(self.mine)
        def _():
            pltpu.make_async_copy(
                self.source.at[self.place["s"] // 2],
                self.target.at[self.place["s"], self.place["h"]],
                self.local,
            ).wait()
            for offset in range(rows):
                self.across_copy(offset, False).wait_send()
                for other in range(2):
                    self.core_copy(offset, other).wait_send()

        @pl.when(jnp.logical_not(self.mine))
        def _():
            for offset in range(rows):
                for other in range(2):
                    self.core_copy(offset, other).wait_recv()


class MemoryScatter:
    def __init__(self, value, sizes):
        self.value = value
        self.sizes = sizes
        rows = sizes["s"]
        self.block = value.shape[2:]
        self.out = jax.ShapeDtypeStruct((2,) + self.block, f32)
        self.in_spec = pl.BlockSpec(memory_space=pltpu.VMEM)
        self.out_spec = pl.BlockSpec(memory_space=pltpu.VMEM)
        self.scratch = [
            pltpu.VMEM(value.shape, value.dtype),
            pltpu.VMEM((rows,) + self.block, value.dtype),
            pltpu.VMEM((2,) + self.block, value.dtype),
            pltpu.SemaphoreType.DMA((2, rows, 2)),
            pltpu.SemaphoreType.DMA((2, rows)),
            pltpu.SemaphoreType.DMA((2, rows)),
        ]
        self.peers = [("s", offset) for offset in range(1, rows)] + [("h", 1), ("c", 1)]

    def prepare(self, refs, place):
        self.source, self.target = refs[0], refs[1]
        self.summed, self.halved, self.landed, self.core, self.across, self.along = refs[2:]
        self.place = place
        self.mine = place["s"] % 2 == place["c"]

    def row(self, offset):
        return flip(self.place["s"], offset)

    def core_copy(self, offset, other):
        h = self.place["h"]
        spot = (self.row(offset), flip(h, 1) if other else h)
        return remote(
            self.source.at[spot],
            self.summed.at[spot],
            self.core.at[0, offset, other],
            self.core.at[1, offset, other],
            "c",
            1,
        )

    def across_copy(self, offset):
        row = self.row(offset)
        return remote(
            self.summed.at[row, flip(self.place["h"], 1)],
            self.halved.at[row],
            self.across.at[0, offset],
            self.across.at[1, offset],
            "h",
            1,
        )

    def along_copy(self, offset, arriving):
        to = self.row(offset)
        return remote(
            self.halved.at[to],
            self.landed.at[to // 2 if arriving else self.place["s"] // 2],
            self.along.at[0, offset],
            self.along.at[1, offset],
            "s",
            offset,
        )

    def events(self):
        rows = self.sizes["s"]
        high, wide = self.block
        orders = list(range(1, rows))[::-1] + [0]

        def first():
            @pl.when(jnp.logical_not(self.mine))
            def _():
                for other in (1, 0):
                    for offset in orders:
                        self.core_copy(offset, other).start()

        def level(offset, other):
            @pl.when(self.mine)
            def _():
                self.core_copy(offset, other).wait_recv()
                h = self.place["h"]
                spot = (self.row(offset), flip(h, 1) if other else h)

                def body(piece):
                    total = self.summed[spot + (piece,)].astype(f32) + self.source[
                        spot + (piece,)
                    ].astype(f32)
                    self.summed[spot + (piece,)] = total.astype(self.summed.dtype)

                each_piece(high, wide, body)
                if other:
                    self.across_copy(offset).start()

        def last(offset):
            @pl.when(self.mine)
            def _():
                self.across_copy(offset).wait_recv()
                row = self.row(offset)

                def body(piece):
                    total = self.halved[(row, piece)].astype(f32) + self.summed[
                        (row, self.place["h"], piece)
                    ].astype(f32)
                    self.halved[(row, piece)] = total.astype(self.halved.dtype)
                    if offset == 0:
                        self.target[(self.place["s"] // 2, piece)] = total

                each_piece(high, wide, body)
                if offset:
                    self.along_copy(offset, False).start()

        found = [(-0.95, first)]
        for number, offset in enumerate(orders):
            found.append((0.05 + 0.1 * number, functools.partial(level, offset, 1)))
        for number, offset in enumerate(orders):
            found.append((0.55 + 0.1 * number, functools.partial(level, offset, 0)))
        for number, offset in enumerate(orders):
            found.append((1.05 + 0.2 * number, functools.partial(last, offset)))
        return found

    def finish(self):
        rows = self.sizes["s"]
        high, wide = self.block
        for offset in range(1, rows):
            @pl.when(self.row(offset) % 2 == self.place["c"])
            def _():
                self.along_copy(offset, True).wait_recv()
                number = self.row(offset) // 2

                def body(piece):
                    self.target[(number, piece)] = self.landed[(number, piece)].astype(f32)

                each_piece(high, wide, body)

        @pl.when(self.mine)
        def _():
            for offset in range(rows):
                self.across_copy(offset).wait_send()
            for offset in range(1, rows):
                self.along_copy(offset, False).wait_send()

        @pl.when(jnp.logical_not(self.mine))
        def _():
            for offset in range(rows):
                for other in range(2):
                    self.core_copy(offset, other).wait_send()


def peers_of(jobs):
    peers = []
    for job in jobs:
        for peer in job.peers:
            if peer not in peers:
                peers.append(peer)
    return peers


def greet(peers, place):
    barrier = pltpu.get_barrier_semaphore()
    middle = is_middle(place["s"])
    awaited = 0
    for peer in peers:
        if peer[0] == "m":
            @pl.when(middle)
            def _():
                pl.semaphore_signal(
                    barrier, inc=1, device_id=across_middle(), device_id_type=pl.DeviceIdType.MESH
                )
            continue
        awaited += 1
        pl.semaphore_signal(
            barrier, inc=1, device_id=peer_of(*peer), device_id_type=pl.DeviceIdType.MESH
        )
    return awaited


def welcome(peers, place, awaited):
    barrier = pltpu.get_barrier_semaphore()
    middle = is_middle(place["s"])
    if ("m", 1) in peers:
        @pl.when(middle)
        def _():
            pl.semaphore_wait(barrier, awaited + 1)

        @pl.when(jnp.logical_not(middle))
        def _():
            pl.semaphore_wait(barrier, awaited)
    else:
        pl.semaphore_wait(barrier, awaited)


def exchange(name, collective_id, jobs):
    values = [getattr(job, "values", None) or [job.value] for job in jobs]
    peers = peers_of(jobs)

    def kernel(*refs):
        total = sum(len(held) for held in values)
        results = refs[total : total + len(jobs)]
        scratch = refs[total + len(jobs) :]
        begin = offset = 0
        place = coordinates()
        awaited = greet(peers, place)
        for number, job in enumerate(jobs):
            end = begin + len(values[number])
            ins = refs[begin:end]
            if hasattr(job, "pack"):
                job.pack(ins, scratch[offset])
                ins, offset = (scratch[offset],), offset + 1
            mine = len(job.scratch) - hasattr(job, "pack")
            job.prepare(tuple(ins) + (results[number],) + tuple(scratch[offset : offset + mine]), place)
            begin, offset = end, offset + mine
        welcome(peers, place, awaited)
        events = [event for job in jobs for event in job.events()]
        for _, act in sorted(events, key=lambda event: event[0]):
            act()
        for job in jobs:
            job.finish()

    return pl.pallas_call(
        kernel,
        name=name,
        out_shape=tuple(job.out for job in jobs),
        in_specs=[job.in_spec for job, held in zip(jobs, values) for _ in held],
        out_specs=tuple(job.out_spec for job in jobs),
        scratch_shapes=[item for job in jobs for item in job.scratch],
        compiler_params=pltpu.CompilerParams(
            collective_id=collective_id, has_side_effects=True, vmem_limit_bytes=60 * 1024 * 1024
        ),
    )(*[value for held in values for value in held])


def packed(block):
    rows, columns = block.shape
    if rows % 16 == 0:
        return block
    return block.reshape(16, rows * columns // 16)


def bucket_edges():
    edges = []
    for target in range(1, 32):
        if target < 16:
            edges.append(target)
        else:
            found = 0
            for distance in range(16, 4096):
                value = 16 + int(math.log(distance / 16.0) / math.log(8.0) * 16.0)
                if found == 0 and value >= target:
                    found = distance
            edges.append(found)
    return edges


def gelu_tanh(value):
    return (
        0.5
        * value
        * (1.0 + jnp.tanh(0.7978845608028654 * (value + 0.044715 * value * value * value)))
    )


def dot(left, right):
    return jnp.einsum("sd,df->sf", left, right, preferred_element_type=f32)


def dot_t(left, right):
    return jnp.einsum("sf,df->sd", left, right, preferred_element_type=f32)


def t_dot(left, right):
    return jnp.einsum("sd,sf->df", left, right, preferred_element_type=f32)


def distance_table(seq):
    edges = np.array(bucket_edges())
    distance = (-np.arange(seq)) % seq
    bucket = (distance[:, None] >= edges[None, :]).sum(axis=1)
    return (np.arange(128)[:, None] == bucket[None, :]).astype(np.float32)


def mm(left, right):
    return lax.dot_general(left, right, (((1,), (0,)), ((), ())), preferred_element_type=f32)


def mm_t(left, right):
    return lax.dot_general(left, right, (((1,), (1,)), ((), ())), preferred_element_type=f32)


def t_mm(left, right):
    return lax.dot_general(left, right, (((0,), (0,)), ((), ())), preferred_element_type=f32)


def inverse_rms(rows):
    return lax.rsqrt(jnp.mean(rows * rows, axis=-1, keepdims=True) + eps)


def rms_back(rows, gain, slope):
    inverse = inverse_rms(rows)
    unit = rows * inverse
    scaled = slope * gain
    back = inverse * (scaled - unit * jnp.mean(unit * scaled, axis=-1, keepdims=True))
    return back, jnp.sum(slope * unit, axis=0, keepdims=True)


def lanes_of(shape):
    return lax.broadcasted_iota(jnp.int32, shape, len(shape) - 1)


def one_half(pair, half):
    inside = (lanes_of(pair.shape) // HEAD) == half
    return jnp.where(inside, pair, jnp.zeros_like(pair))


def both_halves(pair):
    return jnp.concatenate([one_half(pair, 0), one_half(pair, 1)], axis=0)


def joined_rows(stacked):
    rows = stacked.shape[0] // 2
    return joined(stacked[:rows], stacked[rows:])


def joined(first, second):
    return jnp.where(lanes_of(first.shape) < HEAD, first, second)


def pair_of(ref, start, pair):
    return ref[:, start + 2 * HEAD * pair : start + 2 * HEAD * (pair + 1)]


FF_STEP = 256


def in_steps(total, step, body, further=0):
    def one(number, carry):
        here = pl.ds(pl.multiple_of(number * step, step), step)
        if further:
            body(here, pl.ds(pl.multiple_of(number * step + further, step), step))
        else:
            body(here)
        return carry

    lax.fori_loop(0, total // step, one, 0)


class Fetch:
    def __init__(self, sources, targets, sems):
        self.copies = [
            pltpu.make_async_copy(source, target, sems.at[number])
            for number, (source, target) in enumerate(zip(sources, targets))
        ]
        self.targets = targets
        self.ready = set()
        for copy in self.copies:
            copy.start()

    def __getitem__(self, number):
        if number not in self.ready:
            self.ready.add(number)
            self.copies[number].wait()
        return self.targets[number]


def enter_kernel(resid_ref, part_c_ref, query_ref, kv_ref, normed_ref, gains_ref):
    row = lax.broadcasted_iota(jnp.int32, (16, GAIN_PAD), 0)
    pick = (row == lanes_of((16, GAIN_PAD))).astype(bf16)
    gains = mm_t(pick, part_c_ref[:, 5 * HD : 5 * HD + GAIN_PAD])
    gains_ref[...] = gains
    resid = resid_ref[...]
    normed = (resid * inverse_rms(resid) * gains[0:1]).astype(bf16)
    normed_ref[...] = normed
    query_ref[...] = mm(normed, part_c_ref[:, :HD]).astype(bf16)
    kv_ref[...] = mm(normed, part_c_ref[:, HD : 3 * HD]).astype(bf16)


def biased_scores(scores, row, first, length):
    bias = pltpu.roll(jnp.broadcast_to(row, scores.shape), 0, 1, stride=1, stride_axis=0)
    query_pos = first + lax.broadcasted_iota(jnp.int32, scores.shape, 0)
    key_pos = lanes_of(scores.shape)
    mask = (key_pos <= query_pos) & (key_pos < length)
    return jnp.where(mask, scores + bias, masked_score)


def softmax_parts(scores):
    highest = jnp.max(scores, axis=-1, keepdims=True)
    total = highest + jnp.log(jnp.sum(jnp.exp(scores - highest), axis=-1, keepdims=True))
    return total, jnp.exp(scores - total)


def query_span(lengths_ref, rows):
    place = coordinates()
    length = lengths_ref[place["s"] // 2, 2 * place["a"] + place["s"] % 2]
    return (2 * place["h"] + place["c"]) * rows, length


def forward_kernel(
    lengths_ref,
    query_ref,
    kv_ref,
    resid0_ref,
    gains_ref,
    table_ref,
    bias_ref,
    mem_kv_hbm,
    part_a_hbm,
    part_b_hbm,
    part_c_hbm,
    attn_self_ref,
    total_self_ref,
    resid1_ref,
    normed_cross_ref,
    query_cross_ref,
    attn_cross_ref,
    total_cross_ref,
    resid2_ref,
    normed_ff_ref,
    gate_up_ref,
    hidden_ref,
    resid3_ref,
    final_ref,
    mem_kv_ref,
    part_a_ref,
    part_b_ref,
    part_c_ref,
    sems,
):
    fetched = Fetch(
        (part_c_hbm, part_b_hbm, mem_kv_hbm, part_a_hbm),
        (part_c_ref, part_b_ref, mem_kv_ref, part_a_ref),
        sems,
    )
    first, length = query_span(lengths_ref, query_ref.shape[0])
    ff = hidden_ref.shape[1]
    bias_rows = pltpu.roll(mm(bias_ref[...], table_ref[:BUCKETS, :]), first, 1)
    lanes = lanes_of(total_self_ref.shape)
    totals = jnp.zeros(total_self_ref.shape, f32)
    for pair in range(HEADS // 2):
        keys, values = pair_of(kv_ref, 0, pair), pair_of(kv_ref, HD, pair)
        outputs = []
        for half in range(2):
            number = 2 * pair + half
            scores = mm_t(one_half(pair_of(query_ref, 0, pair), half), keys)
            scores = biased_scores(scores, bias_rows[number : number + 1], first, length)
            total, shares = softmax_parts(scores)
            totals = jnp.where(lanes == number, total, totals)
            outputs.append(mm(shares.astype(bf16), values))
        attn_self_ref[:, 2 * HEAD * pair : 2 * HEAD * (pair + 1)] = joined(*outputs).astype(bf16)
    total_self_ref[...] = totals

    part_c = fetched[0]
    resid1 = resid0_ref[...] + mm_t(attn_self_ref[...], part_c[:, 3 * HD : 4 * HD])
    resid1_ref[...] = resid1
    normed = (resid1 * inverse_rms(resid1) * gains_ref[1:2]).astype(bf16)
    normed_cross_ref[...] = normed
    query_cross_ref[...] = mm(normed, part_c[:, 4 * HD : 5 * HD]).astype(bf16)

    part_b = fetched[1]
    mem_kv_ref = fetched[2]
    total_cross_ref[...] = jnp.zeros(total_cross_ref.shape, f32)

    def cross_pair(place, place_v):
        keys, values = mem_kv_ref[:, place], mem_kv_ref[:, place_v]
        outputs = []
        for half in range(2):
            scores = mm_t(one_half(query_cross_ref[:, place], half), keys)
            total, shares = softmax_parts(scores)
            number = place.start // HEAD + half
            total_cross_ref[...] = jnp.where(lanes == number, total, total_cross_ref[...])
            outputs.append(mm(shares.astype(bf16), values))
        attn_cross_ref[:, place] = joined(*outputs).astype(bf16)

    in_steps(HD, 2 * HEAD, cross_pair, HD)
    resid2 = resid1_ref[...] + mm_t(attn_cross_ref[...], part_b[:, ff + 2 * HD :])
    resid2_ref[...] = resid2
    normed_ff_ref[...] = (resid2 * inverse_rms(resid2) * gains_ref[2:3]).astype(bf16)

    part_a = fetched[3]

    def feed(here, there):
        gate = mm(normed_ff_ref[...], part_a[:, here])
        up = mm(normed_ff_ref[...], part_a[:, there])
        gate_up_ref[:, here] = gate
        gate_up_ref[:, there] = up
        hidden_ref[:, here] = (gelu_tanh(gate) * up).astype(bf16)

    in_steps(ff, FF_STEP, feed, ff)
    resid3 = resid2_ref[...] + mm_t(hidden_ref[...], part_b[:, :ff])
    resid3_ref[...] = resid3
    final_ref[...] = (resid3 * inverse_rms(resid3) * gains_ref[3:4]).astype(bf16)


def attention_back(query, keys, values, scores, total, out_slope):
    shares = jnp.exp(scores - total)
    share_slope = mm_t(out_slope, values)
    inner = jnp.sum(shares * share_slope, axis=-1, keepdims=True)
    score_slope = shares * (share_slope - inner)
    rounded = score_slope.astype(bf16)
    return (
        rounded,
        mm(rounded, keys),
        t_mm(rounded, query),
        t_mm(shares.astype(bf16), out_slope),
    )


def backward_kernel(
    lengths_ref,
    slope_ref,
    resid3_ref,
    hidden_ref,
    gate_up_ref,
    normed_ff_ref,
    resid2_ref,
    attn_cross_ref,
    query_cross_ref,
    total_cross_ref,
    normed_cross_ref,
    resid1_ref,
    attn_self_ref,
    query_ref,
    kv_ref,
    total_self_ref,
    gains_ref,
    table_ref,
    bias_ref,
    mem_kv_hbm,
    part_a_hbm,
    part_b_hbm,
    part_c_hbm,
    grad_b_hbm,
    gate_up_slope_ref,
    cross_kv_slope_ref,
    grad_c_ref,
    query_slope_ref,
    kv_slope_ref,
    grad1_ref,
    norm_grads_ref,
    bias_grad_ref,
    mem_kv_ref,
    part_a_ref,
    part_b_ref,
    part_c_ref,
    grad_b_ref,
    cross_query_slope_ref,
    sems,
    out_sems,
):
    fetched = Fetch(
        (part_b_hbm, part_a_hbm, mem_kv_hbm, part_c_hbm),
        (part_b_ref, part_a_ref, mem_kv_ref, part_c_ref),
        sems,
    )
    first, length = query_span(lengths_ref, query_ref.shape[0])
    ff = hidden_ref.shape[1]
    width = resid3_ref.shape[1]
    norm_grads_ref[...] = jnp.zeros_like(norm_grads_ref)

    grad3, norm_grad = rms_back(resid3_ref[...], gains_ref[3:4], slope_ref[...])
    norm_grads_ref[3:4] = norm_grad
    down_in = grad3.astype(bf16)
    part_b = fetched[0]

    def feed_back(here, there):
        hidden_slope = mm(down_in, part_b[:, here])
        gate, up = gate_up_ref[:, here], gate_up_ref[:, there]
        inner = jnp.tanh(0.7978845608028654 * (gate + 0.044715 * gate * gate * gate))
        activated = 0.5 * gate * (1.0 + inner)
        steep = 0.5 * (1.0 + inner) + 0.5 * gate * (1.0 - inner * inner) * (
            0.7978845608028654 * (1.0 + 3.0 * 0.044715 * gate * gate)
        )
        gate_up_slope_ref[:, here] = (hidden_slope * up * steep).astype(bf16)
        gate_up_slope_ref[:, there] = (hidden_slope * activated).astype(bf16)
        grad_b_ref[:, here] = t_mm(down_in, hidden_ref[:, here]).astype(bf16)

    in_steps(ff, FF_STEP, feed_back, ff)
    part_a = fetched[1]
    back, norm_grad = rms_back(
        resid2_ref[...], gains_ref[2:3], mm_t(gate_up_slope_ref[...], part_a[...])
    )
    norm_grads_ref[2:3] = norm_grad
    grad2 = grad3 + back

    cross_in = grad2.astype(bf16)
    grad_b_ref[:, ff:] = t_mm(cross_in, attn_cross_ref[...]).astype(bf16)
    copy_b = pltpu.make_async_copy(grad_b_ref, grad_b_hbm, out_sems.at[0])
    copy_b.start()
    out_slope = mm(cross_in, part_b[:, ff + 2 * HD :]).astype(bf16)
    mem_kv = fetched[2]
    cross_query_slope_ref[...] = out_slope

    def cross_pair_back(place, place_v):
        keys, values = mem_kv[:, place], mem_kv[:, place_v]
        lanes = lanes_of(total_cross_ref.shape)
        totals = [
            jnp.sum(
                jnp.where(lanes == place.start // HEAD + half, total_cross_ref[...], 0.0),
                axis=-1,
                keepdims=True,
            )
            for half in range(2)
        ]
        query = both_halves(query_cross_ref[:, place])
        part = attention_back(
            query,
            keys,
            values,
            mm_t(query, keys),
            jnp.concatenate(totals, axis=0),
            both_halves(cross_query_slope_ref[:, place]),
        )
        cross_query_slope_ref[:, place] = joined_rows(part[1]).astype(bf16)
        cross_kv_slope_ref[:, place] = part[2].astype(bf16)
        cross_kv_slope_ref[:, place_v] = part[3].astype(bf16)

    in_steps(HD, 2 * HEAD, cross_pair_back, HD)
    part_c = fetched[3]
    query_slope = cross_query_slope_ref[...]
    grad_c_ref[:, HD : 2 * HD] = t_mm(normed_cross_ref[...], query_slope).astype(bf16)
    back, norm_grad = rms_back(
        resid1_ref[...], gains_ref[1:2], mm_t(query_slope, part_c[:, 4 * HD : 5 * HD])
    )
    norm_grads_ref[1:2] = norm_grad
    grad1 = grad2 + back
    grad1_ref[...] = grad1

    self_in = grad1.astype(bf16)
    grad_c_ref[:, :HD] = t_mm(self_in, attn_self_ref[...]).astype(bf16)
    out_slope = mm(self_in, part_c[:, 3 * HD : 4 * HD]).astype(bf16)
    bias_rows = pltpu.roll(mm(bias_ref[...], table_ref[:BUCKETS, :]), first, 1)
    bias_sums = jnp.zeros((8, bias_rows.shape[1]), f32)
    rows, seq = query_ref.shape[0], kv_ref.shape[0]
    reverse = lax.broadcasted_iota(jnp.int32, (rows, rows), 0) + lanes_of((rows, rows)) == rows - 1
    reverse = reverse.astype(bf16)
    for pair in range(HEADS // 2):
        place = slice(2 * HEAD * pair, 2 * HEAD * (pair + 1))
        place_v = slice(HD + 2 * HEAD * pair, HD + 2 * HEAD * (pair + 1))
        keys, values = kv_ref[:, place], kv_ref[:, place_v]
        query = both_halves(query_ref[:, place])
        products = mm_t(query, keys)
        scores, totals = [], []
        for half in range(2):
            number = 2 * pair + half
            scores.append(
                biased_scores(
                    products[half * rows : (half + 1) * rows],
                    bias_rows[number : number + 1],
                    first,
                    length,
                )
            )
            totals.append(total_self_ref[:, number : number + 1])
        part = attention_back(
            query,
            keys,
            values,
            jnp.concatenate(scores, axis=0),
            jnp.concatenate(totals, axis=0),
            both_halves(out_slope[:, place]),
        )
        for half in range(2):
            turned = mm(reverse, part[0][half * rows : (half + 1) * rows])
            turned = pltpu.roll(turned, 0, 1, stride=1, stride_axis=0)
            where = lax.broadcasted_iota(jnp.int32, bias_sums.shape, 0) == 2 * pair + half
            bias_sums = jnp.where(where, jnp.sum(turned, axis=0, keepdims=True), bias_sums)
        query_slope_ref[:, place] = joined_rows(part[1]).astype(bf16)
        kv_slope_ref[:, place] = part[2].astype(bf16)
        kv_slope_ref[:, place_v] = part[3].astype(bf16)
    bias_sums = pltpu.roll(bias_sums, 2 * seq + 1 - rows - first, 1)
    high = bias_sums.astype(bf16)
    rest = bias_sums - high.astype(f32)
    middle = rest.astype(bf16)
    low = (rest - middle.astype(f32)).astype(bf16)
    table = table_ref[...]
    bias_grad_ref[...] = mm_t(high, table) + (mm_t(middle, table) + mm_t(low, table))
    copy_b.wait()


def project_memory(held, result):
    memory, weight = held
    step = min(256, memory.shape[0])

    def one(number, carry):
        rows = pl.ds(pl.multiple_of(number * step, step), step)
        result[rows, :] = mm(memory[rows, :], weight[...]).astype(bf16)
        return carry

    lax.fori_loop(0, memory.shape[0] // step, one, 0)


def gate_up_grads(held, result):
    normed, slope = held

    def one(here):
        result[:, here] = t_mm(normed[...], slope[:, here]).astype(bf16)

    in_steps(slope.shape[1], 2 * FF_STEP, one)


def memory_weight_grads(held, result):
    memory, slope, others = held
    ff = others.shape[1] - HD
    result[:, :ff] = others[:, :ff]
    result[:, ff + 2 * HD :] = others[:, ff:]

    def one(here, there):
        result[:, there] = t_mm(memory[...], slope[:, here]).astype(bf16)

    in_steps(2 * HD, FF_STEP, one, ff)


def memory_slopes(held, result):
    slope, weight = held
    step = min(256, slope.shape[0])

    def one(number, carry):
        rows = pl.ds(pl.multiple_of(number * step, step), step)
        result[rows, :] = mm_t(slope[rows, :], weight[...]).astype(bf16)
        return carry

    lax.fori_loop(0, slope.shape[0] // step, one, 0)


def leave_kernel(
    query_slope_ref,
    kv_slope_ref,
    resid0_ref,
    grad1_ref,
    gains_ref,
    norm_grads_ref,
    part_c_ref,
    grad0_ref,
    all_grads_ref,
):
    slope = mm_t(query_slope_ref[...], part_c_ref[:, :HD])
    slope = slope + mm_t(kv_slope_ref[...], part_c_ref[:, HD : 3 * HD])
    back, norm_grad = rms_back(resid0_ref[...], gains_ref[0:1], slope)
    grad0_ref[...] = (grad1_ref[...] + back).astype(bf16)
    where = lax.broadcasted_iota(jnp.int32, norm_grads_ref.shape, 0) == 0
    all_grads_ref[...] = jnp.where(where, norm_grad, norm_grads_ref[...])


def self_weight_grads(held, result):
    query_slope, kv_slope, normed, norm_grads, others = held
    result[:, :HD] = t_mm(normed[...], query_slope[...]).astype(bf16)
    result[:, HD : 3 * HD] = t_mm(normed[...], kv_slope[...]).astype(bf16)
    result[:, 3 * HD : 5 * HD] = others[...]
    row = lax.broadcasted_iota(jnp.int32, (norm_grads.shape[0], GAIN_PAD), 0)
    spread = (row == lanes_of(row.shape)).astype(bf16)
    result[:, 5 * HD :] = t_mm(norm_grads[...].astype(bf16), spread).astype(bf16)


def local_kernel(name, kernel, outs, args, spaces="", out_spaces="", scratch=()):
    space = {"v": pltpu.VMEM, "s": pltpu.SMEM, "a": pl.ANY}
    spaces = spaces or "v" * len(args)
    out_spaces = out_spaces or "v" * len(outs)
    return pl.pallas_call(
        kernel,
        name=name,
        out_shape=tuple(jax.ShapeDtypeStruct(shape, dtype) for shape, dtype in outs),
        in_specs=[pl.BlockSpec(memory_space=space[letter]) for letter in spaces],
        out_specs=tuple(pl.BlockSpec(memory_space=space[letter]) for letter in out_spaces),
        scratch_shapes=list(scratch),
        compiler_params=pltpu.CompilerParams(vmem_limit_bytes=60 * 1024 * 1024),
    )(*args)


def pack_columns(pieces, block):
    start = 0
    for piece in pieces:
        if piece.shape[0] == 1:
            break
        block[:, start : start + piece.shape[1]] = piece[...]
        start += piece.shape[1]
    gains = pieces[-4:]
    if gains[0].shape[0] == 1:
        rows = gains[0].shape[1]
        where = lax.broadcasted_iota(jnp.int32, (16, rows), 0)
        stacked = jnp.zeros((16, rows), f32)
        for number, gain in enumerate(gains):
            stacked = jnp.where(where == number, gain[...].astype(f32), stacked)
        pick = lax.broadcasted_iota(jnp.int32, (16, GAIN_PAD), 0) == lanes_of((16, GAIN_PAD))
        block[:, start:] = t_mm(stacked.astype(bf16), pick.astype(bf16)).astype(bf16)


def pack_rows(pieces, block):
    start = 0
    for piece in pieces:
        block[start : start + piece.shape[0], :] = piece[...]
        start += piece.shape[0]


def pack_ids(pieces, block):
    block[...] = jnp.zeros_like(block)
    for number, piece in enumerate(pieces):
        micro, _, count = piece.shape
        for which in range(micro):
            block[micro * number + which : micro * number + which + 1, :count] = piece[which]


def tail_kernel(lengths_ref, *refs):
    (a_ref, b_ref, c_ref, small_ref, memory_ref, embedding_ref, head_ref), outs = refs[:7], refs[7:]
    (loss_ref, memory_out, embedding_out, head_out, bias_out), outs = outs[:5], outs[5:]
    memory_out[...] = memory_ref[...]
    embedding_out[...] = embedding_ref[...]
    head_out[...] = head_ref[...]
    total = jnp.sum(small_ref[...], axis=0)
    count = 0
    for first in range(lengths_ref.shape[0]):
        for second in range(lengths_ref.shape[1]):
            count = count + lengths_ref[first, second]
    loss_ref[...] = jnp.sum(total[8:], keepdims=True) / count.astype(f32)
    bias_out[...] = total[:HEADS, :BUCKETS]
    for ref, pieces in ((a_ref, outs[:2]), (b_ref, outs[2:6]), (c_ref, outs[6:11])):
        start = 0
        for piece in pieces:
            piece[...] = ref[:, start : start + piece.shape[1]]
            start += piece.shape[1]
    turned = jnp.transpose(c_ref[:, 5 * HD :])
    for number, piece in enumerate(outs[11:]):
        piece[...] = turned[number : number + 1]


def vocabulary(name, collective_id, final_rows, head_rows, targets, lengths, sizes):
    span, width = head_rows.shape
    tok_dev = final_rows.shape[0]
    lines = sizes["s"]
    blocks = 2 * lines
    step_rows = min(512, span)
    gather = Gather(final_rows, "sh", "sh", sizes)
    direct = DirectGather(jax.ShapeDtypeStruct((blocks, tok_dev), f32), sizes)
    scatter = Scatter(jax.ShapeDtypeStruct((lines, 2, tok_dev, width), bf16), "hs", "sh", sizes)
    jobs = (gather, direct, scatter)
    peers = peers_of(jobs)

    def kernel(*refs):
        final_ref, head_ref, targets_ref, lengths_ref = refs[:4]
        slope_ref, head_part_ref, loss_ref = refs[4:7]
        states, totals, own_total, logits, turned, value, picked_ref, log_total_ref = refs[7:15]
        rest = refs[15:]
        place = coordinates()
        awaited = greet(peers, place)
        counts = [len(job.scratch) for job in jobs]
        gather.prepare((final_ref, states) + rest[: counts[0]], place)
        direct.prepare((own_total, totals) + rest[counts[0] : counts[0] + counts[1]], place)
        scatter.prepare((value, slope_ref) + rest[counts[0] + counts[1] :], place)
        welcome(peers, place, awaited)
        position = place["s"]
        half = position // 2

        def spot(token, other):
            far, second = token // 2, token % 2
            near_row = position + second * (1 - 2 * (position % 2))
            far_row = 2 - half + second * (1 - 2 * half)
            row = near_row + far * (far_row - near_row)
            side = place["h"] + other * (1 - 2 * place["h"])
            return row, side, 2 * row + side

        def chunk_of(number):
            return pl.ds(pl.multiple_of(number * step_rows, step_rows), step_rows)

        def hits(number, target):
            rows = lax.broadcasted_iota(jnp.int32, (step_rows, tok_dev), 0) + number * step_rows
            return rows == target

        def bring(step):
            token, other = step // 2, step % 2
            if step == 0:
                gather.line_first()
                gather.launch((1, (0,), 1))
                gather.local.wait()
                gather.local_done = True
            if other:
                gather.arrive((1, (token,), 1))
                if token + 1 < lines:
                    gather.line_next(token + 1)
                    gather.launch((1, (token + 1,), 1))

        def forward_step(step, carry):
            for number in range(blocks):
                pl.when(step == number)(functools.partial(bring, number))
            row, side, number = spot(step // 2, step % 2)
            block = states[row, side]
            target = targets_ref[pl.ds(number, 1), :]

            def scores(chunk, best):
                found = mm_t(head_ref[chunk_of(chunk), :], block)
                logits[number, chunk_of(chunk), :] = found
                return jnp.maximum(best, jnp.max(found, axis=0, keepdims=True))

            count = span // step_rows
            best = lax.fori_loop(0, count, scores, jnp.full((1, tok_dev), -3.0e38, f32))

            def spread(chunk, sums):
                found = logits[number, chunk_of(chunk), :]
                hit = hits(chunk, target)
                return (
                    sums[0] + jnp.sum(jnp.exp(found - best), axis=0, keepdims=True),
                    sums[1] + jnp.sum(jnp.where(hit, found, 0.0), axis=0, keepdims=True),
                )

            zero = jnp.zeros((1, tok_dev), f32)
            total, picked = lax.fori_loop(0, count, spread, (zero, zero))
            own_total[pl.ds(number, 1), :] = best + jnp.log(total)
            picked_ref[pl.ds(number, 1), :] = picked
            return carry

        lax.fori_loop(0, blocks, forward_step, 0)
        direct.begin()
        direct.receive()
        parts = totals[...].reshape((blocks,) + own_total.shape)
        top = jnp.max(parts, axis=0)
        log_total_ref[...] = top + jnp.log(jnp.sum(jnp.exp(parts - top[None]), axis=0))

        def backward_step(step, carry):
            row, side, number = spot(lines - 1 - step // 2, 1 - step % 2)
            lanes = pl.ds(pl.multiple_of(number * tok_dev, tok_dev), tok_dev)
            target = targets_ref[pl.ds(number, 1), :]
            log_total = log_total_ref[pl.ds(number, 1), :]
            length = lengths_ref[row // 2, 2 * place["a"] + row % 2]
            spots = (2 * side + place["c"]) * tok_dev + lax.broadcasted_iota(jnp.int32, (1, tok_dev), 1)
            live = jnp.where(spots < length, 1.0, 0.0)
            shown = log_total * (1 - jnp.minimum(2 * position + place["h"], 1)).astype(f32)
            loss_ref[pl.ds(number, 1), :] = live * (shown - picked_ref[pl.ds(number, 1), :])

            def slopes(chunk, inner):
                share = jnp.exp(logits[number, chunk_of(chunk), :] - log_total)
                slope = (share - jnp.where(hits(chunk, target), 1.0, 0.0)) * live
                turned[chunk_of(chunk), lanes] = slope.astype(bf16)
                return inner

            lax.fori_loop(0, span // step_rows, slopes, 0)
            value[row, side] = t_mm(turned[:, lanes], head_ref[...]).astype(bf16)
            for which in range(lines):
                pl.when(step == 2 * which)(
                    functools.partial(scatter.launch, 0, (lines - 1 - which,), 1)
                )
            return carry

        lax.fori_loop(0, blocks, backward_step, 0)
        for token in (3, 2):
            scatter.reduce(0, (token,))
            scatter.line_step(token, middles=False)

        def head_chunk(number, carry):
            rows = pl.ds(pl.multiple_of(number * 256, 256), 256)
            every = states[...].reshape(blocks * tok_dev, width)
            head_part_ref[rows, :] = mm(turned[rows, :], every).astype(bf16)
            return carry

        lax.fori_loop(0, span // 256, head_chunk, 0)
        scatter.line_step(3, ends=False)
        scatter.line_step(2, ends=False)
        for token in (1, 0):
            scatter.reduce(0, (token,))
            scatter.line_step(token)
        gather.finish()
        direct.drain()
        scatter.finish()

    vmem = pl.BlockSpec(memory_space=pltpu.VMEM)
    rows = jax.ShapeDtypeStruct((blocks, tok_dev), f32)
    return pl.pallas_call(
        kernel,
        name=name,
        out_shape=(scatter.out, jax.ShapeDtypeStruct(head_rows.shape, bf16), rows),
        in_specs=[vmem] * 3 + [pl.BlockSpec(memory_space=pltpu.SMEM)],
        out_specs=(vmem,) * 3,
        scratch_shapes=[
            pltpu.VMEM(gather.out.shape, bf16),
            pltpu.VMEM(direct.out.shape, f32),
            pltpu.VMEM((blocks, tok_dev), f32),
            pltpu.VMEM((blocks, span, tok_dev), f32),
            pltpu.VMEM((span, blocks * tok_dev), bf16),
            pltpu.VMEM(scatter.value.shape, bf16),
            pltpu.VMEM((blocks, tok_dev), f32),
            pltpu.VMEM((blocks, tok_dev), f32),
        ]
        + [item for job in jobs for item in job.scratch],
        compiler_params=pltpu.CompilerParams(
            collective_id=collective_id, has_side_effects=True, vmem_limit_bytes=60 * 1024 * 1024
        ),
    )(final_rows, head_rows, targets, lengths)


def opening(name, collective_id, weights, embedding, ids, memory, head, sizes):
    voc_dev, width = embedding.shape
    n_gy = 2 * sizes["s"]
    n_gx = 2 * sizes["a"]
    span = n_gx * voc_dev
    lines = sizes["s"]
    micro, _, seq_dev = ids[0].shape
    tok_dev = 2 * seq_dev
    table = Gather(embedding, "ac", "ac", sizes)
    codes = DirectGather(jax.ShapeDtypeStruct((8, 128), jnp.int32), sizes, "shc")
    memories = MemoryGather(memory, sizes)
    heads = Gather(head, "ac", "ac", sizes, "", 20)
    sums = Scatter(jax.ShapeDtypeStruct((lines, 2, tok_dev, width), bf16), "hs", "sh", sizes)
    jobs = list(weights) + [table, codes, memories, heads, sums]
    peers = peers_of(jobs)
    operands = [list(job.values) for job in weights] + [[embedding], list(ids), [memory], [head]]
    flat = [value for group in operands for value in group]

    def kernel(*refs):
        ins = list(refs[: len(flat)])
        outs = list(refs[len(flat) : len(flat) + 8])
        rest = list(refs[len(flat) + 8 :])
        place = coordinates()
        awaited = greet(peers, place)

        def take(source, count):
            taken = tuple(source[:count])
            del source[:count]
            return taken

        rows_ref, value, code, ids_ref = (rest.pop(0) for _ in range(4))
        for job in weights:
            pieces = take(ins, len(job.values))
            block = rest.pop(0)
            job.pack(pieces, block)
            job.prepare((block, outs.pop(0)) + take(rest, len(job.scratch) - 1), place)
        table.prepare((ins.pop(0), rows_ref) + take(rest, len(table.scratch)), place)
        pack_ids(take(ins, 2), code)
        local_ref, target_ref = outs.pop(0), outs.pop(0)
        codes.prepare((code, ids_ref) + take(rest, len(codes.scratch)), place)
        memories.prepare((ins.pop(0), outs.pop(0)) + take(rest, len(memories.scratch)), place)
        heads.prepare((ins.pop(0), outs.pop(0)) + take(rest, len(heads.scratch)), place)
        sums.prepare((value, outs.pop(0)) + take(rest, len(sums.scratch)), place)
        welcome(peers, place, awaited)

        def tables_here():
            codes.receive()
            table.local.wait()
            table.local_done = True
            for transfer in table.transfers:
                table.arrive(transfer)

        def pick(token):
            row = along_line(place["s"], token)

            def one(other, carry):
                side = place["h"] + (1 - other) * (1 - 2 * place["h"])
                indices = []
                for kind, ref in enumerate((local_ref, target_ref)):
                    line = pl.ds(micro * kind + row // 2, 1)
                    index = jnp.concatenate(
                        [
                            ids_ref[2 * side + place["c"], which, row % 2, line, :][:, :seq_dev]
                            for which in range(2)
                        ],
                        axis=1,
                    )
                    shard = index // voc_dev
                    held = shard % n_gy == 2 * place["s"] + place["h"]
                    index = jnp.where(held, shard // n_gy * voc_dev + index % voc_dev, -1)
                    ref[pl.ds(2 * row + side, 1), :] = index
                    indices.append(index)
                index = indices[0]
                at = lax.broadcasted_iota(jnp.int32, (span, tok_dev), 0) == index
                every = rows_ref[...].reshape(span, width)
                value[row, side] = t_mm(jnp.where(at, 1.0, 0.0).astype(bf16), every).astype(bf16)
                pl.when(other == 0)(functools.partial(sums.launch, 0, (token,), 1))
                return carry

            lax.fori_loop(0, 2, one, 0)

        events = [event for job in list(weights) + [memories, heads] for event in job.events()]
        events.append((-2, codes.begin))
        for transfer in table.transfers:
            level, unit, _ = transfer
            key = -1 if level == 0 else TABLE_KEY if unit[0] else 0.1
            events.append((key, functools.partial(table.launch, transfer)))
        events.append((TABLE_KEY + 0.05, tables_here))
        for number, token in enumerate((3, 2, 1, 0)):
            events.append((PICK_KEY + PICK_STEP * number, functools.partial(pick, token)))
            key = SUM_KEY + SUM_STEP * number
            events.append((key, functools.partial(sums.reduce, 0, (token,))))
            if token:
                events.append((key + 0.01, functools.partial(sums.line_step, token, middles=False)))
                events.append((LINE_KEY + SUM_STEP * number, functools.partial(sums.line_step, token, ends=False)))
            else:
                events.append((LINE_KEY + SUM_STEP * number, functools.partial(sums.line_step, token)))
        for _, act in sorted(events, key=lambda event: event[0]):
            act()
        for job in jobs:
            if job is codes:
                job.drain()
            else:
                job.finish()

    vmem = pl.BlockSpec(memory_space=pltpu.VMEM)
    anywhere = pl.BlockSpec(memory_space=pl.ANY)
    scratch = [
        pltpu.VMEM(table.out.shape, bf16),
        pltpu.VMEM(sums.value.shape, bf16),
        pltpu.VMEM((8, 128), jnp.int32),
        pltpu.VMEM(codes.out.shape, jnp.int32),
    ]
    places = jax.ShapeDtypeStruct((n_gy, tok_dev), jnp.int32)
    return pl.pallas_call(
        kernel,
        name=name,
        out_shape=tuple(job.out for job in weights)
        + (places, places, memories.out, heads.out, sums.out),
        in_specs=[vmem] * len(flat),
        out_specs=(anywhere,) * 3 + (vmem, vmem, anywhere, anywhere, vmem),
        scratch_shapes=scratch + [item for job in jobs for item in job.scratch],
        compiler_params=pltpu.CompilerParams(
            collective_id=collective_id, has_side_effects=True, vmem_limit_bytes=60 * 1024 * 1024
        ),
    )(*flat)


TABLE_KEY, PICK_KEY, PICK_STEP, SUM_KEY, SUM_STEP, LINE_KEY = 0.55, 0.65, 0.05, 1.3, 0.3, 1.9


def per_device(
    target_ids,
    labels,
    lengths,
    memory,
    embedding,
    head,
    gain_self,
    w_query,
    w_key,
    w_value,
    w_out,
    relative_bias,
    gain_cross,
    c_query,
    c_key,
    c_value,
    c_out,
    gain_ff,
    w_gate,
    w_up,
    w_down,
    gain_final,
):
    micro = target_ids.shape[0]
    seq_dev = target_ids.shape[2]
    mem_dev = memory.shape[2]
    voc_dev, width = embedding.shape
    ff = w_gate.shape[1]
    n_gx = lax.axis_size("gx")
    n_gy = lax.axis_size("gy")
    column = lax.axis_index("gy")
    row_group = lax.axis_index("gx")
    devices = n_gx * n_gy
    sizes = {"a": n_gx // 2, "c": 2, "s": n_gy // 2, "h": 2}
    assert sizes["s"] == 2 * micro
    place = coordinates()
    seq = seq_dev * n_gy
    plane = sizes["s"] * seq
    tok_dev = seq // 4
    tokens = plane // 2
    span = n_gx * voc_dev
    merged = "" if sizes["a"] == 2 else "ashc"

    rows_dev = width // devices
    whole_tiles = rows_dev % 16 == 0
    groups = (
        (w_gate, w_up),
        (w_down, c_key, c_value, c_out),
        (w_query, w_key, w_value, w_out, c_query),
    )
    gains = (gain_self, gain_cross, gain_ff, gain_final)
    widths = [sum(piece.shape[1] for piece in group) for group in groups]
    widths[2] += GAIN_PAD
    orders = ("shac", "shac", "sahc")
    ways_back = ("cahs", "chas", "chas")
    if whole_tiles:
        operands = list(groups)
        operands[2] += tuple(gain.reshape(1, rows_dev) for gain in gains)
        weights = [
            PackedGather(
                group,
                jax.ShapeDtypeStruct((rows_dev, count), bf16),
                pack_columns,
                order,
                "acsh",
                sizes,
                merged,
            )
            for group, count, order in zip(operands, widths, orders)
        ]
    else:
        shards = [jnp.concatenate(group, axis=1) for group in groups]
        columns_of = jnp.pad(jnp.stack(gains, axis=1), ((0, 0), (0, GAIN_PAD - 4)))
        shards[2] = jnp.concatenate([shards[2], columns_of], axis=1)
        weights = [
            Gather(packed(part), order, "acsh", sizes, merged) for part, order in zip(shards, orders)
        ]
    small_tables = whole_tiles and span <= 2048 and tok_dev == 128
    if small_tables:
        part_a, part_b, part_c, local_ids, targets, memory_all, head_rows, resid0 = opening(
            "start",
            0,
            weights,
            embedding,
            (target_ids, labels),
            memory.reshape(micro, mem_dev, width),
            head,
            sizes,
        )
    else:
        part_a, part_b, part_c, embed_rows, ids, memory_all = exchange(
            "gather_weights",
            0,
            weights
            + [
                Gather(embedding, "ac", "ac", sizes, "", 20),
                PackedGather(
                    (target_ids, labels),
                    jax.ShapeDtypeStruct((8, 128), jnp.int32),
                    pack_ids,
                    "shc",
                    "shc",
                    sizes,
                    "shc",
                ),
                MemoryGather(memory.reshape(micro, mem_dev, width), sizes),
            ],
        )
    part_a, part_b, part_c = (
        full.reshape(width, count) for full, count in zip((part_a, part_b, part_c), widths)
    )
    memory_all = memory_all.reshape(n_gy * mem_dev, width)
    if small_tables:
        local_ids = local_ids.reshape(tokens)
    else:
        ids = ids[..., : 2 * micro, :seq_dev].reshape(n_gy, 2, 2, micro, seq_dev)
        ids = ids.transpose(2, 3, 1, 0, 4).reshape(2, sizes["s"] * 2, 2, tok_dev)
        ids = lax.dynamic_index_in_dim(ids, place["c"], axis=2, keepdims=False).reshape(2, tokens)

        def local_of(index):
            shard = index // voc_dev
            return jnp.where(shard % n_gy == column, shard // n_gy * voc_dev + index % voc_dev, -1)

        local_ids = local_of(ids[0])
        targets = local_of(ids[1])
    columns = jnp.arange(span, dtype=jnp.int32)

    tok_layout = (sizes["s"], 2, tok_dev, width)
    if not small_tables:
        chosen = (local_ids[:, None] == columns[None, :]).astype(bf16)
        picked_rows = dot(chosen, embed_rows.reshape(span, width)).astype(bf16)
        resid0, head_rows = exchange(
            "rows",
            1,
            [
                Scatter(picked_rows.reshape(tok_layout), "hs", "sh", sizes),
                Gather(head, "ac", "ac", sizes, "", 20),
            ],
        )
    head_rows = head_rows.reshape(span, width)

    plane_lengths = lax.dynamic_slice_in_dim(lengths, 2 * place["a"], 2, axis=1).reshape(-1)
    table = jnp.asarray(distance_table(seq), bf16)
    query_self, own_kv, normed_self, gain_rows = local_kernel(
        "enter",
        enter_kernel,
        [((tok_dev, HD), bf16), ((tok_dev, 2 * HD), bf16), ((tok_dev, width), bf16), ((16, width), f32)],
        [resid0, part_c],
    )
    self_kv_all, mem_kv = exchange(
        "self_keys",
        2,
        [
            Gather(own_kv, "hc", "hc", sizes),
            Work(
                (memory_all, part_b),
                ((n_gy * mem_dev, 2 * HD), bf16),
                project_memory,
                0.5,
                (None, (ff, 2 * HD)),
            ),
        ],
    )
    self_kv_all = self_kv_all.reshape(seq, 2 * HD)
    rows_f32, rows_bf16, rows_heads = ((tok_dev, width), f32), ((tok_dev, width), bf16), ((tok_dev, HD), bf16)
    totals_shape = ((tok_dev, 128), f32)
    (
        attn_self,
        total_self,
        resid1,
        normed_cross,
        query_cross,
        attn_cross,
        total_cross,
        resid2,
        normed_ff,
        gate_up,
        hidden,
        resid3,
        final_rows,
    ) = local_kernel(
        "forward",
        forward_kernel,
        [
            rows_heads,
            totals_shape,
            rows_f32,
            rows_bf16,
            rows_heads,
            rows_heads,
            totals_shape,
            rows_f32,
            rows_bf16,
            ((tok_dev, 2 * ff), f32),
            ((tok_dev, ff), bf16),
            rows_f32,
            rows_bf16,
        ],
        [lengths, query_self, self_kv_all, resid0, gain_rows, table, relative_bias]
        + [mem_kv, part_a, part_b, part_c],
        "svvvvvvaaaa",
        scratch=[pltpu.VMEM(full.shape, bf16) for full in (mem_kv, part_a, part_b, part_c)]
        + [pltpu.SemaphoreType.DMA((4,))],
    )

    if small_tables:
        final_slope, head_part, loss_rows = vocabulary(
            "vocabulary", 3, final_rows, head_rows, targets, lengths, sizes
        )
    else:
        index = jnp.arange(tokens, dtype=jnp.int32)
        position = (2 * (index // tok_dev % 2) + place["c"]) * tok_dev + index % tok_dev
        alive = (position < jnp.repeat(plane_lengths, 2 * tok_dev)).astype(f32)
        (states,) = exchange("final_rows", 3, [Gather(final_rows, "sh", "sh", sizes, merged)])
        states = states.reshape(tokens, width)
        logits = dot_t(states, head_rows)
        highest = jnp.max(logits, axis=1)
        own_total = highest + jnp.log(jnp.sum(jnp.exp(logits - highest[:, None]), axis=1))
        (totals,) = exchange("totals", 4, [DirectGather(own_total.reshape(tokens // 128, 128), sizes)])
        totals = totals.reshape(n_gy, tokens)
        top = jnp.max(totals, axis=0)
        log_total = top + jnp.log(jnp.sum(jnp.exp(totals - top[None]), axis=0))
        hit = columns[None, :] == targets[:, None]
        picked = jnp.sum(jnp.where(hit, logits, 0.0), axis=1)
        slope = jnp.exp(logits - log_total[:, None]) - hit.astype(f32)
        slope = (slope * alive[:, None]).astype(bf16)
        head_part = t_dot(slope, states).astype(bf16)
        final_part = dot(slope, head_rows).astype(bf16)
        (final_slope,) = exchange(
            "final_slopes", 5, [Scatter(final_part.reshape(tok_layout), "hs", "sh", sizes)]
        )
        loss_rows = alive * (jnp.where(column == 0, log_total, 0.0) - picked)
        loss_rows = loss_rows.reshape(tokens // 128, 128)

    (
        part_grad_b,
        gate_up_slope,
        cross_kv_slope,
        part_grad_c,
        query_slope,
        kv_slope,
        grad1,
        norm_grads,
        bias_grad,
    ) = (
        local_kernel(
            "backward",
            backward_kernel,
            [
                ((width, ff + HD), bf16),
                ((tok_dev, 2 * ff), bf16),
                (mem_kv.shape, bf16),
                ((width, 2 * HD), bf16),
                rows_heads,
                ((seq, 2 * HD), bf16),
                rows_f32,
                (gain_rows.shape, f32),
                ((8, 128), f32),
            ],
            [lengths, final_slope, resid3, hidden, gate_up, normed_ff, resid2, attn_cross]
            + [query_cross, total_cross, normed_cross, resid1, attn_self, query_self, self_kv_all]
            + [total_self, gain_rows, table, relative_bias, mem_kv, part_a, part_b, part_c],
            "s" + "v" * 18 + "a" * 4,
            "a" + "v" * 8,
            [pltpu.VMEM(full.shape, bf16) for full in (mem_kv, part_a, part_b, part_c)]
            + [
                pltpu.VMEM((width, ff + HD), bf16),
                pltpu.VMEM((tok_dev, HD), bf16),
                pltpu.SemaphoreType.DMA((4,)),
                pltpu.SemaphoreType.DMA((1,)),
            ],
        )
    )
    kv_slope, grad_a, grad_b, memory_part = exchange(
        "key_slopes",
        6,
        [
            Scatter(kv_slope.reshape(2, 2, tok_dev, 2 * HD), "ch", "hc", sizes, "", bf16),
            Work((normed_ff, gate_up_slope), (part_a.shape, bf16), gate_up_grads, 0.9),
            Work(
                (memory_all, cross_kv_slope, part_grad_b), (part_b.shape, bf16), memory_weight_grads, 0.91
            ),
            Work(
                (cross_kv_slope, part_b),
                (memory_all.shape, bf16),
                memory_slopes,
                0.92,
                (None, (ff, 2 * HD)),
            ),
        ],
    )
    grad0, norm_grads = local_kernel(
        "leave",
        leave_kernel,
        [rows_bf16, (gain_rows.shape, f32)],
        [query_slope, kv_slope, resid0, grad1, gain_rows, norm_grads, part_c],
    )
    slopes, grad_c, head_grad = exchange(
        "row_slopes",
        7,
        [
            Gather(grad0, "sh", "sh", sizes, merged),
            Work(
                (query_slope, kv_slope, normed_self, norm_grads, part_grad_c),
                (part_c.shape, bf16),
                self_weight_grads,
                0.5,
            ),
            Scatter(head_part.reshape(sizes["a"], 2, voc_dev, width), "ca", "ac", sizes),
        ],
    )
    embed_part = t_dot(
        (local_ids[:, None] == columns[None, :]).astype(bf16), slopes.reshape(tokens, width)
    ).astype(bf16)
    sums = (grad_a, grad_b, grad_c)
    device_layout = (sizes["a"], 2, sizes["s"], 2)
    blocks = [part.reshape(device_layout + packed_shape(part, devices)) for part in sums]
    grad_a, grad_b, grad_c, embedding_grad, memory_grad, small = exchange(
        "scatter_weights",
        8,
        [
            Scatter(part, order, "acsh", sizes, merged)
            for part, order in zip(blocks, ways_back)
        ]
        + [
            Scatter(embed_part.reshape(sizes["a"], 2, voc_dev, width), "ca", "ac", sizes),
            MemoryScatter(memory_part.reshape(sizes["s"], 2, mem_dev, width), sizes),
            PackedGather(
                (bias_grad, loss_rows),
                jax.ShapeDtypeStruct((16, 128), f32),
                pack_rows,
                "shac",
                "acsh",
                sizes,
                "ashc",
            ),
        ],
    )
    small = small.reshape(devices, 16, 128)
    memory_grad = memory_grad.reshape(micro, 1, mem_dev, width)
    if whole_tiles:
        pieces = [piece.shape[1] for group in groups for piece in group]
        outs = [
            ((1, 1), f32),
            (memory_grad.shape, f32),
            (embedding_grad.shape, f32),
            (head_grad.shape, f32),
            ((HEADS, BUCKETS), f32),
        ]
        outs += [((rows_dev, count), f32) for count in pieces] + [((1, rows_dev), f32)] * 4
        results = local_kernel(
            "tail",
            tail_kernel,
            outs,
            [lengths, grad_a, grad_b, grad_c, small, memory_grad, embedding_grad, head_grad],
            "s" + "v" * 7,
        )
        loss, memory_grad, embedding_grad, head_grad, bias_total = results[:5]
        loss = loss.reshape(())
        cut = results[5:16]
        gain_out = [gain.reshape(rows_dev) for gain in results[16:]]
    else:
        grad_a, grad_b, grad_c = (
            grad.reshape(rows_dev, count) for grad, count in zip((grad_a, grad_b, grad_c), widths)
        )
        small = jnp.sum(small, axis=0)
        loss = jnp.sum(small[8:]) / jnp.sum(lengths).astype(f32)
        bias_total = small[:HEADS, :BUCKETS]
        cut = []
        for grad, group in zip((grad_a, grad_b, grad_c), groups):
            start = 0
            for piece in group:
                cut.append(grad[:, start : start + piece.shape[1]])
                start += piece.shape[1]
        gain_out = [grad_c[:, 5 * HD + number] for number in range(4)]
    gate_grad, up_grad, down_grad, c_key_grad, c_value_grad, c_out_grad = cut[:6]
    query_grad, key_grad, value_grad, out_grad, c_query_grad = cut[6:]
    return (
        loss,
        memory_grad,
        embedding_grad,
        head_grad,
        gain_out[0],
        query_grad,
        key_grad,
        value_grad,
        out_grad,
        bias_total,
        gain_out[1],
        c_query_grad,
        c_key_grad,
        c_value_grad,
        c_out_grad,
        gain_out[2],
        gate_grad,
        up_grad,
        down_grad,
        gain_out[3],
    )


def packed_shape(part, count):
    rows, columns = part.shape[0] // count, part.shape[1]
    if rows % 16 == 0:
        return (rows, columns)
    return (16, rows * columns // 16)


def solution(mesh):
    placed = (
        P(None, "gx", "gy"),
        P(None, "gx", "gy"),
        P(),
        P(None, "gx", "gy", None),
        P(("gx", "gy"), None),
        P(("gx", "gy"), None),
        P(("gx", "gy")),
        P(("gx", "gy"), None),
        P(("gx", "gy"), None),
        P(("gx", "gy"), None),
        P(("gx", "gy"), None),
        P(),
        P(("gx", "gy")),
        P(("gx", "gy"), None),
        P(("gx", "gy"), None),
        P(("gx", "gy"), None),
        P(("gx", "gy"), None),
        P(("gx", "gy")),
        P(("gx", "gy"), None),
        P(("gx", "gy"), None),
        P(("gx", "gy"), None),
        P(("gx", "gy")),
    )
    return jax.shard_map(
        per_device,
        mesh=mesh,
        in_specs=placed,
        out_specs=(
            P(),
            P(None, "gx", "gy", None),
            P(("gx", "gy"), None),
            P(("gx", "gy"), None),
            P(("gx", "gy")),
            P(("gx", "gy"), None),
            P(("gx", "gy"), None),
            P(("gx", "gy"), None),
            P(("gx", "gy"), None),
            P(),
            P(("gx", "gy")),
            P(("gx", "gy"), None),
            P(("gx", "gy"), None),
            P(("gx", "gy"), None),
            P(("gx", "gy"), None),
            P(("gx", "gy")),
            P(("gx", "gy"), None),
            P(("gx", "gy"), None),
            P(("gx", "gy"), None),
            P(("gx", "gy")),
        ),
        check_vma=False,
    )
```

```python
import functools
import itertools
import math

import jax
import jax.numpy as jnp
import numpy as np
from jax import lax
from jax.experimental import pallas as pl
from jax.experimental.pallas import tpu as pltpu
from jax.sharding import PartitionSpec as P

HEADS = 6
HEAD = 64
HD = HEADS * HEAD
BUCKETS = 32
GAIN_PAD = 128

eps = 1e-06
masked_score = -1000000000.0
bf16 = jnp.bfloat16
f32 = jnp.float32


def flip(position, offset):
    moved = position
    weight = 1
    while weight <= offset:
        if offset & weight:
            moved = moved + weight * (1 - 2 * ((position // weight) % 2))
        weight *= 2
    return moved


def coordinates():
    gx, gy = lax.axis_index("gx"), lax.axis_index("gy")
    return {"a": gx // 2, "c": gx % 2, "s": gy // 2, "h": gy % 2}


def peer_of(dim, offset):
    gx, gy = lax.axis_index("gx"), lax.axis_index("gy")
    if dim == "a":
        return {"gx": 2 * flip(gx // 2, offset) + gx % 2}
    if dim == "c":
        return {"gx": flip(gx, 1)}
    if dim == "plane":
        s, h, c = offset + (0,) * (3 - len(offset))
        there = {"gy": 2 * flip(gy // 2, s) + flip(gy % 2, h)}
        if c:
            there["gx"] = flip(gx, 1)
        return there
    if dim == "s":
        return {"gy": 2 * flip(gy // 2, offset) + gy % 2}
    return {"gy": flip(gy, 1)}


def remote(source, target, send, recv, dim, offset):
    return pltpu.make_async_remote_copy(
        src_ref=source,
        dst_ref=target,
        send_sem=send,
        recv_sem=recv,
        device_id=peer_of(dim, offset),
        device_id_type=pl.DeviceIdType.MESH,
    )


def along_line(position, step):
    half = position // 2
    return (position, flip(position, 1), 2 - half, 3 - 3 * half)[step]


def is_middle(position):
    return (position + 1) // 2 == 1


def across_middle():
    gy = lax.axis_index("gy")
    return {"gy": 2 * (3 - gy // 2) + gy % 2}


def spot_of(dim, position, offset):
    return along_line(position, offset) if dim == "s" else flip(position, offset)


def remote_to(source, target, send, recv, device):
    return pltpu.make_async_remote_copy(
        src_ref=source,
        dst_ref=target,
        send_sem=send,
        recv_sem=recv,
        device_id=device,
        device_id_type=pl.DeviceIdType.MESH,
    )


def each_piece(rows, columns, body, width=16384):
    step = rows
    while step * columns > width and step % 32 == 0:
        step //= 2
    if step == rows:
        body(slice(None))
        return

    def piece(number, carry):
        body(pl.ds(pl.multiple_of(number * step, step), step))
        return carry

    lax.fori_loop(0, rows // step, piece, 0)


LINE_PEERS = [("s", 1), ("m", 1)]


class Gather:
    def __init__(self, block, order, layout, sizes, merged="", late=0):
        self.value = block
        self.late = late
        self.order, self.layout, self.sizes, self.merged = order, layout, sizes, merged
        self.out = jax.ShapeDtypeStruct(tuple(sizes[d] for d in layout) + block.shape, block.dtype)
        self.in_spec = pl.BlockSpec(memory_space=pltpu.VMEM)
        self.out_spec = pl.BlockSpec(memory_space=pl.ANY)
        self.transfers = []
        for level, dim in enumerate(order):
            ranges = [(None,) if d in merged else range(sizes[d]) for d in order[:level]]
            for unit in itertools.product(*ranges):
                for offset in range(1, sizes[dim]):
                    self.transfers.append((level, unit, offset))
        self.index = {transfer: number for number, transfer in enumerate(self.transfers)}
        count = len(self.transfers)
        self.line = order[0] == "s"
        self.scratch = [
            pltpu.SemaphoreType.DMA((count,)),
            pltpu.SemaphoreType.DMA((count,)),
            pltpu.SemaphoreType.DMA,
            pltpu.SemaphoreType.DMA((5,)),
        ]
        self.peers = [(d, offset) for d in order for offset in range(1, sizes[d]) if d != "s"]
        if self.line:
            self.peers += LINE_PEERS

    def prepare(self, refs, place):
        self.source, self.target, self.send, self.recv, self.local_sem, self.line_send = refs
        self.place = place
        self.local = pltpu.make_async_copy(
            self.source, self.target.at[tuple(place[d] for d in self.layout)], self.local_sem
        )
        self.local.start()
        self.local_done = False
        self.arrived = set()
        self.sent = []

    def region(self, level, unit, offset):
        where = dict(self.place)
        for d, moved in zip(self.order[:level], unit):
            where[d] = slice(None) if moved is None else spot_of(d, self.place[d], moved)
        if offset:
            dim = self.order[level]
            where[dim] = spot_of(dim, self.place[dim], offset)
        return self.target.at[tuple(where[d] for d in self.layout)]

    def needs(self, level, unit):
        if level == 0:
            return []
        last, before = unit[-1], unit[:-1]
        if last is None:
            dim = self.order[level - 1]
            return self.needs(level - 1, before) + [
                (level - 1, before, offset) for offset in range(1, self.sizes[dim])
            ]
        if last == 0:
            return self.needs(level - 1, before)
        return [(level - 1, before, last)]

    def arrive(self, transfer):
        if transfer in self.arrived:
            return
        self.arrived.add(transfer)
        level, unit, offset = transfer
        number = self.index[transfer]
        there = self.region(level, unit, offset)
        if self.line and level == 0:
            offset = 1
        remote(
            there, there, self.send.at[number], self.recv.at[number], self.order[level], offset
        ).wait_recv()

    def line_copy(self, number):
        held, there = ((0, 1), (0, 2), (1, 3), (2, 2), (3, 3))[number]
        target = self.region(0, (), held)
        device = peer_of("s", 1) if number in (0, 3, 4) else across_middle()
        recv = self.recv.at[self.index[(0, (), there)]]
        source = target if held else self.source
        return remote_to(source, target, self.line_send.at[number], recv, device)

    def line_first(self):
        self.line_copy(0).start()

        @pl.when(is_middle(self.place["s"]))
        def _():
            self.line_copy(1).start()

    def line_next(self, step):
        self.arrive((0, (), step))

        @pl.when(is_middle(self.place["s"]))
        def _():
            self.line_copy(step + 1).start()

    def copy(self, transfer):
        level, unit, offset = transfer
        number = self.index[transfer]
        target = self.region(level, unit, 0)
        own = all(moved == 0 for moved in unit)
        return remote(
            self.source if own else target,
            target,
            self.send.at[number],
            self.recv.at[number],
            self.order[level],
            offset,
        )

    def launch(self, transfer):
        level, unit, offset = transfer
        for need in self.needs(level, unit):
            self.arrive(need)
        if None in unit and not self.local_done:
            self.local.wait()
            self.local_done = True
        self.copy(transfer).start()
        self.sent.append(transfer)

    def events(self):
        found = []
        if self.line:
            found.append((0, self.line_first))
            for step in (1, 2, 3):
                found.append((step, functools.partial(self.line_next, step)))
        for transfer in self.transfers:
            level, unit, offset = transfer
            if self.line and level == 0:
                continue
            key = 0.1 * level + 0.01 * offset
            for d, moved in zip(self.order, unit):
                key += self.sizes[d] - 1 if moved is None else moved
            if self.late and self.needs(level, unit):
                key += self.late
            found.append((key, functools.partial(self.launch, transfer)))
        return found

    def finish(self):
        if not self.local_done:
            self.local.wait()
        for transfer in self.transfers:
            self.arrive(transfer)
        for transfer in self.sent:
            self.copy(transfer).wait_send()
        if self.line:
            self.line_copy(0).wait_send()

            @pl.when(is_middle(self.place["s"]))
            def _():
                for number in range(1, 5):
                    self.line_copy(number).wait_send()


class Work:
    def __init__(self, values, out, act, key, columns=None):
        self.values, self.act, self.key = list(values), act, key
        self.columns = columns or [None] * len(self.values)
        self.out = jax.ShapeDtypeStruct(*out)
        self.in_spec = self.out_spec = pl.BlockSpec(memory_space=pl.ANY)
        shapes = [
            value.shape if cut is None else (value.shape[0], cut[1])
            for value, cut in zip(self.values, self.columns)
        ]
        self.scratch = [pltpu.VMEM(shape, value.dtype) for shape, value in zip(shapes, self.values)]
        self.scratch += [pltpu.VMEM(*out), pltpu.SemaphoreType.DMA((len(shapes) + 1,))]
        self.peers = []

    def prepare(self, refs, place):
        count = len(self.values)
        self.held, self.result, sems = refs[count + 1 : 2 * count + 1], refs[-2], refs[-1]
        self.copies = []
        for number, (source, cut, held) in enumerate(zip(refs, self.columns, self.held)):
            source = source if cut is None else source.at[:, cut[0] : cut[0] + cut[1]]
            self.copies.append(pltpu.make_async_copy(source, held, sems.at[number]))
            self.copies[-1].start()
        self.back = pltpu.make_async_copy(self.result, refs[count], sems.at[count])

    def events(self):
        return [(self.key, self.run)]

    def run(self):
        for copy in self.copies:
            copy.wait()
        self.act(self.held, self.result)
        self.back.start()

    def finish(self):
        self.back.wait()


class EmbedPart:
    def __init__(self, ids, span, gather):
        self.value, self.gather = ids, gather
        gather.out_spec = pl.BlockSpec(memory_space=pltpu.VMEM)
        width = gather.value.shape[1]
        self.out = jax.ShapeDtypeStruct((span, width), bf16)
        self.in_spec = self.out_spec = pl.BlockSpec(memory_space=pltpu.VMEM)
        self.scratch = [pltpu.VMEM((span, ids.shape[0] * ids.shape[1]), bf16)]
        self.peers = []

    def prepare(self, refs, place):
        self.ids, self.result, self.chosen = refs

    def events(self):
        return [(0.6, self.choose), (15, self.run)]

    def choose(self):
        blocks, wide = self.ids.shape
        span = self.chosen.shape[0]

        def one(number, carry):
            at = lax.broadcasted_iota(jnp.int32, (span, wide), 0) == self.ids[pl.ds(number, 1), :]
            lanes = pl.ds(pl.multiple_of(number * wide, wide), wide)
            self.chosen[:, lanes] = jnp.where(at, 1.0, 0.0).astype(bf16)
            return carry

        lax.fori_loop(0, blocks, one, 0)

    def run(self):
        gather = self.gather
        gather.local.wait()
        gather.local_done = True
        for transfer in gather.transfers:
            gather.arrive(transfer)
        span, width = self.result.shape

        def one(number, carry):
            rows = pl.ds(pl.multiple_of(number * 256, 256), 256)
            every = gather.target[...].reshape(self.chosen.shape[1], width)
            self.result[rows, :] = mm(self.chosen[rows, :], every).astype(bf16)
            return carry

        lax.fori_loop(0, span // 256, one, 0)

    def finish(self):
        pass


class PackedGather(Gather):
    def __init__(self, values, block, pack, *args):
        super().__init__(block, *args)
        self.values, self.pack = values, pack
        self.scratch = [pltpu.VMEM(block.shape, block.dtype)] + self.scratch


class DirectGather:
    def __init__(self, block, sizes, dims="sh"):
        self.value = block
        self.dims = dims
        shape = tuple(sizes[d] for d in dims)
        self.out = jax.ShapeDtypeStruct(shape + block.shape, block.dtype)
        self.in_spec = pl.BlockSpec(memory_space=pltpu.VMEM)
        self.out_spec = pl.BlockSpec(memory_space=pltpu.VMEM)
        self.offsets = list(itertools.product(*(range(size) for size in shape)))[1:]
        count = len(self.offsets)
        self.scratch = [pltpu.SemaphoreType.DMA((count,)), pltpu.SemaphoreType.DMA((count,))]
        self.peers = [("plane", offset) for offset in self.offsets]

    def prepare(self, refs, place):
        self.source, self.target, self.send, self.recv = refs
        self.place = place

    def copy(self, number, arriving):
        offset = self.offsets[number]
        spot = tuple(
            flip(self.place[d], moved) if arriving else self.place[d] for d, moved in zip(self.dims, offset)
        )
        return remote_to(
            self.source,
            self.target.at[spot],
            self.send.at[number],
            self.recv.at[number],
            peer_of("plane", offset),
        )

    def events(self):
        return [(0, self.begin)]

    def begin(self):
        for number in range(len(self.offsets)):
            self.copy(number, False).start()
        self.target[tuple(self.place[d] for d in self.dims)] = self.source[...]

    def finish(self):
        self.receive()
        self.drain()

    def receive(self):
        for number in range(len(self.offsets)):
            self.copy(number, True).wait_recv()

    def drain(self):
        for number in range(len(self.offsets)):
            self.copy(number, False).wait_send()


class Scatter:
    def __init__(self, value, order, layout, sizes, merged="", out_dtype=f32):
        self.value = value
        self.order, self.layout, self.sizes, self.merged = order, layout, sizes, merged
        self.block = value.shape[len(layout) :]
        self.out = jax.ShapeDtypeStruct(self.block, out_dtype)
        self.in_spec = pl.BlockSpec(memory_space=pltpu.VMEM)
        self.out_spec = pl.BlockSpec(memory_space=pltpu.VMEM)
        self.line = order[-1] == "s"
        self.levels = len(order)
        self.units = []
        self.scratch = []
        self.layouts = [layout]
        for level, dim in enumerate(order):
            later = order[level + 1 :]
            ranges = [(None,) if d in merged else range(sizes[d]) for d in later]
            units = sorted(
                itertools.product(*ranges),
                key=lambda unit: (-(unit[-1] or 0) if unit else 0, -sum(moved or 0 for moved in unit)),
            )
            self.units.append(units)
            left = "".join(d for d in self.layouts[-1] if d != dim)
            self.layouts.append(left)
            self.scratch.append(
                pltpu.VMEM(
                    (5 if dim == "s" else sizes[dim] - 1,)
                    + tuple(sizes[d] for d in left)
                    + self.block,
                    value.dtype,
                )
            )
        self.index = {}
        for level, dim in enumerate(order):
            for unit in self.units[level]:
                for offset in range(1, sizes[dim]):
                    self.index[(level, unit, offset)] = len(self.index)
        count = len(self.index)
        self.scratch += [
            pltpu.SemaphoreType.DMA((count,)),
            pltpu.SemaphoreType.DMA((count,)),
            pltpu.SemaphoreType.DMA((2, 5)),
        ]
        self.peers = [(d, offset) for d in order for offset in range(1, sizes[d]) if d != "s"]
        if self.line:
            self.peers += LINE_PEERS

    def prepare(self, refs, place):
        self.source, self.target = refs[0], refs[1]
        self.landing = refs[2 : 2 + self.levels]
        self.send, self.recv, self.line_sems = refs[2 + self.levels :]
        self.place = place
        self.sent = []

    def held(self, level):
        return self.source if level == 0 else self.landing[level - 1].at[0]

    def later(self, level, unit):
        where = {}
        for d, moved in zip(self.order[level + 1 :], unit):
            where[d] = slice(None) if moved is None else spot_of(d, self.place[d], moved)
        return where

    def copy(self, level, unit, offset):
        number = self.index[(level, unit, offset)]
        dim = self.order[level]
        where = self.later(level, unit)
        landed = self.landing[level].at[
            (offset - 1,) + tuple(where[d] for d in self.layouts[level + 1])
        ]
        where[dim] = flip(self.place[dim], offset)
        source = self.held(level).at[tuple(where[d] for d in self.layouts[level])]
        return remote(source, landed, self.send.at[number], self.recv.at[number], dim, offset)

    def launch(self, level, unit, offset):
        self.copy(level, unit, offset).start()
        self.sent.append((level, unit, offset))

    def reduce(self, level, unit):
        dim = self.order[level]
        size = self.sizes[dim]
        for offset in range(1, size):
            self.copy(level, unit, offset).wait_recv()
        where = self.later(level, unit)
        free = [d for d in self.order[level + 1 :] if isinstance(where[d], slice)]
        total = math.prod(self.sizes[d] for d in free)
        rows, columns = self.block
        last = level == self.levels - 1

        def one(number, carry):
            at = dict(where)
            rest = number
            for d in free:
                at[d] = rest % self.sizes[d]
                rest = rest // self.sizes[d]
            spot = tuple(at[d] for d in self.layouts[level + 1])
            at[dim] = self.place[dim]
            mine = tuple(at[d] for d in self.layouts[level])

            def body(piece):
                if not last and size == 2:
                    self.landing[level][(0,) + spot + (piece,)] += self.held(level)[mine + (piece,)]
                    return
                result = self.held(level)[mine + (piece,)].astype(f32)
                for offset in range(1, size):
                    result = result + self.landing[level][(offset - 1,) + spot + (piece,)].astype(f32)
                if last:
                    self.target[(piece,)] = result.astype(self.target.dtype)
                else:
                    self.landing[level][(0,) + spot + (piece,)] = result.astype(self.landing[level].dtype)

            each_piece(rows, columns, body)
            return carry

        if total == 1:
            one(0, 0)
        else:
            lax.fori_loop(0, total, one, 0)
        if not last and not (self.line and level == self.levels - 2):
            ahead, rest = unit[0], unit[1:]
            if ahead is None:
                offsets = range(1, self.sizes[self.order[level + 1]])
            else:
                offsets = [ahead] if ahead else []
            for offset in offsets:
                self.launch(level + 1, rest, offset)

    def line_copy(self, number):
        step, slot = ((1, 0), (2, 1), (3, 2), (3, 3), (2, 4))[number]
        level = self.levels - 1
        block = self.held(level).at[along_line(self.place["s"], step)]
        landed = self.landing[level].at[slot]
        device = peer_of("s", 1) if number < 3 else across_middle()
        return remote_to(block, landed, self.line_sems.at[0, number], self.line_sems.at[1, number], device)

    def line_step(self, step, ends=True, middles=True):
        level = self.levels - 1
        middle = is_middle(self.place["s"])
        rows, columns = self.block
        held, landing = self.held(level), self.landing[level]
        position = along_line(self.place["s"], step)

        def pass_on():
            arrived = (0, 3, 1, 2)[step]
            self.line_copy(arrived).wait_recv()

            def body(piece):
                held[(position, piece)] += landing[(arrived, piece)]

            each_piece(rows, columns, body)
            self.line_copy((0, 0, 4, 3)[step]).start()

        if step:
            if ends:
                pl.when(jnp.logical_not(middle))(lambda: self.line_copy(step - 1).start())
            if middles:
                pl.when(middle)(pass_on)
            return

        self.line_copy(0).wait_recv()

        @pl.when(middle)
        def _():
            self.line_copy(4).wait_recv()

            def body(piece):
                result = held[(position, piece)].astype(f32) + landing[(0, piece)].astype(f32)
                self.target[(piece,)] = (result + landing[(4, piece)].astype(f32)).astype(
                    self.target.dtype
                )

            each_piece(rows, columns, body)

        @pl.when(jnp.logical_not(middle))
        def _():
            def body(piece):
                result = held[(position, piece)].astype(f32) + landing[(0, piece)].astype(f32)
                self.target[(piece,)] = result.astype(self.target.dtype)

            each_piece(rows, columns, body)

    def events(self):
        found = []
        for number, unit in enumerate(self.units[0]):
            for offset in range(1, self.sizes[self.order[0]]):
                found.append(
                    (-1 + 0.001 * number, functools.partial(self.launch, 0, unit, offset))
                )
        spread = 4 if self.line else 1
        for level in range(self.levels - self.line):
            count = len(self.units[level])
            for number, unit in enumerate(self.units[level]):
                late = 0
                if self.order[-1] == "a":
                    late = 20 if level == self.levels - 1 else 0.9
                found.append(
                    (late + level + spread * number / count, functools.partial(self.reduce, level, unit))
                )
        if self.line:
            for number, step in enumerate((3, 2, 1, 0)):
                found.append(
                    (self.levels - 1 + number + 0.5, functools.partial(self.line_step, step))
                )
        return found

    def finish(self):
        for transfer in self.sent:
            self.copy(*transfer).wait_send()
        if self.line:
            self.line_copy(0).wait_send()
            middle = is_middle(self.place["s"])

            @pl.when(middle)
            def _():
                for number in (3, 4):
                    self.line_copy(number).wait_send()

            @pl.when(jnp.logical_not(middle))
            def _():
                for number in (1, 2):
                    self.line_copy(number).wait_send()


class MemoryGather:
    def __init__(self, memory, sizes):
        self.value = memory
        self.sizes = sizes
        self.out = jax.ShapeDtypeStruct((sizes["s"], 2) + memory.shape[1:], memory.dtype)
        self.in_spec = pl.BlockSpec(memory_space=pltpu.VMEM)
        self.out_spec = pl.BlockSpec(memory_space=pl.ANY)
        rows = sizes["s"]
        self.scratch = [
            pltpu.SemaphoreType.DMA((2, rows)),
            pltpu.SemaphoreType.DMA((2, rows)),
            pltpu.SemaphoreType.DMA((2, rows, 2)),
            pltpu.SemaphoreType.DMA,
        ]
        self.peers = [("s", offset) for offset in range(1, rows)] + [("h", 1), ("c", 1)]

    def prepare(self, refs, place):
        self.source, self.target, self.along, self.across, self.core, self.local = refs
        self.place = place
        self.mine = place["s"] % 2 == place["c"]

    def row(self, offset):
        return flip(self.place["s"], offset)

    def along_copy(self, offset, arriving):
        to = self.row(offset)
        spot = to if arriving else self.place["s"]
        return remote(
            self.source.at[self.place["s"] // 2 if arriving else to // 2],
            self.target.at[spot, self.place["h"]],
            self.along.at[0, offset],
            self.along.at[1, offset],
            "s",
            offset,
        )

    def across_copy(self, offset, arriving):
        h = self.place["h"]
        own = self.target.at[self.row(offset), 1 - h if arriving else h]
        if offset == 0 and not arriving:
            source = self.source.at[self.place["s"] // 2]
        else:
            source = own
        return remote(source, own, self.across.at[0, offset], self.across.at[1, offset], "h", 1)

    def core_copy(self, offset, other):
        h = self.place["h"]
        own = self.target.at[self.row(offset), 1 - h if other else h]
        source = self.source.at[self.place["s"] // 2] if offset == 0 and not other else own
        return remote(source, own, self.core.at[0, offset, other], self.core.at[1, offset, other], "c", 1)

    def events(self):
        rows = self.sizes["s"]

        def first():
            for offset in range(1, rows):
                @pl.when(self.row(offset) % 2 == self.place["c"])
                def _():
                    self.along_copy(offset, False).start()

            @pl.when(self.mine)
            def _():
                pltpu.make_async_copy(
                    self.source.at[self.place["s"] // 2],
                    self.target.at[self.place["s"], self.place["h"]],
                    self.local,
                ).start()
                self.across_copy(0, False).start()
                self.core_copy(0, 0).start()

        def arrival(offset):
            @pl.when(self.mine)
            def _():
                self.along_copy(offset, True).wait_recv()
                self.across_copy(offset, False).start()
                self.core_copy(offset, 0).start()

        def other(offset):
            @pl.when(self.mine)
            def _():
                self.across_copy(offset, True).wait_recv()
                self.core_copy(offset, 1).start()

        found = [(0.05, first)]
        for offset in range(1, rows):
            found.append((offset + 0.05, functools.partial(arrival, offset)))
        for offset in range(rows):
            found.append((rows + offset, functools.partial(other, offset)))
        return found

    def finish(self):
        rows = self.sizes["s"]
        for offset in range(1, rows):
            @pl.when(self.row(offset) % 2 == self.place["c"])
            def _():
                self.along_copy(offset, False).wait_send()

        @pl.when(self.mine)
        def _():
            pltpu.make_async_copy(
                self.source.at[self.place["s"] // 2],
                self.target.at[self.place["s"], self.place["h"]],
                self.local,
            ).wait()
            for offset in range(rows):
                self.across_copy(offset, False).wait_send()
                for other in range(2):
                    self.core_copy(offset, other).wait_send()

        @pl.when(jnp.logical_not(self.mine))
        def _():
            for offset in range(rows):
                for other in range(2):
                    self.core_copy(offset, other).wait_recv()


class MemoryScatter:
    def __init__(self, value, sizes):
        self.value = value
        self.sizes = sizes
        rows = sizes["s"]
        self.block = value.shape[2:]
        self.out = jax.ShapeDtypeStruct((2,) + self.block, f32)
        self.in_spec = pl.BlockSpec(memory_space=pltpu.VMEM)
        self.out_spec = pl.BlockSpec(memory_space=pltpu.VMEM)
        self.scratch = [
            pltpu.VMEM(value.shape, value.dtype),
            pltpu.VMEM((rows,) + self.block, value.dtype),
            pltpu.VMEM((2,) + self.block, value.dtype),
            pltpu.SemaphoreType.DMA((2, rows, 2)),
            pltpu.SemaphoreType.DMA((2, rows)),
            pltpu.SemaphoreType.DMA((2, rows)),
        ]
        self.peers = [("s", offset) for offset in range(1, rows)] + [("h", 1), ("c", 1)]

    def prepare(self, refs, place):
        self.source, self.target = refs[0], refs[1]
        self.summed, self.halved, self.landed, self.core, self.across, self.along = refs[2:]
        self.place = place
        self.mine = place["s"] % 2 == place["c"]

    def row(self, offset):
        return flip(self.place["s"], offset)

    def core_copy(self, offset, other):
        h = self.place["h"]
        spot = (self.row(offset), flip(h, 1) if other else h)
        return remote(
            self.source.at[spot],
            self.summed.at[spot],
            self.core.at[0, offset, other],
            self.core.at[1, offset, other],
            "c",
            1,
        )

    def across_copy(self, offset):
        row = self.row(offset)
        return remote(
            self.summed.at[row, flip(self.place["h"], 1)],
            self.halved.at[row],
            self.across.at[0, offset],
            self.across.at[1, offset],
            "h",
            1,
        )

    def along_copy(self, offset, arriving):
        to = self.row(offset)
        return remote(
            self.halved.at[to],
            self.landed.at[to // 2 if arriving else self.place["s"] // 2],
            self.along.at[0, offset],
            self.along.at[1, offset],
            "s",
            offset,
        )

    def events(self):
        rows = self.sizes["s"]
        high, wide = self.block
        orders = list(range(1, rows))[::-1] + [0]

        def first():
            @pl.when(jnp.logical_not(self.mine))
            def _():
                for other in (1, 0):
                    for offset in orders:
                        self.core_copy(offset, other).start()

        def level(offset, other):
            @pl.when(self.mine)
            def _():
                self.core_copy(offset, other).wait_recv()
                h = self.place["h"]
                spot = (self.row(offset), flip(h, 1) if other else h)

                def body(piece):
                    total = self.summed[spot + (piece,)].astype(f32) + self.source[
                        spot + (piece,)
                    ].astype(f32)
                    self.summed[spot + (piece,)] = total.astype(self.summed.dtype)

                each_piece(high, wide, body)
                if other:
                    self.across_copy(offset).start()

        def last(offset):
            @pl.when(self.mine)
            def _():
                self.across_copy(offset).wait_recv()
                row = self.row(offset)

                def body(piece):
                    total = self.halved[(row, piece)].astype(f32) + self.summed[
                        (row, self.place["h"], piece)
                    ].astype(f32)
                    self.halved[(row, piece)] = total.astype(self.halved.dtype)
                    if offset == 0:
                        self.target[(self.place["s"] // 2, piece)] = total

                each_piece(high, wide, body)
                if offset:
                    self.along_copy(offset, False).start()

        found = [(-0.95, first)]
        for number, offset in enumerate(orders):
            found.append((0.05 + 0.1 * number, functools.partial(level, offset, 1)))
        for number, offset in enumerate(orders):
            found.append((0.55 + 0.1 * number, functools.partial(level, offset, 0)))
        for number, offset in enumerate(orders):
            found.append((1.05 + 0.2 * number, functools.partial(last, offset)))
        return found

    def finish(self):
        rows = self.sizes["s"]
        high, wide = self.block
        for offset in range(1, rows):
            @pl.when(self.row(offset) % 2 == self.place["c"])
            def _():
                self.along_copy(offset, True).wait_recv()
                number = self.row(offset) // 2

                def body(piece):
                    self.target[(number, piece)] = self.landed[(number, piece)].astype(f32)

                each_piece(high, wide, body)

        @pl.when(self.mine)
        def _():
            for offset in range(rows):
                self.across_copy(offset).wait_send()
            for offset in range(1, rows):
                self.along_copy(offset, False).wait_send()

        @pl.when(jnp.logical_not(self.mine))
        def _():
            for offset in range(rows):
                for other in range(2):
                    self.core_copy(offset, other).wait_send()


def peers_of(jobs):
    peers = []
    for job in jobs:
        for peer in job.peers:
            if peer not in peers:
                peers.append(peer)
    return peers


def greet(peers, place):
    barrier = pltpu.get_barrier_semaphore()
    middle = is_middle(place["s"])
    awaited = 0
    for peer in peers:
        if peer[0] == "m":
            @pl.when(middle)
            def _():
                pl.semaphore_signal(
                    barrier, inc=1, device_id=across_middle(), device_id_type=pl.DeviceIdType.MESH
                )
            continue
        awaited += 1
        pl.semaphore_signal(
            barrier, inc=1, device_id=peer_of(*peer), device_id_type=pl.DeviceIdType.MESH
        )
    return awaited


def welcome(peers, place, awaited):
    barrier = pltpu.get_barrier_semaphore()
    middle = is_middle(place["s"])
    if ("m", 1) in peers:
        @pl.when(middle)
        def _():
            pl.semaphore_wait(barrier, awaited + 1)

        @pl.when(jnp.logical_not(middle))
        def _():
            pl.semaphore_wait(barrier, awaited)
    else:
        pl.semaphore_wait(barrier, awaited)


def exchange(name, collective_id, jobs):
    values = [getattr(job, "values", None) or [job.value] for job in jobs]
    peers = peers_of(jobs)

    def kernel(*refs):
        total = sum(len(held) for held in values)
        results = refs[total : total + len(jobs)]
        scratch = refs[total + len(jobs) :]
        begin = offset = 0
        place = coordinates()
        awaited = greet(peers, place)
        for number, job in enumerate(jobs):
            end = begin + len(values[number])
            ins = refs[begin:end]
            if hasattr(job, "pack"):
                job.pack(ins, scratch[offset])
                ins, offset = (scratch[offset],), offset + 1
            mine = len(job.scratch) - hasattr(job, "pack")
            job.prepare(tuple(ins) + (results[number],) + tuple(scratch[offset : offset + mine]), place)
            begin, offset = end, offset + mine
        welcome(peers, place, awaited)
        events = [event for job in jobs for event in job.events()]
        for _, act in sorted(events, key=lambda event: event[0]):
            act()
        for job in jobs:
            job.finish()

    return pl.pallas_call(
        kernel,
        name=name,
        out_shape=tuple(job.out for job in jobs),
        in_specs=[job.in_spec for job, held in zip(jobs, values) for _ in held],
        out_specs=tuple(job.out_spec for job in jobs),
        scratch_shapes=[item for job in jobs for item in job.scratch],
        compiler_params=pltpu.CompilerParams(
            collective_id=collective_id, has_side_effects=True, vmem_limit_bytes=60 * 1024 * 1024
        ),
    )(*[value for held in values for value in held])


def packed(block):
    rows, columns = block.shape
    if rows % 16 == 0:
        return block
    return block.reshape(16, rows * columns // 16)


def bucket_edges():
    edges = []
    for target in range(1, 32):
        if target < 16:
            edges.append(target)
        else:
            found = 0
            for distance in range(16, 4096):
                value = 16 + int(math.log(distance / 16.0) / math.log(8.0) * 16.0)
                if found == 0 and value >= target:
                    found = distance
            edges.append(found)
    return edges


def gelu_tanh(value):
    return (
        0.5
        * value
        * (1.0 + jnp.tanh(0.7978845608028654 * (value + 0.044715 * value * value * value)))
    )


def dot(left, right):
    return jnp.einsum("sd,df->sf", left, right, preferred_element_type=f32)


def dot_t(left, right):
    return jnp.einsum("sf,df->sd", left, right, preferred_element_type=f32)


def t_dot(left, right):
    return jnp.einsum("sd,sf->df", left, right, preferred_element_type=f32)


def distance_table(seq):
    edges = np.array(bucket_edges())
    distance = (-np.arange(seq)) % seq
    bucket = (distance[:, None] >= edges[None, :]).sum(axis=1)
    return (np.arange(128)[:, None] == bucket[None, :]).astype(np.float32)


def mm(left, right):
    return lax.dot_general(left, right, (((1,), (0,)), ((), ())), preferred_element_type=f32)


def mm_t(left, right):
    return lax.dot_general(left, right, (((1,), (1,)), ((), ())), preferred_element_type=f32)


def t_mm(left, right):
    return lax.dot_general(left, right, (((0,), (0,)), ((), ())), preferred_element_type=f32)


def inverse_rms(rows):
    return lax.rsqrt(jnp.mean(rows * rows, axis=-1, keepdims=True) + eps)


def rms_back(rows, gain, slope):
    inverse = inverse_rms(rows)
    unit = rows * inverse
    scaled = slope * gain
    back = inverse * (scaled - unit * jnp.mean(unit * scaled, axis=-1, keepdims=True))
    return back, jnp.sum(slope * unit, axis=0, keepdims=True)


def lanes_of(shape):
    return lax.broadcasted_iota(jnp.int32, shape, len(shape) - 1)


def one_half(pair, half):
    inside = (lanes_of(pair.shape) // HEAD) == half
    return jnp.where(inside, pair, jnp.zeros_like(pair))


def both_halves(pair):
    return jnp.concatenate([one_half(pair, 0), one_half(pair, 1)], axis=0)


def joined_rows(stacked):
    rows = stacked.shape[0] // 2
    return joined(stacked[:rows], stacked[rows:])


def joined(first, second):
    return jnp.where(lanes_of(first.shape) < HEAD, first, second)


def pair_of(ref, start, pair):
    return ref[:, start + 2 * HEAD * pair : start + 2 * HEAD * (pair + 1)]


FF_STEP = 256


def in_steps(total, step, body, further=0):
    def one(number, carry):
        here = pl.ds(pl.multiple_of(number * step, step), step)
        if further:
            body(here, pl.ds(pl.multiple_of(number * step + further, step), step))
        else:
            body(here)
        return carry

    lax.fori_loop(0, total // step, one, 0)


class Fetch:
    def __init__(self, sources, targets, sems):
        self.copies = [
            pltpu.make_async_copy(source, target, sems.at[number])
            for number, (source, target) in enumerate(zip(sources, targets))
        ]
        self.targets = targets
        self.ready = set()
        for copy in self.copies:
            copy.start()

    def __getitem__(self, number):
        if number not in self.ready:
            self.ready.add(number)
            self.copies[number].wait()
        return self.targets[number]


def enter_kernel(resid_ref, part_c_ref, query_ref, kv_ref, normed_ref, gains_ref):
    row = lax.broadcasted_iota(jnp.int32, (16, GAIN_PAD), 0)
    pick = (row == lanes_of((16, GAIN_PAD))).astype(bf16)
    gains = mm_t(pick, part_c_ref[:, 5 * HD : 5 * HD + GAIN_PAD])
    gains_ref[...] = gains
    resid = resid_ref[...]
    normed = (resid * inverse_rms(resid) * gains[0:1]).astype(bf16)
    normed_ref[...] = normed
    query_ref[...] = mm(normed, part_c_ref[:, :HD]).astype(bf16)
    kv_ref[...] = mm(normed, part_c_ref[:, HD : 3 * HD]).astype(bf16)


def biased_scores(scores, row, first, length):
    bias = pltpu.roll(jnp.broadcast_to(row, scores.shape), 0, 1, stride=1, stride_axis=0)
    query_pos = first + lax.broadcasted_iota(jnp.int32, scores.shape, 0)
    key_pos = lanes_of(scores.shape)
    mask = (key_pos <= query_pos) & (key_pos < length)
    return jnp.where(mask, scores + bias, masked_score)


def softmax_parts(scores):
    highest = jnp.max(scores, axis=-1, keepdims=True)
    total = highest + jnp.log(jnp.sum(jnp.exp(scores - highest), axis=-1, keepdims=True))
    return total, jnp.exp(scores - total)


def query_span(lengths_ref, rows):
    place = coordinates()
    length = lengths_ref[place["s"] // 2, 2 * place["a"] + place["s"] % 2]
    return (2 * place["h"] + place["c"]) * rows, length


def forward_kernel(
    lengths_ref,
    query_ref,
    kv_ref,
    resid0_ref,
    gains_ref,
    table_ref,
    bias_ref,
    mem_kv_hbm,
    part_a_hbm,
    part_b_hbm,
    part_c_hbm,
    attn_self_ref,
    total_self_ref,
    resid1_ref,
    normed_cross_ref,
    query_cross_ref,
    attn_cross_ref,
    total_cross_ref,
    resid2_ref,
    normed_ff_ref,
    gate_up_ref,
    hidden_ref,
    resid3_ref,
    final_ref,
    mem_kv_ref,
    part_a_ref,
    part_b_ref,
    part_c_ref,
    sems,
):
    fetched = Fetch(
        (part_c_hbm, part_b_hbm, mem_kv_hbm, part_a_hbm),
        (part_c_ref, part_b_ref, mem_kv_ref, part_a_ref),
        sems,
    )
    first, length = query_span(lengths_ref, query_ref.shape[0])
    ff = hidden_ref.shape[1]
    bias_rows = pltpu.roll(mm(bias_ref[...], table_ref[:BUCKETS, :]), first, 1)
    lanes = lanes_of(total_self_ref.shape)
    totals = jnp.zeros(total_self_ref.shape, f32)
    for pair in range(HEADS // 2):
        keys, values = pair_of(kv_ref, 0, pair), pair_of(kv_ref, HD, pair)
        outputs = []
        for half in range(2):
            number = 2 * pair + half
            scores = mm_t(one_half(pair_of(query_ref, 0, pair), half), keys)
            scores = biased_scores(scores, bias_rows[number : number + 1], first, length)
            total, shares = softmax_parts(scores)
            totals = jnp.where(lanes == number, total, totals)
            outputs.append(mm(shares.astype(bf16), values))
        attn_self_ref[:, 2 * HEAD * pair : 2 * HEAD * (pair + 1)] = joined(*outputs).astype(bf16)
    total_self_ref[...] = totals

    part_c = fetched[0]
    resid1 = resid0_ref[...] + mm_t(attn_self_ref[...], part_c[:, 3 * HD : 4 * HD])
    resid1_ref[...] = resid1
    normed = (resid1 * inverse_rms(resid1) * gains_ref[1:2]).astype(bf16)
    normed_cross_ref[...] = normed
    query_cross_ref[...] = mm(normed, part_c[:, 4 * HD : 5 * HD]).astype(bf16)

    part_b = fetched[1]
    mem_kv_ref = fetched[2]
    total_cross_ref[...] = jnp.zeros(total_cross_ref.shape, f32)

    def cross_pair(place, place_v):
        keys, values = mem_kv_ref[:, place], mem_kv_ref[:, place_v]
        outputs = []
        for half in range(2):
            scores = mm_t(one_half(query_cross_ref[:, place], half), keys)
            total, shares = softmax_parts(scores)
            number = place.start // HEAD + half
            total_cross_ref[...] = jnp.where(lanes == number, total, total_cross_ref[...])
            outputs.append(mm(shares.astype(bf16), values))
        attn_cross_ref[:, place] = joined(*outputs).astype(bf16)

    in_steps(HD, 2 * HEAD, cross_pair, HD)
    resid2 = resid1_ref[...] + mm_t(attn_cross_ref[...], part_b[:, ff + 2 * HD :])
    resid2_ref[...] = resid2
    normed_ff_ref[...] = (resid2 * inverse_rms(resid2) * gains_ref[2:3]).astype(bf16)

    part_a = fetched[3]

    def feed(here, there):
        gate = mm(normed_ff_ref[...], part_a[:, here])
        up = mm(normed_ff_ref[...], part_a[:, there])
        gate_up_ref[:, here] = gate
        gate_up_ref[:, there] = up
        hidden_ref[:, here] = (gelu_tanh(gate) * up).astype(bf16)

    in_steps(ff, FF_STEP, feed, ff)
    resid3 = resid2_ref[...] + mm_t(hidden_ref[...], part_b[:, :ff])
    resid3_ref[...] = resid3
    final_ref[...] = (resid3 * inverse_rms(resid3) * gains_ref[3:4]).astype(bf16)


def attention_back(query, keys, values, scores, total, out_slope):
    shares = jnp.exp(scores - total)
    share_slope = mm_t(out_slope, values)
    inner = jnp.sum(shares * share_slope, axis=-1, keepdims=True)
    score_slope = shares * (share_slope - inner)
    rounded = score_slope.astype(bf16)
    return (
        rounded,
        mm(rounded, keys),
        t_mm(rounded, query),
        t_mm(shares.astype(bf16), out_slope),
    )


def backward_kernel(
    lengths_ref,
    slope_ref,
    resid3_ref,
    hidden_ref,
    gate_up_ref,
    normed_ff_ref,
    resid2_ref,
    attn_cross_ref,
    query_cross_ref,
    total_cross_ref,
    normed_cross_ref,
    resid1_ref,
    attn_self_ref,
    query_ref,
    kv_ref,
    total_self_ref,
    gains_ref,
    table_ref,
    bias_ref,
    mem_kv_hbm,
    part_a_hbm,
    part_b_hbm,
    part_c_hbm,
    grad_b_hbm,
    gate_up_slope_ref,
    cross_kv_slope_ref,
    grad_c_ref,
    query_slope_ref,
    kv_slope_ref,
    grad1_ref,
    norm_grads_ref,
    bias_grad_ref,
    mem_kv_ref,
    part_a_ref,
    part_b_ref,
    part_c_ref,
    grad_b_ref,
    cross_query_slope_ref,
    sems,
    out_sems,
):
    fetched = Fetch(
        (part_b_hbm, part_a_hbm, mem_kv_hbm, part_c_hbm),
        (part_b_ref, part_a_ref, mem_kv_ref, part_c_ref),
        sems,
    )
    first, length = query_span(lengths_ref, query_ref.shape[0])
    ff = hidden_ref.shape[1]
    width = resid3_ref.shape[1]
    norm_grads_ref[...] = jnp.zeros_like(norm_grads_ref)

    grad3, norm_grad = rms_back(resid3_ref[...], gains_ref[3:4], slope_ref[...])
    norm_grads_ref[3:4] = norm_grad
    down_in = grad3.astype(bf16)
    part_b = fetched[0]

    def feed_back(here, there):
        hidden_slope = mm(down_in, part_b[:, here])
        gate, up = gate_up_ref[:, here], gate_up_ref[:, there]
        inner = jnp.tanh(0.7978845608028654 * (gate + 0.044715 * gate * gate * gate))
        activated = 0.5 * gate * (1.0 + inner)
        steep = 0.5 * (1.0 + inner) + 0.5 * gate * (1.0 - inner * inner) * (
            0.7978845608028654 * (1.0 + 3.0 * 0.044715 * gate * gate)
        )
        gate_up_slope_ref[:, here] = (hidden_slope * up * steep).astype(bf16)
        gate_up_slope_ref[:, there] = (hidden_slope * activated).astype(bf16)
        grad_b_ref[:, here] = t_mm(down_in, hidden_ref[:, here]).astype(bf16)

    in_steps(ff, FF_STEP, feed_back, ff)
    part_a = fetched[1]
    back, norm_grad = rms_back(
        resid2_ref[...], gains_ref[2:3], mm_t(gate_up_slope_ref[...], part_a[...])
    )
    norm_grads_ref[2:3] = norm_grad
    grad2 = grad3 + back

    cross_in = grad2.astype(bf16)
    grad_b_ref[:, ff:] = t_mm(cross_in, attn_cross_ref[...]).astype(bf16)
    copy_b = pltpu.make_async_copy(grad_b_ref, grad_b_hbm, out_sems.at[0])
    copy_b.start()
    out_slope = mm(cross_in, part_b[:, ff + 2 * HD :]).astype(bf16)
    mem_kv = fetched[2]
    cross_query_slope_ref[...] = out_slope

    def cross_pair_back(place, place_v):
        keys, values = mem_kv[:, place], mem_kv[:, place_v]
        lanes = lanes_of(total_cross_ref.shape)
        totals = [
            jnp.sum(
                jnp.where(lanes == place.start // HEAD + half, total_cross_ref[...], 0.0),
                axis=-1,
                keepdims=True,
            )
            for half in range(2)
        ]
        query = both_halves(query_cross_ref[:, place])
        part = attention_back(
            query,
            keys,
            values,
            mm_t(query, keys),
            jnp.concatenate(totals, axis=0),
            both_halves(cross_query_slope_ref[:, place]),
        )
        cross_query_slope_ref[:, place] = joined_rows(part[1]).astype(bf16)
        cross_kv_slope_ref[:, place] = part[2].astype(bf16)
        cross_kv_slope_ref[:, place_v] = part[3].astype(bf16)

    in_steps(HD, 2 * HEAD, cross_pair_back, HD)
    part_c = fetched[3]
    query_slope = cross_query_slope_ref[...]
    grad_c_ref[:, HD : 2 * HD] = t_mm(normed_cross_ref[...], query_slope).astype(bf16)
    back, norm_grad = rms_back(
        resid1_ref[...], gains_ref[1:2], mm_t(query_slope, part_c[:, 4 * HD : 5 * HD])
    )
    norm_grads_ref[1:2] = norm_grad
    grad1 = grad2 + back
    grad1_ref[...] = grad1

    self_in = grad1.astype(bf16)
    grad_c_ref[:, :HD] = t_mm(self_in, attn_self_ref[...]).astype(bf16)
    out_slope = mm(self_in, part_c[:, 3 * HD : 4 * HD]).astype(bf16)
    bias_rows = pltpu.roll(mm(bias_ref[...], table_ref[:BUCKETS, :]), first, 1)
    bias_sums = jnp.zeros((8, bias_rows.shape[1]), f32)
    rows, seq = query_ref.shape[0], kv_ref.shape[0]
    reverse = lax.broadcasted_iota(jnp.int32, (rows, rows), 0) + lanes_of((rows, rows)) == rows - 1
    reverse = reverse.astype(bf16)
    for pair in range(HEADS // 2):
        place = slice(2 * HEAD * pair, 2 * HEAD * (pair + 1))
        place_v = slice(HD + 2 * HEAD * pair, HD + 2 * HEAD * (pair + 1))
        keys, values = kv_ref[:, place], kv_ref[:, place_v]
        query = both_halves(query_ref[:, place])
        products = mm_t(query, keys)
        scores, totals = [], []
        for half in range(2):
            number = 2 * pair + half
            scores.append(
                biased_scores(
                    products[half * rows : (half + 1) * rows],
                    bias_rows[number : number + 1],
                    first,
                    length,
                )
            )
            totals.append(total_self_ref[:, number : number + 1])
        part = attention_back(
            query,
            keys,
            values,
            jnp.concatenate(scores, axis=0),
            jnp.concatenate(totals, axis=0),
            both_halves(out_slope[:, place]),
        )
        for half in range(2):
            turned = mm(reverse, part[0][half * rows : (half + 1) * rows])
            turned = pltpu.roll(turned, 0, 1, stride=1, stride_axis=0)
            where = lax.broadcasted_iota(jnp.int32, bias_sums.shape, 0) == 2 * pair + half
            bias_sums = jnp.where(where, jnp.sum(turned, axis=0, keepdims=True), bias_sums)
        query_slope_ref[:, place] = joined_rows(part[1]).astype(bf16)
        kv_slope_ref[:, place] = part[2].astype(bf16)
        kv_slope_ref[:, place_v] = part[3].astype(bf16)
    bias_sums = pltpu.roll(bias_sums, 2 * seq + 1 - rows - first, 1)
    high = bias_sums.astype(bf16)
    rest = bias_sums - high.astype(f32)
    middle = rest.astype(bf16)
    low = (rest - middle.astype(f32)).astype(bf16)
    table = table_ref[...]
    bias_grad_ref[...] = mm_t(high, table) + (mm_t(middle, table) + mm_t(low, table))
    copy_b.wait()


def project_memory(held, result):
    memory, weight = held
    step = min(256, memory.shape[0])

    def one(number, carry):
        rows = pl.ds(pl.multiple_of(number * step, step), step)
        result[rows, :] = mm(memory[rows, :], weight[...]).astype(bf16)
        return carry

    lax.fori_loop(0, memory.shape[0] // step, one, 0)


def gate_up_grads(held, result):
    normed, slope = held

    def one(here):
        result[:, here] = t_mm(normed[...], slope[:, here]).astype(bf16)

    in_steps(slope.shape[1], 2 * FF_STEP, one)


def memory_weight_grads(held, result):
    memory, slope, others = held
    ff = others.shape[1] - HD
    result[:, :ff] = others[:, :ff]
    result[:, ff + 2 * HD :] = others[:, ff:]

    def one(here, there):
        result[:, there] = t_mm(memory[...], slope[:, here]).astype(bf16)

    in_steps(2 * HD, FF_STEP, one, ff)


def memory_slopes(held, result):
    slope, weight = held
    step = min(256, slope.shape[0])

    def one(number, carry):
        rows = pl.ds(pl.multiple_of(number * step, step), step)
        result[rows, :] = mm_t(slope[rows, :], weight[...]).astype(bf16)
        return carry

    lax.fori_loop(0, slope.shape[0] // step, one, 0)


def leave_kernel(
    query_slope_ref,
    kv_slope_ref,
    resid0_ref,
    grad1_ref,
    gains_ref,
    norm_grads_ref,
    part_c_ref,
    grad0_ref,
    all_grads_ref,
):
    slope = mm_t(query_slope_ref[...], part_c_ref[:, :HD])
    slope = slope + mm_t(kv_slope_ref[...], part_c_ref[:, HD : 3 * HD])
    back, norm_grad = rms_back(resid0_ref[...], gains_ref[0:1], slope)
    grad0_ref[...] = (grad1_ref[...] + back).astype(bf16)
    where = lax.broadcasted_iota(jnp.int32, norm_grads_ref.shape, 0) == 0
    all_grads_ref[...] = jnp.where(where, norm_grad, norm_grads_ref[...])


def self_weight_grads(held, result):
    query_slope, kv_slope, normed, norm_grads, others = held
    result[:, :HD] = t_mm(normed[...], query_slope[...]).astype(bf16)
    result[:, HD : 3 * HD] = t_mm(normed[...], kv_slope[...]).astype(bf16)
    result[:, 3 * HD : 5 * HD] = others[...]
    row = lax.broadcasted_iota(jnp.int32, (norm_grads.shape[0], GAIN_PAD), 0)
    spread = (row == lanes_of(row.shape)).astype(bf16)
    result[:, 5 * HD :] = t_mm(norm_grads[...].astype(bf16), spread).astype(bf16)


def local_kernel(name, kernel, outs, args, spaces="", out_spaces="", scratch=()):
    space = {"v": pltpu.VMEM, "s": pltpu.SMEM, "a": pl.ANY}
    spaces = spaces or "v" * len(args)
    out_spaces = out_spaces or "v" * len(outs)
    return pl.pallas_call(
        kernel,
        name=name,
        out_shape=tuple(jax.ShapeDtypeStruct(shape, dtype) for shape, dtype in outs),
        in_specs=[pl.BlockSpec(memory_space=space[letter]) for letter in spaces],
        out_specs=tuple(pl.BlockSpec(memory_space=space[letter]) for letter in out_spaces),
        scratch_shapes=list(scratch),
        compiler_params=pltpu.CompilerParams(vmem_limit_bytes=60 * 1024 * 1024),
    )(*args)


def pack_columns(pieces, block):
    start = 0
    for piece in pieces:
        if piece.shape[0] == 1:
            break
        block[:, start : start + piece.shape[1]] = piece[...]
        start += piece.shape[1]
    gains = pieces[-4:]
    if gains[0].shape[0] == 1:
        rows = gains[0].shape[1]
        where = lax.broadcasted_iota(jnp.int32, (16, rows), 0)
        stacked = jnp.zeros((16, rows), f32)
        for number, gain in enumerate(gains):
            stacked = jnp.where(where == number, gain[...].astype(f32), stacked)
        pick = lax.broadcasted_iota(jnp.int32, (16, GAIN_PAD), 0) == lanes_of((16, GAIN_PAD))
        block[:, start:] = t_mm(stacked.astype(bf16), pick.astype(bf16)).astype(bf16)


def pack_rows(pieces, block):
    start = 0
    for piece in pieces:
        block[start : start + piece.shape[0], :] = piece[...]
        start += piece.shape[0]


def pack_ids(pieces, block):
    block[...] = jnp.zeros_like(block)
    for number, piece in enumerate(pieces):
        micro, _, count = piece.shape
        for which in range(micro):
            block[micro * number + which : micro * number + which + 1, :count] = piece[which]


def tail_kernel(lengths_ref, *refs):
    (a_ref, b_ref, c_ref, small_ref, memory_ref, embedding_ref, head_ref), outs = refs[:7], refs[7:]
    (loss_ref, memory_out, embedding_out, head_out, bias_out), outs = outs[:5], outs[5:]
    memory_out[...] = memory_ref[...]
    embedding_out[...] = embedding_ref[...]
    head_out[...] = head_ref[...]
    total = jnp.sum(small_ref[...], axis=0)
    count = 0
    for first in range(lengths_ref.shape[0]):
        for second in range(lengths_ref.shape[1]):
            count = count + lengths_ref[first, second]
    loss_ref[...] = jnp.sum(total[8:], keepdims=True) / count.astype(f32)
    bias_out[...] = total[:HEADS, :BUCKETS]
    for ref, pieces in ((a_ref, outs[:2]), (b_ref, outs[2:6]), (c_ref, outs[6:11])):
        start = 0
        for piece in pieces:
            piece[...] = ref[:, start : start + piece.shape[1]]
            start += piece.shape[1]
    turned = jnp.transpose(c_ref[:, 5 * HD :])
    for number, piece in enumerate(outs[11:]):
        piece[...] = turned[number : number + 1]


def vocabulary(name, collective_id, final_rows, head_rows, targets, lengths, sizes):
    span, width = head_rows.shape
    tok_dev = final_rows.shape[0]
    lines = sizes["s"]
    blocks = 2 * lines
    step_rows = min(512, span)
    gather = Gather(final_rows, "sh", "sh", sizes)
    direct = DirectGather(jax.ShapeDtypeStruct((blocks, tok_dev), f32), sizes)
    scatter = Scatter(jax.ShapeDtypeStruct((lines, 2, tok_dev, width), bf16), "hs", "sh", sizes)
    jobs = (gather, direct, scatter)
    peers = peers_of(jobs)

    def kernel(*refs):
        final_ref, head_ref, targets_ref, lengths_ref = refs[:4]
        slope_ref, head_part_ref, loss_ref = refs[4:7]
        states, totals, own_total, logits, turned, value, picked_ref, log_total_ref = refs[7:15]
        rest = refs[15:]
        place = coordinates()
        awaited = greet(peers, place)
        counts = [len(job.scratch) for job in jobs]
        gather.prepare((final_ref, states) + rest[: counts[0]], place)
        direct.prepare((own_total, totals) + rest[counts[0] : counts[0] + counts[1]], place)
        scatter.prepare((value, slope_ref) + rest[counts[0] + counts[1] :], place)
        welcome(peers, place, awaited)
        position = place["s"]
        half = position // 2

        def spot(token, other):
            far, second = token // 2, token % 2
            near_row = position + second * (1 - 2 * (position % 2))
            far_row = 2 - half + second * (1 - 2 * half)
            row = near_row + far * (far_row - near_row)
            side = place["h"] + other * (1 - 2 * place["h"])
            return row, side, 2 * row + side

        def chunk_of(number):
            return pl.ds(pl.multiple_of(number * step_rows, step_rows), step_rows)

        def hits(number, target):
            rows = lax.broadcasted_iota(jnp.int32, (step_rows, tok_dev), 0) + number * step_rows
            return rows == target

        def bring(step):
            token, other = step // 2, step % 2
            if step == 0:
                gather.line_first()
                gather.launch((1, (0,), 1))
                gather.local.wait()
                gather.local_done = True
            if other:
                gather.arrive((1, (token,), 1))
                if token + 1 < lines:
                    gather.line_next(token + 1)
                    gather.launch((1, (token + 1,), 1))

        def forward_step(step, carry):
            for number in range(blocks):
                pl.when(step == number)(functools.partial(bring, number))
            row, side, number = spot(step // 2, step % 2)
            block = states[row, side]
            target = targets_ref[pl.ds(number, 1), :]

            def scores(chunk, best):
                found = mm_t(head_ref[chunk_of(chunk), :], block)
                logits[number, chunk_of(chunk), :] = found
                return jnp.maximum(best, jnp.max(found, axis=0, keepdims=True))

            count = span // step_rows
            best = lax.fori_loop(0, count, scores, jnp.full((1, tok_dev), -3.0e38, f32))

            def spread(chunk, sums):
                found = logits[number, chunk_of(chunk), :]
                hit = hits(chunk, target)
                return (
                    sums[0] + jnp.sum(jnp.exp(found - best), axis=0, keepdims=True),
                    sums[1] + jnp.sum(jnp.where(hit, found, 0.0), axis=0, keepdims=True),
                )

            zero = jnp.zeros((1, tok_dev), f32)
            total, picked = lax.fori_loop(0, count, spread, (zero, zero))
            own_total[pl.ds(number, 1), :] = best + jnp.log(total)
            picked_ref[pl.ds(number, 1), :] = picked
            return carry

        lax.fori_loop(0, blocks, forward_step, 0)
        direct.begin()
        direct.receive()
        parts = totals[...].reshape((blocks,) + own_total.shape)
        top = jnp.max(parts, axis=0)
        log_total_ref[...] = top + jnp.log(jnp.sum(jnp.exp(parts - top[None]), axis=0))

        def backward_step(step, carry):
            row, side, number = spot(lines - 1 - step // 2, 1 - step % 2)
            lanes = pl.ds(pl.multiple_of(number * tok_dev, tok_dev), tok_dev)
            target = targets_ref[pl.ds(number, 1), :]
            log_total = log_total_ref[pl.ds(number, 1), :]
            length = lengths_ref[row // 2, 2 * place["a"] + row % 2]
            spots = (2 * side + place["c"]) * tok_dev + lax.broadcasted_iota(jnp.int32, (1, tok_dev), 1)
            live = jnp.where(spots < length, 1.0, 0.0)
            shown = log_total * (1 - jnp.minimum(2 * position + place["h"], 1)).astype(f32)
            loss_ref[pl.ds(number, 1), :] = live * (shown - picked_ref[pl.ds(number, 1), :])

            def slopes(chunk, inner):
                share = jnp.exp(logits[number, chunk_of(chunk), :] - log_total)
                slope = (share - jnp.where(hits(chunk, target), 1.0, 0.0)) * live
                turned[chunk_of(chunk), lanes] = slope.astype(bf16)
                return inner

            lax.fori_loop(0, span // step_rows, slopes, 0)
            value[row, side] = t_mm(turned[:, lanes], head_ref[...]).astype(bf16)
            for which in range(lines):
                pl.when(step == 2 * which)(
                    functools.partial(scatter.launch, 0, (lines - 1 - which,), 1)
                )
            return carry

        lax.fori_loop(0, blocks, backward_step, 0)
        for token in (3, 2):
            scatter.reduce(0, (token,))
            scatter.line_step(token, middles=False)

        def head_chunk(number, carry):
            rows = pl.ds(pl.multiple_of(number * 256, 256), 256)
            every = states[...].reshape(blocks * tok_dev, width)
            head_part_ref[rows, :] = mm(turned[rows, :], every).astype(bf16)
            return carry

        lax.fori_loop(0, span // 256, head_chunk, 0)
        scatter.line_step(3, ends=False)
        scatter.line_step(2, ends=False)
        for token in (1, 0):
            scatter.reduce(0, (token,))
            scatter.line_step(token)
        gather.finish()
        direct.drain()
        scatter.finish()

    vmem = pl.BlockSpec(memory_space=pltpu.VMEM)
    rows = jax.ShapeDtypeStruct((blocks, tok_dev), f32)
    return pl.pallas_call(
        kernel,
        name=name,
        out_shape=(scatter.out, jax.ShapeDtypeStruct(head_rows.shape, bf16), rows),
        in_specs=[vmem] * 3 + [pl.BlockSpec(memory_space=pltpu.SMEM)],
        out_specs=(vmem,) * 3,
        scratch_shapes=[
            pltpu.VMEM(gather.out.shape, bf16),
            pltpu.VMEM(direct.out.shape, f32),
            pltpu.VMEM((blocks, tok_dev), f32),
            pltpu.VMEM((blocks, span, tok_dev), f32),
            pltpu.VMEM((span, blocks * tok_dev), bf16),
            pltpu.VMEM(scatter.value.shape, bf16),
            pltpu.VMEM((blocks, tok_dev), f32),
            pltpu.VMEM((blocks, tok_dev), f32),
        ]
        + [item for job in jobs for item in job.scratch],
        compiler_params=pltpu.CompilerParams(
            collective_id=collective_id, has_side_effects=True, vmem_limit_bytes=60 * 1024 * 1024
        ),
    )(final_rows, head_rows, targets, lengths)


def opening(name, collective_id, weights, embedding, ids, memory, head, sizes):
    voc_dev, width = embedding.shape
    n_gy = 2 * sizes["s"]
    n_gx = 2 * sizes["a"]
    span = n_gx * voc_dev
    lines = sizes["s"]
    micro, _, seq_dev = ids[0].shape
    tok_dev = 2 * seq_dev
    table = Gather(embedding, "ac", "ac", sizes)
    codes = DirectGather(jax.ShapeDtypeStruct((8, 128), jnp.int32), sizes, "shc")
    memories = MemoryGather(memory, sizes)
    heads = Gather(head, "ac", "ac", sizes, "", 20)
    sums = Scatter(jax.ShapeDtypeStruct((lines, 2, tok_dev, width), bf16), "hs", "sh", sizes)
    jobs = list(weights) + [table, codes, memories, heads, sums]
    peers = peers_of(jobs)
    operands = [list(job.values) for job in weights] + [[embedding], list(ids), [memory], [head]]
    flat = [value for group in operands for value in group]

    def kernel(*refs):
        ins = list(refs[: len(flat)])
        outs = list(refs[len(flat) : len(flat) + 8])
        rest = list(refs[len(flat) + 8 :])
        place = coordinates()
        awaited = greet(peers, place)

        def take(source, count):
            taken = tuple(source[:count])
            del source[:count]
            return taken

        rows_ref, value, code, ids_ref = (rest.pop(0) for _ in range(4))
        for job in weights:
            pieces = take(ins, len(job.values))
            block = rest.pop(0)
            job.pack(pieces, block)
            job.prepare((block, outs.pop(0)) + take(rest, len(job.scratch) - 1), place)
        table.prepare((ins.pop(0), rows_ref) + take(rest, len(table.scratch)), place)
        pack_ids(take(ins, 2), code)
        local_ref, target_ref = outs.pop(0), outs.pop(0)
        codes.prepare((code, ids_ref) + take(rest, len(codes.scratch)), place)
        memories.prepare((ins.pop(0), outs.pop(0)) + take(rest, len(memories.scratch)), place)
        heads.prepare((ins.pop(0), outs.pop(0)) + take(rest, len(heads.scratch)), place)
        sums.prepare((value, outs.pop(0)) + take(rest, len(sums.scratch)), place)
        welcome(peers, place, awaited)

        def tables_here():
            codes.receive()
            table.local.wait()
            table.local_done = True
            for transfer in table.transfers:
                table.arrive(transfer)

        def pick(token):
            row = along_line(place["s"], token)

            def one(other, carry):
                side = place["h"] + (1 - other) * (1 - 2 * place["h"])
                indices = []
                for kind, ref in enumerate((local_ref, target_ref)):
                    line = pl.ds(micro * kind + row // 2, 1)
                    index = jnp.concatenate(
                        [
                            ids_ref[2 * side + place["c"], which, row % 2, line, :][:, :seq_dev]
                            for which in range(2)
                        ],
                        axis=1,
                    )
                    shard = index // voc_dev
                    held = shard % n_gy == 2 * place["s"] + place["h"]
                    index = jnp.where(held, shard // n_gy * voc_dev + index % voc_dev, -1)
                    ref[pl.ds(2 * row + side, 1), :] = index
                    indices.append(index)
                index = indices[0]
                at = lax.broadcasted_iota(jnp.int32, (span, tok_dev), 0) == index
                every = rows_ref[...].reshape(span, width)
                value[row, side] = t_mm(jnp.where(at, 1.0, 0.0).astype(bf16), every).astype(bf16)
                pl.when(other == 0)(functools.partial(sums.launch, 0, (token,), 1))
                return carry

            lax.fori_loop(0, 2, one, 0)

        events = [event for job in list(weights) + [memories, heads] for event in job.events()]
        events.append((-2, codes.begin))
        for transfer in table.transfers:
            level, unit, _ = transfer
            key = -1 if level == 0 else TABLE_KEY if unit[0] else 0.1
            events.append((key, functools.partial(table.launch, transfer)))
        events.append((TABLE_KEY + 0.05, tables_here))
        for number, token in enumerate((3, 2, 1, 0)):
            events.append((PICK_KEY + PICK_STEP * number, functools.partial(pick, token)))
            key = SUM_KEY + SUM_STEP * number
            events.append((key, functools.partial(sums.reduce, 0, (token,))))
            if token:
                events.append((key + 0.01, functools.partial(sums.line_step, token, middles=False)))
                events.append((LINE_KEY + SUM_STEP * number, functools.partial(sums.line_step, token, ends=False)))
            else:
                events.append((LINE_KEY + SUM_STEP * number, functools.partial(sums.line_step, token)))
        for _, act in sorted(events, key=lambda event: event[0]):
            act()
        for job in jobs:
            if job is codes:
                job.drain()
            else:
                job.finish()

    vmem = pl.BlockSpec(memory_space=pltpu.VMEM)
    anywhere = pl.BlockSpec(memory_space=pl.ANY)
    scratch = [
        pltpu.VMEM(table.out.shape, bf16),
        pltpu.VMEM(sums.value.shape, bf16),
        pltpu.VMEM((8, 128), jnp.int32),
        pltpu.VMEM(codes.out.shape, jnp.int32),
    ]
    places = jax.ShapeDtypeStruct((n_gy, tok_dev), jnp.int32)
    return pl.pallas_call(
        kernel,
        name=name,
        out_shape=tuple(job.out for job in weights)
        + (places, places, memories.out, heads.out, sums.out),
        in_specs=[vmem] * len(flat),
        out_specs=(anywhere,) * 3 + (vmem, vmem, anywhere, anywhere, vmem),
        scratch_shapes=scratch + [item for job in jobs for item in job.scratch],
        compiler_params=pltpu.CompilerParams(
            collective_id=collective_id, has_side_effects=True, vmem_limit_bytes=60 * 1024 * 1024
        ),
    )(*flat)


TABLE_KEY, PICK_KEY, PICK_STEP, SUM_KEY, SUM_STEP, LINE_KEY = 0.55, 0.65, 0.05, 1.3, 0.3, 1.9


def per_device(
    target_ids,
    labels,
    lengths,
    memory,
    embedding,
    head,
    gain_self,
    w_query,
    w_key,
    w_value,
    w_out,
    relative_bias,
    gain_cross,
    c_query,
    c_key,
    c_value,
    c_out,
    gain_ff,
    w_gate,
    w_up,
    w_down,
    gain_final,
):
    micro = target_ids.shape[0]
    seq_dev = target_ids.shape[2]
    mem_dev = memory.shape[2]
    voc_dev, width = embedding.shape
    ff = w_gate.shape[1]
    n_gx = lax.axis_size("gx")
    n_gy = lax.axis_size("gy")
    column = lax.axis_index("gy")
    row_group = lax.axis_index("gx")
    devices = n_gx * n_gy
    sizes = {"a": n_gx // 2, "c": 2, "s": n_gy // 2, "h": 2}
    assert sizes["s"] == 2 * micro
    place = coordinates()
    seq = seq_dev * n_gy
    plane = sizes["s"] * seq
    tok_dev = seq // 4
    tokens = plane // 2
    span = n_gx * voc_dev
    merged = "" if sizes["a"] == 2 else "ashc"

    rows_dev = width // devices
    whole_tiles = rows_dev % 16 == 0
    groups = (
        (w_gate, w_up),
        (w_down, c_key, c_value, c_out),
        (w_query, w_key, w_value, w_out, c_query),
    )
    gains = (gain_self, gain_cross, gain_ff, gain_final)
    widths = [sum(piece.shape[1] for piece in group) for group in groups]
    widths[2] += GAIN_PAD
    orders = ("shac", "shac", "sahc")
    ways_back = ("cahs", "chas", "chas")
    if whole_tiles:
        operands = list(groups)
        operands[2] += tuple(gain.reshape(1, rows_dev) for gain in gains)
        weights = [
            PackedGather(
                group,
                jax.ShapeDtypeStruct((rows_dev, count), bf16),
                pack_columns,
                order,
                "acsh",
                sizes,
                merged,
            )
            for group, count, order in zip(operands, widths, orders)
        ]
    else:
        shards = [jnp.concatenate(group, axis=1) for group in groups]
        columns_of = jnp.pad(jnp.stack(gains, axis=1), ((0, 0), (0, GAIN_PAD - 4)))
        shards[2] = jnp.concatenate([shards[2], columns_of], axis=1)
        weights = [
            Gather(packed(part), order, "acsh", sizes, merged) for part, order in zip(shards, orders)
        ]
    small_tables = whole_tiles and span <= 2048 and tok_dev == 128
    if small_tables:
        part_a, part_b, part_c, local_ids, targets, memory_all, head_rows, resid0 = opening(
            "start",
            0,
            weights,
            embedding,
            (target_ids, labels),
            memory.reshape(micro, mem_dev, width),
            head,
            sizes,
        )
    else:
        part_a, part_b, part_c, embed_rows, ids, memory_all = exchange(
            "gather_weights",
            0,
            weights
            + [
                Gather(embedding, "ac", "ac", sizes, "", 20),
                PackedGather(
                    (target_ids, labels),
                    jax.ShapeDtypeStruct((8, 128), jnp.int32),
                    pack_ids,
                    "shc",
                    "shc",
                    sizes,
                    "shc",
                ),
                MemoryGather(memory.reshape(micro, mem_dev, width), sizes),
            ],
        )
    part_a, part_b, part_c = (
        full.reshape(width, count) for full, count in zip((part_a, part_b, part_c), widths)
    )
    memory_all = memory_all.reshape(n_gy * mem_dev, width)
    if small_tables:
        local_ids = local_ids.reshape(tokens)
    else:
        ids = ids[..., : 2 * micro, :seq_dev].reshape(n_gy, 2, 2, micro, seq_dev)
        ids = ids.transpose(2, 3, 1, 0, 4).reshape(2, sizes["s"] * 2, 2, tok_dev)
        ids = lax.dynamic_index_in_dim(ids, place["c"], axis=2, keepdims=False).reshape(2, tokens)

        def local_of(index):
            shard = index // voc_dev
            return jnp.where(shard % n_gy == column, shard // n_gy * voc_dev + index % voc_dev, -1)

        local_ids = local_of(ids[0])
        targets = local_of(ids[1])
    columns = jnp.arange(span, dtype=jnp.int32)

    tok_layout = (sizes["s"], 2, tok_dev, width)
    if not small_tables:
        chosen = (local_ids[:, None] == columns[None, :]).astype(bf16)
        picked_rows = dot(chosen, embed_rows.reshape(span, width)).astype(bf16)
        resid0, head_rows = exchange(
            "rows",
            1,
            [
                Scatter(picked_rows.reshape(tok_layout), "hs", "sh", sizes),
                Gather(head, "ac", "ac", sizes, "", 20),
            ],
        )
    head_rows = head_rows.reshape(span, width)

    plane_lengths = lax.dynamic_slice_in_dim(lengths, 2 * place["a"], 2, axis=1).reshape(-1)
    table = jnp.asarray(distance_table(seq), bf16)
    query_self, own_kv, normed_self, gain_rows = local_kernel(
        "enter",
        enter_kernel,
        [((tok_dev, HD), bf16), ((tok_dev, 2 * HD), bf16), ((tok_dev, width), bf16), ((16, width), f32)],
        [resid0, part_c],
    )
    self_kv_all, mem_kv = exchange(
        "self_keys",
        2,
        [
            Gather(own_kv, "hc", "hc", sizes),
            Work(
                (memory_all, part_b),
                ((n_gy * mem_dev, 2 * HD), bf16),
                project_memory,
                0.5,
                (None, (ff, 2 * HD)),
            ),
        ],
    )
    self_kv_all = self_kv_all.reshape(seq, 2 * HD)
    rows_f32, rows_bf16, rows_heads = ((tok_dev, width), f32), ((tok_dev, width), bf16), ((tok_dev, HD), bf16)
    totals_shape = ((tok_dev, 128), f32)
    (
        attn_self,
        total_self,
        resid1,
        normed_cross,
        query_cross,
        attn_cross,
        total_cross,
        resid2,
        normed_ff,
        gate_up,
        hidden,
        resid3,
        final_rows,
    ) = local_kernel(
        "forward",
        forward_kernel,
        [
            rows_heads,
            totals_shape,
            rows_f32,
            rows_bf16,
            rows_heads,
            rows_heads,
            totals_shape,
            rows_f32,
            rows_bf16,
            ((tok_dev, 2 * ff), f32),
            ((tok_dev, ff), bf16),
            rows_f32,
            rows_bf16,
        ],
        [lengths, query_self, self_kv_all, resid0, gain_rows, table, relative_bias]
        + [mem_kv, part_a, part_b, part_c],
        "svvvvvvaaaa",
        scratch=[pltpu.VMEM(full.shape, bf16) for full in (mem_kv, part_a, part_b, part_c)]
        + [pltpu.SemaphoreType.DMA((4,))],
    )

    if small_tables:
        final_slope, head_part, loss_rows = vocabulary(
            "vocabulary", 3, final_rows, head_rows, targets, lengths, sizes
        )
    else:
        index = jnp.arange(tokens, dtype=jnp.int32)
        position = (2 * (index // tok_dev % 2) + place["c"]) * tok_dev + index % tok_dev
        alive = (position < jnp.repeat(plane_lengths, 2 * tok_dev)).astype(f32)
        (states,) = exchange("final_rows", 3, [Gather(final_rows, "sh", "sh", sizes, merged)])
        states = states.reshape(tokens, width)
        logits = dot_t(states, head_rows)
        highest = jnp.max(logits, axis=1)
        own_total = highest + jnp.log(jnp.sum(jnp.exp(logits - highest[:, None]), axis=1))
        (totals,) = exchange("totals", 4, [DirectGather(own_total.reshape(tokens // 128, 128), sizes)])
        totals = totals.reshape(n_gy, tokens)
        top = jnp.max(totals, axis=0)
        log_total = top + jnp.log(jnp.sum(jnp.exp(totals - top[None]), axis=0))
        hit = columns[None, :] == targets[:, None]
        picked = jnp.sum(jnp.where(hit, logits, 0.0), axis=1)
        slope = jnp.exp(logits - log_total[:, None]) - hit.astype(f32)
        slope = (slope * alive[:, None]).astype(bf16)
        head_part = t_dot(slope, states).astype(bf16)
        final_part = dot(slope, head_rows).astype(bf16)
        (final_slope,) = exchange(
            "final_slopes", 5, [Scatter(final_part.reshape(tok_layout), "hs", "sh", sizes)]
        )
        loss_rows = alive * (jnp.where(column == 0, log_total, 0.0) - picked)
        loss_rows = loss_rows.reshape(tokens // 128, 128)

    (
        part_grad_b,
        gate_up_slope,
        cross_kv_slope,
        part_grad_c,
        query_slope,
        kv_slope,
        grad1,
        norm_grads,
        bias_grad,
    ) = (
        local_kernel(
            "backward",
            backward_kernel,
            [
                ((width, ff + HD), bf16),
                ((tok_dev, 2 * ff), bf16),
                (mem_kv.shape, bf16),
                ((width, 2 * HD), bf16),
                rows_heads,
                ((seq, 2 * HD), bf16),
                rows_f32,
                (gain_rows.shape, f32),
                ((8, 128), f32),
            ],
            [lengths, final_slope, resid3, hidden, gate_up, normed_ff, resid2, attn_cross]
            + [query_cross, total_cross, normed_cross, resid1, attn_self, query_self, self_kv_all]
            + [total_self, gain_rows, table, relative_bias, mem_kv, part_a, part_b, part_c],
            "s" + "v" * 18 + "a" * 4,
            "a" + "v" * 8,
            [pltpu.VMEM(full.shape, bf16) for full in (mem_kv, part_a, part_b, part_c)]
            + [
                pltpu.VMEM((width, ff + HD), bf16),
                pltpu.VMEM((tok_dev, HD), bf16),
                pltpu.SemaphoreType.DMA((4,)),
                pltpu.SemaphoreType.DMA((1,)),
            ],
        )
    )
    kv_slope, grad_a, grad_b, memory_part = exchange(
        "key_slopes",
        6,
        [
            Scatter(kv_slope.reshape(2, 2, tok_dev, 2 * HD), "ch", "hc", sizes, "", bf16),
            Work((normed_ff, gate_up_slope), (part_a.shape, bf16), gate_up_grads, 0.9),
            Work(
                (memory_all, cross_kv_slope, part_grad_b), (part_b.shape, bf16), memory_weight_grads, 0.91
            ),
            Work(
                (cross_kv_slope, part_b),
                (memory_all.shape, bf16),
                memory_slopes,
                0.92,
                (None, (ff, 2 * HD)),
            ),
        ],
    )
    grad0, norm_grads = local_kernel(
        "leave",
        leave_kernel,
        [rows_bf16, (gain_rows.shape, f32)],
        [query_slope, kv_slope, resid0, grad1, gain_rows, norm_grads, part_c],
    )
    slope_gather = Gather(grad0, "sh", "sh", sizes, merged)
    embed_job = [EmbedPart(local_ids.reshape(n_gy, tok_dev), span, slope_gather)] if small_tables else []
    slopes, grad_c, head_grad, *embed_part = exchange(
        "row_slopes",
        7,
        [
            slope_gather,
            Work(
                (query_slope, kv_slope, normed_self, norm_grads, part_grad_c),
                (part_c.shape, bf16),
                self_weight_grads,
                0.5,
            ),
            Scatter(head_part.reshape(sizes["a"], 2, voc_dev, width), "ca", "ac", sizes),
        ]
        + embed_job,
    )
    if small_tables:
        embed_part = embed_part[0]
    else:
        embed_part = t_dot(
            (local_ids[:, None] == columns[None, :]).astype(bf16), slopes.reshape(tokens, width)
        ).astype(bf16)
    sums = (grad_a, grad_b, grad_c)
    device_layout = (sizes["a"], 2, sizes["s"], 2)
    blocks = [part.reshape(device_layout + packed_shape(part, devices)) for part in sums]
    grad_a, grad_b, grad_c, embedding_grad, memory_grad, small = exchange(
        "scatter_weights",
        8,
        [
            Scatter(part, order, "acsh", sizes, merged)
            for part, order in zip(blocks, ways_back)
        ]
        + [
            Scatter(embed_part.reshape(sizes["a"], 2, voc_dev, width), "ca", "ac", sizes),
            MemoryScatter(memory_part.reshape(sizes["s"], 2, mem_dev, width), sizes),
            PackedGather(
                (bias_grad, loss_rows),
                jax.ShapeDtypeStruct((16, 128), f32),
                pack_rows,
                "shac",
                "acsh",
                sizes,
                "ashc",
            ),
        ],
    )
    small = small.reshape(devices, 16, 128)
    memory_grad = memory_grad.reshape(micro, 1, mem_dev, width)
    if whole_tiles:
        pieces = [piece.shape[1] for group in groups for piece in group]
        outs = [
            ((1, 1), f32),
            (memory_grad.shape, f32),
            (embedding_grad.shape, f32),
            (head_grad.shape, f32),
            ((HEADS, BUCKETS), f32),
        ]
        outs += [((rows_dev, count), f32) for count in pieces] + [((1, rows_dev), f32)] * 4
        results = local_kernel(
            "tail",
            tail_kernel,
            outs,
            [lengths, grad_a, grad_b, grad_c, small, memory_grad, embedding_grad, head_grad],
            "s" + "v" * 7,
        )
        loss, memory_grad, embedding_grad, head_grad, bias_total = results[:5]
        loss = loss.reshape(())
        cut = results[5:16]
        gain_out = [gain.reshape(rows_dev) for gain in results[16:]]
    else:
        grad_a, grad_b, grad_c = (
            grad.reshape(rows_dev, count) for grad, count in zip((grad_a, grad_b, grad_c), widths)
        )
        small = jnp.sum(small, axis=0)
        loss = jnp.sum(small[8:]) / jnp.sum(lengths).astype(f32)
        bias_total = small[:HEADS, :BUCKETS]
        cut = []
        for grad, group in zip((grad_a, grad_b, grad_c), groups):
            start = 0
            for piece in group:
                cut.append(grad[:, start : start + piece.shape[1]])
                start += piece.shape[1]
        gain_out = [grad_c[:, 5 * HD + number] for number in range(4)]
    gate_grad, up_grad, down_grad, c_key_grad, c_value_grad, c_out_grad = cut[:6]
    query_grad, key_grad, value_grad, out_grad, c_query_grad = cut[6:]
    return (
        loss,
        memory_grad,
        embedding_grad,
        head_grad,
        gain_out[0],
        query_grad,
        key_grad,
        value_grad,
        out_grad,
        bias_total,
        gain_out[1],
        c_query_grad,
        c_key_grad,
        c_value_grad,
        c_out_grad,
        gain_out[2],
        gate_grad,
        up_grad,
        down_grad,
        gain_out[3],
    )


def packed_shape(part, count):
    rows, columns = part.shape[0] // count, part.shape[1]
    if rows % 16 == 0:
        return (rows, columns)
    return (16, rows * columns // 16)


def solution(mesh):
    placed = (
        P(None, "gx", "gy"),
        P(None, "gx", "gy"),
        P(),
        P(None, "gx", "gy", None),
        P(("gx", "gy"), None),
        P(("gx", "gy"), None),
        P(("gx", "gy")),
        P(("gx", "gy"), None),
        P(("gx", "gy"), None),
        P(("gx", "gy"), None),
        P(("gx", "gy"), None),
        P(),
        P(("gx", "gy")),
        P(("gx", "gy"), None),
        P(("gx", "gy"), None),
        P(("gx", "gy"), None),
        P(("gx", "gy"), None),
        P(("gx", "gy")),
        P(("gx", "gy"), None),
        P(("gx", "gy"), None),
        P(("gx", "gy"), None),
        P(("gx", "gy")),
    )
    return jax.shard_map(
        per_device,
        mesh=mesh,
        in_specs=placed,
        out_specs=(
            P(),
            P(None, "gx", "gy", None),
            P(("gx", "gy"), None),
            P(("gx", "gy"), None),
            P(("gx", "gy")),
            P(("gx", "gy"), None),
            P(("gx", "gy"), None),
            P(("gx", "gy"), None),
            P(("gx", "gy"), None),
            P(),
            P(("gx", "gy")),
            P(("gx", "gy"), None),
            P(("gx", "gy"), None),
            P(("gx", "gy"), None),
            P(("gx", "gy"), None),
            P(("gx", "gy")),
            P(("gx", "gy"), None),
            P(("gx", "gy"), None),
            P(("gx", "gy"), None),
            P(("gx", "gy")),
        ),
        check_vma=False,
    )
```
